32 devices in a mesh: img: 8 (over z, x), seq: 4 (over y, core).
Axes of the slice: x: 2, y: 2, z: 4, core: 2. Of those that a mesh axis runs over, the one named last changes fastest.
Arguments:
- tokens: bfloat16 [16, 680, 1024], P('img', 'seq'), may hold values from -6 to 6
- cotangent: bfloat16 [16, 680, 1024], P('img', 'seq'), may hold values from -6 to 6
- condition: float32 [16, 1024], P('img'), may hold values from -6 to 6
- scale_sizes: int32 [16, 10], P('img'), may hold values from 1 to 256, 680 in all within a row
- mod_weight: float32 [1024, 6144], P(('img', 'seq')), may hold values from -0.1875 to 0.1875
- mod_bias: float32 [6144], P(('img', 'seq')), may hold values from -1.8 to 1.8
- attn_weight: float32 [1024, 3072], P(('img', 'seq')), may hold values from -0.1875 to 0.1875
- query_bias: float32 [1024], P(('img', 'seq')), may hold values from -3 to 3
- value_bias: float32 [1024], P(('img', 'seq')), may hold values from -3 to 3
- out_weight: float32 [1024, 1024], P(('img', 'seq')), may hold values from -0.75 to 0.75
- out_bias: float32 [1024], P(('img', 'seq')), may hold values from -1.8 to 1.8
- expand_weight: float32 [1024, 4096], P(('img', 'seq')), may hold values from -0.1875 to 0.1875
- expand_bias: float32 [4096], P(('img', 'seq')), may hold values from -3 to 3
- shrink_weight: float32 [4096, 1024], P(('img', 'seq')), may hold values from -0.09375 to 0.09375
- shrink_bias: float32 [1024], P(('img', 'seq')), may hold values from -1.8 to 1.8
- log_scale: float32 [16], replicated, may hold values from 2.1 to 3.1
Outputs:
- layer_out: bfloat16 [16, 680, 1024], P('img', 'seq')
- token_grad: bfloat16 [16, 680, 1024], P('img', 'seq')
- condition_grad: float32 [16, 1024], P('img')
- modweight_grad: float32 [1024, 6144], P(('img', 'seq'))
- modbias_grad: float32 [6144], P(('img', 'seq'))
- attnweight_grad: float32 [1024, 3072], P(('img', 'seq'))
- querybias_grad: float32 [1024], P(('img', 'seq'))
- valuebias_grad: float32 [1024], P(('img', 'seq'))
- outweight_grad: float32 [1024, 1024], P(('img', 'seq'))
- outbias_grad: float32 [1024], P(('img', 'seq'))
- expandw_grad: float32 [1024, 4096], P(('img', 'seq'))
- expandb_grad: float32 [4096], P(('img', 'seq'))
- shrinkw_grad: float32 [4096, 1024], P(('img', 'seq'))
- shrinkb_grad: float32 [1024], P(('img', 'seq'))
- logscale_grad: float32 [16], replicated
The draws below stay inside these ranges and needn't reach their ends.
Inputs may be any that keep to these rules, and one draw needn't show every extreme that they name: `scale_sizes`: each row holds 10 scale sizes that sum to 680; the largest is 256.
All inputs are finite; a program needn't handle non-finite values.
Results may differ from the reference program's by a relative error of at most 0.025.
Values may be sent and summed in bfloat16 or wider, within the bound.
A program may use at most 256 MiB of HBM per device.

```python
import math
import jax
import jax.numpy as jnp
import numpy as np
from jax import lax

D = 1024
H = 16
FF = 4096
L = 680
NSCALE = 10
MOST = 256
IMG_GRP = 2
IMAGES = 16


def raised(drawn, own_key, source, target, blocks, factor):
    def block_of(axis_at):
        return (jnp.arange(drawn.shape[axis_at]) // (drawn.shape[axis_at] // blocks)).reshape((-1,) + (1,) * (drawn.ndim - 1 - axis_at))

    near = jax.random.permutation(own_key, blocks)[block_of(target)]
    far = (block_of(target) + blocks // 2) % blocks
    return jnp.where((block_of(source) == near) | (block_of(source) == far), factor * drawn, drawn)


def steps_of(key, extent, shards, smallest, top_value):
    def one(dim, shards_of):
        draws = jax.random.uniform(jax.random.fold_in(jax.random.fold_in(key, 6), dim), (shards_of,), jnp.float32, smallest / len(shards), top_value / len(shards))
        return jnp.repeat(jnp.exp(draws), extent[dim] // shards_of).reshape((-1,) + (1,) * (len(extent) - dim - 1))

    gain = one(*shards[0])
    for cut in shards[1:]:
        gain = gain * one(*cut)
    return gain


def profile(number_of, total, limit, lean):
    portions = [(1 << 20) // math.isqrt(rank ** lean) + 1 for rank in range(2, number_of + 1)]
    spare, given = total - limit - (number_of - 1), [1] * (number_of - 1)
    while spare > 0:
        free = [i for i in range(number_of - 1) if given[i] < limit]
        pool, budget = sum([portions[i] for i in free]), spare
        for i in free:
            more = min(limit - given[i], max(1, budget * portions[i] // pool), spare)
            given[i] = given[i] + more
            spare = spare - more
    return np.array([limit] + given)


def ragged_sizes(key, amount, total, limit, lean):
    if amount == 2:
        one = jax.random.randint(key, (), max(1, total - limit), min(limit, total - 1) + 1)
        return jnp.stack([one, total - one])
    lengths = jnp.asarray(profile(amount, total, limit, lean), jnp.int32)
    couples = (amount - 1) // 2
    donor, taker = lengths[1:1 + 2 * couples:2], lengths[2:2 + 2 * couples:2]
    slack = jnp.minimum(donor - 1, limit - taker)
    moved = jax.random.randint(jax.random.fold_in(key, 1), (couples,), 0, 1 << 20) % (slack + 1)
    lengths = lengths.at[1:1 + 2 * couples:2].set(donor - moved).at[2:2 + 2 * couples:2].set(taker + moved)
    return lengths[jax.random.permutation(jax.random.fold_in(key, 2), amount)]


def noise(key, dims, scale, most, cuts=(), kind=jnp.bfloat16):
    values = scale * jax.random.normal(key, dims, jnp.float32)
    if cuts:
        values = values * steps_of(key, dims, cuts, -0.22, 0.18)
    return jnp.clip(values, -most, most).astype(kind)


def bell_draw_with(rng, extent, scale, most, cuts, heavy, kind=jnp.bfloat16):
    values = scale * jax.random.normal(rng, extent, jnp.float32)
    if cuts:
        values = values * steps_of(rng, extent, cuts, -0.22, 0.18)
    return jnp.clip(raised(values, jax.random.fold_in(rng, 3), *heavy), -most, most).astype(kind)


def setup_inputs(seed: int = 0) -> dict:
    arg_keys = jax.random.split(jax.random.key(seed), 17)
    tokens = bell_draw_with(arg_keys[0], (IMAGES, L, D), 1.0, 6.0, ((0, 8), (1, 4)), (0, 2, 8, 2.0))
    cotangent = bell_draw_with(arg_keys[1], (IMAGES, L, D), 1.0, 6.0, ((0, 8), (1, 4)), (0, 2, 8, 2.0))
    condition = noise(arg_keys[2], (IMAGES, D), 1.0, 6.0, ((0, 8),), jnp.float32)
    scale_sizes = jax.vmap(lambda own: ragged_sizes(own, NSCALE, L, MOST, 2))(jax.random.split(arg_keys[3], IMAGES)).reshape((IMAGES, NSCALE)).astype(jnp.int32)
    mod_weight = noise(arg_keys[4], (D, 6 * D), D ** -0.5, 0.1875, ((0, 32),), jnp.float32)
    mod_bias = noise(arg_keys[5], (6 * D,), 0.3, 1.8, ((0, 32),), jnp.float32)
    attn_weight = noise(arg_keys[6], (D, 3 * D), D ** -0.5, 0.1875, ((0, 32),), jnp.float32)
    query_bias = noise(arg_keys[7], (D,), 0.5, 3.0, ((0, 32),), jnp.float32)
    value_bias = noise(arg_keys[8], (D,), 0.5, 3.0, ((0, 32),), jnp.float32)
    out_weight = noise(arg_keys[9], (D, D), (D // 16) ** -0.5, 0.75, ((0, 32),), jnp.float32)
    out_bias = noise(arg_keys[10], (D,), 0.3, 1.8, ((0, 32),), jnp.float32)
    expand_weight = noise(arg_keys[11], (D, FF), D ** -0.5, 0.1875, ((0, 32),), jnp.float32)
    expand_bias = noise(arg_keys[12], (FF,), 0.5, 3.0, ((0, 32),), jnp.float32)
    shrink_weight = noise(arg_keys[13], (FF, D), FF ** -0.5, 0.09375, ((0, 32),), jnp.float32)
    shrink_bias = noise(arg_keys[14], (D,), 0.3, 1.8, ((0, 32),), jnp.float32)
    log_scale = jnp.clip(jax.random.uniform(arg_keys[15], (H,), jnp.float32, 2.1, 3.1), 2.1, 3.1)
    return dict(tokens=tokens, cotangent=cotangent, condition=condition, scale_sizes=scale_sizes, mod_weight=mod_weight, mod_bias=mod_bias, attn_weight=attn_weight, query_bias=query_bias, value_bias=value_bias, out_weight=out_weight, out_bias=out_bias, expand_weight=expand_weight, expand_bias=expand_bias, shrink_weight=shrink_weight, shrink_bias=shrink_bias, log_scale=log_scale)


@jax.custom_vjp
def low(v):
    return lax.optimization_barrier(v.astype(jnp.bfloat16)).astype(jnp.float32)

@jax.custom_vjp
def low_back(v):
    return v

def low_keep(v):
    return (low(v), None)

def low_pass(kept, grad):
    return (grad,)

def back_keep(v):
    return (v, None)

def back_low(kept, grad):
    return (low(grad),)
low.defvjp(low_keep, low_pass)
low_back.defvjp(back_keep, back_low)
HIGH = lax.Precision.HIGHEST

def normalize(values):
    centered = values - lax.optimization_barrier(jnp.mean(values, axis=-1, keepdims=True))
    return centered * lax.rsqrt(lax.optimization_barrier(jnp.mean(centered * centered, axis=-1, keepdims=True)) + 1e-06)

def unit_rows(values):
    return values * lax.rsqrt(lax.optimization_barrier(jnp.sum(values * values, axis=-1, keepdims=True)) + 1e-06)

def scale_ids(sizes, length):
    ends = jnp.cumsum(sizes, axis=-1).astype(jnp.int32)
    positions = jnp.arange(length, dtype=jnp.int32)
    return lax.optimization_barrier(jnp.sum((positions[None, :, None] >= ends[:, None, :]).astype(jnp.int32), axis=-1)).astype(jnp.int32)

def attend_image(query, keys, values, ids):
    scores = low_back(jnp.einsum('qhd,khd->hqk', query, keys, precision=HIGH))
    visible = ids[None, :] <= ids[:, None]
    masked = jnp.where(visible[None], scores, -1e+30)
    top = lax.optimization_barrier(jnp.max(masked, axis=-1, keepdims=True))
    expo = jnp.exp(masked - top)
    probs = low(expo / lax.optimization_barrier(jnp.sum(expo, axis=-1, keepdims=True)))
    return jnp.einsum('hqk,khd->qhd', probs, values, precision=HIGH)

def layer(params, resid_in, condition, ids):
    mod_weight, mod_bias, attn_weight, query_bias, value_bias, out_weight, out_bias, expand_weight, expand_bias, shrink_weight, shrink_bias, log_scale = params
    mod_weight = low(mod_weight)
    mod_bias = low(mod_bias)
    attn_weight = low(attn_weight)
    query_bias = low(query_bias)
    value_bias = low(value_bias)
    out_weight = low(out_weight)
    out_bias = low(out_bias)
    expand_weight = low(expand_weight)
    expand_bias = low(expand_bias)
    shrink_weight = low(shrink_weight)
    shrink_bias = low(shrink_bias)
    images, length, width = resid_in.shape
    heads = log_scale.shape[0]
    headdim = width // heads
    silu_cond = low(jax.nn.silu(condition))
    modulation = jnp.dot(silu_cond, mod_weight, precision=HIGH) + mod_bias
    gain_attn, gain_mlp, scale_attn, scale_mlp, shift_attn, shift_mlp = jnp.split(modulation[:, None, :], 6, axis=-1)
    attn_input = low(normalize(resid_in) * (1.0 + scale_attn) + shift_attn)
    packed = low_back(jnp.matmul(attn_input, attn_weight, precision=HIGH))
    query_raw = (packed[..., :width] + query_bias).reshape(images, length, heads, headdim)
    key_raw = packed[..., width:2 * width].reshape(images, length, heads, headdim)
    value_raw = packed[..., 2 * width:] + value_bias
    query_low = low_back(low(unit_rows(query_raw) * jnp.exp(log_scale)[:, None]))
    key_low = low_back(low(unit_rows(key_raw)))
    value_low = low_back(low(value_raw)).reshape(images, length, heads, headdim)
    checked = jax.checkpoint(attend_image)
    context = lax.map(lambda item: checked(item[0], item[1], item[2], item[3]), (query_low, key_low, value_low, ids))
    context_low = low_back(low(context.reshape(images, length, width)))
    attn_out = low_back(jnp.matmul(context_low, out_weight, precision=HIGH) + out_bias)
    resid_mid = resid_in + gain_attn * attn_out
    mlp_input = low(normalize(resid_mid) * (1.0 + scale_mlp) + shift_mlp)
    expanded = low_back(jnp.matmul(mlp_input, expand_weight, precision=HIGH) + expand_bias)
    activated = low(jax.nn.gelu(expanded, approximate=True))
    shrunk = low_back(jnp.matmul(activated, shrink_weight, precision=HIGH) + shrink_bias)
    return resid_mid + gain_mlp * shrunk

def reference(tokens, cotangent, condition, scale_sizes, mod_weight, mod_bias, attn_weight, query_bias, value_bias, out_weight, out_bias, expand_weight, expand_bias, shrink_weight, shrink_bias, log_scale):
    group = IMG_GRP
    groups_total = IMAGES // group
    params = (mod_weight, mod_bias, attn_weight, query_bias, value_bias, out_weight, out_bias, expand_weight, expand_bias, shrink_weight, shrink_bias, log_scale)

    def split_groups(array):
        return array.reshape((groups_total, group) + array.shape[1:])
    stacked = (split_groups(tokens.astype(jnp.float32)), split_groups(cotangent.astype(jnp.float32)), split_groups(condition), split_groups(scale_sizes))

    def visit(totals, item):
        resid_in, grad_out, cond_rows, sizes = item
        ids = scale_ids(sizes, L)
        result, pull = jax.vjp(lambda weights, inputs, conds: layer(weights, inputs, conds, ids), params, resid_in, cond_rows)
        grad_params, grad_in, grad_cond = pull(grad_out)
        totals = jax.tree.map(lambda total_part, new_part: total_part + new_part, totals, grad_params)
        return (totals, (result.astype(jnp.bfloat16), grad_in.astype(jnp.bfloat16), grad_cond))
    zeros = jax.tree.map(jnp.zeros_like, params)
    totals, (outputs, grads_in, grads_cond) = lax.scan(visit, zeros, stacked)
    return (outputs.reshape(IMAGES, L, D), grads_in.reshape(IMAGES, L, D), grads_cond.reshape(IMAGES, D), totals[0], totals[1], totals[2], totals[3], totals[4], totals[5], totals[6], totals[7], totals[8], totals[9], totals[10], totals[11])
```

```python
import functools

import jax
import jax.numpy as jnp
from jax import lax
from jax.experimental import pallas as pl
from jax.experimental.pallas import tpu as pltpu
from jax.sharding import PartitionSpec as P

HIGH = lax.Precision.HIGHEST
MESH = pl.DeviceIdType.MESH
bf16 = jnp.bfloat16
f32 = jnp.float32
VM = pltpu.VMEM
LIMIT = 56 << 20


def greet(axis, peers):
    barrier = pltpu.get_barrier_semaphore()
    for peer in peers:
        pl.semaphore_signal(barrier, inc=1, device_id={axis: peer}, device_id_type=MESH)
    pl.semaphore_wait(barrier, len(peers))


def direct_kernel(axis, n, everyone, src_rel, dst_rel, x_ref, out_ref, send_sem, recv_sem):
    me = lax.axis_index(axis)
    greet(axis, [me ^ j for j in range(1, n)])
    copies = []
    for j in range(1, n):
        peer = me ^ j
        copy = pltpu.make_async_remote_copy(
            src_ref=x_ref if everyone else x_ref.at[j if src_rel else peer],
            dst_ref=out_ref.at[j if dst_rel else me],
            send_sem=send_sem.at[j],
            recv_sem=recv_sem.at[j],
            device_id={axis: peer},
            device_id_type=MESH,
        )
        copy.start()
        copies.append(copy)
    own = x_ref[...] if everyone else x_ref[0 if src_rel else me]
    out_ref[0 if dst_rel else me] = own
    for copy in copies:
        copy.wait()


def direct(x, axis, cid, everyone=False, src_rel=False, dst_rel=False):
    n = lax.axis_size(axis)
    shape = ((n,) + x.shape) if everyone else x.shape
    return pl.pallas_call(
        functools.partial(direct_kernel, axis, n, everyone, src_rel, dst_rel),
        out_shape=jax.ShapeDtypeStruct(shape, x.dtype),
        in_specs=[pl.BlockSpec(memory_space=VM)],
        out_specs=pl.BlockSpec(memory_space=VM),
        scratch_shapes=[pltpu.SemaphoreType.DMA((n,)), pltpu.SemaphoreType.DMA((n,))],
        compiler_params=pltpu.CompilerParams(collective_id=cid, has_side_effects=True),
        name=f"direct_{cid}",
    )(x)


def gather_kernel(axis, n, x_ref, out_ref, own_sem, send_sem, recv_sem):
    me = lax.axis_index(axis)
    chunks = x_ref.shape[0]
    outer = n // 2
    greet(axis, [me ^ 1] + [me ^ (2 * o) for o in range(1, outer)])

    def remote(src, block, c, j, peer):
        return pltpu.make_async_remote_copy(
            src_ref=src,
            dst_ref=out_ref.at[block, c],
            send_sem=send_sem.at[j, c],
            recv_sem=recv_sem.at[j, c],
            device_id={axis: peer},
            device_id_type=MESH,
        )

    keep = pltpu.make_async_copy(x_ref, out_ref.at[0], own_sem)
    keep.start()
    sends = []
    for c in range(chunks):
        for o in range(1, outer):
            copy = remote(x_ref.at[c], 2 * o, c, 2 * o, me ^ (2 * o))
            copy.start()
            sends.append(copy)
    near = []
    for c in range(chunks):
        copy = remote(x_ref.at[c], 1, c, 1, me ^ 1)
        copy.start()
        near.append(copy)
    for i, copy in enumerate(sends):
        c, o = divmod(i, outer - 1)
        o += 1
        copy.wait_recv()
        hand = remote(out_ref.at[2 * o, c], 2 * o + 1, c, 2 * o + 1, me ^ 1)
        hand.start()
        near.append(hand)
    for copy in sends:
        copy.wait_send()
    for copy in near:
        copy.wait()
    keep.wait()


def gather_rel(x, axis, cid):
    n = lax.axis_size(axis)
    return pl.pallas_call(
        functools.partial(gather_kernel, axis, n),
        out_shape=jax.ShapeDtypeStruct((n,) + x.shape, x.dtype),
        in_specs=[pl.BlockSpec(memory_space=VM)],
        out_specs=pl.BlockSpec(memory_space=pl.ANY),
        scratch_shapes=[
            pltpu.SemaphoreType.DMA,
            pltpu.SemaphoreType.DMA((n, x.shape[0])),
            pltpu.SemaphoreType.DMA((n, x.shape[0])),
        ],
        compiler_params=pltpu.CompilerParams(
            collective_id=cid, has_side_effects=True, vmem_limit_bytes=LIMIT
        ),
        name=f"gather_{cid}",
    )(x)


def scatter_kernel(axis, n, rel, x_ref, out_ref, near_buf, send_buf, far_buf, s1, r1, s2, r2):
    me = lax.axis_index(axis)
    chunks = x_ref.shape[1]
    outer = n // 2
    greet(axis, [me ^ 1] + [me ^ (2 * o) for o in range(1, outer)])

    def block(j):
        return j if rel else me ^ j

    near = {}
    order = list(range(1, outer)) + [0]
    for o in order:
        for c in range(chunks):
            copy = pltpu.make_async_remote_copy(
                src_ref=x_ref.at[block(2 * o + 1), c],
                dst_ref=near_buf.at[o, c],
                send_sem=s1.at[o, c],
                recv_sem=r1.at[o, c],
                device_id={axis: me ^ 1},
                device_id_type=MESH,
            )
            copy.start()
            near[o, c] = copy
    far = []
    for o in order[:-1]:
        for c in range(chunks):
            near[o, c].wait_recv()
            total = x_ref[block(2 * o), c].astype(f32) + near_buf[o, c].astype(f32)
            send_buf[o, c] = total.astype(send_buf.dtype)
            copy = pltpu.make_async_remote_copy(
                src_ref=send_buf.at[o, c],
                dst_ref=far_buf.at[o, c],
                send_sem=s2.at[o, c],
                recv_sem=r2.at[o, c],
                device_id={axis: me ^ (2 * o)},
                device_id_type=MESH,
            )
            copy.start()
            far.append((o, c, copy))
    for c in range(chunks):
        near[0, c].wait_recv()
        out_ref[c] = x_ref[block(0), c].astype(f32) + near_buf[0, c].astype(f32)
    for o, c, copy in far:
        copy.wait_recv()
        out_ref[c] = out_ref[c] + far_buf[o, c].astype(f32)
    for copy in near.values():
        copy.wait_send()
    for _, _, copy in far:
        copy.wait_send()


def scatter_sum(x, axis, cid, rel):
    n = lax.axis_size(axis)
    inner = x.shape[1:]
    half = (n // 2,) + inner
    sems = pltpu.SemaphoreType.DMA((n // 2, inner[0]))
    return pl.pallas_call(
        functools.partial(scatter_kernel, axis, n, rel),
        out_shape=jax.ShapeDtypeStruct(inner, f32),
        in_specs=[pl.BlockSpec(memory_space=VM)],
        out_specs=pl.BlockSpec(memory_space=VM),
        scratch_shapes=[VM(half, x.dtype), VM(half, x.dtype), VM(half, x.dtype), sems, sems, sems, sems],
        compiler_params=pltpu.CompilerParams(
            collective_id=cid, has_side_effects=True, vmem_limit_bytes=LIMIT
        ),
        name=f"scatter_{cid}",
    )(x)


def half_sums(values, low_half):
    first = jnp.sum(jnp.where(low_half, values, 0.0), axis=-1, keepdims=True)
    second = jnp.sum(jnp.where(low_half, 0.0, values), axis=-1, keepdims=True)
    return jnp.where(low_half, first, second)


def dot(a, b, dims):
    return lax.dot_general(a, b, (dims, ((), ())), preferred_element_type=f32)


def load_heads(p_ref, b_ref, rows):
    both = p_ref[...].reshape(rows, 384)
    query = both[:, :128] + b_ref[0, :, :128]
    key = both[:, 128:256]
    value = both[:, 256:] + b_ref[0, :, 256:]
    low_half = lax.broadcasted_iota(jnp.int32, (rows, 128), 1) < 64
    r_query = lax.rsqrt(half_sums(query * query, low_half) + 1e-06)
    r_key = lax.rsqrt(half_sums(key * key, low_half) + 1e-06)
    return query, key, value, low_half, r_query, r_key


def attend_kernel(p_ref, b_ref, es_ref, sk_ref, sq_ref, o_ref, k_buf, v_buf):
    blocks, _, rows_b, _ = p_ref.shape
    rows = blocks * rows_b
    query, key, value, low_half, r_query, r_key = load_heads(p_ref, b_ref, rows)
    query_low = query * r_query * es_ref[0]
    k_buf[...] = (key * r_key).astype(bf16).reshape(blocks, rows_b, 128)
    v_buf[...] = value.astype(bf16).reshape(blocks, rows_b, 128)
    sid_q = sq_ref[0]
    parts = []
    for h in range(2):
        mine = low_half if h == 0 else jnp.logical_not(low_half)
        q_t = jnp.transpose(jnp.where(mine, query_low, 0.0)).astype(bf16)

        def step(b, carry, q_t=q_t):
            total, acc = carry
            scores = dot(k_buf[b], q_t, ((1,), (0,)))
            expo = jnp.where(sk_ref[0, b] <= sid_q, jnp.exp(scores), 0.0)
            total = total + jnp.sum(expo, axis=0, keepdims=True)
            acc = acc + dot(v_buf[b], expo.astype(bf16), ((0,), (0,)))
            return total, acc

        total, acc = lax.fori_loop(
            0, blocks, step, (jnp.zeros((1, rows), f32), jnp.zeros((128, rows), f32))
        )
        parts.append((acc / total)[64 * h : 64 * h + 64])
    out = jnp.transpose(jnp.concatenate(parts, axis=0))
    o_ref[...] = out.astype(bf16).reshape(o_ref.shape)


def attend_back_kernel(
    p_ref, do_ref, b_ref, es_ref, sk_ref, sq_ref, dp_ref, st_ref, k_buf, v_buf, e_buf, g_buf, dk_buf, dv_buf
):
    blocks, _, rows_b, _ = p_ref.shape
    rows = blocks * rows_b
    query, key, value, low_half, r_query, r_key = load_heads(p_ref, b_ref, rows)
    scale = es_ref[0]
    q_unit = query * r_query
    k_unit = key * r_key
    q_full = q_unit * scale
    k_buf[...] = k_unit.astype(bf16).reshape(blocks, rows_b, 128)
    v_buf[...] = value.astype(bf16).reshape(blocks, rows_b, 128)
    d_out = do_ref[...].reshape(rows, 128).astype(f32)
    sid_q = sq_ref[0]
    parts = []
    for h in range(2):
        mine = low_half if h == 0 else jnp.logical_not(low_half)
        q_f = jnp.where(mine, q_full, 0.0)
        do_f = jnp.where(mine, d_out, 0.0)
        q_h = q_f.astype(bf16)
        do_h = do_f.astype(bf16)
        q_t = jnp.transpose(q_f).astype(bf16)
        do_t = jnp.transpose(do_f).astype(bf16)

        def first(b, carry, q_t=q_t, do_t=do_t):
            total, mixed = carry
            scores = dot(k_buf[b], q_t, ((1,), (0,)))
            expo = jnp.where(sk_ref[0, b] <= sid_q, jnp.exp(scores), 0.0)
            grad = dot(v_buf[b], do_t, ((1,), (0,)))
            e_buf[b] = expo
            g_buf[b] = grad
            total = total + jnp.sum(expo, axis=0, keepdims=True)
            mixed = mixed + jnp.sum(expo * grad, axis=0, keepdims=True)
            return total, mixed

        zero = jnp.zeros((1, rows), f32)
        total, mixed = lax.fori_loop(0, blocks, first, (zero, zero))
        inverse = 1.0 / total
        delta = mixed * inverse

        def second(b, acc, inverse=inverse, delta=delta, q_h=q_h, do_h=do_h, h=h):
            probs = e_buf[b] * inverse
            scores_grad = (probs * (g_buf[b] - delta)).astype(bf16)
            dv = dot(probs.astype(bf16), do_h, ((1,), (0,)))
            dk = dot(scores_grad, q_h, ((1,), (0,)))
            if h == 0:
                dv_buf[b] = dv
                dk_buf[b] = dk
            else:
                dv_buf[b] = dv_buf[b] + dv
                dk_buf[b] = dk_buf[b] + dk
            return acc + dot(k_buf[b], scores_grad, ((0,), (0,)))

        acc = lax.fori_loop(0, blocks, second, jnp.zeros((128, rows), f32))
        parts.append(acc[64 * h : 64 * h + 64])
    dq = jnp.transpose(jnp.concatenate(parts, axis=0)).astype(bf16).astype(f32)
    dk = dk_buf[...].reshape(rows, 128).astype(bf16).astype(f32)
    dv = dv_buf[...].reshape(rows, 128).astype(bf16).astype(f32)
    dq_raw = scale * r_query * (dq - q_unit * half_sums(q_unit * dq, low_half))
    dk_raw = r_key * (dk - k_unit * half_sums(k_unit * dk, low_half))
    together = jnp.concatenate([dq_raw, dk_raw, dv], axis=1).astype(bf16)
    dp_ref[...] = together.reshape(dp_ref.shape)
    sums = [
        jnp.sum(dq_raw, axis=0, keepdims=True),
        jnp.sum(dv, axis=0, keepdims=True),
        jnp.sum(dq * q_full, axis=0, keepdims=True),
        jnp.zeros((5, 128), f32),
    ]
    st_ref[0, 0] = jnp.concatenate(sums, axis=0)


def attention_specs(blocks, rows_b):
    rows = blocks * rows_b
    wide = pl.BlockSpec((blocks, 1, rows_b, 384), lambda g, p: (0, g, 0, p))
    slim = pl.BlockSpec((blocks, 1, rows_b, 128), lambda g, p: (0, g, 0, p))
    rest = [
        pl.BlockSpec((1, 1, 384), lambda g, p: (p, 0, 0)),
        pl.BlockSpec((1, 1, 128), lambda g, p: (p, 0, 0)),
        pl.BlockSpec((1, blocks, rows_b, 1), lambda g, p: (g, 0, 0, 0)),
        pl.BlockSpec((1, 1, rows), lambda g, p: (g, 0, 0)),
    ]
    return wide, slim, rest


def attend(packed, bias, scale, sid_k, sid_q):
    blocks, images, rows_b, width = packed.shape
    pairs = width // 384
    wide, slim, rest = attention_specs(blocks, rows_b)
    return pl.pallas_call(
        attend_kernel,
        grid=(images, pairs),
        out_shape=jax.ShapeDtypeStruct((blocks, images, rows_b, pairs * 128), bf16),
        in_specs=[wide] + rest,
        out_specs=slim,
        scratch_shapes=[VM((blocks, rows_b, 128), bf16), VM((blocks, rows_b, 128), bf16)],
        compiler_params=pltpu.CompilerParams(vmem_limit_bytes=LIMIT),
        name="attend",
    )(packed, bias, scale, sid_k, sid_q)


def attend_back(packed, d_out, bias, scale, sid_k, sid_q):
    blocks, images, rows_b, width = packed.shape
    pairs = width // 384
    rows = blocks * rows_b
    wide, slim, rest = attention_specs(blocks, rows_b)
    return pl.pallas_call(
        attend_back_kernel,
        grid=(images, pairs),
        out_shape=(
            jax.ShapeDtypeStruct(packed.shape, bf16),
            jax.ShapeDtypeStruct((images, pairs, 8, 128), f32),
        ),
        in_specs=[wide, slim] + rest,
        out_specs=(wide, pl.BlockSpec((1, 1, 8, 128), lambda g, p: (g, p, 0, 0))),
        scratch_shapes=[
            VM((blocks, rows_b, 128), bf16),
            VM((blocks, rows_b, 128), bf16),
            VM((blocks, rows_b, rows), f32),
            VM((blocks, rows_b, rows), f32),
            VM((blocks, rows_b, 128), f32),
            VM((blocks, rows_b, 128), f32),
        ],
        compiler_params=pltpu.CompilerParams(vmem_limit_bytes=LIMIT),
        name="attend_back",
    )(packed, d_out, bias, scale, sid_k, sid_q)


def normalize(values):
    centered = values - jnp.mean(values, axis=-1, keepdims=True)
    return centered * lax.rsqrt(jnp.mean(centered * centered, axis=-1, keepdims=True) + 1e-06)


def norm_back(values, grad_rows):
    return jax.vjp(normalize, values)[1](grad_rows)[0]


def gelu_tanh(values):
    return jax.nn.gelu(values, approximate=True)


def pad_to(x, size, axis):
    widths = [(0, 0)] * x.ndim
    widths[axis] = (0, size - x.shape[axis])
    return jnp.pad(x, widths)


def flat_rows(vector):
    size = -(-vector.shape[-1] // 1024) * 1024
    vector = pad_to(vector, size, vector.ndim - 1)
    return vector.reshape(vector.shape[:-1] + (size // 128, 128))


def mm(a, b):
    return jnp.dot(a, b, preferred_element_type=f32)


def mm_nt(a, b):
    return lax.dot_general(a, b, (((1,), (1,)), ((), ())), preferred_element_type=f32)


def mm_tn(a, b):
    return lax.dot_general(a, b, (((0,), (0,)), ((), ())), preferred_element_type=f32)


def body(
    tokens,
    cotangent,
    condition,
    scale_sizes,
    mod_weight,
    mod_bias,
    attn_weight,
    query_bias,
    value_bias,
    out_weight,
    out_bias,
    expand_weight,
    expand_bias,
    shrink_weight,
    shrink_bias,
    log_scale,
):
    images, rows, width = tokens.shape
    heads = log_scale.shape[0]
    headdim = width // heads
    seq_n = lax.axis_size("seq")
    img_n = lax.axis_size("img")
    seq_i = lax.axis_index("seq")
    img_i = lax.axis_index("img")
    rank = img_i * seq_n + seq_i
    ranks = img_n * seq_n
    own = width // ranks
    rows_p = -(-rows // 16) * 16
    dim_l = width // seq_n
    pairs = dim_l // 128
    hidden = expand_bias.shape[0] * ranks
    hid_l = hidden // seq_n
    hid_o = hidden // ranks
    mods = mod_weight.shape[1]
    mod_o = mods // ranks

    attn_cut = (
        attn_weight.astype(bf16)
        .reshape(own, 3, seq_n, pairs, 128)
        .transpose(2, 0, 3, 1, 4)
        .reshape(seq_n, own, 3 * dim_l)
    )
    exp_cut = (
        expand_weight.astype(bf16)
        .reshape(own, img_n, seq_n, hid_o)
        .transpose(2, 0, 1, 3)
        .reshape(seq_n, own, hid_l)
    )
    out_cut = jnp.broadcast_to(out_weight.astype(bf16)[None], (seq_n, own, width))
    cut = direct(jnp.concatenate([attn_cut, exp_cut, out_cut], axis=2), "seq", 1)
    cut = cut.reshape(seq_n * own, 3 * dim_l + hid_l + width)
    attn_w = lax.all_gather(cut[:, : 3 * dim_l], "img", axis=0, tiled=True)
    out_w = lax.all_gather(cut[:, 3 * dim_l + hid_l :], "img", axis=0, tiled=True)
    exp_w = lax.all_gather(cut[:, 3 * dim_l : 3 * dim_l + hid_l], "img", axis=0, tiled=True)
    shr_w = lax.all_gather(shrink_weight.astype(bf16), "img", axis=0, tiled=True)

    silu_cond = jax.nn.silu(condition).astype(bf16)
    small_bias = jnp.concatenate([query_bias, value_bias, out_bias, shrink_bias, expand_bias])
    small = jnp.concatenate([silu_cond.astype(f32).reshape(-1), small_bias.astype(bf16).astype(f32)])
    small_n = small.shape[0]
    small_all = direct(flat_rows(small), "img", 2, everyone=True).reshape(img_n, -1)
    cond_all = small_all[:, : images * width].reshape(img_n * images, width)
    bias_col = small_all[:, images * width : small_n]
    cond_mine = lax.dynamic_slice_in_dim(cond_all, rank * own, own, 1).astype(bf16)
    modw_low = mod_weight.astype(bf16)
    mod_part = mm(cond_mine, modw_low)
    bias_here = lax.dynamic_update_slice_in_dim(
        jnp.zeros((mods,), f32), mod_bias.astype(bf16).astype(f32), rank * mod_o, 0
    )
    mod_part = mod_part + bias_here[None]
    mod_img = direct(mod_part.reshape(img_n, images * mods // 128, 128), "img", 3)
    mod_img = jnp.sum(mod_img, axis=0).reshape(-1)
    mod_send = flat_rows(jnp.concatenate([mod_img, bias_col.reshape(-1)]))
    mod_all = direct(mod_send, "seq", 4, everyone=True).reshape(seq_n, -1)
    modulation = jnp.sum(mod_all[:, : images * mods], axis=0).reshape(images, mods)
    bias_n = bias_col.shape[1]
    bias_all = mod_all[:, images * mods : images * mods + img_n * bias_n]
    bias_all = bias_all.reshape(seq_n, img_n, bias_n).transpose(1, 0, 2)
    q_bias = bias_all[:, :, :own].reshape(width)
    v_bias = bias_all[:, :, own : 2 * own].reshape(width)
    o_bias = bias_all[:, :, 2 * own : 3 * own].reshape(width)
    s_bias = bias_all[:, :, 3 * own : 4 * own].reshape(width)
    e_bias = lax.dynamic_slice_in_dim(bias_all[:, :, 4 * own :], seq_i, 1, 1).reshape(hid_l)
    qb_l = lax.dynamic_slice_in_dim(q_bias, seq_i * dim_l, dim_l, 0).reshape(pairs, 1, 128)
    vb_l = lax.dynamic_slice_in_dim(v_bias, seq_i * dim_l, dim_l, 0).reshape(pairs, 1, 128)
    pair_bias = jnp.concatenate([qb_l, jnp.zeros_like(qb_l), vb_l], axis=2)
    head_scale = jnp.exp(jnp.repeat(log_scale, headdim))
    pair_scale = lax.dynamic_slice_in_dim(head_scale, seq_i * dim_l, dim_l, 0).reshape(pairs, 1, 128)
    gain_attn, gain_mlp, scale_attn, scale_mlp, shift_attn, shift_mlp = jnp.split(
        modulation[:, None, :], 6, axis=-1
    )

    ends = jnp.cumsum(scale_sizes, axis=-1)
    offset = jnp.arange(rows_p, dtype=jnp.int32)
    place = (seq_i ^ jnp.arange(seq_n, dtype=jnp.int32))[:, None] * rows + offset[None]
    sid = jnp.sum((place[None, :, :, None] >= ends[:, None, None, :]).astype(jnp.int32), axis=-1)
    sid_q = sid.reshape(images, 1, seq_n * rows_p)
    sid_k = jnp.where(offset[None, None] < rows, sid, 1 << 20)[..., None]

    resid_in = pad_to(tokens, rows_p, 1).astype(f32)
    grad_out = pad_to(cotangent, rows_p, 1).astype(f32)
    all_rows = seq_n * images * rows_p

    normed_in = normalize(resid_in)
    attn_input = (normed_in * (1.0 + scale_attn) + shift_attn).astype(bf16)
    h1 = gather_rel(attn_input, "seq", 5).reshape(all_rows, width)
    packed = mm(h1, attn_w).reshape(seq_n, images, rows_p, 3 * dim_l)
    context = attend(packed, pair_bias, pair_scale, sid_k, sid_q)
    context = direct(context, "seq", 6, src_rel=True)
    context_low = context.transpose(1, 2, 0, 3).reshape(images * rows_p, width)
    attn_out = (mm(context_low, out_w) + o_bias).reshape(images, rows_p, width)
    resid_mid = resid_in + gain_attn * attn_out
    normed_mid = normalize(resid_mid)
    mlp_input = (normed_mid * (1.0 + scale_mlp) + shift_mlp).astype(bf16)
    h2 = gather_rel(mlp_input, "seq", 7).reshape(all_rows, width)
    expanded = mm(h2, exp_w) + e_bias
    activated = gelu_tanh(expanded).astype(bf16)
    shrunk_part = mm(activated, shr_w).astype(bf16).reshape(seq_n, images, rows_p, width)
    shrunk = scatter_sum(shrunk_part, "seq", 8, True) + s_bias
    layer_out = (resid_mid + gain_mlp * shrunk).astype(bf16)

    grad_gain_mlp = jnp.sum(grad_out * shrunk, axis=1)
    grad_shrunk = (grad_out * gain_mlp).astype(bf16)
    shrb_part = jnp.sum(grad_shrunk.astype(f32), axis=(0, 1))
    df = gather_rel(grad_shrunk, "seq", 9).reshape(all_rows, width)
    shrw_part = mm_tn(activated, df).astype(bf16)
    shrw_own = lax.psum_scatter(shrw_part, "img", scatter_dimension=0, tiled=True).astype(f32)
    grad_act = mm_nt(df, shr_w)
    grad_exp = jax.vjp(gelu_tanh, expanded)[1](grad_act)[0].astype(bf16)
    expb_part = jnp.sum(grad_exp.astype(f32), axis=0)
    expw_part = mm_tn(h2, grad_exp).astype(bf16)
    expw_blk = lax.psum_scatter(expw_part, "img", scatter_dimension=0, tiled=True)
    grad_mlp_part = mm_nt(grad_exp, exp_w).astype(bf16).reshape(seq_n, images, rows_p, width)
    grad_mlp_input = scatter_sum(grad_mlp_part, "seq", 10, True)
    grad_scale_mlp = jnp.sum(grad_mlp_input * normed_mid, axis=1)
    grad_shift_mlp = jnp.sum(grad_mlp_input, axis=1)
    grad_mid = grad_out + norm_back(resid_mid, grad_mlp_input * (1.0 + scale_mlp))
    grad_gain_attn = jnp.sum(grad_mid * attn_out, axis=1)
    grad_attn_out = (grad_mid * gain_attn).astype(bf16)
    outb_part = jnp.sum(grad_attn_out.astype(f32), axis=(0, 1))
    da = grad_attn_out.reshape(images * rows_p, width)
    outw_part = mm_tn(context_low, da).astype(bf16)
    outw_blk = lax.psum_scatter(outw_part, "img", scatter_dimension=0, tiled=True)
    grad_context = mm_nt(da, out_w).astype(bf16)
    grad_context = grad_context.reshape(images, rows_p, seq_n, dim_l).transpose(2, 0, 1, 3)
    grad_context = direct(grad_context, "seq", 11, dst_rel=True)
    grad_packed, sums = attend_back(packed, grad_context, pair_bias, pair_scale, sid_k, sid_q)
    sums = jnp.sum(sums, axis=0)
    qb_part = sums[:, 0].reshape(dim_l)
    vb_part = sums[:, 1].reshape(dim_l)
    logs_part = jnp.sum(sums[:, 2].reshape(dim_l // headdim, headdim), axis=1)
    grad_packed = grad_packed.reshape(all_rows, 3 * dim_l)
    grad_in_part = mm_nt(grad_packed, attn_w).astype(bf16).reshape(seq_n, images, rows_p, width)
    attnw_part = mm_tn(h1, grad_packed).astype(bf16)
    grad_attn_input = scatter_sum(grad_in_part, "seq", 12, True)
    grad_scale_attn = jnp.sum(grad_attn_input * normed_in, axis=1)
    grad_shift_attn = jnp.sum(grad_attn_input, axis=1)
    token_grad = grad_mid + norm_back(resid_in, grad_attn_input * (1.0 + scale_attn))
    token_grad = token_grad.astype(bf16)

    cut_rows = seq_n * own
    attnw_blk = scatter_sum(
        attnw_part.reshape(img_n, seq_n, own, 3 * dim_l), "img", 13, False
    ).astype(bf16)
    back_cut = jnp.concatenate(
        [
            attnw_blk.reshape(seq_n, own, 3 * dim_l),
            expw_blk.reshape(seq_n, own, hid_l),
            outw_blk.reshape(seq_n, own, width),
        ],
        axis=2,
    )
    back_cut = direct(back_cut, "seq", 14).astype(f32)
    attnw_own = (
        back_cut[:, :, : 3 * dim_l]
        .reshape(seq_n, own, pairs, 3, 128)
        .transpose(1, 3, 0, 2, 4)
        .reshape(own, 3 * width)
    )
    expw_own = (
        back_cut[:, :, 3 * dim_l : 3 * dim_l + hid_l]
        .reshape(seq_n, own, img_n, hid_o)
        .transpose(1, 2, 0, 3)
        .reshape(own, hidden)
    )
    outw_own = jnp.sum(back_cut[:, :, 3 * dim_l + hid_l :], axis=0)

    grad_mod = jnp.concatenate(
        [grad_gain_attn, grad_gain_mlp, grad_scale_attn, grad_scale_mlp, grad_shift_attn, grad_shift_mlp],
        axis=-1,
    )
    mine = jnp.concatenate(
        [grad_mod.reshape(-1), shrb_part, outb_part, qb_part, vb_part, logs_part, expb_part]
    )
    seen = direct(flat_rows(mine), "seq", 15, everyone=True).reshape(seq_n, -1)
    at = images * mods
    grad_mod = jnp.sum(seen[:, :at], axis=0)
    shrb_sum = jnp.sum(seen[:, at : at + width], axis=0).reshape(img_n, seq_n, own)
    at += width
    outb_sum = jnp.sum(seen[:, at : at + width], axis=0).reshape(img_n, seq_n, own)
    at += width
    qb_sum = seen[:, at : at + dim_l].reshape(img_n, seq_n, own)
    at += dim_l
    vb_sum = seen[:, at : at + dim_l].reshape(img_n, seq_n, own)
    at += dim_l
    logs_sum = seen[:, at : at + heads // seq_n].reshape(heads)
    bias_mine = jnp.stack([shrb_sum, outb_sum, qb_sum, vb_sum], axis=2)
    bias_mine = lax.dynamic_slice_in_dim(bias_mine, seq_i, 1, 1).reshape(img_n, 4 * own)
    block = jnp.concatenate(
        [
            jnp.broadcast_to(grad_mod[None], (img_n, images * mods)),
            bias_mine,
            expb_part.reshape(img_n, hid_o),
            jnp.broadcast_to(logs_sum[None], (img_n, heads)),
        ],
        axis=1,
    )
    got = direct(flat_rows(block), "img", 16).reshape(img_n, -1)
    at = images * mods
    grad_mod_all = got[:, :at].reshape(img_n * images, mods)
    tail = jnp.sum(got[:, at:], axis=0)
    shrb_own = tail[:own]
    outb_own = tail[own : 2 * own]
    qb_own = tail[2 * own : 3 * own]
    vb_own = tail[3 * own : 4 * own]
    expb_own = tail[4 * own : 4 * own + hid_o]
    logs_total = tail[4 * own + hid_o : 4 * own + hid_o + heads]
    modw_own = lax.dot_general(
        cond_mine.astype(f32), grad_mod_all, (((0,), (0,)), ((), ())), precision=HIGH
    )
    modb_own = lax.dynamic_slice_in_dim(jnp.sum(grad_mod_all, axis=0), rank * mod_o, mod_o, 0)
    grad_silu = lax.dot_general(
        grad_mod_all, modw_low.astype(f32), (((1,), (1,)), ((), ())), precision=HIGH
    )
    grad_silu = direct(flat_rows(grad_silu.reshape(img_n, images * own)), "img", 17)
    grad_silu = direct(grad_silu[:, 0], "seq", 18, everyone=True)
    grad_silu = grad_silu[:, :, : images * own].reshape(seq_n, img_n, images, own)
    grad_silu = grad_silu.transpose(2, 1, 0, 3).reshape(images, width)
    cond_grad = jax.vjp(jax.nn.silu, condition)[1](grad_silu)[0]
    return (
        layer_out[:, :rows],
        token_grad[:, :rows],
        cond_grad,
        modw_own,
        modb_own,
        attnw_own,
        qb_own,
        vb_own,
        outw_own,
        outb_own,
        expw_own,
        expb_own,
        shrw_own,
        shrb_own,
        logs_total,
    )


def solution(mesh):
    both = P(("img", "seq"))
    rows = P(("img", "seq"), None)
    return jax.shard_map(
        body,
        mesh=mesh,
        in_specs=(
            P("img", "seq", None),
            P("img", "seq", None),
            P("img", None),
            P("img", None),
            rows,
            both,
            rows,
            both,
            both,
            rows,
            both,
            rows,
            both,
            rows,
            both,
            P(),
        ),
        out_specs=(
            P("img", "seq", None),
            P("img", "seq", None),
            P("img", None),
            rows,
            both,
            rows,
            both,
            both,
            rows,
            both,
            rows,
            both,
            rows,
            both,
            P(),
        ),
        check_vma=False,
    )
```

```python
import functools

import jax
import jax.numpy as jnp
from jax import lax
from jax.experimental import pallas as pl
from jax.experimental.pallas import tpu as pltpu
from jax.sharding import PartitionSpec as P

HIGH = lax.Precision.HIGHEST
MESH = pl.DeviceIdType.MESH
bf16 = jnp.bfloat16
f32 = jnp.float32
VM = pltpu.VMEM
LIMIT = 56 << 20


class Plan:
    def __init__(self, ins, out, scratch, peers, count, bind, out_space=VM):
        self.ins, self.out, self.out_space = ins, out, out_space
        self.scratch, self.peers, self.count, self.bind = scratch, peers, count, bind


def remote(src, dst, send, recv, axis, peer):
    return pltpu.make_async_remote_copy(
        src_ref=src, dst_ref=dst, send_sem=send, recv_sem=recv, device_id={axis: peer}, device_id_type=MESH
    )


def each(low, high, run):
    def once(i, carry):
        run(i)
        return carry

    lax.fori_loop(low, high, once, 0)


def direct(x, axis, everyone=False, src_rel=False, dst_rel=False):
    n = lax.axis_size(axis)

    def bind(x_ref, out_ref, send, recv):
        me = lax.axis_index(axis)

        def copy(j):
            src = x_ref if everyone else x_ref.at[j if src_rel else me ^ j]
            return remote(src, out_ref.at[j if dst_rel else me], send.at[j], recv.at[j], axis, me ^ j)

        def start():
            for j in range(1, n):
                copy(j).start()
            out_ref[0 if dst_rel else me] = x_ref[...] if everyone else x_ref[0 if src_rel else me]

        def finish():
            for j in range(1, n):
                copy(j).wait()

        return start, None, finish

    shape = ((n,) + x.shape) if everyone else x.shape
    sems = pltpu.SemaphoreType.DMA((n,))
    peers = [(axis, j) for j in range(1, n)]
    return Plan([x], jax.ShapeDtypeStruct(shape, x.dtype), [sems, sems], peers, 0, bind)


def two_level(axis, n):
    return [(axis, 1)] + [(axis, 2 * o) for o in range(1, n // 2)]


def gather(x, axis, rel, inside=False):
    n = lax.axis_size(axis)
    outer = n // 2
    chunks = x.shape[0]

    def bind(x_ref, out_ref, own, send, recv):
        me = lax.axis_index(axis)

        def place(sender, j, c):
            block = j if rel else sender
            return out_ref.at[c, block] if inside else out_ref.at[block, c]

        def keep(c):
            return pltpu.make_async_copy(x_ref.at[c], place(me, 0, c), own.at[c])

        def push(j, c):
            return remote(x_ref.at[c], place(me, j, c), send.at[j, c], recv.at[j, c], axis, me ^ j)

        def hand(j, c):
            far = me ^ j
            return remote(
                place(far, j, c), place(far, j + 1, c), send.at[j + 1, c], recv.at[j + 1, c], axis, me ^ 1
            )

        def start():
            def first(c):
                for o in range(1, outer):
                    push(2 * o, c).start()

            def second(c):
                push(1, c).start()
                keep(c).start()

            each(0, chunks, first)
            each(0, chunks, second)

        def step(c):
            for o in range(1, outer):
                push(2 * o, c).wait_recv()
                hand(2 * o, c).start()

        def finish():
            def last(c):
                for o in range(1, outer):
                    push(2 * o, c).wait_send()
                    hand(2 * o, c).wait()
                push(1, c).wait()
                keep(c).wait()

            each(0, chunks, last)

        return start, step, finish

    sems = pltpu.SemaphoreType.DMA((n, chunks))
    shape = (chunks, n) + x.shape[1:] if inside else (n,) + x.shape
    out = jax.ShapeDtypeStruct(shape, x.dtype)
    scratch = [pltpu.SemaphoreType.DMA((chunks,)), sems, sems]
    return Plan([x], out, scratch, two_level(axis, n), chunks, bind, pl.ANY)


def scatter_sum(x, axis, rel, dtype=jnp.float32, inside=False):
    n = lax.axis_size(axis)
    outer = n // 2
    chunks = x.shape[0 if inside else 1]

    def bind(x_ref, out_ref, near_buf, send_buf, far_buf, s1, r1, s2, r2):
        me = lax.axis_index(axis)

        def part(j, c):
            block = j if rel else me ^ j
            return x_ref.at[c, block] if inside else x_ref.at[block, c]

        def near(o, c):
            return remote(part(2 * o + 1, c), near_buf.at[o, c], s1.at[o, c], r1.at[o, c], axis, me ^ 1)

        def far(o, c):
            return remote(send_buf.at[o, c], far_buf.at[o, c], s2.at[o, c], r2.at[o, c], axis, me ^ (2 * o))

        def start():
            def first(c):
                for o in range(1, outer):
                    near(o, c).start()

            each(0, chunks, first)
            each(0, chunks, lambda c: near(0, c).start())

        def step(c):
            for o in range(1, outer):
                near(o, c).wait_recv()
                total = part(2 * o, c)[...].astype(f32) + near_buf[o, c].astype(f32)
                send_buf[o, c] = total.astype(send_buf.dtype)
                far(o, c).start()

        def finish():
            def last(c):
                near(0, c).wait_recv()
                total = part(0, c)[...].astype(f32) + near_buf[0, c].astype(f32)
                for o in range(1, outer):
                    far(o, c).wait_recv()
                    total = total + far_buf[o, c].astype(f32)
                out_ref[c] = total.astype(dtype)
                for o in range(outer):
                    near(o, c).wait_send()
                for o in range(1, outer):
                    far(o, c).wait_send()

            each(0, chunks, last)

        return start, step, finish

    inner = (chunks,) + x.shape[2:]
    half = VM((outer,) + inner, x.dtype)
    sems = pltpu.SemaphoreType.DMA((outer, chunks))
    out = jax.ShapeDtypeStruct(inner, dtype)
    return Plan([x], out, [half, half, half, sems, sems, sems, sems], two_level(axis, n), chunks, bind)


class Session:
    def __init__(self, plans, more_peers=()):
        self.plans = plans
        self.ins = [x for p in plans for x in p.ins]
        self.outs = [p.out for p in plans]
        self.in_specs = [pl.BlockSpec(memory_space=VM)] * len(self.ins)
        self.out_specs = [pl.BlockSpec(memory_space=p.out_space) for p in plans]
        self.scratch = [scr for p in plans for scr in p.scratch]
        self.peers = sorted({peer for p in plans for peer in p.peers} | set(more_peers))

    def greet(self):
        barrier = pltpu.get_barrier_semaphore()
        for axis, j in self.peers:
            pl.semaphore_signal(barrier, inc=1, device_id={axis: lax.axis_index(axis) ^ j}, device_id_type=MESH)
        pl.semaphore_wait(barrier, len(self.peers))

    def bind(self, ins, outs, scratch):
        at_in = at_scr = 0
        self.bound = []
        for p, out in zip(self.plans, outs):
            mine = ins[at_in : at_in + len(p.ins)]
            own = scratch[at_scr : at_scr + len(p.scratch)]
            self.bound.append((p.count,) + p.bind(*mine, out, *own))
            at_in += len(p.ins)
            at_scr += len(p.scratch)

    def start(self):
        for _, start, _, _ in self.bound:
            start()

    def steps(self, i, total):
        for count, _, step, _ in self.bound:
            if count == total:
                step(i)
            elif count:
                each((i * count) // total, ((i + 1) * count) // total, step)

    def finish(self):
        for _, _, _, finish in self.bound:
            finish()


def params(cid):
    return pltpu.CompilerParams(collective_id=cid, has_side_effects=True, vmem_limit_bytes=LIMIT)


def exchange(cid, *plans):
    session = Session(plans)
    ins, outs = len(session.ins), len(plans)
    turns = max(p.count for p in plans)

    def kernel(*refs):
        session.greet()
        session.bind(refs[:ins], refs[ins : ins + outs], refs[ins + outs :])
        session.start()
        if turns:
            each(0, turns, lambda i: session.steps(i, turns))
        session.finish()

    got = pl.pallas_call(
        kernel,
        out_shape=tuple(session.outs),
        in_specs=session.in_specs,
        out_specs=tuple(session.out_specs),
        scratch_shapes=session.scratch,
        compiler_params=params(cid),
        name=f"exchange_{cid}",
    )(*session.ins)
    return got[0] if len(plans) == 1 else got


def half_sums(values, low_half):
    first = jnp.sum(jnp.where(low_half, values, 0.0), axis=-1, keepdims=True)
    second = jnp.sum(jnp.where(low_half, 0.0, values), axis=-1, keepdims=True)
    return jnp.where(low_half, first, second)


def dot(a, b, dims):
    return lax.dot_general(a, b, (dims, ((), ())), preferred_element_type=f32)


def lanes(start, size):
    return pl.ds(pl.multiple_of(start, 128), size)


def load_heads(p_ref, bias, g, p, rows):
    both = p_ref[:, g, :, lanes(p * 384, 384)].reshape(rows, 384)
    query = both[:, :128] + bias[:, :128]
    key = both[:, 128:256]
    value = both[:, 256:] + bias[:, 256:]
    low_half = lax.broadcasted_iota(jnp.int32, (rows, 128), 1) < 64
    r_query = lax.rsqrt(half_sums(query * query, low_half) + 1e-06)
    r_key = lax.rsqrt(half_sums(key * key, low_half) + 1e-06)
    return query, key, value, low_half, r_query, r_key


def attend(cid, packed, bias, scale, sid_k, sid_q, plans):
    blocks, images, rows_b, wide = packed.shape
    pairs = wide // 384
    rows = blocks * rows_b
    turns = images * pairs
    width = pairs * 128 * blocks
    session = Session(plans, [("seq", j) for j in range(1, blocks)])
    ins, outs = 5 + len(session.ins), 1 + len(plans)

    def kernel(*refs):
        p_ref, b_ref, es_ref, sk_ref, sq_ref = refs[:5]
        o_ref = refs[ins]
        k_buf, v_buf, o_buf, o_send, o_recv = refs[ins + outs : ins + outs + 5]
        me = lax.axis_index("seq")
        session.greet()
        session.bind(refs[5:ins], refs[ins + 1 : ins + outs], refs[ins + outs + 5 :])
        session.start()

        def ship(i, j):
            g, p = i // pairs, i % pairs
            return remote(
                o_buf.at[i, j],
                o_ref.at[g, :, lanes((me * pairs + p) * 128, 128)],
                o_send.at[j, i],
                o_recv.at[j, i],
                "seq",
                me ^ j,
            )

        def turn(i):
            g, p = i // pairs, i % pairs
            query, key, value, low_half, r_query, r_key = load_heads(p_ref, b_ref[p], g, p, rows)
            query_low = query * r_query * es_ref[p]
            k_buf[...] = (key * r_key).astype(bf16).reshape(blocks, rows_b, 128)
            v_buf[...] = value.astype(bf16).reshape(blocks, rows_b, 128)
            sid_q = sq_ref[g]
            parts = []
            for h in range(2):
                mine = low_half if h == 0 else jnp.logical_not(low_half)
                q_t = jnp.transpose(jnp.where(mine, query_low, 0.0)).astype(bf16)

                def step(b, carry, q_t=q_t):
                    total, acc = carry
                    scores = dot(k_buf[b], q_t, ((1,), (0,)))
                    expo = jnp.where(sk_ref[g, b] <= sid_q, jnp.exp(scores), 0.0)
                    total = total + jnp.sum(expo, axis=0, keepdims=True)
                    acc = acc + dot(v_buf[b], expo.astype(bf16), ((0,), (0,)))
                    return total, acc

                total, acc = lax.fori_loop(
                    0, blocks, step, (jnp.zeros((1, rows), f32), jnp.zeros((128, rows), f32))
                )
                parts.append((acc / total)[64 * h : 64 * h + 64])
            out = jnp.transpose(jnp.concatenate(parts, axis=0)).astype(bf16).reshape(blocks, rows_b, 128)
            o_buf[i] = out
            o_ref[g, :, lanes((me * pairs + p) * 128, 128)] = out[0]
            for j in range(1, blocks):
                ship(i, j).start()
            session.steps(i, turns)

        each(0, turns, turn)
        session.finish()

        def last(i):
            for j in range(1, blocks):
                ship(i, j).wait()

        each(0, turns, last)

    full = pl.BlockSpec(memory_space=VM)
    sems = pltpu.SemaphoreType.DMA((blocks, turns))
    return pl.pallas_call(
        kernel,
        out_shape=tuple([jax.ShapeDtypeStruct((images, rows_b, width), bf16)] + session.outs),
        in_specs=[full] * 5 + session.in_specs,
        out_specs=tuple([full] + session.out_specs),
        scratch_shapes=[
            VM((blocks, rows_b, 128), bf16),
            VM((blocks, rows_b, 128), bf16),
            VM((turns, blocks, rows_b, 128), bf16),
            sems,
            sems,
        ]
        + session.scratch,
        compiler_params=params(cid),
        name="attend",
    )(packed, bias, scale, sid_k, sid_q, *session.ins)


def attend_back(cid, packed, d_out, bias, scale, sid_k, sid_q, plans):
    blocks, images, rows_b, wide = packed.shape
    pairs = wide // 384
    rows = blocks * rows_b
    turns = images * pairs
    session = Session(plans, [("seq", j) for j in range(1, blocks)])
    ins, outs = 6 + len(session.ins), 2 + len(plans)

    def kernel(*refs):
        p_ref, do_ref, b_ref, es_ref, sk_ref, sq_ref = refs[:6]
        dp_ref, st_ref = refs[ins : ins + 2]
        k_buf, v_buf, e_buf, g_buf, dk_buf, dv_buf, do_buf, o_send, o_recv = refs[ins + outs : ins + outs + 9]
        me = lax.axis_index("seq")
        session.greet()

        def ship(i, j):
            g, p = i // pairs, i % pairs
            return remote(
                do_ref.at[g, :, lanes(((me ^ j) * pairs + p) * 128, 128)],
                do_buf.at[i, j],
                o_send.at[j, i],
                o_recv.at[j, i],
                "seq",
                me ^ j,
            )

        def send(i):
            for j in range(1, blocks):
                ship(i, j).start()

        each(0, turns, send)
        session.bind(refs[6:ins], refs[ins + 2 : ins + outs], refs[ins + outs + 9 :])
        session.start()

        def turn(i):
            g, p = i // pairs, i % pairs
            query, key, value, low_half, r_query, r_key = load_heads(p_ref, b_ref[p], g, p, rows)
            scale_row = es_ref[p]
            q_unit = query * r_query
            k_unit = key * r_key
            q_full = q_unit * scale_row
            k_buf[...] = k_unit.astype(bf16).reshape(blocks, rows_b, 128)
            v_buf[...] = value.astype(bf16).reshape(blocks, rows_b, 128)
            do_buf[i, 0] = do_ref[g, :, lanes((me * pairs + p) * 128, 128)]
            for j in range(1, blocks):
                ship(i, j).wait_recv()
            d_out = do_buf[i].reshape(rows, 128).astype(f32)
            sid_q = sq_ref[g]
            parts = []
            for h in range(2):
                mine = low_half if h == 0 else jnp.logical_not(low_half)
                q_f = jnp.where(mine, q_full, 0.0)
                do_f = jnp.where(mine, d_out, 0.0)
                q_h = q_f.astype(bf16)
                do_h = do_f.astype(bf16)
                q_t = jnp.transpose(q_f).astype(bf16)
                do_t = jnp.transpose(do_f).astype(bf16)

                def first(b, carry, q_t=q_t, do_t=do_t):
                    total, mixed = carry
                    scores = dot(k_buf[b], q_t, ((1,), (0,)))
                    expo = jnp.where(sk_ref[g, b] <= sid_q, jnp.exp(scores), 0.0)
                    grad = dot(v_buf[b], do_t, ((1,), (0,)))
                    e_buf[b] = expo
                    g_buf[b] = grad
                    total = total + jnp.sum(expo, axis=0, keepdims=True)
                    mixed = mixed + jnp.sum(expo * grad, axis=0, keepdims=True)
                    return total, mixed

                zero = jnp.zeros((1, rows), f32)
                total, mixed = lax.fori_loop(0, blocks, first, (zero, zero))
                inverse = 1.0 / total
                delta = mixed * inverse

                def second(b, acc, inverse=inverse, delta=delta, q_h=q_h, do_h=do_h, h=h):
                    probs = e_buf[b] * inverse
                    scores_grad = (probs * (g_buf[b] - delta)).astype(bf16)
                    dv = dot(probs.astype(bf16), do_h, ((1,), (0,)))
                    dk = dot(scores_grad, q_h, ((1,), (0,)))
                    if h == 0:
                        dv_buf[b] = dv
                        dk_buf[b] = dk
                    else:
                        dv_buf[b] = dv_buf[b] + dv
                        dk_buf[b] = dk_buf[b] + dk
                    return acc + dot(k_buf[b], scores_grad, ((0,), (0,)))

                acc = lax.fori_loop(0, blocks, second, jnp.zeros((128, rows), f32))
                parts.append(acc[64 * h : 64 * h + 64])
            dq = jnp.transpose(jnp.concatenate(parts, axis=0)).astype(bf16).astype(f32)
            dk = dk_buf[...].reshape(rows, 128).astype(bf16).astype(f32)
            dv = dv_buf[...].reshape(rows, 128).astype(bf16).astype(f32)
            dq_raw = scale_row * r_query * (dq - q_unit * half_sums(q_unit * dq, low_half))
            dk_raw = r_key * (dk - k_unit * half_sums(k_unit * dk, low_half))
            together = jnp.concatenate([dq_raw, dk_raw, dv], axis=1).astype(bf16)
            dp_ref[:, g, :, lanes(p * 384, 384)] = together.reshape(blocks, rows_b, 384)
            sums = [
                jnp.sum(dq_raw, axis=0, keepdims=True),
                jnp.sum(dv, axis=0, keepdims=True),
                jnp.sum(dq * q_full, axis=0, keepdims=True),
                jnp.zeros((5, 128), f32),
            ]
            st_ref[i] = jnp.concatenate(sums, axis=0)
            session.steps(i, turns)

        each(0, turns, turn)
        session.finish()

        def last(i):
            for j in range(1, blocks):
                ship(i, j).wait_send()

        each(0, turns, last)

    full = pl.BlockSpec(memory_space=VM)
    sems = pltpu.SemaphoreType.DMA((blocks, turns))
    return pl.pallas_call(
        kernel,
        out_shape=tuple(
            [jax.ShapeDtypeStruct(packed.shape, bf16), jax.ShapeDtypeStruct((turns, 8, 128), f32)] + session.outs
        ),
        in_specs=[full] * 6 + session.in_specs,
        out_specs=tuple([full] * 2 + session.out_specs),
        scratch_shapes=[
            VM((blocks, rows_b, 128), bf16),
            VM((blocks, rows_b, 128), bf16),
            VM((blocks, rows_b, rows), f32),
            VM((blocks, rows_b, rows), f32),
            VM((blocks, rows_b, 128), f32),
            VM((blocks, rows_b, 128), f32),
            VM((turns, blocks, rows_b, 128), bf16),
            sems,
            sems,
        ]
        + session.scratch,
        compiler_params=params(cid),
        name="attend_back",
    )(packed, d_out, bias, scale, sid_k, sid_q, *session.ins)


def normalize(values):
    centered = values - jnp.mean(values, axis=-1, keepdims=True)
    return centered * lax.rsqrt(jnp.mean(centered * centered, axis=-1, keepdims=True) + 1e-06)


def norm_back(values, grad_rows):
    return jax.vjp(normalize, values)[1](grad_rows)[0]


def gelu_tanh(values):
    return jax.nn.gelu(values, approximate=True)


def pad_to(x, size, axis):
    widths = [(0, 0)] * x.ndim
    widths[axis] = (0, size - x.shape[axis])
    return jnp.pad(x, widths)


def flat_rows(vector):
    size = -(-vector.shape[-1] // 1024) * 1024
    vector = pad_to(vector, size, vector.ndim - 1)
    return vector.reshape(vector.shape[:-1] + (size // 128, 128))


def mm(a, b):
    return jnp.dot(a, b, preferred_element_type=f32)


def mm_nt(a, b):
    return lax.dot_general(a, b, (((1,), (1,)), ((), ())), preferred_element_type=f32)


def mm_tn(a, b):
    return lax.dot_general(a, b, (((0,), (0,)), ((), ())), preferred_element_type=f32)


def body(
    tokens,
    cotangent,
    condition,
    scale_sizes,
    mod_weight,
    mod_bias,
    attn_weight,
    query_bias,
    value_bias,
    out_weight,
    out_bias,
    expand_weight,
    expand_bias,
    shrink_weight,
    shrink_bias,
    log_scale,
):
    images, rows, width = tokens.shape
    heads = log_scale.shape[0]
    headdim = width // heads
    seq_n = lax.axis_size("seq")
    img_n = lax.axis_size("img")
    seq_i = lax.axis_index("seq")
    img_i = lax.axis_index("img")
    rank = img_i * seq_n + seq_i
    ranks = img_n * seq_n
    own = width // ranks
    rows_p = -(-rows // 16) * 16
    dim_l = width // seq_n
    pairs = dim_l // 128
    hidden = expand_bias.shape[0] * ranks
    hid_l = hidden // seq_n
    hid_o = hidden // ranks
    mods = mod_weight.shape[1]
    mod_o = mods // ranks

    mod_l = mods // seq_n
    blk = own * seq_n

    attn_cut = (
        attn_weight.astype(bf16)
        .reshape(own, 3, seq_n, pairs, 128)
        .transpose(2, 0, 3, 1, 4)
        .reshape(seq_n, own, 3 * dim_l)
    )
    exp_cut = (
        expand_weight.astype(bf16)
        .reshape(own, img_n, seq_n, hid_o)
        .transpose(2, 0, 1, 3)
        .reshape(seq_n, own, hid_l)
    )
    mod_cut = mod_weight.astype(bf16).reshape(own, seq_n, mod_l).transpose(1, 0, 2)
    silu_cond = jax.nn.silu(condition).astype(bf16).astype(f32)
    small_bias = jnp.concatenate([query_bias, value_bias, out_bias, shrink_bias, expand_bias, mod_bias])
    small_bias = small_bias.astype(bf16).astype(f32)
    bias_n = small_bias.shape[0]
    cond_cut = silu_cond.reshape(images, img_n, blk).transpose(1, 0, 2).reshape(img_n, images * blk)
    small = jnp.concatenate([cond_cut, jnp.broadcast_to(small_bias[None], (img_n, bias_n))], axis=1)
    cut, small_all, out_img = exchange(
        1,
        direct(jnp.concatenate([mod_cut, attn_cut, exp_cut], axis=2), "seq"),
        direct(flat_rows(small), "img"),
        gather(out_weight.astype(bf16)[None], "img", False),
    )
    out_img = out_img.reshape(img_n, own, width)
    cut = cut.reshape(blk, mod_l + 3 * dim_l + hid_l)
    modw_cut = cut[:, :mod_l]
    attn_b = cut[:, mod_l : mod_l + 3 * dim_l]
    exp_b = cut[:, mod_l + 3 * dim_l :]

    def weight_chunks(x):
        step = max(blk // 4, 8)
        return x.reshape(x.shape[:-2] + (blk // step, step, x.shape[-1]))

    def hidden_chunks(x):
        step = max(hid_o // 4, 8)
        return x.reshape(x.shape[:-2] + (hid_o // step, step, x.shape[-1]))

    small_all = small_all.reshape(img_n, -1)
    cond_mine = small_all[:, : images * blk].reshape(img_n * images, blk).astype(bf16)
    bias_col = small_all[:, images * blk : images * blk + bias_n]
    mod_part = mm(cond_mine, modw_cut).reshape(img_n, images * mod_l)
    mod_img, out_w = exchange(2, direct(flat_rows(mod_part), "img"), gather(out_img, "seq", False, True))
    mod_img = jnp.sum(mod_img, axis=0)
    out_w = out_w.reshape(width, width)
    mod_img = mod_img.reshape(-1)[: images * mod_l]
    mod_send = flat_rows(jnp.concatenate([mod_img, bias_col.reshape(-1)]))
    mod_all = exchange(3, direct(mod_send, "seq", everyone=True)).reshape(seq_n, -1)
    modulation = mod_all[:, : images * mod_l].reshape(seq_n, images, mod_l).transpose(1, 0, 2)
    bias_all = mod_all[:, images * mod_l : images * mod_l + img_n * bias_n]
    bias_all = bias_all.reshape(seq_n, img_n, bias_n).transpose(1, 0, 2)
    q_bias = bias_all[:, :, :own].reshape(width)
    v_bias = bias_all[:, :, own : 2 * own].reshape(width)
    o_bias = bias_all[:, :, 2 * own : 3 * own].reshape(width)
    s_bias = bias_all[:, :, 3 * own : 4 * own].reshape(width)
    e_bias = bias_all[:, :, 4 * own : 4 * own + hid_o]
    e_bias = lax.dynamic_slice_in_dim(e_bias, seq_i, 1, 1).reshape(hid_l)
    m_bias = bias_all[:, :, 4 * own + hid_o :].reshape(mods)
    modulation = modulation.reshape(images, mods) + m_bias[None]
    qb_l = lax.dynamic_slice_in_dim(q_bias, seq_i * dim_l, dim_l, 0).reshape(pairs, 1, 128)
    vb_l = lax.dynamic_slice_in_dim(v_bias, seq_i * dim_l, dim_l, 0).reshape(pairs, 1, 128)
    pair_bias = jnp.concatenate([qb_l, jnp.zeros_like(qb_l), vb_l], axis=2)
    head_scale = jnp.exp(jnp.repeat(log_scale, headdim))
    pair_scale = lax.dynamic_slice_in_dim(head_scale, seq_i * dim_l, dim_l, 0).reshape(pairs, 1, 128)
    gain_attn, gain_mlp, scale_attn, scale_mlp, shift_attn, shift_mlp = jnp.split(
        modulation[:, None, :], 6, axis=-1
    )

    ends = jnp.cumsum(scale_sizes, axis=-1)
    offset = jnp.arange(rows_p, dtype=jnp.int32)
    place = (seq_i ^ jnp.arange(seq_n, dtype=jnp.int32))[:, None] * rows + offset[None]
    sid = jnp.sum((place[None, :, :, None] >= ends[:, None, None, :]).astype(jnp.int32), axis=-1)
    sid_q = sid.reshape(images, 1, seq_n * rows_p)
    sid_k = jnp.where(offset[None, None] < rows, sid, 1 << 20)[..., None]

    resid_in = pad_to(tokens, rows_p, 1).astype(f32)
    grad_out = pad_to(cotangent, rows_p, 1).astype(f32)
    local = images * rows_p
    all_rows = seq_n * local

    def chunked(x):
        return x.reshape(x.shape[: x.ndim - 3] + (local // 32, 32, width))

    normed_in = normalize(resid_in)
    attn_input = (normed_in * (1.0 + scale_attn) + shift_attn).astype(bf16)
    h1, attn_w = exchange(5, gather(chunked(attn_input), "seq", True), gather(weight_chunks(attn_b), "img", False))
    h1 = h1.reshape(all_rows, width)
    attn_w = attn_w.reshape(width, 3 * dim_l)
    packed = mm(h1, attn_w).reshape(seq_n, images, rows_p, 3 * dim_l)
    grad_shrunk = (grad_out * gain_mlp).astype(bf16)
    context_low, df, exp_w = attend(
        6,
        packed,
        pair_bias,
        pair_scale,
        sid_k,
        sid_q,
        [gather(chunked(grad_shrunk), "seq", True), gather(weight_chunks(exp_b), "img", False)],
    )
    context_low = context_low.reshape(local, width)
    df = df.reshape(all_rows, width)
    exp_w = exp_w.reshape(width, hid_l)
    attn_out = (mm(context_low, out_w) + o_bias).reshape(images, rows_p, width)
    resid_mid = resid_in + gain_attn * attn_out
    normed_mid = normalize(resid_mid)
    mlp_input = (normed_mid * (1.0 + scale_mlp) + shift_mlp).astype(bf16)
    h2, shr_w = exchange(
        7,
        gather(chunked(mlp_input), "seq", True),
        gather(hidden_chunks(shrink_weight.astype(bf16)), "img", False),
    )
    h2 = h2.reshape(all_rows, width)
    shr_w = shr_w.reshape(hid_l, width)
    expanded = mm(h2, exp_w) + e_bias
    activated = gelu_tanh(expanded).astype(bf16)

    shrb_part = jnp.sum(grad_shrunk.astype(f32), axis=(0, 1))
    grad_act = mm_nt(df, shr_w)
    grad_exp = jax.vjp(gelu_tanh, expanded)[1](grad_act)[0].astype(bf16)
    grad_mlp_part = mm_nt(grad_exp, exp_w).astype(bf16).reshape(seq_n, images, rows_p, width)
    shrw_part = mm_tn(activated, df).astype(bf16).reshape(img_n, hid_o, width)
    grad_mlp_input, shrw_own = exchange(
        10,
        scatter_sum(chunked(grad_mlp_part), "seq", True),
        scatter_sum(hidden_chunks(shrw_part), "img", False),
    )
    grad_mlp_input = grad_mlp_input.reshape(images, rows_p, width)
    shrw_own = shrw_own.reshape(hid_o, width)
    expb_part = jnp.sum(grad_exp.astype(f32), axis=0)
    expw_part = mm_tn(h2, grad_exp).astype(bf16).reshape(img_n, blk, hid_l)
    shrunk_part = mm(activated, shr_w).astype(bf16).reshape(seq_n, images, rows_p, width)

    grad_scale_mlp = jnp.sum(grad_mlp_input * normed_mid, axis=1)
    grad_shift_mlp = jnp.sum(grad_mlp_input, axis=1)
    grad_mid = grad_out + norm_back(resid_mid, grad_mlp_input * (1.0 + scale_mlp))
    grad_gain_attn = jnp.sum(grad_mid * attn_out, axis=1)
    grad_attn_out = (grad_mid * gain_attn).astype(bf16)
    outb_part = jnp.sum(grad_attn_out.astype(f32), axis=(0, 1))
    da = grad_attn_out.reshape(local, width)
    grad_context = mm_nt(da, out_w).astype(bf16)
    grad_context = grad_context.reshape(images, rows_p, width)
    outw_part = mm_tn(context_low, da).astype(bf16).reshape(img_n, seq_n, own, width)
    grad_packed, sums, expw_blk, shrunk, outw_blk = attend_back(
        11,
        packed,
        grad_context,
        pair_bias,
        pair_scale,
        sid_k,
        sid_q,
        [
            scatter_sum(weight_chunks(expw_part), "img", False, bf16),
            scatter_sum(chunked(shrunk_part), "seq", True),
            scatter_sum(outw_part, "seq", False, bf16, True),
        ],
    )
    shrunk = shrunk.reshape(images, rows_p, width) + s_bias
    layer_out = (resid_mid + gain_mlp * shrunk).astype(bf16)
    grad_gain_mlp = jnp.sum(grad_out * shrunk, axis=1)
    sums = jnp.sum(sums.reshape(images, pairs, 8, 128), axis=0)
    qb_part = sums[:, 0].reshape(dim_l)
    vb_part = sums[:, 1].reshape(dim_l)
    logs_part = jnp.sum(sums[:, 2].reshape(dim_l // headdim, headdim), axis=1)
    grad_packed = grad_packed.reshape(all_rows, 3 * dim_l)
    grad_in_part = mm_nt(grad_packed, attn_w).astype(bf16).reshape(seq_n, images, rows_p, width)
    attnw_part = mm_tn(h1, grad_packed).astype(bf16)
    grad_attn_input, attnw_blk, outw_own = exchange(
        12,
        scatter_sum(chunked(grad_in_part), "seq", True),
        scatter_sum(weight_chunks(attnw_part.reshape(img_n, blk, 3 * dim_l)), "img", False, bf16),
        scatter_sum(outw_blk.reshape(img_n, 1, own, width), "img", False),
    )
    outw_own = outw_own.reshape(own, width)
    grad_attn_input = grad_attn_input.reshape(images, rows_p, width)
    grad_scale_attn = jnp.sum(grad_attn_input * normed_in, axis=1)
    grad_shift_attn = jnp.sum(grad_attn_input, axis=1)
    token_grad = grad_mid + norm_back(resid_in, grad_attn_input * (1.0 + scale_attn))
    token_grad = token_grad.astype(bf16)

    grad_mod = jnp.concatenate(
        [grad_gain_attn, grad_gain_mlp, grad_scale_attn, grad_scale_mlp, grad_shift_attn, grad_shift_mlp],
        axis=-1,
    )
    grad_mod = grad_mod.reshape(images, seq_n, mod_l).transpose(1, 0, 2).reshape(seq_n, images * mod_l)
    mine = jnp.concatenate([shrb_part, outb_part, qb_part, vb_part, logs_part])
    mine = jnp.concatenate([grad_mod, jnp.broadcast_to(mine[None], (seq_n, mine.shape[0]))], axis=1)
    seen = exchange(13, direct(flat_rows(mine), "seq")).reshape(seq_n, -1)
    at = images * mod_l
    grad_mod = jnp.sum(seen[:, :at], axis=0)
    shrb_sum = jnp.sum(seen[:, at : at + width], axis=0).reshape(img_n, seq_n, own)
    at += width
    outb_sum = jnp.sum(seen[:, at : at + width], axis=0).reshape(img_n, seq_n, own)
    at += width
    qb_sum = seen[:, at : at + dim_l].reshape(img_n, seq_n, own)
    at += dim_l
    vb_sum = seen[:, at : at + dim_l].reshape(img_n, seq_n, own)
    at += dim_l
    logs_sum = seen[:, at : at + heads // seq_n].reshape(heads)
    bias_mine = jnp.stack([shrb_sum, outb_sum, qb_sum, vb_sum], axis=2)
    bias_mine = lax.dynamic_slice_in_dim(bias_mine, seq_i, 1, 1).reshape(img_n, 4 * own)
    block = jnp.concatenate(
        [
            jnp.broadcast_to(grad_mod[None], (img_n, images * mod_l)),
            bias_mine,
            expb_part.reshape(img_n, hid_o),
            jnp.broadcast_to(logs_sum[None], (img_n, heads)),
        ],
        axis=1,
    )
    got = exchange(14, direct(flat_rows(block), "img")).reshape(img_n, -1)
    at = images * mod_l
    grad_mod_all = got[:, :at].reshape(img_n * images, mod_l)
    tail = jnp.sum(got[:, at:], axis=0)
    shrb_own = tail[:own]
    outb_own = tail[own : 2 * own]
    qb_own = tail[2 * own : 3 * own]
    vb_own = tail[3 * own : 4 * own]
    expb_own = tail[4 * own : 4 * own + hid_o]
    logs_total = tail[4 * own + hid_o : 4 * own + hid_o + heads]

    modw_blk = mm_tn(cond_mine, grad_mod_all.astype(bf16))
    grad_silu = lax.dot_general(
        grad_mod_all, modw_cut.astype(f32), (((1,), (1,)), ((), ())), precision=HIGH
    )
    modb_all = jnp.sum(grad_mod_all, axis=0)
    back_cut = jnp.concatenate(
        [
            modw_blk.astype(bf16).reshape(seq_n, own, mod_l),
            attnw_blk.reshape(seq_n, own, 3 * dim_l),
            expw_blk.reshape(seq_n, own, hid_l),
        ],
        axis=2,
    )
    back_cut, modb_all, grad_silu = exchange(
        15,
        direct(back_cut, "seq"),
        direct(flat_rows(modb_all), "seq", everyone=True),
        direct(flat_rows(grad_silu.reshape(img_n, images * blk)), "img"),
    )
    grad_silu = exchange(16, direct(grad_silu, "seq", everyone=True)).reshape(seq_n, img_n, -1)
    grad_silu = jnp.sum(grad_silu[:, :, : images * blk], axis=0).reshape(img_n, images, blk)
    grad_silu = grad_silu.transpose(1, 0, 2).reshape(images, width)
    cond_grad = jax.vjp(jax.nn.silu, condition)[1](grad_silu)[0]
    back_cut = back_cut.astype(f32)
    modw_own = back_cut[:, :, :mod_l].transpose(1, 0, 2).reshape(own, mods)
    attnw_own = (
        back_cut[:, :, mod_l : mod_l + 3 * dim_l]
        .reshape(seq_n, own, pairs, 3, 128)
        .transpose(1, 3, 0, 2, 4)
        .reshape(own, 3 * width)
    )
    expw_own = (
        back_cut[:, :, mod_l + 3 * dim_l : mod_l + 3 * dim_l + hid_l]
        .reshape(seq_n, own, img_n, hid_o)
        .transpose(1, 2, 0, 3)
        .reshape(own, hidden)
    )
    modb_all = modb_all.reshape(seq_n, -1)[:, :mod_l].reshape(mods)
    modb_own = lax.dynamic_slice_in_dim(modb_all, rank * mod_o, mod_o, 0)
    return (
        layer_out[:, :rows],
        token_grad[:, :rows],
        cond_grad,
        modw_own,
        modb_own,
        attnw_own,
        qb_own,
        vb_own,
        outw_own,
        outb_own,
        expw_own,
        expb_own,
        shrw_own,
        shrb_own,
        logs_total,
    )


def solution(mesh):
    both = P(("img", "seq"))
    rows = P(("img", "seq"), None)
    return jax.shard_map(
        body,
        mesh=mesh,
        in_specs=(
            P("img", "seq", None),
            P("img", "seq", None),
            P("img", None),
            P("img", None),
            rows,
            both,
            rows,
            both,
            both,
            rows,
            both,
            rows,
            both,
            rows,
            both,
            P(),
        ),
        out_specs=(
            P("img", "seq", None),
            P("img", "seq", None),
            P("img", None),
            rows,
            both,
            rows,
            both,
            both,
            rows,
            both,
            rows,
            both,
            rows,
            both,
            P(),
        ),
        check_vma=False,
    )
```

```python
from types import SimpleNamespace

import jax
import jax.numpy as jnp
from jax import lax
from jax.experimental import pallas as pl
from jax.experimental.pallas import tpu as pltpu
from jax.sharding import PartitionSpec as P

HIGH = lax.Precision.HIGHEST
MESH = pl.DeviceIdType.MESH
bf16 = jnp.bfloat16
f32 = jnp.float32
VM = pltpu.VMEM
LIMIT = 56 << 20


class Plan:
    def __init__(self, ins, out, scratch, peers, count, bind, out_space=VM):
        self.ins, self.out, self.out_space = ins, out, out_space
        self.scratch, self.peers, self.count, self.bind = scratch, peers, count, bind
        self.window = None

    def during(self, low, high):
        self.window = (low, high)
        return self


def remote(src, dst, send, recv, axis, peer):
    return pltpu.make_async_remote_copy(
        src_ref=src, dst_ref=dst, send_sem=send, recv_sem=recv, device_id={axis: peer}, device_id_type=MESH
    )


def each(low, high, run):
    def once(i, carry):
        run(i)
        return carry

    lax.fori_loop(low, high, once, 0)


def direct_ops(axis, x_ref, out_ref, send, recv, everyone=False, src_rel=False, dst_rel=False):
    n = lax.axis_size(axis)
    me = lax.axis_index(axis)

    def copy(j):
        src = x_ref if everyone else x_ref.at[j if src_rel else me ^ j]
        return remote(src, out_ref.at[j if dst_rel else me], send.at[j], recv.at[j], axis, me ^ j)

    def start():
        for j in range(1, n):
            copy(j).start()
        out_ref[0 if dst_rel else me] = x_ref[...] if everyone else x_ref[0 if src_rel else me]

    def finish():
        for j in range(1, n):
            copy(j).wait()

    return start, finish


def two_level(axis, n):
    return [(axis, 1)] + [(axis, 2 * o) for o in range(1, n // 2)]


def gather_ops(axis, rel, x_ref, out_ref, own, send, recv, inside=False):
    n = lax.axis_size(axis)
    outer = n // 2
    chunks = x_ref.shape[0]
    me = lax.axis_index(axis)

    def place(sender, j, c):
        block = j if rel else sender
        return out_ref.at[c, block] if inside else out_ref.at[block, c]

    def keep(c):
        return pltpu.make_async_copy(x_ref.at[c], place(me, 0, c), own.at[c])

    def push(j, c):
        return remote(x_ref.at[c], place(me, j, c), send.at[j, c], recv.at[j, c], axis, me ^ j)

    def hand(j, c):
        far = me ^ j
        return remote(place(far, j, c), place(far, j + 1, c), send.at[j + 1, c], recv.at[j + 1, c], axis, me ^ 1)

    def start():
        def first(c):
            for o in range(1, outer):
                push(2 * o, c).start()

        def second(c):
            push(1, c).start()
            if own is not None:
                keep(c).start()

        each(0, chunks, first)
        each(0, chunks, second)

    def step(c):
        for o in range(1, outer):
            push(2 * o, c).wait_recv()
            hand(2 * o, c).start()

    def near():
        each(0, chunks, lambda c: push(1, c).wait_recv())

    def handed(o):
        each(0, chunks, lambda c: hand(2 * o, c).wait_recv())

    def sent():
        def last(c):
            for o in range(1, outer):
                push(2 * o, c).wait_send()
                hand(2 * o, c).wait_send()
            push(1, c).wait_send()
            if own is not None:
                keep(c).wait()

        each(0, chunks, last)

    def finish():
        near()
        for o in range(1, outer):
            handed(o)
        sent()

    return SimpleNamespace(start=start, step=step, near=near, handed=handed, sent=sent, finish=finish)


def gather(x, axis, rel, inside=False):
    n = lax.axis_size(axis)
    chunks = x.shape[0]

    def bind(x_ref, out_ref, own, send, recv):
        return gather_ops(axis, rel, x_ref, out_ref, own, send, recv, inside)

    sems = pltpu.SemaphoreType.DMA((n, chunks))
    shape = (chunks, n) + x.shape[1:] if inside else (n,) + x.shape
    out = jax.ShapeDtypeStruct(shape, x.dtype)
    scratch = [pltpu.SemaphoreType.DMA((chunks,)), sems, sems]
    return Plan([x], out, scratch, two_level(axis, n), chunks, bind, pl.ANY)


def scatter_ops(axis, rel, x_ref, out_ref, near_buf, send_buf, far_buf, s1, r1, s2, r2, inside=False):
    n = lax.axis_size(axis)
    outer = n // 2
    chunks = out_ref.shape[0]
    me = lax.axis_index(axis)

    def part(j, c):
        block = j if rel else me ^ j
        return x_ref.at[c, block] if inside else x_ref.at[block, c]

    def near(o, c):
        return remote(part(2 * o + 1, c), near_buf.at[o, c], s1.at[o, c], r1.at[o, c], axis, me ^ 1)

    def far(o, c):
        return remote(send_buf.at[o, c], far_buf.at[o, c], s2.at[o, c], r2.at[o, c], axis, me ^ (2 * o))

    def start_outer():
        def first(c):
            for o in range(1, outer):
                near(o, c).start()

        each(0, chunks, first)

    def start_inner():
        each(0, chunks, lambda c: near(0, c).start())

    def start():
        start_outer()
        start_inner()

    def step(c):
        for o in range(1, outer):
            near(o, c).wait_recv()
            total = part(2 * o, c)[...].astype(f32) + near_buf[o, c].astype(f32)
            send_buf[o, c] = total.astype(send_buf.dtype)
            far(o, c).start()

    def finish():
        def last(c):
            near(0, c).wait_recv()
            total = part(0, c)[...].astype(f32) + near_buf[0, c].astype(f32)
            for o in range(1, outer):
                far(o, c).wait_recv()
                total = total + far_buf[o, c].astype(f32)
            out_ref[c] = total.astype(out_ref.dtype)
            for o in range(outer):
                near(o, c).wait_send()
            for o in range(1, outer):
                far(o, c).wait_send()

        each(0, chunks, last)

    return SimpleNamespace(
        start=start, start_outer=start_outer, start_inner=start_inner, step=step, finish=finish
    )


def scatter_scratch(n, inner, dtype):
    half = VM((n // 2,) + inner, dtype)
    sems = pltpu.SemaphoreType.DMA((n // 2, inner[0]))
    return [half, half, half, sems, sems, sems, sems]


def scatter_sum(x, axis, rel, dtype=jnp.float32, inside=False):
    n = lax.axis_size(axis)
    chunks = x.shape[0 if inside else 1]
    inner = (chunks,) + x.shape[2:]

    def bind(*refs):
        return scatter_ops(axis, rel, *refs, inside=inside)

    out = jax.ShapeDtypeStruct(inner, dtype)
    return Plan([x], out, scatter_scratch(n, inner, x.dtype), two_level(axis, n), chunks, bind)


class Session:
    def __init__(self, plans, more_peers=()):
        self.plans = plans
        self.ins = [x for p in plans for x in p.ins]
        self.outs = [p.out for p in plans]
        self.in_specs = [pl.BlockSpec(memory_space=VM)] * len(self.ins)
        self.out_specs = [pl.BlockSpec(memory_space=p.out_space) for p in plans]
        self.scratch = [scr for p in plans for scr in p.scratch]
        self.peers = sorted({peer for p in plans for peer in p.peers} | set(more_peers))

    def greet(self):
        barrier = pltpu.get_barrier_semaphore()
        for axis, j in self.peers:
            pl.semaphore_signal(barrier, inc=1, device_id={axis: lax.axis_index(axis) ^ j}, device_id_type=MESH)
        pl.semaphore_wait(barrier, len(self.peers))

    def bind(self, ins, outs, scratch):
        at_in = at_scr = 0
        self.bound = []
        for p, out in zip(self.plans, outs):
            mine = ins[at_in : at_in + len(p.ins)]
            own = scratch[at_scr : at_scr + len(p.scratch)]
            self.bound.append((p.count, p.window, p.bind(*mine, out, *own)))
            at_in += len(p.ins)
            at_scr += len(p.scratch)

    def start(self):
        for _, _, ops in self.bound:
            ops.start()

    def steps(self, i, total):
        for count, window, ops in self.bound:
            low, high = window or (0, total)
            span = high - low

            def some(ops=ops, count=count, low=low, span=span):
                if count == span:
                    ops.step(i - low)
                else:
                    each(((i - low) * count) // span, ((i - low + 1) * count) // span, ops.step)

            if not count:
                continue
            if span == total:
                some()
            else:
                pl.when(jnp.logical_and(i >= low, i < high))(some)

    def finish(self):
        for _, _, ops in self.bound:
            ops.finish()


def everyone_else(*axes):
    return [(axis, j) for axis in axes for j in range(1, lax.axis_size(axis))]


def pairs_of_sems(*axes):
    return [pltpu.SemaphoreType.DMA((lax.axis_size(axis),)) for axis in axes for _ in range(2)]


def params(cid):
    return pltpu.CompilerParams(collective_id=cid, has_side_effects=True, vmem_limit_bytes=LIMIT)


def opening(cid, mod_cut, attn_cut, exp_cut, small, images, plans):
    seq_n, own, mod_l = mod_cut.shape
    img_n, rows, _ = small.shape
    head = seq_n * images
    tiles = mod_l // 128
    slim = -(-tiles * images // 8) * 8
    session = Session(plans)
    session.peers = everyone_else("img", "seq")
    ins, outs = 4 + len(session.ins), 6 + len(plans)

    def kernel(*refs):
        mod_ref, attn_ref, exp_ref, small_ref = refs[:4]
        modo_ref, bias_ref, lhs_ref, modw_ref, attnw_ref, expw_ref = refs[ins : ins + 6]
        small_all, part_buf, part_all, sum_buf = refs[ins + outs : ins + outs + 4]
        sems = refs[ins + outs + 4 : ins + outs + 18]
        session.greet()
        small_go, small_end = direct_ops("img", small_ref, small_all, *sems[:2])
        mod_go, mod_end = direct_ops("seq", mod_ref, modw_ref, *sems[2:4])
        attn_go, attn_end = direct_ops("seq", attn_ref, attnw_ref, *sems[4:6])
        exp_go, exp_end = direct_ops("seq", exp_ref, expw_ref, *sems[12:14])
        session.bind(refs[4:ins], refs[ins + 6 : ins + outs], refs[ins + outs + 18 :])
        small_go()
        mod_go()
        attn_go()
        exp_go()
        session.start()
        part_buf[...] = jnp.zeros_like(part_buf)
        small_end()
        bias_go, bias_end = direct_ops("seq", small_all.at[:, head:], bias_ref, *sems[6:8], everyone=True)
        bias_go()
        for i in range(img_n):
            for q in range(seq_n):
                lhs_ref[q, i * images : (i + 1) * images] = small_all[i, q * images : (q + 1) * images]
        mod_end()
        part = jnp.zeros((img_n * images, mod_l), f32)
        for q in range(seq_n):
            part = part + dot(lhs_ref[q][:, :own].astype(bf16), modw_ref[q], ((1,), (0,)))
        for i in range(img_n):
            for t in range(tiles):
                part_buf[i, t * images : (t + 1) * images] = part[
                    i * images : (i + 1) * images, t * 128 : (t + 1) * 128
                ]
        part_go, part_end = direct_ops("img", part_buf, part_all, *sems[8:10])
        part_go()
        session.steps(0, 1)
        part_end()
        total = part_all[0]
        for i in range(1, img_n):
            total = total + part_all[i]
        sum_buf[...] = total
        sum_go, sum_end = direct_ops("seq", sum_buf, modo_ref, *sems[10:12], everyone=True)
        sum_go()
        bias_end()
        sum_end()
        attn_end()
        exp_end()
        session.finish()

    full = pl.BlockSpec(memory_space=VM)
    return pl.pallas_call(
        kernel,
        out_shape=tuple(
            [
                jax.ShapeDtypeStruct((seq_n, slim, 128), f32),
                jax.ShapeDtypeStruct((seq_n, img_n, rows - head, 128), f32),
                jax.ShapeDtypeStruct((seq_n, img_n * images, 128), f32),
                jax.ShapeDtypeStruct(mod_cut.shape, bf16),
                jax.ShapeDtypeStruct(attn_cut.shape, bf16),
                jax.ShapeDtypeStruct(exp_cut.shape, bf16),
            ]
            + session.outs
        ),
        in_specs=[full] * 4 + session.in_specs,
        out_specs=tuple([full] * 6 + session.out_specs),
        scratch_shapes=[
            VM(small.shape, f32),
            VM((img_n, slim, 128), f32),
            VM((img_n, slim, 128), f32),
            VM((slim, 128), f32),
        ]
        + pairs_of_sems("img", "seq", "seq", "seq", "img", "seq", "seq")
        + session.scratch,
        compiler_params=params(cid),
        name="opening",
    )(mod_cut, attn_cut, exp_cut, small, *session.ins)


def closing(cid, mine, expb, lhs, modw, back, images, pairs):
    seq_n, own, mod_l = modw.shape
    img_n = expb.shape[0]
    rows = mine.shape[1]
    head = seq_n * images
    tiles = mod_l // 128
    slim = -(-tiles * images // 8) * 8
    share = img_n // seq_n
    cut = back.shape[2]
    dim_l = pairs * 128
    width = dim_l * seq_n
    hid_l = cut - 3 * dim_l
    hid_o = hid_l // img_n
    aligned = hid_o % 128 == 0
    flat = -(-tiles // 8) * 8

    def kernel(
        mine_ref, expb_ref, lhs_ref, modw_ref, back_ref,
        modw_own, attn_own, exp_own, bias_ref, modb_ref, cond_ref,
        seen, block, got, dd, mw_send, mw_recv, mb_send, gs_send, gs_all, gs_seen, back_all, *sems
    ):
        barrier = Session([], everyone_else("img", "seq"))
        barrier.greet()
        mine_go, mine_end = direct_ops("seq", mine_ref, seen, *sems[:2])
        back_go, back_end = direct_ops("seq", back_ref, back_all, *sems[2:4])
        mine_go()
        back_go()
        block[...] = jnp.zeros_like(block)
        gs_send[...] = jnp.zeros_like(gs_send)
        mb_send[...] = jnp.zeros_like(mb_send)
        mine_end()
        total = seen[0]
        for q in range(1, seq_n):
            total = total + seen[q]
        at = slim + 2 * img_n
        for i in range(img_n):
            block[i, :slim] = total[:slim]
            block[i, slim : slim + 1] = total[slim + i : slim + i + 1]
            block[i, slim + 1 : slim + 2] = total[slim + img_n + i : slim + img_n + i + 1]
            row = at + 8 + i % share
            block[i, slim + 2 : slim + 3] = seen[i // share, row : row + 1]
            block[i, slim + 3 : slim + 4] = seen[i // share, row + share : row + share + 1]
            block[i, slim + 4 : slim + 5] = expb_ref[i : i + 1]
            block[i, slim + 5 : slim + 6] = total[at : at + 1]
        img_go, img_end = direct_ops("img", block, got, *sems[4:6])
        img_go()
        back_end()
        for q in range(seq_n):
            for p in range(pairs):
                for k in range(3):
                    to = k * width + q * dim_l + p * 128
                    at_c = p * 384 + k * 128
                    attn_own[:, to : to + 128] = back_all[q, :, at_c : at_c + 128].astype(f32)
            if aligned:
                for i in range(img_n):
                    to = (i * seq_n + q) * hid_o
                    at_c = 3 * dim_l + i * hid_o
                    exp_own[:, to : to + hid_o] = back_all[q, :, at_c : at_c + hid_o].astype(f32)
            else:
                exp_own[:, q * hid_l : (q + 1) * hid_l] = back_all[q, :, 3 * dim_l :].astype(f32)
        img_end()
        sums = got[0]
        for i in range(1, img_n):
            sums = sums + got[i]
        bias_ref[...] = sums[slim:]
        for t in range(tiles):
            mb_send[t : t + 1] = jnp.sum(sums[t * images : (t + 1) * images], axis=0, keepdims=True)
            for i in range(img_n):
                dd[i * images : (i + 1) * images, t * 128 : (t + 1) * 128] = got[i, t * images : (t + 1) * images]
        grad = dd[...]
        high = grad.astype(bf16)
        low = (grad - high.astype(f32)).astype(bf16)
        for q in range(seq_n):
            out = dot(high, modw_ref[q], ((1,), (1,))) + dot(low, modw_ref[q], ((1,), (1,)))
            for i in range(img_n):
                gs_send[i, q * images : (q + 1) * images, :own] = out[i * images : (i + 1) * images]
        gs_go, gs_end = direct_ops("img", gs_send, gs_all, *sems[6:8])
        gs_go()
        for q in range(seq_n):
            mw_send[q] = dot(lhs_ref[q][:, :own].astype(bf16), high, ((0,), (0,))).astype(bf16)
        mb_go, mb_end = direct_ops("seq", mb_send, modb_ref, *sems[10:12], everyone=True)
        mb_go()
        gs_end()
        all_go, all_end = direct_ops("seq", gs_all, gs_seen, *sems[12:14], everyone=True)
        all_go()
        mw_go, mw_end = direct_ops("seq", mw_send, mw_recv, *sems[8:10])
        mw_go()
        mb_end()
        all_end()
        out = gs_seen[0]
        for q in range(1, seq_n):
            out = out + gs_seen[q]
        cond_ref[...] = out
        mw_end()
        for q in range(seq_n):
            modw_own[:, q * mod_l : (q + 1) * mod_l] = mw_recv[q].astype(f32)

    full = pl.BlockSpec(memory_space=VM)
    got = pl.pallas_call(
        kernel,
        out_shape=(
            jax.ShapeDtypeStruct((own, mod_l * seq_n), f32),
            jax.ShapeDtypeStruct((own, 3 * width), f32),
            jax.ShapeDtypeStruct((own, hid_l * seq_n), f32),
            jax.ShapeDtypeStruct((8, 128), f32),
            jax.ShapeDtypeStruct((seq_n, flat, 128), f32),
            jax.ShapeDtypeStruct((img_n, head, 128), f32),
        ),
        in_specs=[full] * 5,
        out_specs=(full,) * 6,
        scratch_shapes=[
            VM((seq_n, rows, 128), f32),
            VM((img_n, slim + 8, 128), f32),
            VM((img_n, slim + 8, 128), f32),
            VM((img_n * images, mod_l), f32),
            VM((seq_n, own, mod_l), bf16),
            VM((seq_n, own, mod_l), bf16),
            VM((flat, 128), f32),
            VM((img_n, head, 128), f32),
            VM((img_n, head, 128), f32),
            VM((seq_n, img_n, head, 128), f32),
            VM(back.shape, bf16),
        ]
        + pairs_of_sems("seq", "seq", "img", "img", "seq", "seq", "seq"),
        compiler_params=params(cid),
        name="closing",
    )(mine, expb, lhs, modw, back)
    got = list(got)
    if not aligned:
        got[2] = got[2].reshape(own, seq_n, img_n, hid_o).transpose(0, 2, 1, 3).reshape(own, hid_l * seq_n)
    return got


def exchange(cid, turns, *plans):
    session = Session(plans)
    ins, outs = len(session.ins), len(plans)

    def kernel(*refs):
        session.greet()
        session.bind(refs[:ins], refs[ins : ins + outs], refs[ins + outs :])
        session.start()
        each(0, turns, lambda i: session.steps(i, turns))
        session.finish()

    got = pl.pallas_call(
        kernel,
        out_shape=tuple(session.outs),
        in_specs=session.in_specs,
        out_specs=tuple(session.out_specs),
        scratch_shapes=session.scratch,
        compiler_params=params(cid),
        name=f"exchange_{cid}",
    )(*session.ins)
    return got[0] if len(plans) == 1 else got


def half_sums(values, low_half):
    first = jnp.sum(jnp.where(low_half, values, 0.0), axis=-1, keepdims=True)
    second = jnp.sum(jnp.where(low_half, 0.0, values), axis=-1, keepdims=True)
    return jnp.where(low_half, first, second)


def dot(a, b, dims):
    return lax.dot_general(a, b, (dims, ((), ())), preferred_element_type=f32)


def lanes(start, size):
    return pl.ds(pl.multiple_of(start, 128), size)


def load_heads(p_ref, bias, g, p, rows):
    both = p_ref[:, g, :, lanes(p * 384, 384)].reshape(rows, 384)
    query = both[:, :128] + bias[:, :128]
    key = both[:, 128:256]
    value = both[:, 256:] + bias[:, 256:]
    low_half = lax.broadcasted_iota(jnp.int32, (rows, 128), 1) < 64
    r_query = lax.rsqrt(half_sums(query * query, low_half) + 1e-06)
    r_key = lax.rsqrt(half_sums(key * key, low_half) + 1e-06)
    return query, key, value, low_half, r_query, r_key


def attend(cid, packed, bias, scale, sid_k, sid_q, plans):
    blocks, images, rows_b, wide = packed.shape
    pairs = wide // 384
    rows = blocks * rows_b
    turns = images * pairs
    width = pairs * 128 * blocks
    session = Session(plans, [("seq", j) for j in range(1, blocks)])
    ins, outs = 5 + len(session.ins), 1 + len(plans)

    def kernel(*refs):
        p_ref, b_ref, es_ref, sk_ref, sq_ref = refs[:5]
        o_ref = refs[ins]
        k_buf, v_buf, o_buf, o_send, o_recv = refs[ins + outs : ins + outs + 5]
        me = lax.axis_index("seq")
        session.greet()
        session.bind(refs[5:ins], refs[ins + 1 : ins + outs], refs[ins + outs + 5 :])
        session.start()

        def ship(i, j):
            g, p = i // pairs, i % pairs
            return remote(
                o_buf.at[i, j],
                o_ref.at[g, :, lanes((me * pairs + p) * 128, 128)],
                o_send.at[j, i],
                o_recv.at[j, i],
                "seq",
                me ^ j,
            )

        def turn(i):
            g, p = i // pairs, i % pairs
            query, key, value, low_half, r_query, r_key = load_heads(p_ref, b_ref[p], g, p, rows)
            query_low = query * r_query * es_ref[p]
            k_buf[...] = (key * r_key).astype(bf16).reshape(blocks, rows_b, 128)
            v_buf[...] = value.astype(bf16).reshape(blocks, rows_b, 128)
            sid_q = sq_ref[g]
            parts = []
            for h in range(2):
                mine = low_half if h == 0 else jnp.logical_not(low_half)
                q_t = jnp.transpose(jnp.where(mine, query_low, 0.0)).astype(bf16)

                def step(b, carry, q_t=q_t):
                    total, acc = carry
                    scores = dot(k_buf[b], q_t, ((1,), (0,)))
                    expo = jnp.where(sk_ref[g, b] <= sid_q, jnp.exp(scores), 0.0)
                    total = total + jnp.sum(expo, axis=0, keepdims=True)
                    acc = acc + dot(v_buf[b], expo.astype(bf16), ((0,), (0,)))
                    return total, acc

                total, acc = lax.fori_loop(
                    0, blocks, step, (jnp.zeros((1, rows), f32), jnp.zeros((128, rows), f32))
                )
                parts.append((acc / total)[64 * h : 64 * h + 64])
            out = jnp.transpose(jnp.concatenate(parts, axis=0)).astype(bf16).reshape(blocks, rows_b, 128)
            o_buf[i] = out
            o_ref[g, :, lanes((me * pairs + p) * 128, 128)] = out[0]
            for j in range(1, blocks):
                ship(i, j).start()
            session.steps(i, turns)

        each(0, turns, turn)
        session.finish()

        def last(i):
            for j in range(1, blocks):
                ship(i, j).wait()

        each(0, turns, last)

    full = pl.BlockSpec(memory_space=VM)
    sems = pltpu.SemaphoreType.DMA((blocks, turns))
    return pl.pallas_call(
        kernel,
        out_shape=tuple([jax.ShapeDtypeStruct((images, rows_b, width), bf16)] + session.outs),
        in_specs=[full] * 5 + session.in_specs,
        out_specs=tuple([full] + session.out_specs),
        scratch_shapes=[
            VM((blocks, rows_b, 128), bf16),
            VM((blocks, rows_b, 128), bf16),
            VM((turns, blocks, rows_b, 128), bf16),
            sems,
            sems,
        ]
        + session.scratch,
        compiler_params=params(cid),
        name="attend",
    )(packed, bias, scale, sid_k, sid_q, *session.ins)


def attend_back(cid, packed, d_out, bias, scale, sid_k, sid_q, plans):
    blocks, images, rows_b, wide = packed.shape
    pairs = wide // 384
    rows = blocks * rows_b
    turns = images * pairs
    session = Session(plans, [("seq", j) for j in range(1, blocks)])
    ins, outs = 6 + len(session.ins), 2 + len(plans)

    def kernel(*refs):
        p_ref, do_ref, b_ref, es_ref, sk_ref, sq_ref = refs[:6]
        dp_ref, st_ref = refs[ins : ins + 2]
        k_buf, v_buf, e_buf, g_buf, dk_buf, dv_buf, do_buf, o_send, o_recv = refs[ins + outs : ins + outs + 9]
        me = lax.axis_index("seq")
        session.greet()

        def ship(i, j):
            g, p = i // pairs, i % pairs
            return remote(
                do_ref.at[g, :, lanes(((me ^ j) * pairs + p) * 128, 128)],
                do_buf.at[i, j],
                o_send.at[j, i],
                o_recv.at[j, i],
                "seq",
                me ^ j,
            )

        def send(i):
            for j in range(1, blocks):
                ship(i, j).start()

        each(0, turns, send)
        session.bind(refs[6:ins], refs[ins + 2 : ins + outs], refs[ins + outs + 9 :])
        session.start()

        def turn(i):
            g, p = i // pairs, i % pairs
            query, key, value, low_half, r_query, r_key = load_heads(p_ref, b_ref[p], g, p, rows)
            scale_row = es_ref[p]
            q_unit = query * r_query
            k_unit = key * r_key
            q_full = q_unit * scale_row
            k_buf[...] = k_unit.astype(bf16).reshape(blocks, rows_b, 128)
            v_buf[...] = value.astype(bf16).reshape(blocks, rows_b, 128)
            do_buf[i, 0] = do_ref[g, :, lanes((me * pairs + p) * 128, 128)]
            for j in range(1, blocks):
                ship(i, j).wait_recv()
            d_out = do_buf[i].reshape(rows, 128).astype(f32)
            sid_q = sq_ref[g]
            parts = []
            for h in range(2):
                mine = low_half if h == 0 else jnp.logical_not(low_half)
                q_f = jnp.where(mine, q_full, 0.0)
                do_f = jnp.where(mine, d_out, 0.0)
                q_h = q_f.astype(bf16)
                do_h = do_f.astype(bf16)
                q_t = jnp.transpose(q_f).astype(bf16)
                do_t = jnp.transpose(do_f).astype(bf16)

                def first(b, carry, q_t=q_t, do_t=do_t):
                    total, mixed = carry
                    scores = dot(k_buf[b], q_t, ((1,), (0,)))
                    expo = jnp.where(sk_ref[g, b] <= sid_q, jnp.exp(scores), 0.0)
                    grad = dot(v_buf[b], do_t, ((1,), (0,)))
                    e_buf[b] = expo
                    g_buf[b] = grad
                    total = total + jnp.sum(expo, axis=0, keepdims=True)
                    mixed = mixed + jnp.sum(expo * grad, axis=0, keepdims=True)
                    return total, mixed

                zero = jnp.zeros((1, rows), f32)
                total, mixed = lax.fori_loop(0, blocks, first, (zero, zero))
                inverse = 1.0 / total
                delta = mixed * inverse

                def second(b, acc, inverse=inverse, delta=delta, q_h=q_h, do_h=do_h, h=h):
                    probs = e_buf[b] * inverse
                    scores_grad = (probs * (g_buf[b] - delta)).astype(bf16)
                    dv = dot(probs.astype(bf16), do_h, ((1,), (0,)))
                    dk = dot(scores_grad, q_h, ((1,), (0,)))
                    if h == 0:
                        dv_buf[b] = dv
                        dk_buf[b] = dk
                    else:
                        dv_buf[b] = dv_buf[b] + dv
                        dk_buf[b] = dk_buf[b] + dk
                    return acc + dot(k_buf[b], scores_grad, ((0,), (0,)))

                acc = lax.fori_loop(0, blocks, second, jnp.zeros((128, rows), f32))
                parts.append(acc[64 * h : 64 * h + 64])
            dq = jnp.transpose(jnp.concatenate(parts, axis=0)).astype(bf16).astype(f32)
            dk = dk_buf[...].reshape(rows, 128).astype(bf16).astype(f32)
            dv = dv_buf[...].reshape(rows, 128).astype(bf16).astype(f32)
            dq_raw = scale_row * r_query * (dq - q_unit * half_sums(q_unit * dq, low_half))
            dk_raw = r_key * (dk - k_unit * half_sums(k_unit * dk, low_half))
            together = jnp.concatenate([dq_raw, dk_raw, dv], axis=1).astype(bf16)
            dp_ref[:, g, :, lanes(p * 384, 384)] = together.reshape(blocks, rows_b, 384)
            sums = [
                jnp.sum(dq_raw, axis=0, keepdims=True),
                jnp.sum(dv, axis=0, keepdims=True),
                jnp.sum(dq * q_full, axis=0, keepdims=True),
                jnp.zeros((5, 128), f32),
            ]
            st_ref[i] = jnp.concatenate(sums, axis=0)
            session.steps(i, turns)

        each(0, turns, turn)
        session.finish()

        def last(i):
            for j in range(1, blocks):
                ship(i, j).wait_send()

        each(0, turns, last)

    full = pl.BlockSpec(memory_space=VM)
    sems = pltpu.SemaphoreType.DMA((blocks, turns))
    return pl.pallas_call(
        kernel,
        out_shape=tuple(
            [jax.ShapeDtypeStruct(packed.shape, bf16), jax.ShapeDtypeStruct((turns, 8, 128), f32)] + session.outs
        ),
        in_specs=[full] * 6 + session.in_specs,
        out_specs=tuple([full] * 2 + session.out_specs),
        scratch_shapes=[
            VM((blocks, rows_b, 128), bf16),
            VM((blocks, rows_b, 128), bf16),
            VM((blocks, rows_b, rows), f32),
            VM((blocks, rows_b, rows), f32),
            VM((blocks, rows_b, 128), f32),
            VM((blocks, rows_b, 128), f32),
            VM((turns, blocks, rows_b, 128), bf16),
            sems,
            sems,
        ]
        + session.scratch,
        compiler_params=params(cid),
        name="attend_back",
    )(packed, d_out, bias, scale, sid_k, sid_q, *session.ins)


def gelu_both(x):
    root = 0.7978845608028654
    square = x * x
    bent = jnp.tanh(root * x * (1.0 + 0.044715 * square))
    half = 0.5 * (1.0 + bent)
    slope = half + 0.5 * x * (1.0 - bent * bent) * (root * (1.0 + 3 * 0.044715 * square))
    return x * half, slope


def feed_forward(cid, mlp_input, grad_parts, shr_own, exp_w, e_bias):
    seq_n, img_n = lax.axis_size("seq"), lax.axis_size("img")
    outer = seq_n // 2
    chunks, size, width = mlp_input.shape
    rows = chunks * size
    hid_l = exp_w.shape[1]
    images = len(grad_parts)
    rows_p = rows // images
    w_chunks, w_size, _ = shr_own.shape
    hid_o = w_chunks * w_size
    tile = 256
    blocks_per_tile = tile // hid_o
    session = Session([], two_level("seq", seq_n) + two_level("img", img_n))

    def kernel(x_ref, *refs):
        df_refs = refs[:images]
        shr_ref, exp_ref, eb_ref, dh2_ref, dshr_own, f_ref, dexp_ref, expb_ref = refs[images : images + 8]
        h2, df, shr, act, slope, dshr, dh2, df_sem, hs, hr, ss, sr, sk, *more = refs[images + 8 :]
        session.greet()
        h2_in = gather_ops("seq", True, x_ref, h2, None, hs, hr)
        shr_in = gather_ops("img", False, shr_ref, shr, sk, ss, sr)
        dh2_out = scatter_ops("seq", True, dh2, dh2_ref, *more[:7])
        dshr_out = scatter_ops("img", False, dshr, dshr_own, *more[7:14])
        h2_in.start()
        shr_in.start()
        loads = [pltpu.make_async_copy(ref, df.at[:, g], df_sem.at[g]) for g, ref in enumerate(df_refs)]
        for load in loads:
            load.start()
        h2[0] = x_ref[...]
        expb_ref[...] = jnp.zeros_like(expb_ref)

        def columns(t):
            return lanes(t * tile, tile)

        def expand(j):
            def run(t):
                u = dot(h2[j].reshape(rows, width), exp_ref[:, columns(t)], ((1,), (0,))) + eb_ref[:, columns(t)]
                value, grad = gelu_both(u)
                act[j, :, columns(t)] = value.astype(bf16)
                slope[j, :, columns(t)] = grad.astype(bf16)

            each(0, hid_l // tile, run)

        def back_act(j):
            def run(t):
                weight = shr[pl.ds(t * blocks_per_tile, blocks_per_tile)].reshape(tile, width)
                grad = dot(df[j].reshape(rows, width), weight, ((1,), (1,)))
                grad = (slope[j, :, columns(t)].astype(f32) * grad).astype(bf16)
                slope[j, :, columns(t)] = grad
                expb_ref[:, columns(t)] += jnp.sum(grad.astype(f32), axis=0, keepdims=True)

            each(0, hid_l // tile, run)

        def back_input(j):
            def run(t):
                weight = exp_ref[pl.ds(pl.multiple_of(t * tile, tile), tile), :]
                part = dot(slope[j], weight, ((1,), (1,)))
                dh2[j, :, :, columns(t)] = part.astype(bf16).reshape(chunks, size, tile)

            each(0, width // tile, run)

        def shrink(j):
            def run(t):
                weight = shr[:, :, :, columns(t)].reshape(hid_l, tile)
                part = dot(act[j], weight, ((1,), (0,)))
                f_ref[j, :, :, columns(t)] = part.astype(bf16).reshape(chunks, size, tile)

            each(0, width // tile, run)

        def shrink_grad(t):
            left = act[:, :, columns(t)].reshape(seq_n * rows, tile)
            part = dot(left, df[...].reshape(seq_n * rows, width), ((0,), (0,)))
            part = part.astype(bf16).reshape(blocks_per_tile, w_chunks, w_size, width)
            dshr[pl.ds(t * blocks_per_tile, blocks_per_tile)] = part

        def expand_grad(t):
            left = h2[:, :, :, columns(t)].reshape(seq_n * rows, tile)
            part = dot(left, slope[...].reshape(seq_n * rows, hid_l), ((0,), (0,)))
            dexp_ref[pl.ds(pl.multiple_of(t * tile, tile), tile), :] = part.astype(bf16)

        expand(0)
        h2_in.near()
        expand(1)
        half = chunks // 2
        each(0, half, h2_in.step)
        each(0, w_chunks // 2, shr_in.step)
        each(half, chunks, h2_in.step)
        for o in range(1, outer):
            expand(2 * o)
        each(w_chunks // 2, w_chunks, shr_in.step)
        for o in range(1, outer):
            h2_in.handed(o)
            expand(2 * o + 1)
        for load in loads:
            load.wait()
        each(0, hid_l // tile, shrink_grad)
        shr_in.near()
        for o in range(1, img_n // 2):
            shr_in.handed(o)
        shr_in.sent()
        dshr_out.start()
        for o in range(1, outer):
            for j in (2 * o + 1, 2 * o):
                back_act(j)
                back_input(j)
        dh2_out.start_outer()
        each(0, chunks, dh2_out.step)
        each(0, w_chunks // 2, dshr_out.step)
        for j in (1, 0):
            back_act(j)
            back_input(j)
        dh2_out.start_inner()
        each(w_chunks // 2, w_chunks, dshr_out.step)
        h2_in.sent()
        for j in range(seq_n):
            shrink(j)
        each(0, width // tile, expand_grad)
        dh2_out.finish()
        dshr_out.finish()

    full = pl.BlockSpec(memory_space=VM)
    any_space = pl.BlockSpec(memory_space=pl.ANY)
    seq_sems = pltpu.SemaphoreType.DMA((seq_n, chunks))
    img_sems = pltpu.SemaphoreType.DMA((img_n, w_chunks))
    return pl.pallas_call(
        kernel,
        out_shape=(
            jax.ShapeDtypeStruct(mlp_input.shape, f32),
            jax.ShapeDtypeStruct(shr_own.shape, f32),
            jax.ShapeDtypeStruct((seq_n,) + mlp_input.shape, bf16),
            jax.ShapeDtypeStruct(exp_w.shape, bf16),
            jax.ShapeDtypeStruct((1, hid_l), f32),
        ),
        in_specs=[full] + [any_space] * images + [full] * 3,
        out_specs=(full,) * 5,
        scratch_shapes=[
            VM((seq_n,) + mlp_input.shape, bf16),
            VM((seq_n, images, rows_p, width), bf16),
            VM((img_n,) + shr_own.shape, bf16),
            VM((seq_n, rows, hid_l), bf16),
            VM((seq_n, rows, hid_l), bf16),
            VM((img_n,) + shr_own.shape, bf16),
            VM((seq_n,) + mlp_input.shape, bf16),
            pltpu.SemaphoreType.DMA((images,)),
            seq_sems,
            seq_sems,
            img_sems,
            img_sems,
            pltpu.SemaphoreType.DMA((w_chunks,)),
        ]
        + scatter_scratch(seq_n, mlp_input.shape, bf16)
        + scatter_scratch(img_n, shr_own.shape, bf16),
        compiler_params=params(cid),
        name="feed_forward",
    )(mlp_input, *grad_parts, shr_own, exp_w, e_bias)


def normalize(values):
    centered = values - jnp.mean(values, axis=-1, keepdims=True)
    return centered * lax.rsqrt(jnp.mean(centered * centered, axis=-1, keepdims=True) + 1e-06)


def norm_back(values, grad_rows):
    return jax.vjp(normalize, values)[1](grad_rows)[0]


def pad_to(x, size, axis):
    widths = [(0, 0)] * x.ndim
    widths[axis] = (0, size - x.shape[axis])
    return jnp.pad(x, widths)


def mm(a, b):
    return jnp.dot(a, b, preferred_element_type=f32)


def mm_nt(a, b):
    return lax.dot_general(a, b, (((1,), (1,)), ((), ())), preferred_element_type=f32)


def mm_tn(a, b):
    return lax.dot_general(a, b, (((0,), (0,)), ((), ())), preferred_element_type=f32)


def body(
    tokens,
    cotangent,
    condition,
    scale_sizes,
    mod_weight,
    mod_bias,
    attn_weight,
    query_bias,
    value_bias,
    out_weight,
    out_bias,
    expand_weight,
    expand_bias,
    shrink_weight,
    shrink_bias,
    log_scale,
):
    images, rows, width = tokens.shape
    heads = log_scale.shape[0]
    headdim = width // heads
    seq_n = lax.axis_size("seq")
    img_n = lax.axis_size("img")
    seq_i = lax.axis_index("seq")
    img_i = lax.axis_index("img")
    rank = img_i * seq_n + seq_i
    ranks = img_n * seq_n
    own = width // ranks
    rows_p = -(-rows // 16) * 16
    dim_l = width // seq_n
    pairs = dim_l // 128
    hidden = expand_bias.shape[0] * ranks
    hid_l = hidden // seq_n
    hid_o = hidden // ranks
    mods = mod_weight.shape[1]
    mod_o = mods // ranks

    mod_l = mods // seq_n
    blk = own * seq_n

    attn_cut = (
        attn_weight.astype(bf16)
        .reshape(own, 3, seq_n, pairs, 128)
        .transpose(2, 0, 3, 1, 4)
        .reshape(seq_n, own, 3 * dim_l)
    )
    exp_cut = (
        expand_weight.astype(bf16)
        .reshape(own, img_n, seq_n, hid_o)
        .transpose(2, 0, 1, 3)
        .reshape(seq_n, own, hid_l)
    )
    mod_cut = mod_weight.astype(bf16).reshape(own, seq_n, mod_l).transpose(1, 0, 2)
    silu_cond = jax.nn.silu(condition).astype(bf16).astype(f32)
    small_bias = jnp.concatenate([query_bias, value_bias, out_bias, shrink_bias, expand_bias, mod_bias])
    small_bias = lax.reduce_precision(small_bias, 8, 7)
    bias_n = small_bias.shape[0]
    bias_rows = -(-bias_n // 1024) * 8
    small_bias = pad_to(small_bias, bias_rows * 128, 0).reshape(1, bias_rows, 128)
    cond_cut = silu_cond.reshape(images, img_n, seq_n, own).transpose(1, 2, 0, 3).reshape(img_n, seq_n * images, own)
    small = jnp.concatenate(
        [pad_to(cond_cut, 128, 2), jnp.broadcast_to(small_bias, (img_n, bias_rows, 128))], axis=1
    )
    mod_all, bias_all, cond_rows, modw_cut, attn_b, exp_b, out_img = opening(
        1,
        mod_cut,
        attn_cut,
        exp_cut,
        small,
        images,
        [gather(out_weight.astype(bf16)[None], "img", False)],
    )
    out_img = out_img.reshape(img_n, own, width)
    attn_b = attn_b.reshape(blk, 3 * dim_l)
    exp_b = exp_b.reshape(blk, hid_l)

    def weight_chunks(x):
        step = max(blk // 4, 8)
        return x.reshape(x.shape[:-2] + (blk // step, step, x.shape[-1]))

    def hidden_chunks(x):
        step = max(hid_o // 4, 16)
        return x.reshape(x.shape[:-2] + (hid_o // step, step, x.shape[-1]))

    tiles = mod_l // 128
    modulation = mod_all[:, : tiles * images].reshape(seq_n, tiles, images, 128).transpose(2, 0, 1, 3)
    bias_all = bias_all.reshape(seq_n, img_n, bias_rows * 128)[:, :, :bias_n].transpose(1, 0, 2)
    q_bias = bias_all[:, :, :own].reshape(width)
    v_bias = bias_all[:, :, own : 2 * own].reshape(width)
    o_bias = bias_all[:, :, 2 * own : 3 * own].reshape(width)
    s_bias = bias_all[:, :, 3 * own : 4 * own].reshape(width)
    e_bias = bias_all[:, :, 4 * own : 4 * own + hid_o]
    e_bias = lax.dynamic_slice_in_dim(e_bias, seq_i, 1, 1).reshape(hid_l)
    m_bias = bias_all[:, :, 4 * own + hid_o :].reshape(mods)
    modulation = modulation.reshape(images, mods) + m_bias[None]
    qb_l = lax.dynamic_slice_in_dim(q_bias, seq_i * dim_l, dim_l, 0).reshape(pairs, 1, 128)
    vb_l = lax.dynamic_slice_in_dim(v_bias, seq_i * dim_l, dim_l, 0).reshape(pairs, 1, 128)
    pair_bias = jnp.concatenate([qb_l, jnp.zeros_like(qb_l), vb_l], axis=2)
    head_scale = jnp.exp(jnp.repeat(log_scale, headdim))
    pair_scale = lax.dynamic_slice_in_dim(head_scale, seq_i * dim_l, dim_l, 0).reshape(pairs, 1, 128)
    gain_attn, gain_mlp, scale_attn, scale_mlp, shift_attn, shift_mlp = jnp.split(
        modulation[:, None, :], 6, axis=-1
    )

    ends = jnp.cumsum(scale_sizes, axis=-1)
    offset = jnp.arange(rows_p, dtype=jnp.int32)
    place = (seq_i ^ jnp.arange(seq_n, dtype=jnp.int32))[:, None] * rows + offset[None]
    sid = jnp.sum((place[None, :, :, None] >= ends[:, None, None, :]).astype(jnp.int32), axis=-1)
    sid_q = sid.reshape(images, 1, seq_n * rows_p)
    sid_k = jnp.where(offset[None, None] < rows, sid, 1 << 20)[..., None]

    resid_in = pad_to(tokens, rows_p, 1).astype(f32)
    grad_out = pad_to(cotangent, rows_p, 1).astype(f32)
    local = images * rows_p
    all_rows = seq_n * local

    def chunked(x):
        return x.reshape(x.shape[: x.ndim - 3] + (local // 32, 32, width))

    normed_in = normalize(resid_in)
    attn_input = (normed_in * (1.0 + scale_attn) + shift_attn).astype(bf16)
    grad_shrunk = (grad_out * gain_mlp).astype(bf16)
    grad_chunks = grad_shrunk.reshape(images, rows_p // 16, 16, width)
    turns = 16
    first = images // 2
    h1, attn_w, *df_first = exchange(
        5,
        turns,
        gather(chunked(attn_input), "seq", True).during(0, turns * 2 // 3),
        gather(weight_chunks(attn_b), "img", False),
        *[gather(grad_chunks[g], "seq", True).during(turns * 2 // 3, turns) for g in range(first)],
    )
    h1 = h1.reshape(all_rows, width)
    attn_w = attn_w.reshape(width, 3 * dim_l)
    packed = mm(h1, attn_w).reshape(seq_n, images, rows_p, 3 * dim_l)
    later = images * pairs // 2
    context_low, out_w, exp_w, *df_second = attend(
        6,
        packed,
        pair_bias,
        pair_scale,
        sid_k,
        sid_q,
        [
            gather(out_img, "seq", False, True).during(0, later),
            gather(weight_chunks(exp_b), "img", False),
        ]
        + [gather(grad_chunks[g], "seq", True).during(later, 2 * later) for g in range(first, images)],
    )
    context_low = context_low.reshape(local, width)
    out_w = out_w.reshape(width, width)
    exp_w = exp_w.reshape(width, hid_l)
    attn_out = (mm(context_low, out_w) + o_bias).reshape(images, rows_p, width)
    resid_mid = resid_in + gain_attn * attn_out
    normed_mid = normalize(resid_mid)
    mlp_input = (normed_mid * (1.0 + scale_mlp) + shift_mlp).astype(bf16)
    df_parts = [x.reshape(seq_n, rows_p, width) for x in df_first + df_second]
    shrb_part = jnp.sum(grad_shrunk.astype(f32), axis=(0, 1))
    grad_mlp_input, shrw_own, shrunk_part, expw_part, expb_part = feed_forward(
        7,
        chunked(mlp_input),
        df_parts,
        hidden_chunks(shrink_weight.astype(bf16)),
        exp_w,
        e_bias.reshape(1, hid_l),
    )
    grad_mlp_input = grad_mlp_input.reshape(images, rows_p, width)
    shrw_own = shrw_own.reshape(hid_o, width)
    expb_part = expb_part.reshape(hid_l)
    expw_part = expw_part.reshape(img_n, blk, hid_l)

    grad_scale_mlp = jnp.sum(grad_mlp_input * normed_mid, axis=1)
    grad_shift_mlp = jnp.sum(grad_mlp_input, axis=1)
    grad_mid = grad_out + norm_back(resid_mid, grad_mlp_input * (1.0 + scale_mlp))
    grad_gain_attn = jnp.sum(grad_mid * attn_out, axis=1)
    grad_attn_out = (grad_mid * gain_attn).astype(bf16)
    outb_part = jnp.sum(grad_attn_out.astype(f32), axis=(0, 1))
    da = grad_attn_out.reshape(local, width)
    grad_context = mm_nt(da, out_w).astype(bf16)
    grad_context = grad_context.reshape(images, rows_p, width)
    outw_part = mm_tn(context_low, da).astype(bf16).reshape(img_n, seq_n, own, width)
    grad_packed, sums, expw_blk, shrunk, outw_blk = attend_back(
        11,
        packed,
        grad_context,
        pair_bias,
        pair_scale,
        sid_k,
        sid_q,
        [
            scatter_sum(weight_chunks(expw_part), "img", False, bf16),
            scatter_sum(shrunk_part, "seq", True),
            scatter_sum(outw_part, "seq", False, bf16, True),
        ],
    )
    shrunk = shrunk.reshape(images, rows_p, width) + s_bias
    layer_out = (resid_mid + gain_mlp * shrunk).astype(bf16)
    grad_gain_mlp = jnp.sum(grad_out * shrunk, axis=1)
    sums = jnp.sum(sums.reshape(images, pairs, 8, 128), axis=0)
    qb_part = sums[:, 0].reshape(dim_l)
    vb_part = sums[:, 1].reshape(dim_l)
    logs_part = jnp.sum(sums[:, 2].reshape(dim_l // headdim, headdim), axis=1)
    grad_packed = grad_packed.reshape(all_rows, 3 * dim_l)
    grad_in_part = mm_nt(grad_packed, attn_w).astype(bf16).reshape(seq_n, images, rows_p, width)
    attnw_part = mm_tn(h1, grad_packed).astype(bf16)
    grad_attn_input, attnw_blk, outw_own = exchange(
        12,
        local // 32,
        scatter_sum(chunked(grad_in_part), "seq", True),
        scatter_sum(weight_chunks(attnw_part.reshape(img_n, blk, 3 * dim_l)), "img", False, bf16),
        scatter_sum(outw_blk.reshape(img_n, 1, own, width), "img", False),
    )
    outw_own = outw_own.reshape(own, width)
    grad_attn_input = grad_attn_input.reshape(images, rows_p, width)
    grad_scale_attn = jnp.sum(grad_attn_input * normed_in, axis=1)
    grad_shift_attn = jnp.sum(grad_attn_input, axis=1)
    token_grad = grad_mid + norm_back(resid_in, grad_attn_input * (1.0 + scale_attn))
    token_grad = token_grad.astype(bf16)

    grad_mod = jnp.concatenate(
        [grad_gain_attn, grad_gain_mlp, grad_scale_attn, grad_scale_mlp, grad_shift_attn, grad_shift_mlp],
        axis=-1,
    )
    grad_mod = grad_mod.reshape(images, seq_n, tiles, 128).transpose(1, 2, 0, 3).reshape(seq_n, tiles * images, 128)
    grad_mod = pad_to(grad_mod, -(-tiles * images // 8) * 8, 1)

    def lined(vector, count):
        return pad_to(vector.reshape(count, -1), 128, 1)

    heads_l = heads // seq_n
    logs_row = lax.dynamic_update_slice_in_dim(jnp.zeros((128,), f32), logs_part, seq_i * heads_l, 0)
    bias_mine = jnp.concatenate(
        [
            lined(shrb_part, img_n),
            lined(outb_part, img_n),
            pad_to(logs_row[None], 8, 0),
            lined(qb_part, img_n // seq_n),
            lined(vb_part, img_n // seq_n),
        ]
    )
    bias_mine = pad_to(bias_mine, -(-bias_mine.shape[0] // 8) * 8, 0)
    mine = jnp.concatenate([grad_mod, jnp.broadcast_to(bias_mine[None], (seq_n,) + bias_mine.shape)], axis=1)
    back_cut = jnp.concatenate(
        [attnw_blk.reshape(seq_n, own, 3 * dim_l), expw_blk.reshape(seq_n, own, hid_l)], axis=2
    )
    modw_own, attnw_own, expw_own, bias_own, modb_all, cond_sum = closing(
        13, mine, lined(expb_part, img_n), cond_rows, modw_cut, back_cut, images, pairs
    )

    def part_of(row):
        return lax.dynamic_slice_in_dim(bias_own[row], seq_i * own, own, 0)

    shrb_own, outb_own, qb_own, vb_own = part_of(0), part_of(1), part_of(2), part_of(3)
    expb_own = bias_own[4, :hid_o]
    logs_total = bias_own[5, :heads]
    modb_own = lax.dynamic_slice_in_dim(modb_all[:, :tiles].reshape(mods), rank * mod_o, mod_o, 0)
    grad_silu = cond_sum[:, :, :own].reshape(img_n, seq_n, images, own).transpose(2, 0, 1, 3).reshape(images, width)
    cond_grad = jax.vjp(jax.nn.silu, condition)[1](grad_silu)[0]
    return (
        layer_out[:, :rows],
        token_grad[:, :rows],
        cond_grad,
        modw_own,
        modb_own,
        attnw_own,
        qb_own,
        vb_own,
        outw_own,
        outb_own,
        expw_own,
        expb_own,
        shrw_own,
        shrb_own,
        logs_total,
    )


def solution(mesh):
    both = P(("img", "seq"))
    rows = P(("img", "seq"), None)
    return jax.shard_map(
        body,
        mesh=mesh,
        in_specs=(
            P("img", "seq", None),
            P("img", "seq", None),
            P("img", None),
            P("img", None),
            rows,
            both,
            rows,
            both,
            both,
            rows,
            both,
            rows,
            both,
            rows,
            both,
            P(),
        ),
        out_specs=(
            P("img", "seq", None),
            P("img", "seq", None),
            P("img", None),
            rows,
            both,
            rows,
            both,
            both,
            rows,
            both,
            rows,
            both,
            rows,
            both,
            P(),
        ),
        check_vma=False,
    )
```

```python
from types import SimpleNamespace

import jax
import jax.numpy as jnp
from jax import lax
from jax.experimental import pallas as pl
from jax.experimental.pallas import tpu as pltpu
from jax.sharding import PartitionSpec as P

HIGH = lax.Precision.HIGHEST
MESH = pl.DeviceIdType.MESH
bf16 = jnp.bfloat16
f32 = jnp.float32
VM = pltpu.VMEM
LIMIT = 56 << 20


class Plan:
    def __init__(self, ins, out, scratch, peers, count, bind, out_space=VM):
        self.ins, self.out, self.out_space = ins, out, out_space
        self.scratch, self.peers, self.count, self.bind = scratch, peers, count, bind
        self.window = None

    def during(self, low, high):
        self.window = (low, high)
        return self


def remote(src, dst, send, recv, axis, peer):
    return pltpu.make_async_remote_copy(
        src_ref=src, dst_ref=dst, send_sem=send, recv_sem=recv, device_id={axis: peer}, device_id_type=MESH
    )


def each(low, high, run):
    def once(i, carry):
        run(i)
        return carry

    lax.fori_loop(low, high, once, 0)


def direct_ops(axis, x_ref, out_ref, send, recv, everyone=False, src_rel=False, dst_rel=False):
    n = lax.axis_size(axis)
    me = lax.axis_index(axis)

    def copy(j):
        src = x_ref if everyone else x_ref.at[j if src_rel else me ^ j]
        return remote(src, out_ref.at[j if dst_rel else me], send.at[j], recv.at[j], axis, me ^ j)

    def start():
        for j in range(1, n):
            copy(j).start()
        out_ref[0 if dst_rel else me] = x_ref[...] if everyone else x_ref[0 if src_rel else me]

    def finish():
        for j in range(1, n):
            copy(j).wait()

    return start, finish


def two_level(axis, n):
    return [(axis, 1)] + [(axis, 2 * o) for o in range(1, n // 2)]


def gather_ops(axis, rel, x_ref, out_ref, own, send, recv, inside=False):
    n = lax.axis_size(axis)
    outer = n // 2
    chunks = x_ref.shape[0]
    me = lax.axis_index(axis)

    def place(sender, j, c):
        block = j if rel else sender
        return out_ref.at[c, block] if inside else out_ref.at[block, c]

    def keep(c):
        return pltpu.make_async_copy(x_ref.at[c], place(me, 0, c), own.at[c])

    def push(j, c):
        return remote(x_ref.at[c], place(me, j, c), send.at[j, c], recv.at[j, c], axis, me ^ j)

    def hand(j, c):
        far = me ^ j
        return remote(place(far, j, c), place(far, j + 1, c), send.at[j + 1, c], recv.at[j + 1, c], axis, me ^ 1)

    def start():
        def first(c):
            for o in range(1, outer):
                push(2 * o, c).start()

        def second(c):
            push(1, c).start()
            if own is not None:
                keep(c).start()

        each(0, chunks, first)
        each(0, chunks, second)

    def step(c):
        for o in range(1, outer):
            push(2 * o, c).wait_recv()
            hand(2 * o, c).start()

    def near():
        each(0, chunks, lambda c: push(1, c).wait_recv())

    def handed(o):
        each(0, chunks, lambda c: hand(2 * o, c).wait_recv())

    def sent():
        def last(c):
            for o in range(1, outer):
                push(2 * o, c).wait_send()
                hand(2 * o, c).wait_send()
            push(1, c).wait_send()
            if own is not None:
                keep(c).wait()

        each(0, chunks, last)

    def finish():
        near()
        for o in range(1, outer):
            handed(o)
        sent()

    return SimpleNamespace(start=start, step=step, near=near, handed=handed, sent=sent, finish=finish)


def gather(x, axis, rel, inside=False):
    n = lax.axis_size(axis)
    chunks = x.shape[0]

    def bind(x_ref, out_ref, own, send, recv):
        return gather_ops(axis, rel, x_ref, out_ref, own, send, recv, inside)

    sems = pltpu.SemaphoreType.DMA((n, chunks))
    shape = (chunks, n) + x.shape[1:] if inside else (n,) + x.shape
    out = jax.ShapeDtypeStruct(shape, x.dtype)
    scratch = [pltpu.SemaphoreType.DMA((chunks,)), sems, sems]
    return Plan([x], out, scratch, two_level(axis, n), chunks, bind, pl.ANY)


def scatter_ops(axis, rel, x_ref, out_ref, near_buf, send_buf, far_buf, s1, r1, s2, r2, inside=False):
    n = lax.axis_size(axis)
    outer = n // 2
    chunks = out_ref.shape[0]
    me = lax.axis_index(axis)

    def part(j, c):
        block = j if rel else me ^ j
        return x_ref.at[c, block] if inside else x_ref.at[block, c]

    def near(o, c):
        return remote(part(2 * o + 1, c), near_buf.at[o, c], s1.at[o, c], r1.at[o, c], axis, me ^ 1)

    def far(o, c):
        return remote(send_buf.at[o, c], far_buf.at[o, c], s2.at[o, c], r2.at[o, c], axis, me ^ (2 * o))

    def start_outer():
        def first(c):
            for o in range(1, outer):
                near(o, c).start()

        each(0, chunks, first)

    def start_inner():
        each(0, chunks, lambda c: near(0, c).start())

    def start():
        start_outer()
        start_inner()

    def step(c):
        for o in range(1, outer):
            near(o, c).wait_recv()
            total = part(2 * o, c)[...].astype(f32) + near_buf[o, c].astype(f32)
            send_buf[o, c] = total.astype(send_buf.dtype)
            far(o, c).start()

    def finish():
        def last(c):
            near(0, c).wait_recv()
            total = part(0, c)[...].astype(f32) + near_buf[0, c].astype(f32)
            for o in range(1, outer):
                far(o, c).wait_recv()
                total = total + far_buf[o, c].astype(f32)
            out_ref[c] = total.astype(out_ref.dtype)
            for o in range(outer):
                near(o, c).wait_send()
            for o in range(1, outer):
                far(o, c).wait_send()

        each(0, chunks, last)

    return SimpleNamespace(
        start=start, start_outer=start_outer, start_inner=start_inner, step=step, finish=finish
    )


def scatter_scratch(n, inner, dtype):
    half = VM((n // 2,) + inner, dtype)
    sems = pltpu.SemaphoreType.DMA((n // 2, inner[0]))
    return [half, half, half, sems, sems, sems, sems]


def scatter_sum(x, axis, rel, dtype=jnp.float32, inside=False):
    n = lax.axis_size(axis)
    chunks = x.shape[0 if inside else 1]
    inner = (chunks,) + x.shape[2:]

    def bind(*refs):
        return scatter_ops(axis, rel, *refs, inside=inside)

    out = jax.ShapeDtypeStruct(inner, dtype)
    return Plan([x], out, scatter_scratch(n, inner, x.dtype), two_level(axis, n), chunks, bind)


class Session:
    def __init__(self, plans, more_peers=()):
        self.plans = plans
        self.ins = [x for p in plans for x in p.ins]
        self.outs = [p.out for p in plans]
        self.in_specs = [pl.BlockSpec(memory_space=VM)] * len(self.ins)
        self.out_specs = [pl.BlockSpec(memory_space=p.out_space) for p in plans]
        self.scratch = [scr for p in plans for scr in p.scratch]
        self.peers = sorted({peer for p in plans for peer in p.peers} | set(more_peers))

    def greet(self):
        barrier = pltpu.get_barrier_semaphore()
        for axis, j in self.peers:
            pl.semaphore_signal(barrier, inc=1, device_id={axis: lax.axis_index(axis) ^ j}, device_id_type=MESH)
        pl.semaphore_wait(barrier, len(self.peers))

    def bind(self, ins, outs, scratch):
        at_in = at_scr = 0
        self.bound = []
        for p, out in zip(self.plans, outs):
            mine = ins[at_in : at_in + len(p.ins)]
            own = scratch[at_scr : at_scr + len(p.scratch)]
            self.bound.append((p.count, p.window, p.bind(*mine, out, *own)))
            at_in += len(p.ins)
            at_scr += len(p.scratch)

    def start(self):
        for _, _, ops in self.bound:
            ops.start()

    def steps(self, i, total):
        for count, window, ops in self.bound:
            low, high = window or (0, total)
            span = high - low

            def some(ops=ops, count=count, low=low, span=span):
                if count == span:
                    ops.step(i - low)
                else:
                    each(((i - low) * count) // span, ((i - low + 1) * count) // span, ops.step)

            if not count:
                continue
            if span == total:
                some()
            else:
                pl.when(jnp.logical_and(i >= low, i < high))(some)

    def finish(self):
        for _, _, ops in self.bound:
            ops.finish()


def everyone_else(*axes):
    return [(axis, j) for axis in axes for j in range(1, lax.axis_size(axis))]


def pairs_of_sems(*axes):
    return [pltpu.SemaphoreType.DMA((lax.axis_size(axis),)) for axis in axes for _ in range(2)]


def params(cid):
    return pltpu.CompilerParams(collective_id=cid, has_side_effects=True, vmem_limit_bytes=LIMIT)


def opening(cid, mod_cut, attn_cut, exp_cut, small, images, plans):
    seq_n, own, mod_l = mod_cut.shape
    img_n, rows, _ = small.shape
    head = seq_n * images
    tiles = mod_l // 128
    slim = -(-tiles * images // 8) * 8
    session = Session(plans)
    session.peers = everyone_else("img", "seq")
    ins, outs = 4 + len(session.ins), 6 + len(plans)

    def kernel(*refs):
        mod_ref, attn_ref, exp_ref, small_ref = refs[:4]
        modo_ref, bias_ref, lhs_ref, modw_ref, attnw_ref, expw_ref = refs[ins : ins + 6]
        small_all, part_buf, part_all, sum_buf = refs[ins + outs : ins + outs + 4]
        sems = refs[ins + outs + 4 : ins + outs + 18]
        session.greet()
        small_go, small_end = direct_ops("img", small_ref, small_all, *sems[:2])
        mod_go, mod_end = direct_ops("seq", mod_ref, modw_ref, *sems[2:4])
        attn_go, attn_end = direct_ops("seq", attn_ref, attnw_ref, *sems[4:6])
        exp_go, exp_end = direct_ops("seq", exp_ref, expw_ref, *sems[12:14])
        session.bind(refs[4:ins], refs[ins + 6 : ins + outs], refs[ins + outs + 18 :])
        small_go()
        mod_go()
        attn_go()
        exp_go()
        session.start()
        part_buf[...] = jnp.zeros_like(part_buf)
        small_end()
        bias_go, bias_end = direct_ops("seq", small_all.at[:, head:], bias_ref, *sems[6:8], everyone=True)
        bias_go()
        for i in range(img_n):
            for q in range(seq_n):
                lhs_ref[q, i * images : (i + 1) * images] = small_all[i, q * images : (q + 1) * images]
        mod_end()
        part = jnp.zeros((img_n * images, mod_l), f32)
        for q in range(seq_n):
            part = part + dot(lhs_ref[q][:, :own].astype(bf16), modw_ref[q], ((1,), (0,)))
        for i in range(img_n):
            for t in range(tiles):
                part_buf[i, t * images : (t + 1) * images] = part[
                    i * images : (i + 1) * images, t * 128 : (t + 1) * 128
                ]
        part_go, part_end = direct_ops("img", part_buf, part_all, *sems[8:10])
        part_go()
        session.steps(0, 1)
        part_end()
        total = part_all[0]
        for i in range(1, img_n):
            total = total + part_all[i]
        sum_buf[...] = total
        sum_go, sum_end = direct_ops("seq", sum_buf, modo_ref, *sems[10:12], everyone=True)
        sum_go()
        bias_end()
        sum_end()
        attn_end()
        exp_end()
        session.finish()

    full = pl.BlockSpec(memory_space=VM)
    return pl.pallas_call(
        kernel,
        out_shape=tuple(
            [
                jax.ShapeDtypeStruct((seq_n, slim, 128), f32),
                jax.ShapeDtypeStruct((seq_n, img_n, rows - head, 128), f32),
                jax.ShapeDtypeStruct((seq_n, img_n * images, 128), f32),
                jax.ShapeDtypeStruct(mod_cut.shape, bf16),
                jax.ShapeDtypeStruct(attn_cut.shape, bf16),
                jax.ShapeDtypeStruct(exp_cut.shape, bf16),
            ]
            + session.outs
        ),
        in_specs=[full] * 4 + session.in_specs,
        out_specs=tuple([full] * 6 + session.out_specs),
        scratch_shapes=[
            VM(small.shape, f32),
            VM((img_n, slim, 128), f32),
            VM((img_n, slim, 128), f32),
            VM((slim, 128), f32),
        ]
        + pairs_of_sems("img", "seq", "seq", "seq", "img", "seq", "seq")
        + session.scratch,
        compiler_params=params(cid),
        name="opening",
    )(mod_cut, attn_cut, exp_cut, small, *session.ins)


def closing(cid, mine, expb, lhs, modw, back, images, pairs):
    seq_n, own, mod_l = modw.shape
    img_n = expb.shape[0]
    rows = mine.shape[1]
    head = seq_n * images
    tiles = mod_l // 128
    slim = -(-tiles * images // 8) * 8
    share = img_n // seq_n
    cut = back.shape[2]
    dim_l = pairs * 128
    width = dim_l * seq_n
    hid_l = cut - 3 * dim_l
    hid_o = hid_l // img_n
    aligned = hid_o % 128 == 0
    flat = -(-tiles // 8) * 8

    def kernel(
        mine_ref, expb_ref, lhs_ref, modw_ref, back_ref,
        modw_own, attn_own, exp_own, bias_ref, modb_ref, cond_ref,
        seen, block, got, dd, mw_send, mw_recv, mb_send, gs_send, gs_all, gs_seen, back_all, *sems
    ):
        barrier = Session([], everyone_else("img", "seq"))
        barrier.greet()
        mine_go, mine_end = direct_ops("seq", mine_ref, seen, *sems[:2])
        back_go, back_end = direct_ops("seq", back_ref, back_all, *sems[2:4])
        mine_go()
        back_go()
        block[...] = jnp.zeros_like(block)
        gs_send[...] = jnp.zeros_like(gs_send)
        mb_send[...] = jnp.zeros_like(mb_send)
        mine_end()
        total = seen[0]
        for q in range(1, seq_n):
            total = total + seen[q]
        at = slim + 2 * img_n
        for i in range(img_n):
            block[i, :slim] = total[:slim]
            block[i, slim : slim + 1] = total[slim + i : slim + i + 1]
            block[i, slim + 1 : slim + 2] = total[slim + img_n + i : slim + img_n + i + 1]
            row = at + 8 + i % share
            block[i, slim + 2 : slim + 3] = seen[i // share, row : row + 1]
            block[i, slim + 3 : slim + 4] = seen[i // share, row + share : row + share + 1]
            block[i, slim + 4 : slim + 5] = expb_ref[i : i + 1]
            block[i, slim + 5 : slim + 6] = total[at : at + 1]
        img_go, img_end = direct_ops("img", block, got, *sems[4:6])
        img_go()
        back_end()
        for q in range(seq_n):
            for p in range(pairs):
                for k in range(3):
                    to = k * width + q * dim_l + p * 128
                    at_c = p * 384 + k * 128
                    attn_own[:, to : to + 128] = back_all[q, :, at_c : at_c + 128].astype(f32)
            if aligned:
                for i in range(img_n):
                    to = (i * seq_n + q) * hid_o
                    at_c = 3 * dim_l + i * hid_o
                    exp_own[:, to : to + hid_o] = back_all[q, :, at_c : at_c + hid_o].astype(f32)
            else:
                exp_own[:, q * hid_l : (q + 1) * hid_l] = back_all[q, :, 3 * dim_l :].astype(f32)
        img_end()
        sums = got[0]
        for i in range(1, img_n):
            sums = sums + got[i]
        bias_ref[...] = sums[slim:]
        for t in range(tiles):
            mb_send[t : t + 1] = jnp.sum(sums[t * images : (t + 1) * images], axis=0, keepdims=True)
            for i in range(img_n):
                dd[i * images : (i + 1) * images, t * 128 : (t + 1) * 128] = got[i, t * images : (t + 1) * images]
        grad = dd[...]
        high = grad.astype(bf16)
        low = (grad - high.astype(f32)).astype(bf16)
        for q in range(seq_n):
            out = dot(high, modw_ref[q], ((1,), (1,))) + dot(low, modw_ref[q], ((1,), (1,)))
            for i in range(img_n):
                gs_send[i, q * images : (q + 1) * images, :own] = out[i * images : (i + 1) * images]
        gs_go, gs_end = direct_ops("img", gs_send, gs_all, *sems[6:8])
        gs_go()
        for q in range(seq_n):
            mw_send[q] = dot(lhs_ref[q][:, :own].astype(bf16), high, ((0,), (0,))).astype(bf16)
        mb_go, mb_end = direct_ops("seq", mb_send, modb_ref, *sems[10:12], everyone=True)
        mb_go()
        gs_end()
        all_go, all_end = direct_ops("seq", gs_all, gs_seen, *sems[12:14], everyone=True)
        all_go()
        mw_go, mw_end = direct_ops("seq", mw_send, mw_recv, *sems[8:10])
        mw_go()
        mb_end()
        all_end()
        out = gs_seen[0]
        for q in range(1, seq_n):
            out = out + gs_seen[q]
        cond_ref[...] = out
        mw_end()
        for q in range(seq_n):
            modw_own[:, q * mod_l : (q + 1) * mod_l] = mw_recv[q].astype(f32)

    full = pl.BlockSpec(memory_space=VM)
    got = pl.pallas_call(
        kernel,
        out_shape=(
            jax.ShapeDtypeStruct((own, mod_l * seq_n), f32),
            jax.ShapeDtypeStruct((own, 3 * width), f32),
            jax.ShapeDtypeStruct((own, hid_l * seq_n), f32),
            jax.ShapeDtypeStruct((8, 128), f32),
            jax.ShapeDtypeStruct((seq_n, flat, 128), f32),
            jax.ShapeDtypeStruct((img_n, head, 128), f32),
        ),
        in_specs=[full] * 5,
        out_specs=(full,) * 6,
        scratch_shapes=[
            VM((seq_n, rows, 128), f32),
            VM((img_n, slim + 8, 128), f32),
            VM((img_n, slim + 8, 128), f32),
            VM((img_n * images, mod_l), f32),
            VM((seq_n, own, mod_l), bf16),
            VM((seq_n, own, mod_l), bf16),
            VM((flat, 128), f32),
            VM((img_n, head, 128), f32),
            VM((img_n, head, 128), f32),
            VM((seq_n, img_n, head, 128), f32),
            VM(back.shape, bf16),
        ]
        + pairs_of_sems("seq", "seq", "img", "img", "seq", "seq", "seq"),
        compiler_params=params(cid),
        name="closing",
    )(mine, expb, lhs, modw, back)
    got = list(got)
    if not aligned:
        got[2] = got[2].reshape(own, seq_n, img_n, hid_o).transpose(0, 2, 1, 3).reshape(own, hid_l * seq_n)
    return got


def opening(cid, mod_cut, attn_cut, exp_cut, small, images, plans):
    seq_n, own, mod_l = mod_cut.shape
    img_n, rows, _ = small.shape
    head = seq_n * images
    tiles = mod_l // 128
    slim = -(-tiles * images // 8) * 8
    session = Session(plans)
    session.peers = everyone_else("img", "seq")
    ins, outs = 4 + len(session.ins), 6 + len(plans)

    def kernel(*refs):
        mod_ref, attn_ref, exp_ref, small_ref = refs[:4]
        modo_ref, bias_ref, lhs_ref, modw_ref, attnw_ref, expw_ref = refs[ins : ins + 6]
        small_all, part_buf, part_all, sum_buf = refs[ins + outs : ins + outs + 4]
        sems = refs[ins + outs + 4 : ins + outs + 18]
        session.greet()
        small_go, small_end = direct_ops("img", small_ref, small_all, *sems[:2])
        mod_go, mod_end = direct_ops("seq", mod_ref, modw_ref, *sems[2:4])
        attn_go, attn_end = direct_ops("seq", attn_ref, attnw_ref, *sems[4:6])
        exp_go, exp_end = direct_ops("seq", exp_ref, expw_ref, *sems[12:14])
        session.bind(refs[4:ins], refs[ins + 6 : ins + outs], refs[ins + outs + 18 :])
        small_go()
        mod_go()
        attn_go()
        exp_go()
        session.start()
        part_buf[...] = jnp.zeros_like(part_buf)
        small_end()
        bias_go, bias_end = direct_ops("seq", small_all.at[:, head:], bias_ref, *sems[6:8], everyone=True)
        bias_go()
        for i in range(img_n):
            for q in range(seq_n):
                lhs_ref[q, i * images : (i + 1) * images] = small_all[i, q * images : (q + 1) * images]
        mod_end()
        part = jnp.zeros((img_n * images, mod_l), f32)
        for q in range(seq_n):
            part = part + dot(lhs_ref[q][:, :own].astype(bf16), modw_ref[q], ((1,), (0,)))
        for i in range(img_n):
            for t in range(tiles):
                part_buf[i, t * images : (t + 1) * images] = part[
                    i * images : (i + 1) * images, t * 128 : (t + 1) * 128
                ]
        part_go, part_end = direct_ops("img", part_buf, part_all, *sems[8:10])
        part_go()
        session.steps(0, 1)
        part_end()
        total = part_all[0]
        for i in range(1, img_n):
            total = total + part_all[i]
        sum_buf[...] = total
        sum_go, sum_end = direct_ops("seq", sum_buf, modo_ref, *sems[10:12], everyone=True)
        sum_go()
        bias_end()
        sum_end()
        attn_end()
        exp_end()
        session.finish()

    full = pl.BlockSpec(memory_space=VM)
    return pl.pallas_call(
        kernel,
        out_shape=tuple(
            [
                jax.ShapeDtypeStruct((seq_n, slim, 128), f32),
                jax.ShapeDtypeStruct((seq_n, img_n, rows - head, 128), f32),
                jax.ShapeDtypeStruct((seq_n, img_n * images, 128), f32),
                jax.ShapeDtypeStruct(mod_cut.shape, bf16),
                jax.ShapeDtypeStruct(attn_cut.shape, bf16),
                jax.ShapeDtypeStruct(exp_cut.shape, bf16),
            ]
            + session.outs
        ),
        in_specs=[full] * 4 + session.in_specs,
        out_specs=tuple([full] * 6 + session.out_specs),
        scratch_shapes=[
            VM(small.shape, f32),
            VM((img_n, slim, 128), f32),
            VM((img_n, slim, 128), f32),
            VM((slim, 128), f32),
        ]
        + pairs_of_sems("img", "seq", "seq", "seq", "img", "seq", "seq")
        + session.scratch,
        compiler_params=params(cid),
        name="opening",
    )(mod_cut, attn_cut, exp_cut, small, *session.ins)


def closing(cid, mine, expb, lhs, modw, back, images, pairs):
    seq_n, own, mod_l = modw.shape
    img_n = expb.shape[0]
    rows = mine.shape[1]
    head = seq_n * images
    tiles = mod_l // 128
    slim = -(-tiles * images // 8) * 8
    share = img_n // seq_n
    cut = back.shape[2]
    dim_l = pairs * 128
    width = dim_l * seq_n
    hid_l = cut - 3 * dim_l
    hid_o = hid_l // img_n
    aligned = hid_o % 128 == 0
    flat = -(-tiles // 8) * 8

    def kernel(
        mine_ref, expb_ref, lhs_ref, modw_ref, back_ref,
        modw_own, attn_own, exp_own, bias_ref, modb_ref, cond_ref,
        seen, block, got, dd, mw_send, mw_recv, mb_send, gs_send, gs_all, gs_seen, back_all, *sems
    ):
        barrier = Session([], everyone_else("img", "seq"))
        barrier.greet()
        mine_go, mine_end = direct_ops("seq", mine_ref, seen, *sems[:2])
        back_go, back_end = direct_ops("seq", back_ref, back_all, *sems[2:4])
        mine_go()
        back_go()
        block[...] = jnp.zeros_like(block)
        gs_send[...] = jnp.zeros_like(gs_send)
        mb_send[...] = jnp.zeros_like(mb_send)
        mine_end()
        total = seen[0]
        for q in range(1, seq_n):
            total = total + seen[q]
        at = slim + 2 * img_n
        for i in range(img_n):
            block[i, :slim] = total[:slim]
            block[i, slim : slim + 1] = total[slim + i : slim + i + 1]
            block[i, slim + 1 : slim + 2] = total[slim + img_n + i : slim + img_n + i + 1]
            row = at + 8 + i % share
            block[i, slim + 2 : slim + 3] = seen[i // share, row : row + 1]
            block[i, slim + 3 : slim + 4] = seen[i // share, row + share : row + share + 1]
            block[i, slim + 4 : slim + 5] = expb_ref[i : i + 1]
            block[i, slim + 5 : slim + 6] = total[at : at + 1]
        img_go, img_end = direct_ops("img", block, got, *sems[4:6])
        img_go()
        back_end()
        for q in range(seq_n):
            for p in range(pairs):
                for k in range(3):
                    to = k * width + q * dim_l + p * 128
                    at_c = p * 384 + k * 128
                    attn_own[:, to : to + 128] = back_all[q, :, at_c : at_c + 128].astype(f32)
            if aligned:
                for i in range(img_n):
                    to = (i * seq_n + q) * hid_o
                    at_c = 3 * dim_l + i * hid_o
                    exp_own[:, to : to + hid_o] = back_all[q, :, at_c : at_c + hid_o].astype(f32)
            else:
                exp_own[:, q * hid_l : (q + 1) * hid_l] = back_all[q, :, 3 * dim_l :].astype(f32)
        img_end()
        sums = got[0]
        for i in range(1, img_n):
            sums = sums + got[i]
        bias_ref[...] = sums[slim:]
        for t in range(tiles):
            mb_send[t : t + 1] = jnp.sum(sums[t * images : (t + 1) * images], axis=0, keepdims=True)
            for i in range(img_n):
                dd[i * images : (i + 1) * images, t * 128 : (t + 1) * 128] = got[i, t * images : (t + 1) * images]
        grad = dd[...]
        high = grad.astype(bf16)
        low = (grad - high.astype(f32)).astype(bf16)
        for q in range(seq_n):
            out = dot(high, modw_ref[q], ((1,), (1,))) + dot(low, modw_ref[q], ((1,), (1,)))
            for i in range(img_n):
                gs_send[i, q * images : (q + 1) * images, :own] = out[i * images : (i + 1) * images]
        gs_go, gs_end = direct_ops("img", gs_send, gs_all, *sems[6:8])
        gs_go()
        for q in range(seq_n):
            mw_send[q] = dot(lhs_ref[q][:, :own].astype(bf16), high, ((0,), (0,))).astype(bf16)
        mb_go, mb_end = direct_ops("seq", mb_send, modb_ref, *sems[10:12], everyone=True)
        mb_go()
        gs_end()
        all_go, all_end = direct_ops("seq", gs_all, gs_seen, *sems[12:14], everyone=True)
        all_go()
        mw_go, mw_end = direct_ops("seq", mw_send, mw_recv, *sems[8:10])
        mw_go()
        mb_end()
        all_end()
        out = gs_seen[0]
        for q in range(1, seq_n):
            out = out + gs_seen[q]
        cond_ref[...] = out
        mw_end()
        for q in range(seq_n):
            modw_own[:, q * mod_l : (q + 1) * mod_l] = mw_recv[q].astype(f32)

    full = pl.BlockSpec(memory_space=VM)
    got = pl.pallas_call(
        kernel,
        out_shape=(
            jax.ShapeDtypeStruct((own, mod_l * seq_n), f32),
            jax.ShapeDtypeStruct((own, 3 * width), f32),
            jax.ShapeDtypeStruct((own, hid_l * seq_n), f32),
            jax.ShapeDtypeStruct((8, 128), f32),
            jax.ShapeDtypeStruct((seq_n, flat, 128), f32),
            jax.ShapeDtypeStruct((img_n, head, 128), f32),
        ),
        in_specs=[full] * 5,
        out_specs=(full,) * 6,
        scratch_shapes=[
            VM((seq_n, rows, 128), f32),
            VM((img_n, slim + 8, 128), f32),
            VM((img_n, slim + 8, 128), f32),
            VM((img_n * images, mod_l), f32),
            VM((seq_n, own, mod_l), bf16),
            VM((seq_n, own, mod_l), bf16),
            VM((flat, 128), f32),
            VM((img_n, head, 128), f32),
            VM((img_n, head, 128), f32),
            VM((seq_n, img_n, head, 128), f32),
            VM(back.shape, bf16),
        ]
        + pairs_of_sems("seq", "seq", "img", "img", "seq", "seq", "seq"),
        compiler_params=params(cid),
        name="closing",
    )(mine, expb, lhs, modw, back)
    got = list(got)
    if not aligned:
        got[2] = got[2].reshape(own, seq_n, img_n, hid_o).transpose(0, 2, 1, 3).reshape(own, hid_l * seq_n)
    return got


def exchange(cid, turns, *plans):
    session = Session(plans)
    ins, outs = len(session.ins), len(plans)

    def kernel(*refs):
        session.greet()
        session.bind(refs[:ins], refs[ins : ins + outs], refs[ins + outs :])
        session.start()
        each(0, turns, lambda i: session.steps(i, turns))
        session.finish()

    got = pl.pallas_call(
        kernel,
        out_shape=tuple(session.outs),
        in_specs=session.in_specs,
        out_specs=tuple(session.out_specs),
        scratch_shapes=session.scratch,
        compiler_params=params(cid),
        name=f"exchange_{cid}",
    )(*session.ins)
    return got[0] if len(plans) == 1 else got


def half_sums(values, low_half):
    first = jnp.sum(jnp.where(low_half, values, 0.0), axis=-1, keepdims=True)
    second = jnp.sum(jnp.where(low_half, 0.0, values), axis=-1, keepdims=True)
    return jnp.where(low_half, first, second)


def dot(a, b, dims):
    return lax.dot_general(a, b, (dims, ((), ())), preferred_element_type=f32)


def lanes(start, size):
    return pl.ds(pl.multiple_of(start, 128), size)


def load_heads(p_ref, bias, g, p, rows):
    both = p_ref[:, g, :, lanes(p * 384, 384)].reshape(rows, 384)
    query = both[:, :128] + bias[:, :128]
    key = both[:, 128:256]
    value = both[:, 256:] + bias[:, 256:]
    low_half = lax.broadcasted_iota(jnp.int32, (rows, 128), 1) < 64
    r_query = lax.rsqrt(half_sums(query * query, low_half) + 1e-06)
    r_key = lax.rsqrt(half_sums(key * key, low_half) + 1e-06)
    return query, key, value, low_half, r_query, r_key


def attend(cid, attn_input, attn_own, bias, scale, sid_k, sid_q, out_img, exp_own, grad_own):
    seq_n, img_n = lax.axis_size("seq"), lax.axis_size("img")
    outer = seq_n // 2
    chunks, size, width = attn_input.shape
    local = chunks * size
    images = sid_q.shape[0]
    rows_b = local // images
    rows = seq_n * rows_b
    wide = attn_own.shape[2]
    pairs = wide // 384
    turns = images * pairs
    tile = 256 if wide % 256 == 0 else 128
    w_chunks = attn_own.shape[0]
    plans = [gather(x, "seq", True) for x in grad_own] + [gather(out_img, "seq", False, True), gather(exp_own, "img", False)]
    session = Session(plans, everyone_else("seq") + two_level("img", img_n))
    ins, outs = 6 + len(session.ins), 4 + len(plans)

    def kernel(*refs):
        x_ref, w_ref, b_ref, es_ref, sk_ref, sq_ref = refs[:6]
        o_ref, p_out, h_out, w_out = refs[ins : ins + 4]
        scratch = refs[ins + outs :]
        h1, attn_w, packed, k_buf, v_buf, o_buf, o_send, o_recv, hs, hr, wk, ws, wr, out_sem = scratch[:14]
        me = lax.axis_index("seq")
        session.greet()
        session.bind(refs[6:ins], refs[ins + 4 : ins + outs], scratch[14:])
        h1_in = gather_ops("seq", True, x_ref, h1, None, hs, hr)
        w_in = gather_ops("img", False, w_ref, attn_w, wk, ws, wr)
        h1_in.start()
        w_in.start()
        session.start()
        *grads, (out_count, _, out_in), (exp_count, _, exp_in) = session.bound
        h1[0] = x_ref[...]

        def ship(i, j):
            g, p = i // pairs, i % pairs
            return remote(
                o_buf.at[i, j],
                o_ref.at[g, :, lanes((me * pairs + p) * 128, 128)],
                o_send.at[j, i],
                o_recv.at[j, i],
                "seq",
                me ^ j,
            )

        each(0, chunks // 2, h1_in.step)
        each(0, w_chunks // 2, w_in.step)
        each(chunks // 2, chunks, h1_in.step)
        each(w_chunks // 2, w_chunks, w_in.step)
        h1_in.near()
        for o in range(1, outer):
            h1_in.handed(o)
        w_in.near()
        for o in range(1, img_n // 2):
            w_in.handed(o)
        w_in.sent()
        quarter = exp_count // 4
        each(0, quarter, exp_in.step)

        def project(k):
            j, t = k // (wide // tile), k % (wide // tile)
            columns = lanes(t * tile, tile)
            part = dot(h1[j].reshape(local, width), attn_w[:, :, :, columns].reshape(width, tile), ((1,), (0,)))
            packed[j, :, :, columns] = part.reshape(images, rows_b, tile)

        each(0, seq_n * (wide // tile), project)
        each(quarter, 2 * quarter, exp_in.step)
        copies = [
            pltpu.make_async_copy(src, dst, out_sem.at[n])
            for n, (src, dst) in enumerate(((packed, p_out), (h1, h_out), (attn_w, w_out)))
        ]
        for copy in copies:
            copy.start()

        def turn(i):
            g, p = i // pairs, i % pairs
            query, key, value, low_half, r_query, r_key = load_heads(packed, b_ref[p], g, p, rows)
            query_low = query * r_query * es_ref[p]
            k_buf[...] = (key * r_key).astype(bf16).reshape(seq_n, rows_b, 128)
            v_buf[...] = value.astype(bf16).reshape(seq_n, rows_b, 128)
            sid_q = sq_ref[g]
            parts = []
            for h in range(2):
                mine = low_half if h == 0 else jnp.logical_not(low_half)
                q_t = jnp.transpose(jnp.where(mine, query_low, 0.0)).astype(bf16)

                def step(b, carry, q_t=q_t):
                    total, acc = carry
                    scores = dot(k_buf[b], q_t, ((1,), (0,)))
                    expo = jnp.where(sk_ref[g, b] <= sid_q, jnp.exp(scores), 0.0)
                    total = total + jnp.sum(expo, axis=0, keepdims=True)
                    acc = acc + dot(v_buf[b], expo.astype(bf16), ((0,), (0,)))
                    return total, acc

                total, acc = lax.fori_loop(
                    0, seq_n, step, (jnp.zeros((1, rows), f32), jnp.zeros((128, rows), f32))
                )
                parts.append((acc / total)[64 * h : 64 * h + 64])
            out = jnp.transpose(jnp.concatenate(parts, axis=0)).astype(bf16).reshape(seq_n, rows_b, 128)
            o_buf[i] = out
            o_ref[g, :, lanes((me * pairs + p) * 128, 128)] = out[0]
            for j in range(1, seq_n):
                ship(i, j).start()

            @pl.when(i == 0)
            def _():
                for count, _, ops in grads:
                    each(0, count, ops.step)

            half = turns // 2

            @pl.when(i == half - 1)
            def _():
                each(2 * quarter, 3 * quarter, exp_in.step)

            @pl.when(i == half)
            def _():
                each(0, out_count, out_in.step)
                each(3 * quarter, exp_count, exp_in.step)

        each(0, turns, turn)
        session.finish()
        h1_in.sent()
        for copy in copies:
            copy.wait()

        def last(i):
            for j in range(1, seq_n):
                ship(i, j).wait()

        each(0, turns, last)

    full = pl.BlockSpec(memory_space=VM)
    any_space = pl.BlockSpec(memory_space=pl.ANY)
    sems = pltpu.SemaphoreType.DMA((seq_n, turns))
    seq_sems = pltpu.SemaphoreType.DMA((seq_n, chunks))
    img_sems = pltpu.SemaphoreType.DMA((img_n, w_chunks))
    packed = (seq_n, images, rows_b, wide)
    return pl.pallas_call(
        kernel,
        out_shape=tuple(
            [
                jax.ShapeDtypeStruct((images, rows_b, width), bf16),
                jax.ShapeDtypeStruct(packed, f32),
                jax.ShapeDtypeStruct((seq_n,) + attn_input.shape, bf16),
                jax.ShapeDtypeStruct((img_n,) + attn_own.shape, bf16),
            ]
            + session.outs
        ),
        in_specs=[full] * 6 + session.in_specs,
        out_specs=tuple([full] + [any_space] * 3 + session.out_specs),
        scratch_shapes=[
            VM((seq_n,) + attn_input.shape, bf16),
            VM((img_n,) + attn_own.shape, bf16),
            VM(packed, f32),
            VM((seq_n, rows_b, 128), bf16),
            VM((seq_n, rows_b, 128), bf16),
            VM((turns, seq_n, rows_b, 128), bf16),
            sems,
            sems,
            seq_sems,
            seq_sems,
            pltpu.SemaphoreType.DMA((w_chunks,)),
            img_sems,
            img_sems,
            pltpu.SemaphoreType.DMA((3,)),
        ]
        + session.scratch,
        compiler_params=params(cid),
        name="attend",
    )(attn_input, attn_own, bias, scale, sid_k, sid_q, *session.ins)


def attend_back(cid, packed, h1, attn_w, d_out, bias, scale, sid_k, sid_q, expw_part, shrunk_part, outw_part):
    seq_n, images, rows_b, wide = packed.shape
    img_n = lax.axis_size("img")
    outer = seq_n // 2
    pairs = wide // 384
    rows = seq_n * rows_b
    turns = images * pairs
    _, chunks, size, width = h1.shape
    local = chunks * size
    _, w_chunks, w_size, _ = attn_w.shape
    own = outw_part.shape[2]
    tile = 256
    blocks_per_tile = tile // (w_chunks * w_size)
    session = Session([], everyone_else("seq") + two_level("img", img_n))
    mids = [
        scatter_scratch(img_n, expw_part.shape[1:], bf16),
        scatter_scratch(seq_n, shrunk_part.shape[1:], bf16),
        scatter_scratch(seq_n, (img_n, own, width), bf16),
        scatter_scratch(img_n, (1, own, width), bf16),
        scatter_scratch(img_n, attn_w.shape[1:], bf16),
        scatter_scratch(seq_n, h1.shape[1:], bf16),
    ]

    def kernel(*refs):
        p_in, h_in, w_in, do_ref, b_ref, es_ref, sk_ref, sq_ref, expw_ref, f_ref, outw_ref = refs[:11]
        st_ref, dh1_own, attn_own, expw_own, f_own, outw_own = refs[11:17]
        scratch = refs[17:]
        p_ref, h_ref, w_ref, dp_ref, dh1, dattn, out_mid, load_sem = scratch[:8]
        k_buf, v_buf, e_buf, g_buf, dk_buf, dv_buf, do_buf, o_send, o_recv = scratch[8:17]
        more = scratch[17:]
        me = lax.axis_index("seq")
        session.greet()

        def ship(i, j):
            g, p = i // pairs, i % pairs
            return remote(
                do_ref.at[g, :, lanes(((me ^ j) * pairs + p) * 128, 128)],
                do_buf.at[i, j],
                o_send.at[j, i],
                o_recv.at[j, i],
                "seq",
                me ^ j,
            )

        def send(i):
            for j in range(1, seq_n):
                ship(i, j).start()

        each(0, turns, send)
        loads = [
            pltpu.make_async_copy(src, dst, load_sem.at[n])
            for n, (src, dst) in enumerate(((p_in, p_ref), (h_in, h_ref), (w_in, w_ref)))
        ]
        for load in loads:
            load.start()
        exp_out = scatter_ops("img", False, expw_ref, expw_own, *more[:7])
        f_out = scatter_ops("seq", True, f_ref, f_own, *more[7:14])
        mid_out = scatter_ops("seq", False, outw_ref, out_mid.at[:, 0], *more[14:21], inside=True)
        outw_out = scatter_ops("img", False, out_mid, outw_own, *more[21:28])
        attn_out = scatter_ops("img", False, dattn, attn_own, *more[28:35])
        dh1_out = scatter_ops("seq", True, dh1, dh1_own, *more[35:42])
        exp_out.start()
        mid_out.start()
        f_out.start()
        exp_chunks = expw_ref.shape[1]
        loads[0].wait()

        def turn(i):
            g, p = i // pairs, i % pairs
            query, key, value, low_half, r_query, r_key = load_heads(p_ref, b_ref[p], g, p, rows)
            scale_row = es_ref[p]
            q_unit = query * r_query
            k_unit = key * r_key
            q_full = q_unit * scale_row
            k_buf[...] = k_unit.astype(bf16).reshape(seq_n, rows_b, 128)
            v_buf[...] = value.astype(bf16).reshape(seq_n, rows_b, 128)
            do_buf[i, 0] = do_ref[g, :, lanes((me * pairs + p) * 128, 128)]
            for j in range(1, seq_n):
                ship(i, j).wait_recv()
            d_out = do_buf[i].reshape(rows, 128).astype(f32)
            sid_q = sq_ref[g]
            parts = []
            for h in range(2):
                mine = low_half if h == 0 else jnp.logical_not(low_half)
                q_f = jnp.where(mine, q_full, 0.0)
                do_f = jnp.where(mine, d_out, 0.0)
                q_h = q_f.astype(bf16)
                do_h = do_f.astype(bf16)
                q_t = jnp.transpose(q_f).astype(bf16)
                do_t = jnp.transpose(do_f).astype(bf16)

                def first(b, carry, q_t=q_t, do_t=do_t):
                    total, mixed = carry
                    scores = dot(k_buf[b], q_t, ((1,), (0,)))
                    expo = jnp.where(sk_ref[g, b] <= sid_q, jnp.exp(scores), 0.0)
                    grad = dot(v_buf[b], do_t, ((1,), (0,)))
                    e_buf[b] = expo
                    g_buf[b] = grad
                    total = total + jnp.sum(expo, axis=0, keepdims=True)
                    mixed = mixed + jnp.sum(expo * grad, axis=0, keepdims=True)
                    return total, mixed

                zero = jnp.zeros((1, rows), f32)
                total, mixed = lax.fori_loop(0, seq_n, first, (zero, zero))
                inverse = 1.0 / total
                delta = mixed * inverse

                def second(b, acc, inverse=inverse, delta=delta, q_h=q_h, do_h=do_h, h=h):
                    probs = e_buf[b] * inverse
                    scores_grad = (probs * (g_buf[b] - delta)).astype(bf16)
                    dv = dot(probs.astype(bf16), do_h, ((1,), (0,)))
                    dk = dot(scores_grad, q_h, ((1,), (0,)))
                    if h == 0:
                        dv_buf[b] = dv
                        dk_buf[b] = dk
                    else:
                        dv_buf[b] = dv_buf[b] + dv
                        dk_buf[b] = dk_buf[b] + dk
                    return acc + dot(k_buf[b], scores_grad, ((0,), (0,)))

                acc = lax.fori_loop(0, seq_n, second, jnp.zeros((128, rows), f32))
                parts.append(acc[64 * h : 64 * h + 64])
            dq = jnp.transpose(jnp.concatenate(parts, axis=0)).astype(bf16).astype(f32)
            dk = dk_buf[...].reshape(rows, 128).astype(bf16).astype(f32)
            dv = dv_buf[...].reshape(rows, 128).astype(bf16).astype(f32)
            dq_raw = scale_row * r_query * (dq - q_unit * half_sums(q_unit * dq, low_half))
            dk_raw = r_key * (dk - k_unit * half_sums(k_unit * dk, low_half))
            together = jnp.concatenate([dq_raw, dk_raw, dv], axis=1).astype(bf16)
            dp_ref[:, g, :, lanes(p * 384, 384)] = together.reshape(seq_n, rows_b, 384)
            sums = [
                jnp.sum(dq_raw, axis=0, keepdims=True),
                jnp.sum(dv, axis=0, keepdims=True),
                jnp.sum(dq * q_full, axis=0, keepdims=True),
                jnp.zeros((5, 128), f32),
            ]
            st_ref[i] = jnp.concatenate(sums, axis=0)

            @pl.when(i == 0)
            def _():
                each(0, img_n, mid_out.step)
                each(0, chunks, f_out.step)

            each((i * exp_chunks) // turns, ((i + 1) * exp_chunks) // turns, exp_out.step)

        each(0, turns, turn)
        mid_out.finish()
        outw_out.start()
        for load in loads[1:]:
            load.wait()

        def columns(t):
            return lanes(t * tile, tile)

        def weight_grad(t):
            left = h_ref[:, :, :, columns(t)].reshape(seq_n * local, tile)
            part = dot(left, dp_ref[...].reshape(seq_n * local, wide), ((0,), (0,)))
            dattn[pl.ds(t * blocks_per_tile, blocks_per_tile)] = part.astype(bf16).reshape(
                blocks_per_tile, w_chunks, w_size, wide
            )

        def input_grad(j):
            def run(t):
                weight = w_ref[pl.ds(t * blocks_per_tile, blocks_per_tile)].reshape(tile, wide)
                part = dot(dp_ref[j].reshape(local, wide), weight, ((1,), (1,)))
                dh1[j, :, :, columns(t)] = part.astype(bf16).reshape(chunks, size, tile)

            each(0, width // tile, run)

        each(0, width // tile, weight_grad)
        attn_out.start()
        outw_out.step(0)
        exp_out.finish()
        for o in range(1, outer):
            for j in (2 * o + 1, 2 * o):
                input_grad(j)
        dh1_out.start_outer()
        each(0, chunks, dh1_out.step)
        each(0, w_chunks // 2, attn_out.step)
        for j in (1, 0):
            input_grad(j)
        dh1_out.start_inner()
        each(w_chunks // 2, w_chunks, attn_out.step)
        outw_out.finish()
        f_out.finish()
        dh1_out.finish()
        attn_out.finish()

        def last(i):
            for j in range(1, seq_n):
                ship(i, j).wait_send()

        each(0, turns, last)

    full = pl.BlockSpec(memory_space=VM)
    any_space = pl.BlockSpec(memory_space=pl.ANY)
    sems = pltpu.SemaphoreType.DMA((seq_n, turns))
    return pl.pallas_call(
        kernel,
        out_shape=(
            jax.ShapeDtypeStruct((turns, 8, 128), f32),
            jax.ShapeDtypeStruct(h1.shape[1:], f32),
            jax.ShapeDtypeStruct(attn_w.shape[1:], bf16),
            jax.ShapeDtypeStruct(expw_part.shape[1:], bf16),
            jax.ShapeDtypeStruct(shrunk_part.shape[1:], f32),
            jax.ShapeDtypeStruct((1, own, width), f32),
        ),
        in_specs=[any_space] * 3 + [full] * 8,
        out_specs=(full,) * 6,
        scratch_shapes=[
            VM(packed.shape, f32),
            VM(h1.shape, bf16),
            VM(attn_w.shape, bf16),
            VM(packed.shape, bf16),
            VM(h1.shape, bf16),
            VM(attn_w.shape, bf16),
            VM((img_n, 1, own, width), bf16),
            pltpu.SemaphoreType.DMA((3,)),
            VM((seq_n, rows_b, 128), bf16),
            VM((seq_n, rows_b, 128), bf16),
            VM((seq_n, rows_b, rows), f32),
            VM((seq_n, rows_b, rows), f32),
            VM((seq_n, rows_b, 128), f32),
            VM((seq_n, rows_b, 128), f32),
            VM((turns, seq_n, rows_b, 128), bf16),
            sems,
            sems,
        ]
        + [x for scratch in mids for x in scratch],
        compiler_params=params(cid),
        name="attend_back",
    )(packed, h1, attn_w, d_out, bias, scale, sid_k, sid_q, expw_part, shrunk_part, outw_part)


def gelu_both(x):
    root = 0.7978845608028654
    square = x * x
    bent = jnp.tanh(root * x * (1.0 + 0.044715 * square))
    half = 0.5 * (1.0 + bent)
    slope = half + 0.5 * x * (1.0 - bent * bent) * (root * (1.0 + 3 * 0.044715 * square))
    return x * half, slope


def feed_forward(cid, mlp_input, grad_parts, grad_own, shr_own, exp_w, e_bias):
    seq_n, img_n = lax.axis_size("seq"), lax.axis_size("img")
    outer = seq_n // 2
    chunks, size, width = mlp_input.shape
    rows = chunks * size
    hid_l = exp_w.shape[1]
    ready, later = len(grad_parts), len(grad_own)
    images = ready + later
    g_chunks, g_size, _ = grad_own[0].shape
    w_chunks, w_size, _ = shr_own.shape
    hid_o = w_chunks * w_size
    tile = 256
    blocks_per_tile = tile // hid_o
    session = Session([], two_level("seq", seq_n) + two_level("img", img_n))

    def kernel(x_ref, *refs):
        df_refs = refs[:images]
        shr_ref, exp_ref, eb_ref, dh2_ref, dshr_own, f_ref, dexp_ref, expb_ref = refs[images : images + 8]
        h2, df, shr, act, slope, dshr, dh2, df_sem, hs, hr, ss, sr, sk, *more = refs[images + 8 :]
        df_in = [
            gather_ops("seq", True, df_refs[ready + g], df.at[:, ready + g], *more[14 + 3 * g : 17 + 3 * g])
            for g in range(later)
        ]
        session.greet()
        h2_in = gather_ops("seq", True, x_ref, h2, None, hs, hr)
        shr_in = gather_ops("img", False, shr_ref, shr, sk, ss, sr)
        dh2_out = scatter_ops("seq", True, dh2, dh2_ref, *more[:7])
        dshr_out = scatter_ops("img", False, dshr, dshr_own, *more[7:14])
        h2_in.start()
        shr_in.start()
        for ops in df_in:
            ops.start()
        loads = [pltpu.make_async_copy(ref, df.at[:, g], df_sem.at[g]) for g, ref in enumerate(df_refs[:ready])]
        for load in loads:
            load.start()
        h2[0] = x_ref[...]
        expb_ref[...] = jnp.zeros_like(expb_ref)

        def columns(t):
            return lanes(t * tile, tile)

        def expand(j):
            def run(t):
                u = dot(h2[j].reshape(rows, width), exp_ref[:, columns(t)], ((1,), (0,))) + eb_ref[:, columns(t)]
                value, grad = gelu_both(u)
                act[j, :, columns(t)] = value.astype(bf16)
                slope[j, :, columns(t)] = grad.astype(bf16)

            each(0, hid_l // tile, run)

        def back_act(j):
            def run(t):
                weight = shr[pl.ds(t * blocks_per_tile, blocks_per_tile)].reshape(tile, width)
                grad = dot(df[j].reshape(rows, width), weight, ((1,), (1,)))
                grad = (slope[j, :, columns(t)].astype(f32) * grad).astype(bf16)
                slope[j, :, columns(t)] = grad
                expb_ref[:, columns(t)] += jnp.sum(grad.astype(f32), axis=0, keepdims=True)

            each(0, hid_l // tile, run)

        def back_input(j):
            def run(t):
                weight = exp_ref[pl.ds(pl.multiple_of(t * tile, tile), tile), :]
                part = dot(slope[j], weight, ((1,), (1,)))
                dh2[j, :, :, columns(t)] = part.astype(bf16).reshape(chunks, size, tile)

            each(0, width // tile, run)

        def shrink(j):
            def run(t):
                weight = shr[:, :, :, columns(t)].reshape(hid_l, tile)
                part = dot(act[j], weight, ((1,), (0,)))
                f_ref[j, :, :, columns(t)] = part.astype(bf16).reshape(chunks, size, tile)

            each(0, width // tile, run)

        def shrink_grad(t):
            left = act[:, :, columns(t)].reshape(seq_n * rows, tile)
            part = dot(left, df[...].reshape(seq_n * rows, width), ((0,), (0,)))
            part = part.astype(bf16).reshape(blocks_per_tile, w_chunks, w_size, width)
            dshr[pl.ds(t * blocks_per_tile, blocks_per_tile)] = part

        def expand_grad(t):
            left = h2[:, :, :, columns(t)].reshape(seq_n * rows, tile)
            part = dot(left, slope[...].reshape(seq_n * rows, hid_l), ((0,), (0,)))
            dexp_ref[pl.ds(pl.multiple_of(t * tile, tile), tile), :] = part.astype(bf16)

        expand(0)
        h2_in.near()
        expand(1)
        half = chunks // 2
        each(0, half, h2_in.step)
        each(0, w_chunks // 2, shr_in.step)
        each(half, chunks, h2_in.step)
        for o in range(1, outer):
            expand(2 * o)
        each(w_chunks // 2, w_chunks, shr_in.step)
        for ops in df_in:
            each(0, g_chunks, ops.step)
        for o in range(1, outer):
            h2_in.handed(o)
            expand(2 * o + 1)
        for ops in df_in:
            ops.finish()
        for load in loads:
            load.wait()
        each(0, hid_l // tile, shrink_grad)
        shr_in.near()
        for o in range(1, img_n // 2):
            shr_in.handed(o)
        shr_in.sent()
        dshr_out.start()
        for o in range(1, outer):
            for j in (2 * o + 1, 2 * o):
                back_act(j)
                back_input(j)
        dh2_out.start_outer()
        each(0, chunks, dh2_out.step)
        each(0, w_chunks // 2, dshr_out.step)
        for j in (1, 0):
            back_act(j)
            back_input(j)
        dh2_out.start_inner()
        each(w_chunks // 2, w_chunks, dshr_out.step)
        h2_in.sent()
        for j in range(seq_n):
            shrink(j)
        each(0, width // tile, expand_grad)
        dh2_out.finish()
        dshr_out.finish()

    full = pl.BlockSpec(memory_space=VM)
    any_space = pl.BlockSpec(memory_space=pl.ANY)
    seq_sems = pltpu.SemaphoreType.DMA((seq_n, chunks))
    img_sems = pltpu.SemaphoreType.DMA((img_n, w_chunks))
    grad_sems = pltpu.SemaphoreType.DMA((seq_n, g_chunks))
    return pl.pallas_call(
        kernel,
        out_shape=(
            jax.ShapeDtypeStruct(mlp_input.shape, f32),
            jax.ShapeDtypeStruct(shr_own.shape, f32),
            jax.ShapeDtypeStruct((seq_n,) + mlp_input.shape, bf16),
            jax.ShapeDtypeStruct(exp_w.shape, bf16),
            jax.ShapeDtypeStruct((1, hid_l), f32),
        ),
        in_specs=[full] + [any_space] * ready + [full] * (later + 3),
        out_specs=(full,) * 5,
        scratch_shapes=[
            VM((seq_n,) + mlp_input.shape, bf16),
            VM((seq_n, images, g_chunks, g_size, width), bf16),
            VM((img_n,) + shr_own.shape, bf16),
            VM((seq_n, rows, hid_l), bf16),
            VM((seq_n, rows, hid_l), bf16),
            VM((img_n,) + shr_own.shape, bf16),
            VM((seq_n,) + mlp_input.shape, bf16),
            pltpu.SemaphoreType.DMA((max(ready, 1),)),
            seq_sems,
            seq_sems,
            img_sems,
            img_sems,
            pltpu.SemaphoreType.DMA((w_chunks,)),
        ]
        + scatter_scratch(seq_n, mlp_input.shape, bf16)
        + scatter_scratch(img_n, shr_own.shape, bf16)
        + [pltpu.SemaphoreType.DMA((g_chunks,)), grad_sems, grad_sems] * later,
        compiler_params=params(cid),
        name="feed_forward",
    )(mlp_input, *grad_parts, *grad_own, shr_own, exp_w, e_bias)


def normalize(values):
    centered = values - jnp.mean(values, axis=-1, keepdims=True)
    return centered * lax.rsqrt(jnp.mean(centered * centered, axis=-1, keepdims=True) + 1e-06)


def norm_back(values, grad_rows):
    return jax.vjp(normalize, values)[1](grad_rows)[0]


def pad_to(x, size, axis):
    widths = [(0, 0)] * x.ndim
    widths[axis] = (0, size - x.shape[axis])
    return jnp.pad(x, widths)


def mm(a, b):
    return jnp.dot(a, b, preferred_element_type=f32)


def mm_nt(a, b):
    return lax.dot_general(a, b, (((1,), (1,)), ((), ())), preferred_element_type=f32)


def mm_tn(a, b):
    return lax.dot_general(a, b, (((0,), (0,)), ((), ())), preferred_element_type=f32)


def body(
    tokens,
    cotangent,
    condition,
    scale_sizes,
    mod_weight,
    mod_bias,
    attn_weight,
    query_bias,
    value_bias,
    out_weight,
    out_bias,
    expand_weight,
    expand_bias,
    shrink_weight,
    shrink_bias,
    log_scale,
):
    images, rows, width = tokens.shape
    heads = log_scale.shape[0]
    headdim = width // heads
    seq_n = lax.axis_size("seq")
    img_n = lax.axis_size("img")
    seq_i = lax.axis_index("seq")
    img_i = lax.axis_index("img")
    rank = img_i * seq_n + seq_i
    ranks = img_n * seq_n
    own = width // ranks
    rows_p = -(-rows // 16) * 16
    dim_l = width // seq_n
    pairs = dim_l // 128
    hidden = expand_bias.shape[0] * ranks
    hid_l = hidden // seq_n
    hid_o = hidden // ranks
    mods = mod_weight.shape[1]
    mod_o = mods // ranks

    mod_l = mods // seq_n
    blk = own * seq_n

    attn_cut = (
        attn_weight.astype(bf16)
        .reshape(own, 3, seq_n, pairs, 128)
        .transpose(2, 0, 3, 1, 4)
        .reshape(seq_n, own, 3 * dim_l)
    )
    exp_cut = (
        expand_weight.astype(bf16)
        .reshape(own, img_n, seq_n, hid_o)
        .transpose(2, 0, 1, 3)
        .reshape(seq_n, own, hid_l)
    )
    mod_cut = mod_weight.astype(bf16).reshape(own, seq_n, mod_l).transpose(1, 0, 2)
    silu_cond = jax.nn.silu(condition).astype(bf16).astype(f32)
    small_bias = jnp.concatenate([query_bias, value_bias, out_bias, shrink_bias, expand_bias, mod_bias])
    small_bias = lax.reduce_precision(small_bias, 8, 7)
    bias_n = small_bias.shape[0]
    bias_rows = -(-bias_n // 1024) * 8
    small_bias = pad_to(small_bias, bias_rows * 128, 0).reshape(1, bias_rows, 128)
    cond_cut = silu_cond.reshape(images, img_n, seq_n, own).transpose(1, 2, 0, 3).reshape(img_n, seq_n * images, own)
    small = jnp.concatenate(
        [pad_to(cond_cut, 128, 2), jnp.broadcast_to(small_bias, (img_n, bias_rows, 128))], axis=1
    )
    mod_all, bias_all, cond_rows, modw_cut, attn_b, exp_b, out_img = opening(
        1,
        mod_cut,
        attn_cut,
        exp_cut,
        small,
        images,
        [gather(out_weight.astype(bf16)[None], "img", False)],
    )
    out_img = out_img.reshape(img_n, own, width)
    attn_b = attn_b.reshape(blk, 3 * dim_l)
    exp_b = exp_b.reshape(blk, hid_l)

    def weight_chunks(x):
        step = max(blk // 4, 8)
        return x.reshape(x.shape[:-2] + (blk // step, step, x.shape[-1]))

    def hidden_chunks(x):
        step = max(hid_o // 4, 16)
        return x.reshape(x.shape[:-2] + (hid_o // step, step, x.shape[-1]))

    tiles = mod_l // 128
    modulation = mod_all[:, : tiles * images].reshape(seq_n, tiles, images, 128).transpose(2, 0, 1, 3)
    bias_all = bias_all.reshape(seq_n, img_n, bias_rows * 128)[:, :, :bias_n].transpose(1, 0, 2)
    q_bias = bias_all[:, :, :own].reshape(width)
    v_bias = bias_all[:, :, own : 2 * own].reshape(width)
    o_bias = bias_all[:, :, 2 * own : 3 * own].reshape(width)
    s_bias = bias_all[:, :, 3 * own : 4 * own].reshape(width)
    e_bias = bias_all[:, :, 4 * own : 4 * own + hid_o]
    e_bias = lax.dynamic_slice_in_dim(e_bias, seq_i, 1, 1).reshape(hid_l)
    m_bias = bias_all[:, :, 4 * own + hid_o :].reshape(mods)
    modulation = modulation.reshape(images, mods) + m_bias[None]
    qb_l = lax.dynamic_slice_in_dim(q_bias, seq_i * dim_l, dim_l, 0).reshape(pairs, 1, 128)
    vb_l = lax.dynamic_slice_in_dim(v_bias, seq_i * dim_l, dim_l, 0).reshape(pairs, 1, 128)
    pair_bias = jnp.concatenate([qb_l, jnp.zeros_like(qb_l), vb_l], axis=2)
    head_scale = jnp.exp(jnp.repeat(log_scale, headdim))
    pair_scale = lax.dynamic_slice_in_dim(head_scale, seq_i * dim_l, dim_l, 0).reshape(pairs, 1, 128)
    gain_attn, gain_mlp, scale_attn, scale_mlp, shift_attn, shift_mlp = jnp.split(
        modulation[:, None, :], 6, axis=-1
    )

    ends = jnp.cumsum(scale_sizes, axis=-1)
    offset = jnp.arange(rows_p, dtype=jnp.int32)
    place = (seq_i ^ jnp.arange(seq_n, dtype=jnp.int32))[:, None] * rows + offset[None]
    sid = jnp.sum((place[None, :, :, None] >= ends[:, None, None, :]).astype(jnp.int32), axis=-1)
    sid_q = sid.reshape(images, 1, seq_n * rows_p)
    sid_k = jnp.where(offset[None, None] < rows, sid, 1 << 20)[..., None]

    resid_in = pad_to(tokens, rows_p, 1).astype(f32)
    grad_out = pad_to(cotangent, rows_p, 1).astype(f32)
    local = images * rows_p

    def chunked(x):
        return x.reshape(x.shape[: x.ndim - 3] + (local // 32, 32, width))

    normed_in = normalize(resid_in)
    attn_input = (normed_in * (1.0 + scale_attn) + shift_attn).astype(bf16)
    grad_shrunk = (grad_out * gain_mlp).astype(bf16)
    grad_chunks = grad_shrunk.reshape(images, rows_p // 16, 16, width)
    ready = images // 2
    context_low, packed, h1, attn_w, *gathered = attend(
        5,
        chunked(attn_input),
        weight_chunks(attn_b),
        pair_bias,
        pair_scale,
        sid_k,
        sid_q,
        out_img,
        weight_chunks(exp_b),
        [grad_chunks[g] for g in range(ready)],
    )
    df_ready, out_w, exp_w = gathered[:ready], gathered[ready], gathered[ready + 1]
    context_low = context_low.reshape(local, width)
    out_w = out_w.reshape(width, width)
    exp_w = exp_w.reshape(width, hid_l)
    attn_out = (mm(context_low, out_w) + o_bias).reshape(images, rows_p, width)
    resid_mid = resid_in + gain_attn * attn_out
    normed_mid = normalize(resid_mid)
    mlp_input = (normed_mid * (1.0 + scale_mlp) + shift_mlp).astype(bf16)
    shrb_part = jnp.sum(grad_shrunk.astype(f32), axis=(0, 1))
    grad_mlp_input, shrw_own, shrunk_part, expw_part, expb_part = feed_forward(
        7,
        chunked(mlp_input),
        df_ready,
        [grad_chunks[g] for g in range(ready, images)],
        hidden_chunks(shrink_weight.astype(bf16)),
        exp_w,
        e_bias.reshape(1, hid_l),
    )
    grad_mlp_input = grad_mlp_input.reshape(images, rows_p, width)
    shrw_own = shrw_own.reshape(hid_o, width)
    expb_part = expb_part.reshape(hid_l)
    expw_part = expw_part.reshape(img_n, blk, hid_l)

    grad_scale_mlp = jnp.sum(grad_mlp_input * normed_mid, axis=1)
    grad_shift_mlp = jnp.sum(grad_mlp_input, axis=1)
    grad_mid = grad_out + norm_back(resid_mid, grad_mlp_input * (1.0 + scale_mlp))
    grad_gain_attn = jnp.sum(grad_mid * attn_out, axis=1)
    grad_attn_out = (grad_mid * gain_attn).astype(bf16)
    outb_part = jnp.sum(grad_attn_out.astype(f32), axis=(0, 1))
    da = grad_attn_out.reshape(local, width)
    grad_context = mm_nt(da, out_w).astype(bf16)
    grad_context = grad_context.reshape(images, rows_p, width)
    outw_part = mm_tn(context_low, da).astype(bf16).reshape(img_n, seq_n, own, width)
    sums, grad_attn_input, attnw_blk, expw_blk, shrunk, outw_own = attend_back(
        11,
        packed,
        h1,
        attn_w,
        grad_context,
        pair_bias,
        pair_scale,
        sid_k,
        sid_q,
        weight_chunks(expw_part),
        shrunk_part,
        outw_part,
    )
    shrunk = shrunk.reshape(images, rows_p, width) + s_bias
    layer_out = (resid_mid + gain_mlp * shrunk).astype(bf16)
    grad_gain_mlp = jnp.sum(grad_out * shrunk, axis=1)
    sums = jnp.sum(sums.reshape(images, pairs, 8, 128), axis=0)
    qb_part = sums[:, 0].reshape(dim_l)
    vb_part = sums[:, 1].reshape(dim_l)
    logs_part = jnp.sum(sums[:, 2].reshape(dim_l // headdim, headdim), axis=1)
    outw_own = outw_own.reshape(own, width)
    grad_attn_input = grad_attn_input.reshape(images, rows_p, width)
    grad_scale_attn = jnp.sum(grad_attn_input * normed_in, axis=1)
    grad_shift_attn = jnp.sum(grad_attn_input, axis=1)
    token_grad = grad_mid + norm_back(resid_in, grad_attn_input * (1.0 + scale_attn))
    token_grad = token_grad.astype(bf16)

    grad_mod = jnp.concatenate(
        [grad_gain_attn, grad_gain_mlp, grad_scale_attn, grad_scale_mlp, grad_shift_attn, grad_shift_mlp],
        axis=-1,
    )
    grad_mod = grad_mod.reshape(images, seq_n, tiles, 128).transpose(1, 2, 0, 3).reshape(seq_n, tiles * images, 128)
    grad_mod = pad_to(grad_mod, -(-tiles * images // 8) * 8, 1)

    def lined(vector, count):
        return pad_to(vector.reshape(count, -1), 128, 1)

    heads_l = heads // seq_n
    logs_row = lax.dynamic_update_slice_in_dim(jnp.zeros((128,), f32), logs_part, seq_i * heads_l, 0)
    bias_mine = jnp.concatenate(
        [
            lined(shrb_part, img_n),
            lined(outb_part, img_n),
            pad_to(logs_row[None], 8, 0),
            lined(qb_part, img_n // seq_n),
            lined(vb_part, img_n // seq_n),
        ]
    )
    bias_mine = pad_to(bias_mine, -(-bias_mine.shape[0] // 8) * 8, 0)
    mine = jnp.concatenate([grad_mod, jnp.broadcast_to(bias_mine[None], (seq_n,) + bias_mine.shape)], axis=1)
    back_cut = jnp.concatenate(
        [attnw_blk.reshape(seq_n, own, 3 * dim_l), expw_blk.reshape(seq_n, own, hid_l)], axis=2
    )
    modw_own, attnw_own, expw_own, bias_own, modb_all, cond_sum = closing(
        13, mine, lined(expb_part, img_n), cond_rows, modw_cut, back_cut, images, pairs
    )

    def part_of(row):
        return lax.dynamic_slice_in_dim(bias_own[row], seq_i * own, own, 0)

    shrb_own, outb_own, qb_own, vb_own = part_of(0), part_of(1), part_of(2), part_of(3)
    expb_own = bias_own[4, :hid_o]
    logs_total = bias_own[5, :heads]
    modb_own = lax.dynamic_slice_in_dim(modb_all[:, :tiles].reshape(mods), rank * mod_o, mod_o, 0)
    grad_silu = cond_sum[:, :, :own].reshape(img_n, seq_n, images, own).transpose(2, 0, 1, 3).reshape(images, width)
    cond_grad = jax.vjp(jax.nn.silu, condition)[1](grad_silu)[0]
    return (
        layer_out[:, :rows],
        token_grad[:, :rows],
        cond_grad,
        modw_own,
        modb_own,
        attnw_own,
        qb_own,
        vb_own,
        outw_own,
        outb_own,
        expw_own,
        expb_own,
        shrw_own,
        shrb_own,
        logs_total,
    )


def solution(mesh):
    both = P(("img", "seq"))
    rows = P(("img", "seq"), None)
    return jax.shard_map(
        body,
        mesh=mesh,
        in_specs=(
            P("img", "seq", None),
            P("img", "seq", None),
            P("img", None),
            P("img", None),
            rows,
            both,
            rows,
            both,
            both,
            rows,
            both,
            rows,
            both,
            rows,
            both,
            P(),
        ),
        out_specs=(
            P("img", "seq", None),
            P("img", "seq", None),
            P("img", None),
            rows,
            both,
            rows,
            both,
            both,
            rows,
            both,
            rows,
            both,
            rows,
            both,
            P(),
        ),
        check_vma=False,
    )
```

```python
from types import SimpleNamespace

import jax
import jax.numpy as jnp
from jax import lax
from jax.experimental import pallas as pl
from jax.experimental.pallas import tpu as pltpu
from jax.sharding import PartitionSpec as P

HIGH = lax.Precision.HIGHEST
MESH = pl.DeviceIdType.MESH
bf16 = jnp.bfloat16
f32 = jnp.float32
VM = pltpu.VMEM
LIMIT = 62 << 20


class Plan:
    def __init__(self, ins, out, scratch, peers, count, bind, out_space=VM):
        self.ins, self.out, self.out_space = ins, out, out_space
        self.scratch, self.peers, self.count, self.bind = scratch, peers, count, bind
        self.window = None

    def during(self, low, high):
        self.window = (low, high)
        return self


def remote(src, dst, send, recv, axis, peer):
    return pltpu.make_async_remote_copy(
        src_ref=src, dst_ref=dst, send_sem=send, recv_sem=recv, device_id={axis: peer}, device_id_type=MESH
    )


def each(low, high, run):
    def once(i, carry):
        run(i)
        return carry

    lax.fori_loop(low, high, once, 0)


def direct_ops(axis, x_ref, out_ref, send, recv, everyone=False, src_rel=False, dst_rel=False):
    n = lax.axis_size(axis)
    me = lax.axis_index(axis)

    def copy(j):
        src = x_ref if everyone else x_ref.at[j if src_rel else me ^ j]
        return remote(src, out_ref.at[j if dst_rel else me], send.at[j], recv.at[j], axis, me ^ j)

    def start():
        for j in range(1, n):
            copy(j).start()
        out_ref[0 if dst_rel else me] = x_ref[...] if everyone else x_ref[0 if src_rel else me]

    def finish():
        for j in range(1, n):
            copy(j).wait()

    return start, finish


def two_level(axis, n):
    return [(axis, 1)] + [(axis, 2 * o) for o in range(1, n // 2)]


def gather_ops(axis, rel, x_ref, out_ref, own, send, recv, inside=False):
    n = lax.axis_size(axis)
    outer = n // 2
    chunks = x_ref.shape[0]
    me = lax.axis_index(axis)

    def place(sender, j, c):
        block = j if rel else sender
        return out_ref.at[c, block] if inside else out_ref.at[block, c]

    def keep(c):
        return pltpu.make_async_copy(x_ref.at[c], place(me, 0, c), own.at[c])

    def push(j, c):
        return remote(x_ref.at[c], place(me, j, c), send.at[j, c], recv.at[j, c], axis, me ^ j)

    def hand(j, c):
        far = me ^ j
        return remote(place(far, j, c), place(far, j + 1, c), send.at[j + 1, c], recv.at[j + 1, c], axis, me ^ 1)

    def start():
        def first(c):
            for o in range(1, outer):
                push(2 * o, c).start()

        def second(c):
            push(1, c).start()
            if own is not None:
                keep(c).start()

        each(0, chunks, first)
        each(0, chunks, second)

    def step(c):
        for o in range(1, outer):
            push(2 * o, c).wait_recv()
            hand(2 * o, c).start()

    def near():
        each(0, chunks, lambda c: push(1, c).wait_recv())

    def handed(o):
        each(0, chunks, lambda c: hand(2 * o, c).wait_recv())

    def sent():
        def last(c):
            for o in range(1, outer):
                push(2 * o, c).wait_send()
                hand(2 * o, c).wait_send()
            push(1, c).wait_send()
            if own is not None:
                keep(c).wait()

        each(0, chunks, last)

    def finish():
        near()
        for o in range(1, outer):
            handed(o)
        sent()

    return SimpleNamespace(start=start, step=step, near=near, handed=handed, sent=sent, finish=finish)


def gather(x, axis, rel, inside=False):
    n = lax.axis_size(axis)
    chunks = x.shape[0]

    def bind(x_ref, out_ref, own, send, recv):
        return gather_ops(axis, rel, x_ref, out_ref, own, send, recv, inside)

    sems = pltpu.SemaphoreType.DMA((n, chunks))
    shape = (chunks, n) + x.shape[1:] if inside else (n,) + x.shape
    out = jax.ShapeDtypeStruct(shape, x.dtype)
    scratch = [pltpu.SemaphoreType.DMA((chunks,)), sems, sems]
    return Plan([x], out, scratch, two_level(axis, n), chunks, bind, pl.ANY)


def scatter_ops(axis, rel, x_ref, out_ref, near_buf, send_buf, far_buf, s1, r1, s2, r2, inside=False, held=None):
    n = lax.axis_size(axis)
    outer = n // 2
    chunks = out_ref.shape[0]
    me = lax.axis_index(axis)

    def part(j, c, ref=x_ref):
        block = j if rel else me ^ j
        return ref.at[c, block] if inside else ref.at[block, c]

    def mine(j, c):
        return part(j, c, x_ref if held is None else held)[...].astype(f32)

    def near(o, c):
        return remote(part(2 * o + 1, c), near_buf.at[o, c], s1.at[o, c], r1.at[o, c], axis, me ^ 1)

    def far(o, c):
        return remote(send_buf.at[o, c], far_buf.at[o, c], s2.at[o, c], r2.at[o, c], axis, me ^ (2 * o))

    def start_outer():
        def first(c):
            for o in range(1, outer):
                near(o, c).start()

        each(0, chunks, first)

    def start_inner():
        each(0, chunks, lambda c: near(0, c).start())

    def start():
        start_outer()
        start_inner()

    def step(c):
        for o in range(1, outer):
            near(o, c).wait_recv()
            total = mine(2 * o, c) + near_buf[o, c].astype(f32)
            send_buf[o, c] = total.astype(send_buf.dtype)
            far(o, c).start()

    def finish():
        def last(c):
            near(0, c).wait_recv()
            total = mine(0, c) + near_buf[0, c].astype(f32)
            for o in range(1, outer):
                far(o, c).wait_recv()
                total = total + far_buf[o, c].astype(f32)
            out_ref[c] = total.astype(out_ref.dtype)
            for o in range(outer):
                near(o, c).wait_send()
            for o in range(1, outer):
                far(o, c).wait_send()

        each(0, chunks, last)

    return SimpleNamespace(
        start=start, start_outer=start_outer, start_inner=start_inner, step=step, finish=finish
    )


def scatter_scratch(n, inner, dtype):
    half = VM((n // 2,) + inner, dtype)
    sems = pltpu.SemaphoreType.DMA((n // 2, inner[0]))
    return [half, half, half, sems, sems, sems, sems]


class Session:
    def __init__(self, plans, more_peers=()):
        self.plans = plans
        self.ins = [x for p in plans for x in p.ins]
        self.outs = [p.out for p in plans]
        self.in_specs = [pl.BlockSpec(memory_space=VM)] * len(self.ins)
        self.out_specs = [pl.BlockSpec(memory_space=p.out_space) for p in plans]
        self.scratch = [scr for p in plans for scr in p.scratch]
        self.peers = sorted({peer for p in plans for peer in p.peers} | set(more_peers))

    def greet(self):
        barrier = pltpu.get_barrier_semaphore()
        for axis, j in self.peers:
            pl.semaphore_signal(barrier, inc=1, device_id={axis: lax.axis_index(axis) ^ j}, device_id_type=MESH)
        pl.semaphore_wait(barrier, len(self.peers))

    def bind(self, ins, outs, scratch):
        at_in = at_scr = 0
        self.bound = []
        for p, out in zip(self.plans, outs):
            mine = ins[at_in : at_in + len(p.ins)]
            own = scratch[at_scr : at_scr + len(p.scratch)]
            self.bound.append((p.count, p.window, p.bind(*mine, out, *own)))
            at_in += len(p.ins)
            at_scr += len(p.scratch)

    def start(self):
        for _, _, ops in self.bound:
            ops.start()

    def steps(self, i, total):
        for count, window, ops in self.bound:
            low, high = window or (0, total)
            span = high - low

            def some(ops=ops, count=count, low=low, span=span):
                if count == span:
                    ops.step(i - low)
                else:
                    each(((i - low) * count) // span, ((i - low + 1) * count) // span, ops.step)

            if not count:
                continue
            if span == total:
                some()
            else:
                pl.when(jnp.logical_and(i >= low, i < high))(some)

    def finish(self):
        for _, _, ops in self.bound:
            ops.finish()


def everyone_else(*axes):
    return [(axis, j) for axis in axes for j in range(1, lax.axis_size(axis))]


def pairs_of_sems(*axes):
    return [pltpu.SemaphoreType.DMA((lax.axis_size(axis),)) for axis in axes for _ in range(2)]


def params(cid):
    return pltpu.CompilerParams(collective_id=cid, has_side_effects=True, vmem_limit_bytes=LIMIT)


def opening(cid, mod_w, attn_w, exp_w, out_w, small, seq_n, images, pairs, early):
    raw = mod_w.dtype == f32
    own, width = out_w.shape
    dim_l = pairs * 128
    img_n, rows, _ = small.shape
    cuts = [x.size // (seq_n * own) for x in (mod_w, attn_w, exp_w)]
    mod_l, _, hid_l = cuts
    hid_o = hid_l // img_n
    head = seq_n * images
    tiles = mod_l // 128
    slim = -(-tiles * images // 8) * 8
    count = max(early, 1)
    shapes = [(seq_n, own, c) for c in cuts]
    session = Session([], everyone_else("img", "seq"))

    def kernel(
        mod_in, attn_in, exp_in, out_in, small_ref,
        modo_ref, bias_ref, lhs_ref, modw_ref, attnw_ref, expw_ref, early_ref, outw_ref,
        small_all, part_buf, part_all, sum_buf, *more
    ):
        if raw:
            mod_ref, attn_ref, exp_ref, out_ref, *sems = more
            out_ref[0] = out_in[...].astype(bf16)
            for q in range(seq_n):
                mod_ref[q] = mod_in[:, q * mod_l : (q + 1) * mod_l].astype(bf16)
        else:
            mod_ref, attn_ref, exp_ref = mod_in, attn_in, exp_in
            out_ref, *sems = more
            out_ref[0] = out_in[...].astype(bf16)
        early_in = gather_ops("img", False, attnw_ref.at[:count], early_ref, *sems[14:17])
        out_go = gather_ops("img", False, out_ref, outw_ref, *sems[17:20])
        session.greet()
        small_go, small_end = direct_ops("img", small_ref, small_all, *sems[:2])
        mod_go, mod_end = direct_ops("seq", mod_ref, modw_ref, *sems[2:4])
        attn_go, attn_end = direct_ops("seq", attn_ref, attnw_ref, *sems[4:6])
        exp_go, exp_end = direct_ops("seq", exp_ref, expw_ref, *sems[12:14])
        small_go()
        mod_go()
        if raw:
            for q in range(seq_n):
                for p in range(pairs):
                    for k in range(3):
                        at = k * width + q * dim_l + p * 128
                        to = p * 384 + k * 128
                        attn_ref[q, :, to : to + 128] = attn_in[:, at : at + 128].astype(bf16)
        attn_go()
        if raw:
            for q in range(seq_n):
                for i in range(img_n):
                    at = (i * seq_n + q) * hid_o
                    exp_ref[q, :, i * hid_o : (i + 1) * hid_o] = exp_in[:, at : at + hid_o].astype(bf16)
        exp_go()
        out_go.start()
        part_buf[...] = jnp.zeros_like(part_buf)
        small_end()
        bias_go, bias_end = direct_ops("seq", small_all.at[:, head:], bias_ref, *sems[6:8], everyone=True)
        bias_go()
        for i in range(img_n):
            for q in range(seq_n):
                lhs_ref[q, i * images : (i + 1) * images] = small_all[i, q * images : (q + 1) * images]
        mod_end()
        part = jnp.zeros((img_n * images, mod_l), f32)
        for q in range(seq_n):
            part = part + dot(lhs_ref[q][:, :own].astype(bf16), modw_ref[q], ((1,), (0,)))
        for i in range(img_n):
            for t in range(tiles):
                part_buf[i, t * images : (t + 1) * images] = part[
                    i * images : (i + 1) * images, t * 128 : (t + 1) * 128
                ]
        part_go, part_end = direct_ops("img", part_buf, part_all, *sems[8:10])
        part_go()
        out_go.step(0)
        attn_end()
        if early:
            early_in.start()
        part_end()
        total = part_all[0]
        for i in range(1, img_n):
            total = total + part_all[i]
        sum_buf[...] = total
        sum_go, sum_end = direct_ops("seq", sum_buf, modo_ref, *sems[10:12], everyone=True)
        sum_go()
        if early:
            each(0, early, early_in.step)
        bias_end()
        sum_end()
        exp_end()
        out_go.finish()
        if early:
            early_in.finish()

    full = pl.BlockSpec(memory_space=VM)
    any_space = pl.BlockSpec(memory_space=pl.ANY)
    sending = [VM(x, bf16) for x in shapes] if raw else []
    return pl.pallas_call(
        kernel,
        out_shape=(
            jax.ShapeDtypeStruct((seq_n, slim, 128), f32),
            jax.ShapeDtypeStruct((seq_n, img_n, rows - head, 128), f32),
            jax.ShapeDtypeStruct((seq_n, img_n * images, 128), f32),
            *[jax.ShapeDtypeStruct(x, bf16) for x in shapes],
            jax.ShapeDtypeStruct((img_n, count) + shapes[1][1:], bf16),
            jax.ShapeDtypeStruct((img_n, 1, own, width), bf16),
        ),
        in_specs=[full] * 5,
        out_specs=(full,) * 6 + (any_space,) * 2,
        scratch_shapes=[
            VM(small.shape, f32),
            VM((img_n, slim, 128), f32),
            VM((img_n, slim, 128), f32),
            VM((slim, 128), f32),
        ]
        + sending
        + [VM((1, own, width), bf16)]
        + pairs_of_sems("img", "seq", "seq", "seq", "img", "seq", "seq")
        + [pltpu.SemaphoreType.DMA((count,))]
        + [pltpu.SemaphoreType.DMA((img_n, count))] * 2
        + [pltpu.SemaphoreType.DMA((1,))]
        + [pltpu.SemaphoreType.DMA((img_n, 1))] * 2,
        compiler_params=params(cid),
        name="opening",
    )(mod_w, attn_w, exp_w, out_w, small)


def finishing(modw, attnw, expw, bias, outw, shrw, heads):
    own, width = outw.shape
    hid_o = shrw.shape[0]

    def kernel(modw_ref, attnw_ref, expw_ref, bias_ref, outw_ref, shrw_ref, *outs):
        for src, out in zip((modw_ref, attnw_ref, expw_ref, outw_ref, shrw_ref), outs):
            out[...] = src[...].astype(f32)
        shift = (128 - lax.axis_index("seq") * own) % 128
        rolled = pltpu.roll(bias_ref[...], shift, 1)
        for row in range(4):
            outs[5 + row][...] = rolled[row : row + 1, :own]
        outs[9][...] = bias_ref[4:5, :hid_o]
        outs[10][...] = bias_ref[5:6, :heads]

    full = pl.BlockSpec(memory_space=VM)
    shapes = [modw.shape, attnw.shape, expw.shape, outw.shape, shrw.shape] + [(1, own)] * 4 + [(1, hid_o), (1, heads)]
    got = pl.pallas_call(
        kernel,
        out_shape=tuple(jax.ShapeDtypeStruct(x, f32) for x in shapes),
        in_specs=[full] * 6,
        out_specs=(full,) * len(shapes),
        compiler_params=pltpu.CompilerParams(vmem_limit_bytes=LIMIT),
        name="finishing",
    )(modw, attnw, expw, bias, outw, shrw)
    return list(got[:5]) + [x.reshape(-1) for x in got[5:]]


def closing(cid, mine, expb, lhs, modw, back, images, pairs):
    seq_n, own, mod_l = modw.shape
    img_n = expb.shape[0]
    rows = mine.shape[1]
    head = seq_n * images
    tiles = mod_l // 128
    slim = -(-tiles * images // 8) * 8
    share = img_n // seq_n
    cut = back.shape[2]
    dim_l = pairs * 128
    width = dim_l * seq_n
    hid_l = cut - 3 * dim_l
    hid_o = hid_l // img_n
    aligned = hid_o % 128 == 0
    flat = -(-tiles // 8) * 8

    def kernel(
        mine_ref, expb_ref, lhs_ref, modw_ref, back_ref,
        modw_own, attn_own, exp_own, bias_ref, modb_ref, cond_ref,
        seen, block, got, dd, mw_send, mw_recv, mb_send, gs_send, gs_all, gs_seen, back_all, *sems
    ):
        barrier = Session([], everyone_else("img", "seq"))
        barrier.greet()
        mine_go, mine_end = direct_ops("seq", mine_ref, seen, *sems[:2])
        back_go, back_end = direct_ops("seq", back_ref, back_all, *sems[2:4])
        mine_go()
        back_go()
        block[...] = jnp.zeros_like(block)
        gs_send[...] = jnp.zeros_like(gs_send)
        mb_send[...] = jnp.zeros_like(mb_send)
        mine_end()
        total = seen[0]
        for q in range(1, seq_n):
            total = total + seen[q]
        at = slim + 2 * img_n
        for i in range(img_n):
            block[i, :slim] = total[:slim]
            block[i, slim : slim + 1] = total[slim + i : slim + i + 1]
            block[i, slim + 1 : slim + 2] = total[slim + img_n + i : slim + img_n + i + 1]
            row = at + 8 + i % share
            block[i, slim + 2 : slim + 3] = seen[i // share, row : row + 1]
            block[i, slim + 3 : slim + 4] = seen[i // share, row + share : row + share + 1]
            block[i, slim + 4 : slim + 5] = expb_ref[i : i + 1]
            block[i, slim + 5 : slim + 6] = total[at : at + 1]
        img_go, img_end = direct_ops("img", block, got, *sems[4:6])
        img_go()
        back_end()
        for q in range(seq_n):
            for p in range(pairs):
                for k in range(3):
                    to = k * width + q * dim_l + p * 128
                    at_c = p * 384 + k * 128
                    attn_own[:, to : to + 128] = back_all[q, :, at_c : at_c + 128]
            if aligned:
                for i in range(img_n):
                    to = (i * seq_n + q) * hid_o
                    at_c = 3 * dim_l + i * hid_o
                    exp_own[:, to : to + hid_o] = back_all[q, :, at_c : at_c + hid_o]
            else:
                exp_own[:, q * hid_l : (q + 1) * hid_l] = back_all[q, :, 3 * dim_l :]
        img_end()
        sums = got[0]
        for i in range(1, img_n):
            sums = sums + got[i]
        bias_ref[...] = sums[slim:]
        for t in range(tiles):
            mb_send[t : t + 1] = jnp.sum(sums[t * images : (t + 1) * images], axis=0, keepdims=True)
            for i in range(img_n):
                dd[i * images : (i + 1) * images, t * 128 : (t + 1) * 128] = got[i, t * images : (t + 1) * images]
        grad = dd[...]
        high = grad.astype(bf16)
        low = (grad - high.astype(f32)).astype(bf16)
        for q in range(seq_n):
            out = dot(high, modw_ref[q], ((1,), (1,))) + dot(low, modw_ref[q], ((1,), (1,)))
            for i in range(img_n):
                gs_send[i, q * images : (q + 1) * images, :own] = out[i * images : (i + 1) * images]
        gs_go, gs_end = direct_ops("img", gs_send, gs_all, *sems[6:8])
        gs_go()
        for q in range(seq_n):
            mw_send[q] = dot(lhs_ref[q][:, :own].astype(bf16), high, ((0,), (0,))).astype(bf16)
        mb_go, mb_end = direct_ops("seq", mb_send, modb_ref, *sems[10:12], everyone=True)
        mb_go()
        gs_end()
        all_go, all_end = direct_ops("seq", gs_all, gs_seen, *sems[12:14], everyone=True)
        all_go()
        mw_go, mw_end = direct_ops("seq", mw_send, mw_recv, *sems[8:10])
        mw_go()
        mb_end()
        all_end()
        out = gs_seen[0]
        for q in range(1, seq_n):
            out = out + gs_seen[q]
        cond_ref[...] = out
        mw_end()
        for q in range(seq_n):
            modw_own[:, q * mod_l : (q + 1) * mod_l] = mw_recv[q]

    full = pl.BlockSpec(memory_space=VM)
    got = pl.pallas_call(
        kernel,
        out_shape=(
            jax.ShapeDtypeStruct((own, mod_l * seq_n), bf16),
            jax.ShapeDtypeStruct((own, 3 * width), bf16),
            jax.ShapeDtypeStruct((own, hid_l * seq_n), bf16),
            jax.ShapeDtypeStruct((8, 128), f32),
            jax.ShapeDtypeStruct((seq_n, flat, 128), f32),
            jax.ShapeDtypeStruct((img_n, head, 128), f32),
        ),
        in_specs=[full] * 5,
        out_specs=(full,) * 6,
        scratch_shapes=[
            VM((seq_n, rows, 128), f32),
            VM((img_n, slim + 8, 128), f32),
            VM((img_n, slim + 8, 128), f32),
            VM((img_n * images, mod_l), f32),
            VM((seq_n, own, mod_l), bf16),
            VM((seq_n, own, mod_l), bf16),
            VM((flat, 128), f32),
            VM((img_n, head, 128), f32),
            VM((img_n, head, 128), f32),
            VM((seq_n, img_n, head, 128), f32),
            VM(back.shape, bf16),
        ]
        + pairs_of_sems("seq", "seq", "img", "img", "seq", "seq", "seq"),
        compiler_params=params(cid),
        name="closing",
    )(mine, expb, lhs, modw, back)
    got = list(got)
    if not aligned:
        got[2] = got[2].reshape(own, seq_n, img_n, hid_o).transpose(0, 2, 1, 3).reshape(own, hid_l * seq_n)
    return got


def half_sums(values, low_half):
    first = jnp.sum(jnp.where(low_half, values, 0.0), axis=-1, keepdims=True)
    second = jnp.sum(jnp.where(low_half, 0.0, values), axis=-1, keepdims=True)
    return jnp.where(low_half, first, second)


def dot(a, b, dims):
    return lax.dot_general(a, b, (dims, ((), ())), preferred_element_type=f32)


def lanes(start, size):
    return pl.ds(pl.multiple_of(start, 128), size)


def load_heads(p_ref, bias, g, p, rows):
    both = p_ref[:, g, :, lanes(p * 384, 384)].reshape(rows, 384)
    query = both[:, :128] + bias[:, :128]
    key = both[:, 128:256]
    value = both[:, 256:] + bias[:, 256:]
    low_half = lax.broadcasted_iota(jnp.int32, (rows, 128), 1) < 64
    r_query = lax.rsqrt(half_sums(query * query, low_half) + 1e-06)
    r_key = lax.rsqrt(half_sums(key * key, low_half) + 1e-06)
    return query, key, value, low_half, r_query, r_key


def attend(cid, attn_input, attn_own, attn_early, early, bias, scale, sid_k, sid_q, out_img, exp_own, grad_own):
    seq_n, img_n = lax.axis_size("seq"), lax.axis_size("img")
    outer = seq_n // 2
    chunks, size, width = attn_input.shape
    local = chunks * size
    images = sid_q.shape[0]
    rows_b = local // images
    rows = seq_n * rows_b
    wide = attn_own.shape[2]
    pairs = wide // 384
    turns = images * pairs
    tile = 256 if wide % 256 == 0 else 128
    w_chunks = attn_own.shape[0]
    plans = [gather(x, "seq", True) for x in grad_own] + [gather(out_img, "seq", False, True), gather(exp_own, "img", False)]
    session = Session(plans, everyone_else("seq") + two_level("img", img_n))
    ins, outs = 7 + len(session.ins), 4 + len(plans)
    weight = (img_n, early + w_chunks) + attn_own.shape[1:]

    def kernel(*refs):
        x_ref, w_ref, early_ref, b_ref, es_ref, sk_ref, sq_ref = refs[:7]
        o_ref, p_out, h_out, w_out = refs[ins : ins + 4]
        scratch = refs[ins + outs :]
        h1, attn_w, packed, o_buf, o_send, o_recv, hs, hr, wk, ws, wr, out_sem, early_sem = scratch[:13]
        me = lax.axis_index("seq")
        session.greet()
        session.bind(refs[7:ins], refs[ins + 4 : ins + outs], scratch[13:])
        h1_in = gather_ops("seq", True, x_ref, h1, None, hs, hr)
        w_in = gather_ops("img", False, w_ref, attn_w.at[:, early:], wk, ws, wr)
        if early:
            load = pltpu.make_async_copy(early_ref, attn_w.at[:, :early], early_sem.at[0])
            load.start()
        h1_in.start()
        w_in.start()
        session.start()
        *grads, (out_count, _, out_in), (exp_count, _, exp_in) = session.bound
        h1[0] = x_ref[...]

        def ship(i, j):
            g, p = i // pairs, i % pairs
            return remote(
                o_buf.at[i, j],
                o_ref.at[g, :, lanes((me * pairs + p) * 128, 128)],
                o_send.at[j, i],
                o_recv.at[j, i],
                "seq",
                me ^ j,
            )

        each(0, chunks // 2, h1_in.step)
        each(0, w_chunks // 2, w_in.step)
        each(chunks // 2, chunks, h1_in.step)
        each(w_chunks // 2, w_chunks, w_in.step)
        h1_in.near()
        for o in range(1, outer):
            h1_in.handed(o)
        w_in.near()
        for o in range(1, img_n // 2):
            w_in.handed(o)
        w_in.sent()
        if early:
            load.wait()
        quarter = exp_count // 4
        each(0, quarter, exp_in.step)

        def project(k):
            j, t = k // (wide // tile), k % (wide // tile)
            columns = lanes(t * tile, tile)
            part = dot(h1[j].reshape(local, width), attn_w[:, :, :, columns].reshape(width, tile), ((1,), (0,)))
            packed[j, :, :, columns] = part.reshape(images, rows_b, tile)

        each(0, seq_n * (wide // tile), project)
        each(quarter, 2 * quarter, exp_in.step)
        copies = [
            pltpu.make_async_copy(src, dst, out_sem.at[n])
            for n, (src, dst) in enumerate(((packed, p_out), (h1, h_out), (attn_w, w_out)))
        ]
        for copy in copies:
            copy.start()

        def turn(i):
            g, p = i // pairs, i % pairs
            query, key, value, low_half, r_query, r_key = load_heads(packed, b_ref[p], g, p, rows)
            query_low = query * r_query * es_ref[p]
            key_t = jnp.transpose(key * r_key).astype(bf16)
            sid_k = sq_ref[g]
            masks = [low_half, jnp.logical_not(low_half)]
            queries = [jnp.where(mine, query_low, 0.0).astype(bf16) for mine in masks]
            values = [jnp.where(mine, value, 1.0).astype(bf16) for mine in masks]
            low_b = low_half[:rows_b]
            for b in range(seq_n):
                seen = sid_k <= sk_ref[g, b]
                parts = []
                for h in range(2):
                    scores = dot(queries[h][b * rows_b : (b + 1) * rows_b], key_t, ((1,), (0,)))
                    expo = jnp.where(seen, jnp.exp(scores), 0.0).astype(bf16)
                    parts.append(dot(expo, values[h], ((1,), (0,))))
                totals = jnp.where(low_b, pltpu.roll(parts[0], 64, 1), pltpu.roll(parts[1], 64, 1))
                o_buf[i, b] = (jnp.where(low_b, parts[0], parts[1]) / totals).astype(bf16)
            o_ref[g, :, lanes((me * pairs + p) * 128, 128)] = o_buf[i, 0]
            for j in range(1, seq_n):
                ship(i, j).start()

            @pl.when(i == 0)
            def _():
                for count, _, ops in grads:
                    each(0, count, ops.step)

            half = turns // 2

            @pl.when(i == half - 1)
            def _():
                each(2 * quarter, 3 * quarter, exp_in.step)

            @pl.when(i == half)
            def _():
                each(0, out_count, out_in.step)
                each(3 * quarter, exp_count, exp_in.step)

        each(0, turns, turn)
        session.finish()
        h1_in.sent()
        for copy in copies:
            copy.wait()

        def last(i):
            for j in range(1, seq_n):
                ship(i, j).wait()

        each(0, turns, last)

    full = pl.BlockSpec(memory_space=VM)
    any_space = pl.BlockSpec(memory_space=pl.ANY)
    sems = pltpu.SemaphoreType.DMA((seq_n, turns))
    seq_sems = pltpu.SemaphoreType.DMA((seq_n, chunks))
    img_sems = pltpu.SemaphoreType.DMA((img_n, w_chunks))
    packed = (seq_n, images, rows_b, wide)
    return pl.pallas_call(
        kernel,
        out_shape=tuple(
            [
                jax.ShapeDtypeStruct((images, rows_b, width), bf16),
                jax.ShapeDtypeStruct(packed, f32),
                jax.ShapeDtypeStruct((seq_n,) + attn_input.shape, bf16),
                jax.ShapeDtypeStruct(weight, bf16),
            ]
            + session.outs
        ),
        in_specs=[full] * 2 + [any_space] + [full] * 4 + session.in_specs,
        out_specs=tuple([full] + [any_space] * 3 + session.out_specs),
        scratch_shapes=[
            VM((seq_n,) + attn_input.shape, bf16),
            VM(weight, bf16),
            VM(packed, f32),
            VM((turns, seq_n, rows_b, 128), bf16),
            sems,
            sems,
            seq_sems,
            seq_sems,
            pltpu.SemaphoreType.DMA((w_chunks,)),
            img_sems,
            img_sems,
            pltpu.SemaphoreType.DMA((3,)),
            pltpu.SemaphoreType.DMA((1,)),
        ]
        + session.scratch,
        compiler_params=params(cid),
        name="attend",
    )(attn_input, attn_own, attn_early, bias, scale, sid_k, sid_q, *session.ins)


def attend_back(cid, packed, h1, attn_w, d_out, bias, scale, sid_k, sid_q, expw_part, shrunk_part, outw_part):
    seq_n, images, rows_b, wide = packed.shape
    img_n = lax.axis_size("img")
    outer = seq_n // 2
    pairs = wide // 384
    rows = seq_n * rows_b
    turns = images * pairs
    _, chunks, size, width = h1.shape
    local = chunks * size
    _, w_chunks, w_size, _ = attn_w.shape
    own = outw_part.shape[2]
    tile = 256
    blocks_per_tile = tile // (w_chunks * w_size)
    session = Session([], everyone_else("seq") + two_level("img", img_n))
    mids = [
        scatter_scratch(img_n, expw_part.shape[1:], bf16),
        scatter_scratch(seq_n, shrunk_part.shape[1:], bf16),
        scatter_scratch(seq_n, (img_n, own, width), bf16),
        scatter_scratch(img_n, (1, own, width), bf16),
        scatter_scratch(img_n, attn_w.shape[1:], bf16),
        scatter_scratch(seq_n, h1.shape[1:], bf16),
    ]

    def kernel(*refs):
        p_in, h_in, w_in, do_ref, b_ref, es_ref, sk_ref, sq_ref, expw_ref, f_ref, outw_ref = refs[:11]
        st_ref, dh1_own, attn_own, expw_own, f_own, outw_own = refs[11:17]
        scratch = refs[17:]
        p_ref, h_ref, w_ref, dp_ref, dh1, dattn, out_mid, load_sem = scratch[:8]
        k_buf, v_buf, e_buf, g_buf, dk_buf, dv_buf, do_buf, o_send, o_recv = scratch[8:17]
        expw_held, f_held, outw_held = scratch[17:20]
        more = scratch[20:]
        me = lax.axis_index("seq")
        session.greet()

        def ship(i, j):
            g, p = i // pairs, i % pairs
            return remote(
                do_ref.at[g, :, lanes(((me ^ j) * pairs + p) * 128, 128)],
                do_buf.at[i, j],
                o_send.at[j, i],
                o_recv.at[j, i],
                "seq",
                me ^ j,
            )

        def send(i):
            for j in range(1, seq_n):
                ship(i, j).start()

        each(0, turns, send)
        loads = [
            pltpu.make_async_copy(src, dst, load_sem.at[n])
            for n, (src, dst) in enumerate(
                (
                    (p_in, p_ref),
                    (outw_ref, outw_held),
                    (f_ref, f_held),
                    (expw_ref, expw_held),
                    (h_in, h_ref),
                    (w_in, w_ref),
                )
            )
        ]
        for load in loads:
            load.start()
        exp_out = scatter_ops("img", False, expw_ref, expw_own, *more[:7], held=expw_held)
        f_out = scatter_ops("seq", True, f_ref, f_own, *more[7:14], held=f_held)
        mid_out = scatter_ops(
            "seq", False, outw_ref, out_mid.at[:, 0], *more[14:21], inside=True, held=outw_held
        )
        outw_out = scatter_ops("img", False, out_mid, outw_own, *more[21:28])
        attn_out = scatter_ops("img", False, dattn, attn_own, *more[28:35])
        dh1_out = scatter_ops("seq", True, dh1, dh1_own, *more[35:42])
        exp_out.start()
        mid_out.start()
        f_out.start()
        exp_chunks = expw_ref.shape[1]
        loads[0].wait()

        def turn(i):
            g, p = i // pairs, i % pairs
            query, key, value, low_half, r_query, r_key = load_heads(p_ref, b_ref[p], g, p, rows)
            scale_row = es_ref[p]
            q_unit = query * r_query
            k_unit = key * r_key
            q_full = q_unit * scale_row
            k_buf[...] = k_unit.astype(bf16).reshape(seq_n, rows_b, 128)
            v_buf[...] = value.astype(bf16).reshape(seq_n, rows_b, 128)
            do_buf[i, 0] = do_ref[g, :, lanes((me * pairs + p) * 128, 128)]
            for j in range(1, seq_n):
                ship(i, j).wait_recv()
            d_out = do_buf[i].reshape(rows, 128).astype(f32)
            sid_q = sq_ref[g]
            masks = [low_half, jnp.logical_not(low_half)]
            q_f = [jnp.where(mine, q_full, 0.0) for mine in masks]
            do_f = [jnp.where(mine, d_out, 0.0) for mine in masks]
            q_h = [x.astype(bf16) for x in q_f]
            do_h = [x.astype(bf16) for x in do_f]
            q_t = [jnp.transpose(x).astype(bf16) for x in q_f]
            do_t = [jnp.transpose(x).astype(bf16) for x in do_f]
            total = [jnp.zeros((1, rows), f32)] * 2
            mixed = [jnp.zeros((1, rows), f32)] * 2
            for b in range(seq_n):
                seen = sk_ref[g, b] <= sid_q
                for h in range(2):
                    scores = dot(k_buf[b], q_t[h], ((1,), (0,)))
                    expo = jnp.where(seen, jnp.exp(scores), 0.0)
                    grad = dot(v_buf[b], do_t[h], ((1,), (0,)))
                    e_buf[h, b] = expo
                    g_buf[h, b] = grad
                    total[h] = total[h] + jnp.sum(expo, axis=0, keepdims=True)
                    mixed[h] = mixed[h] + jnp.sum(expo * grad, axis=0, keepdims=True)
            inverse = [1.0 / x for x in total]
            delta = [x * y for x, y in zip(mixed, inverse)]
            acc = [jnp.zeros((128, rows), f32)] * 2
            for b in range(seq_n):
                dv = dk = jnp.zeros((rows_b, 128), f32)
                for h in range(2):
                    probs = e_buf[h, b] * inverse[h]
                    scores_grad = (probs * (g_buf[h, b] - delta[h])).astype(bf16)
                    dv = dv + dot(probs.astype(bf16), do_h[h], ((1,), (0,)))
                    dk = dk + dot(scores_grad, q_h[h], ((1,), (0,)))
                    acc[h] = acc[h] + dot(k_buf[b], scores_grad, ((0,), (0,)))
                dv_buf[b] = dv
                dk_buf[b] = dk
            parts = [acc[0][:64], acc[1][64:]]
            dq = jnp.transpose(jnp.concatenate(parts, axis=0)).astype(bf16).astype(f32)
            dk = dk_buf[...].reshape(rows, 128).astype(bf16).astype(f32)
            dv = dv_buf[...].reshape(rows, 128).astype(bf16).astype(f32)
            dq_raw = scale_row * r_query * (dq - q_unit * half_sums(q_unit * dq, low_half))
            dk_raw = r_key * (dk - k_unit * half_sums(k_unit * dk, low_half))
            together = jnp.concatenate([dq_raw, dk_raw, dv], axis=1).astype(bf16)
            dp_ref[:, g, :, lanes(p * 384, 384)] = together.reshape(seq_n, rows_b, 384)
            sums = [
                jnp.sum(dq_raw, axis=0, keepdims=True),
                jnp.sum(dv, axis=0, keepdims=True),
                jnp.sum(dq * q_full, axis=0, keepdims=True),
                jnp.zeros((5, 128), f32),
            ]
            st_ref[i] = jnp.concatenate(sums, axis=0)

            @pl.when(i == 0)
            def _():
                for load in loads[1:4]:
                    load.wait()
                each(0, img_n, mid_out.step)
                each(0, chunks, f_out.step)

            each((i * exp_chunks) // turns, ((i + 1) * exp_chunks) // turns, exp_out.step)

        each(0, turns, turn)
        mid_out.finish()
        outw_out.start()
        for load in loads[4:]:
            load.wait()

        def columns(t):
            return lanes(t * tile, tile)

        def weight_grad(t):
            left = h_ref[:, :, :, columns(t)].reshape(seq_n * local, tile)
            part = dot(left, dp_ref[...].reshape(seq_n * local, wide), ((0,), (0,)))
            dattn[pl.ds(t * blocks_per_tile, blocks_per_tile)] = part.astype(bf16).reshape(
                blocks_per_tile, w_chunks, w_size, wide
            )

        def input_grad(j):
            def run(t):
                weight = w_ref[pl.ds(t * blocks_per_tile, blocks_per_tile)].reshape(tile, wide)
                part = dot(dp_ref[j].reshape(local, wide), weight, ((1,), (1,)))
                dh1[j, :, :, columns(t)] = part.astype(bf16).reshape(chunks, size, tile)

            each(0, width // tile, run)

        each(0, width // tile, weight_grad)
        attn_out.start()
        outw_out.step(0)
        exp_out.finish()
        for o in range(1, outer):
            for j in (2 * o + 1, 2 * o):
                input_grad(j)
        dh1_out.start_outer()
        each(0, chunks, dh1_out.step)
        each(0, w_chunks // 2, attn_out.step)
        input_grad(1)
        each(w_chunks // 2, (3 * w_chunks) // 4, attn_out.step)
        input_grad(0)
        dh1_out.start_inner()
        each((3 * w_chunks) // 4, w_chunks, attn_out.step)
        outw_out.finish()
        f_out.finish()
        dh1_out.finish()
        attn_out.finish()

        def last(i):
            for j in range(1, seq_n):
                ship(i, j).wait_send()

        each(0, turns, last)

    full = pl.BlockSpec(memory_space=VM)
    any_space = pl.BlockSpec(memory_space=pl.ANY)
    sems = pltpu.SemaphoreType.DMA((seq_n, turns))
    return pl.pallas_call(
        kernel,
        out_shape=(
            jax.ShapeDtypeStruct((turns, 8, 128), f32),
            jax.ShapeDtypeStruct(h1.shape[1:], f32),
            jax.ShapeDtypeStruct(attn_w.shape[1:], bf16),
            jax.ShapeDtypeStruct(expw_part.shape[1:], bf16),
            jax.ShapeDtypeStruct(shrunk_part.shape[1:], f32),
            jax.ShapeDtypeStruct((1, own, width), f32),
        ),
        in_specs=[any_space] * 3 + [full] * 5 + [any_space] * 3,
        out_specs=(full,) * 6,
        scratch_shapes=[
            VM(packed.shape, f32),
            VM(h1.shape, bf16),
            VM(attn_w.shape, bf16),
            VM(packed.shape, bf16),
            VM(h1.shape, bf16),
            VM(attn_w.shape, bf16),
            VM((img_n, 1, own, width), bf16),
            pltpu.SemaphoreType.DMA((6,)),
            VM((seq_n, rows_b, 128), bf16),
            VM((seq_n, rows_b, 128), bf16),
            VM((2, seq_n, rows_b, rows), f32),
            VM((2, seq_n, rows_b, rows), f32),
            VM((seq_n, rows_b, 128), f32),
            VM((seq_n, rows_b, 128), f32),
            VM((turns, seq_n, rows_b, 128), bf16),
            sems,
            sems,
            VM(expw_part.shape, bf16),
            VM(shrunk_part.shape, bf16),
            VM(outw_part.shape, bf16),
        ]
        + [x for scratch in mids for x in scratch],
        compiler_params=params(cid),
        name="attend_back",
    )(packed, h1, attn_w, d_out, bias, scale, sid_k, sid_q, expw_part, shrunk_part, outw_part)


def gelu_both(x):
    root = 0.7978845608028654
    square = x * x
    bent = jnp.tanh(root * x * (1.0 + 0.044715 * square))
    half = 0.5 * (1.0 + bent)
    slope = half + 0.5 * x * (1.0 - bent * bent) * (root * (1.0 + 3 * 0.044715 * square))
    return x * half, slope


def feed_forward(cid, mlp_input, grad_parts, grad_own, shr_own, exp_w, e_bias):
    seq_n, img_n = lax.axis_size("seq"), lax.axis_size("img")
    outer = seq_n // 2
    chunks, size, width = mlp_input.shape
    rows = chunks * size
    hid_l = exp_w.shape[1]
    ready, later = len(grad_parts), len(grad_own)
    images = ready + later
    g_chunks, g_size, _ = grad_own[0].shape
    w_chunks, w_size, _ = shr_own.shape
    hid_o = w_chunks * w_size
    tile = 256
    blocks_per_tile = tile // hid_o
    session = Session([], two_level("seq", seq_n) + two_level("img", img_n))

    def kernel(x_ref, *refs):
        df_refs = refs[:images]
        shr_ref, exp_ref, eb_ref, dh2_ref, dshr_own, f_ref, dexp_ref, expb_ref = refs[images : images + 8]
        h2, df, shr, act, slope, dshr, dh2, df_sem, hs, hr, ss, sr, sk, shr_low, *more = refs[images + 8 :]
        shr_low[...] = shr_ref[...].astype(bf16)
        df_in = [
            gather_ops("seq", True, df_refs[ready + g], df.at[:, ready + g], *more[14 + 3 * g : 17 + 3 * g])
            for g in range(later)
        ]
        session.greet()
        h2_in = gather_ops("seq", True, x_ref, h2, None, hs, hr)
        shr_in = gather_ops("img", False, shr_low, shr, sk, ss, sr)
        dh2_out = scatter_ops("seq", True, dh2, dh2_ref, *more[:7])
        dshr_out = scatter_ops("img", False, dshr, dshr_own, *more[7:14])
        h2_in.start()
        shr_in.start()
        for ops in df_in:
            ops.start()
        loads = [pltpu.make_async_copy(ref, df.at[:, g], df_sem.at[g]) for g, ref in enumerate(df_refs[:ready])]
        for load in loads:
            load.start()
        h2[0] = x_ref[...]
        expb_ref[...] = jnp.zeros_like(expb_ref)

        def columns(t):
            return lanes(t * tile, tile)

        def expand(j):
            def run(t):
                u = dot(h2[j].reshape(rows, width), exp_ref[:, columns(t)], ((1,), (0,))) + eb_ref[:, columns(t)]
                value, grad = gelu_both(u)
                act[j, :, columns(t)] = value.astype(bf16)
                slope[j, :, columns(t)] = grad.astype(bf16)

            each(0, hid_l // tile, run)

        def back_act(j):
            def run(t):
                weight = shr[pl.ds(t * blocks_per_tile, blocks_per_tile)].reshape(tile, width)
                grad = dot(df[j].reshape(rows, width), weight, ((1,), (1,)))
                grad = (slope[j, :, columns(t)].astype(f32) * grad).astype(bf16)
                slope[j, :, columns(t)] = grad
                expb_ref[:, columns(t)] += jnp.sum(grad.astype(f32), axis=0, keepdims=True)

            each(0, hid_l // tile, run)

        def back_input(j):
            def run(t):
                weight = exp_ref[pl.ds(pl.multiple_of(t * tile, tile), tile), :]
                part = dot(slope[j], weight, ((1,), (1,)))
                dh2[j, :, :, columns(t)] = part.astype(bf16).reshape(chunks, size, tile)

            each(0, width // tile, run)

        def shrink(j):
            def run(t):
                weight = shr[:, :, :, columns(t)].reshape(hid_l, tile)
                part = dot(act[j], weight, ((1,), (0,)))
                f_ref[j, :, :, columns(t)] = part.astype(bf16).reshape(chunks, size, tile)

            each(0, width // tile, run)

        def shrink_grad(t):
            left = act[:, :, columns(t)].reshape(seq_n * rows, tile)
            part = dot(left, df[...].reshape(seq_n * rows, width), ((0,), (0,)))
            part = part.astype(bf16).reshape(blocks_per_tile, w_chunks, w_size, width)
            dshr[pl.ds(t * blocks_per_tile, blocks_per_tile)] = part

        def expand_grad(t):
            left = h2[:, :, :, columns(t)].reshape(seq_n * rows, tile)
            part = dot(left, slope[...].reshape(seq_n * rows, hid_l), ((0,), (0,)))
            dexp_ref[pl.ds(pl.multiple_of(t * tile, tile), tile), :] = part.astype(bf16)

        expand(0)
        h2_in.near()
        expand(1)
        half = chunks // 2
        each(0, half, h2_in.step)
        each(0, w_chunks // 2, shr_in.step)
        each(half, chunks, h2_in.step)
        for o in range(1, outer):
            expand(2 * o)
        each(w_chunks // 2, w_chunks, shr_in.step)
        for ops in df_in:
            each(0, g_chunks, ops.step)
        for o in range(1, outer):
            h2_in.handed(o)
            expand(2 * o + 1)
        for ops in df_in:
            ops.finish()
        for load in loads:
            load.wait()
        each(0, hid_l // tile, shrink_grad)
        shr_in.near()
        for o in range(1, img_n // 2):
            shr_in.handed(o)
        shr_in.sent()
        dshr_out.start()
        for o in range(1, outer):
            for j in (2 * o + 1, 2 * o):
                back_act(j)
                back_input(j)
        def dshr_steps(k):
            each((k * w_chunks) // 4, ((k + 1) * w_chunks) // 4, dshr_out.step)

        dh2_out.start_outer()
        dshr_steps(0)
        each(0, chunks, dh2_out.step)
        back_act(1)
        dshr_steps(1)
        back_input(1)
        back_act(0)
        dshr_steps(2)
        back_input(0)
        dh2_out.start_inner()
        shrink(0)
        dshr_steps(3)
        h2_in.sent()
        for j in range(1, seq_n):
            shrink(j)
        each(0, width // tile, expand_grad)
        dh2_out.finish()
        dshr_out.finish()

    full = pl.BlockSpec(memory_space=VM)
    any_space = pl.BlockSpec(memory_space=pl.ANY)
    seq_sems = pltpu.SemaphoreType.DMA((seq_n, chunks))
    img_sems = pltpu.SemaphoreType.DMA((img_n, w_chunks))
    grad_sems = pltpu.SemaphoreType.DMA((seq_n, g_chunks))
    return pl.pallas_call(
        kernel,
        out_shape=(
            jax.ShapeDtypeStruct(mlp_input.shape, f32),
            jax.ShapeDtypeStruct(shr_own.shape, f32),
            jax.ShapeDtypeStruct((seq_n,) + mlp_input.shape, bf16),
            jax.ShapeDtypeStruct(exp_w.shape, bf16),
            jax.ShapeDtypeStruct((1, hid_l), f32),
        ),
        in_specs=[full] + [any_space] * ready + [full] * (later + 3),
        out_specs=(full,) * 5,
        scratch_shapes=[
            VM((seq_n,) + mlp_input.shape, bf16),
            VM((seq_n, images, g_chunks, g_size, width), bf16),
            VM((img_n,) + shr_own.shape, bf16),
            VM((seq_n, rows, hid_l), bf16),
            VM((seq_n, rows, hid_l), bf16),
            VM((img_n,) + shr_own.shape, bf16),
            VM((seq_n,) + mlp_input.shape, bf16),
            pltpu.SemaphoreType.DMA((max(ready, 1),)),
            seq_sems,
            seq_sems,
            img_sems,
            img_sems,
            pltpu.SemaphoreType.DMA((w_chunks,)),
            VM(shr_own.shape, bf16),
        ]
        + scatter_scratch(seq_n, mlp_input.shape, bf16)
        + scatter_scratch(img_n, shr_own.shape, bf16)
        + [pltpu.SemaphoreType.DMA((g_chunks,)), grad_sems, grad_sems] * later,
        compiler_params=params(cid),
        name="feed_forward",
    )(mlp_input, *grad_parts, *grad_own, shr_own, exp_w, e_bias)


def normalize(values):
    centered = values - jnp.mean(values, axis=-1, keepdims=True)
    return centered * lax.rsqrt(jnp.mean(centered * centered, axis=-1, keepdims=True) + 1e-06)


def norm_back(values, grad_rows):
    return jax.vjp(normalize, values)[1](grad_rows)[0]


def pad_to(x, size, axis):
    widths = [(0, 0)] * x.ndim
    widths[axis] = (0, size - x.shape[axis])
    return jnp.pad(x, widths)


def mm(a, b):
    return jnp.dot(a, b, preferred_element_type=f32)


def mm_nt(a, b):
    return lax.dot_general(a, b, (((1,), (1,)), ((), ())), preferred_element_type=f32)


def mm_tn(a, b):
    return lax.dot_general(a, b, (((0,), (0,)), ((), ())), preferred_element_type=f32)


def body(
    tokens,
    cotangent,
    condition,
    scale_sizes,
    mod_weight,
    mod_bias,
    attn_weight,
    query_bias,
    value_bias,
    out_weight,
    out_bias,
    expand_weight,
    expand_bias,
    shrink_weight,
    shrink_bias,
    log_scale,
):
    images, rows, width = tokens.shape
    heads = log_scale.shape[0]
    headdim = width // heads
    seq_n = lax.axis_size("seq")
    img_n = lax.axis_size("img")
    seq_i = lax.axis_index("seq")
    img_i = lax.axis_index("img")
    rank = img_i * seq_n + seq_i
    ranks = img_n * seq_n
    own = width // ranks
    rows_p = -(-rows // 16) * 16
    dim_l = width // seq_n
    pairs = dim_l // 128
    hidden = expand_bias.shape[0] * ranks
    hid_l = hidden // seq_n
    hid_o = hidden // ranks
    mods = mod_weight.shape[1]
    mod_o = mods // ranks

    mod_l = mods // seq_n
    blk = own * seq_n

    weights = (mod_weight, attn_weight, expand_weight)
    if own % 16 or hid_o % 128:
        attn_cut = (
            attn_weight.astype(bf16)
            .reshape(own, 3, seq_n, pairs, 128)
            .transpose(2, 0, 3, 1, 4)
            .reshape(seq_n, own, 3 * dim_l)
        )
        exp_cut = (
            expand_weight.astype(bf16)
            .reshape(own, img_n, seq_n, hid_o)
            .transpose(2, 0, 1, 3)
            .reshape(seq_n, own, hid_l)
        )
        mod_cut = mod_weight.astype(bf16).reshape(own, seq_n, mod_l).transpose(1, 0, 2)
        weights = (mod_cut, attn_cut, exp_cut)
    silu_cond = jax.nn.silu(condition).astype(bf16).astype(f32)
    small_bias = jnp.concatenate([query_bias, value_bias, out_bias, shrink_bias, expand_bias, mod_bias])
    small_bias = lax.reduce_precision(small_bias, 8, 7)
    bias_n = small_bias.shape[0]
    bias_rows = -(-bias_n // 1024) * 8
    small_bias = pad_to(small_bias, bias_rows * 128, 0).reshape(1, bias_rows, 128)
    cond_cut = silu_cond.reshape(images, img_n, seq_n, own).transpose(1, 2, 0, 3).reshape(img_n, seq_n * images, own)
    small = jnp.concatenate(
        [pad_to(cond_cut, 128, 2), jnp.broadcast_to(small_bias, (img_n, bias_rows, 128))], axis=1
    )
    early = seq_n // 4 if own % 16 == 0 else 0
    mod_all, bias_all, cond_rows, modw_cut, attn_b, exp_b, attn_early, out_img = opening(
        1, *weights, out_weight, small, seq_n, images, pairs, early
    )
    out_img = out_img.reshape(img_n, own, width)
    if early:
        attn_b = attn_b[early:]
    exp_b = exp_b.reshape(blk, hid_l)

    def weight_chunks(x):
        step = blk // 8 if blk % 128 == 0 else blk // 4
        return x.reshape(x.shape[:-2] + (blk // step, step, x.shape[-1]))

    def hidden_chunks(x):
        step = 16
        return x.reshape(x.shape[:-2] + (hid_o // step, step, x.shape[-1]))

    tiles = mod_l // 128
    modulation = mod_all[:, : tiles * images].reshape(seq_n, tiles, images, 128).transpose(2, 0, 1, 3)
    bias_all = bias_all.reshape(seq_n, img_n, bias_rows * 128)[:, :, :bias_n].transpose(1, 0, 2)
    q_bias = bias_all[:, :, :own].reshape(width)
    v_bias = bias_all[:, :, own : 2 * own].reshape(width)
    o_bias = bias_all[:, :, 2 * own : 3 * own].reshape(width)
    s_bias = bias_all[:, :, 3 * own : 4 * own].reshape(width)
    e_bias = bias_all[:, :, 4 * own : 4 * own + hid_o]
    e_bias = lax.dynamic_slice_in_dim(e_bias, seq_i, 1, 1).reshape(hid_l)
    m_bias = bias_all[:, :, 4 * own + hid_o :].reshape(mods)
    modulation = modulation.reshape(images, mods) + m_bias[None]
    qb_l = lax.dynamic_slice_in_dim(q_bias, seq_i * dim_l, dim_l, 0).reshape(pairs, 1, 128)
    vb_l = lax.dynamic_slice_in_dim(v_bias, seq_i * dim_l, dim_l, 0).reshape(pairs, 1, 128)
    pair_bias = jnp.concatenate([qb_l, jnp.zeros_like(qb_l), vb_l], axis=2)
    head_scale = jnp.exp(jnp.repeat(log_scale, headdim))
    pair_scale = lax.dynamic_slice_in_dim(head_scale, seq_i * dim_l, dim_l, 0).reshape(pairs, 1, 128)
    gain_attn, gain_mlp, scale_attn, scale_mlp, shift_attn, shift_mlp = jnp.split(
        modulation[:, None, :], 6, axis=-1
    )

    scales = jnp.arange(scale_sizes.shape[1])
    ends = jnp.sum(jnp.where(scales[:, None] <= scales[None], scale_sizes[:, :, None], 0), axis=1)
    offset = jnp.arange(rows_p, dtype=jnp.int32)
    place = (seq_i ^ jnp.arange(seq_n, dtype=jnp.int32))[:, None] * rows + offset[None]
    sid = jnp.sum((place[None, :, :, None] >= ends[:, None, None, :]).astype(jnp.int32), axis=-1)
    sid = jnp.where(offset[None, None] < rows, sid, 1 << 20)
    sid_q = sid.reshape(images, 1, seq_n * rows_p)
    sid_k = sid[..., None]

    resid_in = pad_to(tokens, rows_p, 1).astype(f32)
    grad_out = pad_to(cotangent, rows_p, 1).astype(f32)
    local = images * rows_p

    def chunked(x):
        return x.reshape(x.shape[: x.ndim - 3] + (local // 32, 32, width))

    normed_in = normalize(resid_in)
    attn_input = (normed_in * (1.0 + scale_attn) + shift_attn).astype(bf16)
    grad_shrunk = (grad_out * gain_mlp).astype(bf16)
    grad_chunks = grad_shrunk.reshape(images, rows_p // 16, 16, width)
    ready = images // 2
    context_low, packed, h1, attn_w, *gathered = attend(
        5,
        chunked(attn_input),
        attn_b if early else weight_chunks(attn_b.reshape(blk, 3 * dim_l)),
        attn_early,
        early,
        pair_bias,
        pair_scale,
        sid_k,
        sid_q,
        out_img,
        weight_chunks(exp_b),
        [grad_chunks[g] for g in range(ready)],
    )
    df_ready, out_w, exp_w = gathered[:ready], gathered[ready], gathered[ready + 1]
    context_low = context_low.reshape(local, width)
    out_w = out_w.reshape(width, width)
    exp_w = exp_w.reshape(width, hid_l)
    attn_out = (mm(context_low, out_w) + o_bias).reshape(images, rows_p, width)
    resid_mid = resid_in + gain_attn * attn_out
    normed_mid = normalize(resid_mid)
    mlp_input = (normed_mid * (1.0 + scale_mlp) + shift_mlp).astype(bf16)
    shrb_part = jnp.sum(grad_shrunk.astype(f32), axis=(0, 1))
    grad_mlp_input, shrw_own, shrunk_part, expw_part, expb_part = feed_forward(
        7,
        chunked(mlp_input),
        df_ready,
        [grad_chunks[g] for g in range(ready, images)],
        hidden_chunks(shrink_weight),
        exp_w,
        e_bias.reshape(1, hid_l),
    )
    grad_mlp_input = grad_mlp_input.reshape(images, rows_p, width)
    shrw_own = shrw_own.reshape(hid_o, width)
    expb_part = expb_part.reshape(hid_l)
    expw_part = expw_part.reshape(img_n, blk, hid_l)

    grad_scale_mlp = jnp.sum(grad_mlp_input * normed_mid, axis=1)
    grad_shift_mlp = jnp.sum(grad_mlp_input, axis=1)
    grad_mid = grad_out + norm_back(resid_mid, grad_mlp_input * (1.0 + scale_mlp))
    grad_gain_attn = jnp.sum(grad_mid * attn_out, axis=1)
    grad_attn_out = (grad_mid * gain_attn).astype(bf16)
    outb_part = jnp.sum(grad_attn_out.astype(f32), axis=(0, 1))
    da = grad_attn_out.reshape(local, width)
    grad_context = mm_nt(da, out_w).astype(bf16)
    grad_context = grad_context.reshape(images, rows_p, width)
    outw_part = mm_tn(context_low, da).astype(bf16).reshape(img_n, seq_n, own, width)
    sums, grad_attn_input, attnw_blk, expw_blk, shrunk, outw_own = attend_back(
        11,
        packed,
        h1,
        attn_w,
        grad_context,
        pair_bias,
        pair_scale,
        sid_k,
        sid_q,
        weight_chunks(expw_part),
        shrunk_part,
        outw_part,
    )
    shrunk = shrunk.reshape(images, rows_p, width) + s_bias
    layer_out = (resid_mid[:, :rows] + gain_mlp * shrunk[:, :rows]).astype(bf16)
    grad_gain_mlp = jnp.sum(grad_out * shrunk, axis=1)
    sums = jnp.sum(sums.reshape(images, pairs, 8, 128), axis=0)
    qb_part = sums[:, 0].reshape(dim_l)
    vb_part = sums[:, 1].reshape(dim_l)
    logs_part = jnp.sum(sums[:, 2].reshape(dim_l // headdim, headdim), axis=1)
    outw_own = outw_own.reshape(own, width)
    grad_attn_input = grad_attn_input.reshape(images, rows_p, width)
    grad_scale_attn = jnp.sum(grad_attn_input * normed_in, axis=1)
    grad_shift_attn = jnp.sum(grad_attn_input, axis=1)
    token_grad = grad_mid[:, :rows] + norm_back(resid_in[:, :rows], grad_attn_input[:, :rows] * (1.0 + scale_attn))
    token_grad = token_grad.astype(bf16)

    grad_mod = jnp.concatenate(
        [grad_gain_attn, grad_gain_mlp, grad_scale_attn, grad_scale_mlp, grad_shift_attn, grad_shift_mlp],
        axis=-1,
    )
    grad_mod = grad_mod.reshape(images, seq_n, tiles, 128).transpose(1, 2, 0, 3).reshape(seq_n, tiles * images, 128)
    grad_mod = pad_to(grad_mod, -(-tiles * images // 8) * 8, 1)

    def lined(vector, count):
        return pad_to(vector.reshape(count, -1), 128, 1)

    heads_l = heads // seq_n
    logs_row = lax.dynamic_update_slice_in_dim(jnp.zeros((128,), f32), logs_part, seq_i * heads_l, 0)
    bias_mine = jnp.concatenate(
        [
            lined(shrb_part, img_n),
            lined(outb_part, img_n),
            pad_to(logs_row[None], 8, 0),
            lined(qb_part, img_n // seq_n),
            lined(vb_part, img_n // seq_n),
        ]
    )
    bias_mine = pad_to(bias_mine, -(-bias_mine.shape[0] // 8) * 8, 0)
    mine = jnp.concatenate([grad_mod, jnp.broadcast_to(bias_mine[None], (seq_n,) + bias_mine.shape)], axis=1)
    back_cut = jnp.concatenate(
        [attnw_blk.reshape(seq_n, own, 3 * dim_l), expw_blk.reshape(seq_n, own, hid_l)], axis=2
    )
    modw_own, attnw_own, expw_own, bias_own, modb_all, cond_sum = closing(
        13, mine, lined(expb_part, img_n), cond_rows, modw_cut, back_cut, images, pairs
    )

    modw_own, attnw_own, expw_own, outw_own, shrw_own, shrb_own, outb_own, qb_own, vb_own, expb_own, logs_total = finishing(
        modw_own, attnw_own, expw_own, bias_own, outw_own, shrw_own, heads
    )
    modb_own = lax.dynamic_slice_in_dim(modb_all[:, :tiles].reshape(mods), rank * mod_o, mod_o, 0)
    grad_silu = cond_sum[:, :, :own].reshape(img_n, seq_n, images, own).transpose(2, 0, 1, 3).reshape(images, width)
    cond_grad = jax.vjp(jax.nn.silu, condition)[1](grad_silu)[0]
    return (
        layer_out,
        token_grad,
        cond_grad,
        modw_own,
        modb_own,
        attnw_own,
        qb_own,
        vb_own,
        outw_own,
        outb_own,
        expw_own,
        expb_own,
        shrw_own,
        shrb_own,
        logs_total,
    )


def solution(mesh):
    both = P(("img", "seq"))
    rows = P(("img", "seq"), None)
    return jax.shard_map(
        body,
        mesh=mesh,
        in_specs=(
            P("img", "seq", None),
            P("img", "seq", None),
            P("img", None),
            P("img", None),
            rows,
            both,
            rows,
            both,
            both,
            rows,
            both,
            rows,
            both,
            rows,
            both,
            P(),
        ),
        out_specs=(
            P("img", "seq", None),
            P("img", "seq", None),
            P("img", None),
            rows,
            both,
            rows,
            both,
            both,
            rows,
            both,
            rows,
            both,
            rows,
            both,
            P(),
        ),
        check_vma=False,
    )
```

```python
from types import SimpleNamespace

import jax
import jax.numpy as jnp
from jax import lax
from jax.experimental import pallas as pl
from jax.experimental.pallas import tpu as pltpu
from jax.sharding import PartitionSpec as P

HIGH = lax.Precision.HIGHEST
MESH = pl.DeviceIdType.MESH
bf16 = jnp.bfloat16
f32 = jnp.float32
VM = pltpu.VMEM
LIMIT = 62 << 20


class Plan:
    def __init__(self, ins, out, scratch, peers, count, bind, out_space=VM):
        self.ins, self.out, self.out_space = ins, out, out_space
        self.scratch, self.peers, self.count, self.bind = scratch, peers, count, bind
        self.window = None

    def during(self, low, high):
        self.window = (low, high)
        return self


def remote(src, dst, send, recv, axis, peer):
    return pltpu.make_async_remote_copy(
        src_ref=src, dst_ref=dst, send_sem=send, recv_sem=recv, device_id={axis: peer}, device_id_type=MESH
    )


def each(low, high, run):
    def once(i, carry):
        run(i)
        return carry

    lax.fori_loop(low, high, once, 0)


def direct_ops(axis, x_ref, out_ref, send, recv, everyone=False, src_rel=False, dst_rel=False):
    n = lax.axis_size(axis)
    me = lax.axis_index(axis)

    def copy(j):
        src = x_ref if everyone else x_ref.at[j if src_rel else me ^ j]
        return remote(src, out_ref.at[j if dst_rel else me], send.at[j], recv.at[j], axis, me ^ j)

    def start():
        for j in range(1, n):
            copy(j).start()
        out_ref[0 if dst_rel else me] = x_ref[...] if everyone else x_ref[0 if src_rel else me]

    def finish():
        for j in range(1, n):
            copy(j).wait()

    return start, finish


def two_level(axis, n):
    return [(axis, 1)] + [(axis, 2 * o) for o in range(1, n // 2)]


def gather_ops(axis, rel, x_ref, out_ref, own, send, recv, inside=False):
    n = lax.axis_size(axis)
    outer = n // 2
    chunks = x_ref.shape[0]
    me = lax.axis_index(axis)

    def place(sender, j, c):
        block = j if rel else sender
        return out_ref.at[c, block] if inside else out_ref.at[block, c]

    def keep(c):
        return pltpu.make_async_copy(x_ref.at[c], place(me, 0, c), own.at[c])

    def push(j, c):
        return remote(x_ref.at[c], place(me, j, c), send.at[j, c], recv.at[j, c], axis, me ^ j)

    def hand(j, c):
        far = me ^ j
        return remote(place(far, j, c), place(far, j + 1, c), send.at[j + 1, c], recv.at[j + 1, c], axis, me ^ 1)

    def start():
        def first(c):
            for o in range(1, outer):
                push(2 * o, c).start()

        def second(c):
            push(1, c).start()
            if own is not None:
                keep(c).start()

        each(0, chunks, first)
        each(0, chunks, second)

    def step(c):
        for o in range(1, outer):
            push(2 * o, c).wait_recv()
            hand(2 * o, c).start()

    def near():
        each(0, chunks, lambda c: push(1, c).wait_recv())

    def handed(o):
        each(0, chunks, lambda c: hand(2 * o, c).wait_recv())

    def sent():
        def last(c):
            for o in range(1, outer):
                push(2 * o, c).wait_send()
                hand(2 * o, c).wait_send()
            push(1, c).wait_send()
            if own is not None:
                keep(c).wait()

        each(0, chunks, last)

    def finish():
        near()
        for o in range(1, outer):
            handed(o)
        sent()

    return SimpleNamespace(start=start, step=step, near=near, handed=handed, sent=sent, finish=finish)


def gather(x, axis, rel, inside=False):
    n = lax.axis_size(axis)
    chunks = x.shape[0]

    def bind(x_ref, out_ref, own, send, recv):
        return gather_ops(axis, rel, x_ref, out_ref, own, send, recv, inside)

    sems = pltpu.SemaphoreType.DMA((n, chunks))
    shape = (chunks, n) + x.shape[1:] if inside else (n,) + x.shape
    out = jax.ShapeDtypeStruct(shape, x.dtype)
    scratch = [pltpu.SemaphoreType.DMA((chunks,)), sems, sems]
    return Plan([x], out, scratch, two_level(axis, n), chunks, bind, pl.ANY)


def scatter_ops(axis, rel, x_ref, out_ref, near_buf, send_buf, far_buf, s1, r1, s2, r2, inside=False, held=None):
    n = lax.axis_size(axis)
    outer = n // 2
    chunks = out_ref.shape[0]
    me = lax.axis_index(axis)

    def part(j, c, ref=x_ref):
        block = j if rel else me ^ j
        return ref.at[c, block] if inside else ref.at[block, c]

    def mine(j, c):
        return part(j, c, x_ref if held is None else held)[...].astype(f32)

    def near(o, c):
        return remote(part(2 * o + 1, c), near_buf.at[o, c], s1.at[o, c], r1.at[o, c], axis, me ^ 1)

    def far(o, c):
        return remote(send_buf.at[o, c], far_buf.at[o, c], s2.at[o, c], r2.at[o, c], axis, me ^ (2 * o))

    def start_outer():
        def first(c):
            for o in range(1, outer):
                near(o, c).start()

        each(0, chunks, first)

    def start_inner():
        each(0, chunks, lambda c: near(0, c).start())

    def start():
        start_outer()
        start_inner()

    def step(c):
        for o in range(1, outer):
            near(o, c).wait_recv()
            total = mine(2 * o, c) + near_buf[o, c].astype(f32)
            send_buf[o, c] = total.astype(send_buf.dtype)
            far(o, c).start()

    def finish():
        def last(c):
            near(0, c).wait_recv()
            total = mine(0, c) + near_buf[0, c].astype(f32)
            for o in range(1, outer):
                far(o, c).wait_recv()
                total = total + far_buf[o, c].astype(f32)
            out_ref[c] = total.astype(out_ref.dtype)
            for o in range(outer):
                near(o, c).wait_send()
            for o in range(1, outer):
                far(o, c).wait_send()

        each(0, chunks, last)

    return SimpleNamespace(
        start=start, start_outer=start_outer, start_inner=start_inner, step=step, finish=finish
    )


def scatter_scratch(n, inner, dtype):
    half = VM((n // 2,) + inner, dtype)
    sems = pltpu.SemaphoreType.DMA((n // 2, inner[0]))
    return [half, half, half, sems, sems, sems, sems]


class Session:
    def __init__(self, plans, more_peers=()):
        self.plans = plans
        self.ins = [x for p in plans for x in p.ins]
        self.outs = [p.out for p in plans]
        self.in_specs = [pl.BlockSpec(memory_space=VM)] * len(self.ins)
        self.out_specs = [pl.BlockSpec(memory_space=p.out_space) for p in plans]
        self.scratch = [scr for p in plans for scr in p.scratch]
        self.peers = sorted({peer for p in plans for peer in p.peers} | set(more_peers))

    def greet(self):
        barrier = pltpu.get_barrier_semaphore()
        for axis, j in self.peers:
            pl.semaphore_signal(barrier, inc=1, device_id={axis: lax.axis_index(axis) ^ j}, device_id_type=MESH)
        pl.semaphore_wait(barrier, len(self.peers))

    def bind(self, ins, outs, scratch):
        at_in = at_scr = 0
        self.bound = []
        for p, out in zip(self.plans, outs):
            mine = ins[at_in : at_in + len(p.ins)]
            own = scratch[at_scr : at_scr + len(p.scratch)]
            self.bound.append((p.count, p.window, p.bind(*mine, out, *own)))
            at_in += len(p.ins)
            at_scr += len(p.scratch)

    def start(self):
        for _, _, ops in self.bound:
            ops.start()

    def steps(self, i, total):
        for count, window, ops in self.bound:
            low, high = window or (0, total)
            span = high - low

            def some(ops=ops, count=count, low=low, span=span):
                if count == span:
                    ops.step(i - low)
                else:
                    each(((i - low) * count) // span, ((i - low + 1) * count) // span, ops.step)

            if not count:
                continue
            if span == total:
                some()
            else:
                pl.when(jnp.logical_and(i >= low, i < high))(some)

    def finish(self):
        for _, _, ops in self.bound:
            ops.finish()


def everyone_else(*axes):
    return [(axis, j) for axis in axes for j in range(1, lax.axis_size(axis))]


def pairs_of_sems(*axes):
    return [pltpu.SemaphoreType.DMA((lax.axis_size(axis),)) for axis in axes for _ in range(2)]


def params(cid):
    return pltpu.CompilerParams(collective_id=cid, has_side_effects=True, vmem_limit_bytes=LIMIT)


def opening(cid, mod_w, attn_w, exp_w, out_w, small, seq_n, images, pairs, early):
    raw = mod_w.dtype == f32
    own, width = out_w.shape
    dim_l = pairs * 128
    img_n, rows, _ = small.shape
    cuts = [x.size // (seq_n * own) for x in (mod_w, attn_w, exp_w)]
    mod_l, _, hid_l = cuts
    hid_o = hid_l // img_n
    head = seq_n * images
    tiles = mod_l // 128
    slim = -(-tiles * images // 8) * 8
    count = max(early, 1)
    shapes = [(seq_n, own, c) for c in cuts]
    session = Session([], everyone_else("img", "seq"))

    def kernel(
        mod_in, attn_in, exp_in, out_in, small_ref,
        modo_ref, bias_ref, lhs_ref, modw_ref, attnw_ref, expw_ref, early_ref, outw_ref,
        small_all, part_buf, part_all, sum_buf, *more
    ):
        if raw:
            mod_ref, attn_ref, exp_ref, out_ref, *sems = more
            out_ref[0] = out_in[...].astype(bf16)
            for q in range(seq_n):
                mod_ref[q] = mod_in[:, q * mod_l : (q + 1) * mod_l].astype(bf16)
        else:
            mod_ref, attn_ref, exp_ref = mod_in, attn_in, exp_in
            out_ref, *sems = more
            out_ref[0] = out_in[...].astype(bf16)
        early_in = gather_ops("img", False, attnw_ref.at[:count], early_ref, *sems[14:17])
        out_go = gather_ops("img", False, out_ref, outw_ref, *sems[17:20])
        session.greet()
        small_go, small_end = direct_ops("img", small_ref, small_all, *sems[:2])
        mod_go, mod_end = direct_ops("seq", mod_ref, modw_ref, *sems[2:4])
        attn_go, attn_end = direct_ops("seq", attn_ref, attnw_ref, *sems[4:6])
        exp_go, exp_end = direct_ops("seq", exp_ref, expw_ref, *sems[12:14])
        small_go()
        mod_go()
        if raw:
            for q in range(seq_n):
                for p in range(pairs):
                    for k in range(3):
                        at = k * width + q * dim_l + p * 128
                        to = p * 384 + k * 128
                        attn_ref[q, :, to : to + 128] = attn_in[:, at : at + 128].astype(bf16)
        attn_go()
        if raw:
            for q in range(seq_n):
                for i in range(img_n):
                    at = (i * seq_n + q) * hid_o
                    exp_ref[q, :, i * hid_o : (i + 1) * hid_o] = exp_in[:, at : at + hid_o].astype(bf16)
        exp_go()
        out_go.start()
        part_buf[...] = jnp.zeros_like(part_buf)
        small_end()
        bias_go, bias_end = direct_ops("seq", small_all.at[:, head:], bias_ref, *sems[6:8], everyone=True)
        bias_go()
        for i in range(img_n):
            for q in range(seq_n):
                lhs_ref[q, i * images : (i + 1) * images] = small_all[i, q * images : (q + 1) * images]
        mod_end()
        part = jnp.zeros((img_n * images, mod_l), f32)
        for q in range(seq_n):
            part = part + dot(lhs_ref[q][:, :own].astype(bf16), modw_ref[q], ((1,), (0,)))
        for i in range(img_n):
            for t in range(tiles):
                part_buf[i, t * images : (t + 1) * images] = part[
                    i * images : (i + 1) * images, t * 128 : (t + 1) * 128
                ]
        part_go, part_end = direct_ops("img", part_buf, part_all, *sems[8:10])
        part_go()
        out_go.step(0)
        attn_end()
        if early:
            early_in.start()
        part_end()
        total = part_all[0]
        for i in range(1, img_n):
            total = total + part_all[i]
        sum_buf[...] = total
        sum_go, sum_end = direct_ops("seq", sum_buf, modo_ref, *sems[10:12], everyone=True)
        sum_go()
        if early:
            each(0, early, early_in.step)
        bias_end()
        sum_end()
        exp_end()
        out_go.finish()
        if early:
            early_in.finish()

    full = pl.BlockSpec(memory_space=VM)
    any_space = pl.BlockSpec(memory_space=pl.ANY)
    sending = [VM(x, bf16) for x in shapes] if raw else []
    return pl.pallas_call(
        kernel,
        out_shape=(
            jax.ShapeDtypeStruct((seq_n, slim, 128), f32),
            jax.ShapeDtypeStruct((seq_n, img_n, rows - head, 128), f32),
            jax.ShapeDtypeStruct((seq_n, img_n * images, 128), f32),
            *[jax.ShapeDtypeStruct(x, bf16) for x in shapes],
            jax.ShapeDtypeStruct((img_n, count) + shapes[1][1:], bf16),
            jax.ShapeDtypeStruct((img_n, 1, own, width), bf16),
        ),
        in_specs=[full] * 5,
        out_specs=(full,) * 6 + (any_space,) * 2,
        scratch_shapes=[
            VM(small.shape, f32),
            VM((img_n, slim, 128), f32),
            VM((img_n, slim, 128), f32),
            VM((slim, 128), f32),
        ]
        + sending
        + [VM((1, own, width), bf16)]
        + pairs_of_sems("img", "seq", "seq", "seq", "img", "seq", "seq")
        + [pltpu.SemaphoreType.DMA((count,))]
        + [pltpu.SemaphoreType.DMA((img_n, count))] * 2
        + [pltpu.SemaphoreType.DMA((1,))]
        + [pltpu.SemaphoreType.DMA((img_n, 1))] * 2,
        compiler_params=params(cid),
        name="opening",
    )(mod_w, attn_w, exp_w, out_w, small)


def finishing(modw, attnw, expw, bias, outw, shrw, heads):
    own, width = outw.shape
    hid_o = shrw.shape[0]

    def kernel(modw_ref, attnw_ref, expw_ref, bias_ref, outw_ref, shrw_ref, *outs):
        for src, out in zip((modw_ref, attnw_ref, expw_ref, outw_ref, shrw_ref), outs):
            out[...] = src[...].astype(f32)
        shift = (128 - lax.axis_index("seq") * own) % 128
        rolled = pltpu.roll(bias_ref[...], shift, 1)
        for row in range(4):
            outs[5 + row][...] = rolled[row : row + 1, :own]
        outs[9][...] = bias_ref[4:5, :hid_o]
        outs[10][...] = bias_ref[5:6, :heads]

    full = pl.BlockSpec(memory_space=VM)
    shapes = [modw.shape, attnw.shape, expw.shape, outw.shape, shrw.shape] + [(1, own)] * 4 + [(1, hid_o), (1, heads)]
    got = pl.pallas_call(
        kernel,
        out_shape=tuple(jax.ShapeDtypeStruct(x, f32) for x in shapes),
        in_specs=[full] * 6,
        out_specs=(full,) * len(shapes),
        compiler_params=pltpu.CompilerParams(vmem_limit_bytes=LIMIT),
        name="finishing",
    )(modw, attnw, expw, bias, outw, shrw)
    return list(got[:5]) + [x.reshape(-1) for x in got[5:]]


def closing(cid, mine, expb, lhs, modw, attn_back, exp_back, images, pairs):
    seq_n, own, mod_l = modw.shape
    img_n = expb.shape[0]
    rows = mine.shape[1]
    head = seq_n * images
    tiles = mod_l // 128
    slim = -(-tiles * images // 8) * 8
    share = img_n // seq_n
    dim_l = pairs * 128
    width = dim_l * seq_n
    hid_l = exp_back.shape[2]
    hid_o = hid_l // img_n
    aligned = hid_o % 128 == 0
    flat = -(-tiles // 8) * 8

    def kernel(
        mine_ref, expb_ref, lhs_ref, modw_ref, attn_ref, exp_ref,
        modw_own, attn_own, exp_own, bias_ref, modb_ref, cond_ref,
        seen, block, got, dd, mw_send, mw_recv, mb_send, gs_send, gs_all, gs_seen, attn_all, exp_all, *sems
    ):
        barrier = Session([], everyone_else("img", "seq"))
        barrier.greet()
        mine_go, mine_end = direct_ops("seq", mine_ref, seen, *sems[:2])
        attn_go, attn_end = direct_ops("seq", attn_ref, attn_all, *sems[2:4])
        exp_go, exp_end = direct_ops("seq", exp_ref, exp_all, *sems[14:16])
        mine_go()
        attn_go()
        exp_go()
        block[...] = jnp.zeros_like(block)
        gs_send[...] = jnp.zeros_like(gs_send)
        mb_send[...] = jnp.zeros_like(mb_send)
        mine_end()
        total = seen[0]
        for q in range(1, seq_n):
            total = total + seen[q]
        at = slim + 2 * img_n
        for i in range(img_n):
            block[i, :slim] = total[:slim]
            block[i, slim : slim + 1] = total[slim + i : slim + i + 1]
            block[i, slim + 1 : slim + 2] = total[slim + img_n + i : slim + img_n + i + 1]
            row = at + 8 + i % share
            block[i, slim + 2 : slim + 3] = seen[i // share, row : row + 1]
            block[i, slim + 3 : slim + 4] = seen[i // share, row + share : row + share + 1]
            block[i, slim + 4 : slim + 5] = expb_ref[i : i + 1]
            block[i, slim + 5 : slim + 6] = total[at : at + 1]
        img_go, img_end = direct_ops("img", block, got, *sems[4:6])
        img_go()
        attn_end()
        exp_end()
        for q in range(seq_n):
            for p in range(pairs):
                for k in range(3):
                    to = k * width + q * dim_l + p * 128
                    at_c = p * 384 + k * 128
                    attn_own[:, to : to + 128] = attn_all[q, :, at_c : at_c + 128]
            if aligned:
                for i in range(img_n):
                    to = (i * seq_n + q) * hid_o
                    exp_own[:, to : to + hid_o] = exp_all[q, :, i * hid_o : (i + 1) * hid_o]
            else:
                exp_own[:, q * hid_l : (q + 1) * hid_l] = exp_all[q]
        img_end()
        sums = got[0]
        for i in range(1, img_n):
            sums = sums + got[i]
        bias_ref[...] = sums[slim:]
        for t in range(tiles):
            mb_send[t : t + 1] = jnp.sum(sums[t * images : (t + 1) * images], axis=0, keepdims=True)
            for i in range(img_n):
                dd[i * images : (i + 1) * images, t * 128 : (t + 1) * 128] = got[i, t * images : (t + 1) * images]
        grad = dd[...]
        high = grad.astype(bf16)
        low = (grad - high.astype(f32)).astype(bf16)
        for q in range(seq_n):
            out = dot(high, modw_ref[q], ((1,), (1,))) + dot(low, modw_ref[q], ((1,), (1,)))
            for i in range(img_n):
                gs_send[i, q * images : (q + 1) * images, :own] = out[i * images : (i + 1) * images]
        gs_go, gs_end = direct_ops("img", gs_send, gs_all, *sems[6:8])
        gs_go()
        for q in range(seq_n):
            mw_send[q] = dot(lhs_ref[q][:, :own].astype(bf16), high, ((0,), (0,))).astype(bf16)
        mb_go, mb_end = direct_ops("seq", mb_send, modb_ref, *sems[10:12], everyone=True)
        mb_go()
        gs_end()
        all_go, all_end = direct_ops("seq", gs_all, gs_seen, *sems[12:14], everyone=True)
        all_go()
        mw_go, mw_end = direct_ops("seq", mw_send, mw_recv, *sems[8:10])
        mw_go()
        mb_end()
        all_end()
        out = gs_seen[0]
        for q in range(1, seq_n):
            out = out + gs_seen[q]
        cond_ref[...] = out
        mw_end()
        for q in range(seq_n):
            modw_own[:, q * mod_l : (q + 1) * mod_l] = mw_recv[q]

    full = pl.BlockSpec(memory_space=VM)
    got = pl.pallas_call(
        kernel,
        out_shape=(
            jax.ShapeDtypeStruct((own, mod_l * seq_n), bf16),
            jax.ShapeDtypeStruct((own, 3 * width), bf16),
            jax.ShapeDtypeStruct((own, hid_l * seq_n), bf16),
            jax.ShapeDtypeStruct((8, 128), f32),
            jax.ShapeDtypeStruct((seq_n, flat, 128), f32),
            jax.ShapeDtypeStruct((img_n, head, 128), f32),
        ),
        in_specs=[full] * 6,
        out_specs=(full,) * 6,
        scratch_shapes=[
            VM((seq_n, rows, 128), f32),
            VM((img_n, slim + 8, 128), f32),
            VM((img_n, slim + 8, 128), f32),
            VM((img_n * images, mod_l), f32),
            VM((seq_n, own, mod_l), bf16),
            VM((seq_n, own, mod_l), bf16),
            VM((flat, 128), f32),
            VM((img_n, head, 128), f32),
            VM((img_n, head, 128), f32),
            VM((seq_n, img_n, head, 128), f32),
            VM(attn_back.shape, bf16),
            VM(exp_back.shape, bf16),
        ]
        + pairs_of_sems("seq", "seq", "img", "img", "seq", "seq", "seq", "seq"),
        compiler_params=params(cid),
        name="closing",
    )(mine, expb, lhs, modw, attn_back, exp_back)
    got = list(got)
    if not aligned:
        got[2] = got[2].reshape(own, seq_n, img_n, hid_o).transpose(0, 2, 1, 3).reshape(own, hid_l * seq_n)
    return got


def half_sums(values, low_half):
    first = jnp.sum(jnp.where(low_half, values, 0.0), axis=-1, keepdims=True)
    second = jnp.sum(jnp.where(low_half, 0.0, values), axis=-1, keepdims=True)
    return jnp.where(low_half, first, second)


def dot(a, b, dims):
    return lax.dot_general(a, b, (dims, ((), ())), preferred_element_type=f32)


def lanes(start, size):
    return pl.ds(pl.multiple_of(start, 128), size)


def load_heads(p_ref, bias, g, p, rows):
    both = p_ref[:, g, :, lanes(p * 384, 384)].reshape(rows, 384)
    query = both[:, :128] + bias[:, :128]
    key = both[:, 128:256]
    value = both[:, 256:] + bias[:, 256:]
    low_half = lax.broadcasted_iota(jnp.int32, (rows, 128), 1) < 64
    r_query = lax.rsqrt(half_sums(query * query, low_half) + 1e-06)
    r_key = lax.rsqrt(half_sums(key * key, low_half) + 1e-06)
    return query, key, value, low_half, r_query, r_key


def some_rows(start, size):
    return pl.ds(pl.multiple_of(start, 16), size)


def centre(v):
    centered = v - jnp.mean(v, axis=-1, keepdims=True)
    factor = lax.rsqrt(jnp.mean(centered * centered, axis=-1, keepdims=True) + 1e-06)
    return centered * factor, factor


def centre_back(normed, factor, grad):
    return factor * (grad - jnp.mean(grad, axis=-1, keepdims=True) - normed * jnp.mean(grad * normed, axis=-1, keepdims=True))


def attend(cid, attn_input, attn_own, attn_early, early, bias, scale, sid_k, sid_q, out_img, exp_own, grad_own):
    seq_n, img_n = lax.axis_size("seq"), lax.axis_size("img")
    outer = seq_n // 2
    chunks, size, width = attn_input.shape
    local = chunks * size
    images = sid_q.shape[0]
    rows_b = local // images
    rows = seq_n * rows_b
    wide = attn_own.shape[2]
    pairs = wide // 384
    turns = images * pairs
    tile = 256 if wide % 256 == 0 else 128
    w_chunks = attn_own.shape[0]
    plans = [gather(x, "seq", True) for x in grad_own] + [gather(out_img, "seq", False, True), gather(exp_own, "img", False)]
    session = Session(plans, everyone_else("seq") + two_level("img", img_n))
    ins, outs = 7 + len(session.ins), 4 + len(plans)
    weight = (img_n, early + w_chunks) + attn_own.shape[1:]

    def kernel(*refs):
        x_ref, w_ref, early_ref, b_ref, es_ref, sk_ref, sq_ref = refs[:7]
        o_ref, p_out, h_out, w_out = refs[ins : ins + 4]
        scratch = refs[ins + outs :]
        h1, attn_w, packed, o_buf, o_send, o_recv, hs, hr, wk, ws, wr, out_sem, early_sem = scratch[:13]
        me = lax.axis_index("seq")
        session.greet()
        session.bind(refs[7:ins], refs[ins + 4 : ins + outs], scratch[13:])
        h1_in = gather_ops("seq", True, x_ref, h1, None, hs, hr)
        w_in = gather_ops("img", False, w_ref, attn_w.at[:, early:], wk, ws, wr)
        if early:
            load = pltpu.make_async_copy(early_ref, attn_w.at[:, :early], early_sem.at[0])
            load.start()
        h1_in.start()
        w_in.start()
        session.start()
        *grads, (out_count, _, out_in), (exp_count, _, exp_in) = session.bound
        h1[0] = x_ref[...]

        def ship(i, j):
            g, p = i // pairs, i % pairs
            return remote(
                o_buf.at[i, j],
                o_ref.at[g, :, lanes((me * pairs + p) * 128, 128)],
                o_send.at[j, i],
                o_recv.at[j, i],
                "seq",
                me ^ j,
            )

        each(0, chunks // 2, h1_in.step)
        each(0, w_chunks // 2, w_in.step)
        each(chunks // 2, chunks, h1_in.step)
        each(w_chunks // 2, w_chunks, w_in.step)
        h1_in.near()
        for o in range(1, outer):
            h1_in.handed(o)
        w_in.near()
        for o in range(1, img_n // 2):
            w_in.handed(o)
        w_in.sent()
        if early:
            load.wait()
        quarter = exp_count // 4
        each(0, quarter, exp_in.step)

        def project(k):
            j, t = k // (wide // tile), k % (wide // tile)
            columns = lanes(t * tile, tile)
            part = dot(h1[j].reshape(local, width), attn_w[:, :, :, columns].reshape(width, tile), ((1,), (0,)))
            packed[j, :, :, columns] = part.reshape(images, rows_b, tile)

        each(0, seq_n * (wide // tile), project)
        each(quarter, 2 * quarter, exp_in.step)
        copies = [
            pltpu.make_async_copy(src, dst, out_sem.at[n])
            for n, (src, dst) in enumerate(((packed, p_out), (h1, h_out), (attn_w, w_out)))
        ]
        for copy in copies:
            copy.start()

        def turn(i):
            g, p = i // pairs, i % pairs
            query, key, value, low_half, r_query, r_key = load_heads(packed, b_ref[p], g, p, rows)
            query_low = query * r_query * es_ref[p]
            key_t = jnp.transpose(key * r_key).astype(bf16)
            sid_k = sq_ref[g]
            masks = [low_half, jnp.logical_not(low_half)]
            queries = [jnp.where(mine, query_low, 0.0).astype(bf16) for mine in masks]
            values = [jnp.where(mine, value, 1.0).astype(bf16) for mine in masks]
            low_b = low_half[:rows_b]
            for b in range(seq_n):
                seen = sid_k <= sk_ref[g, b]
                parts = []
                for h in range(2):
                    scores = dot(queries[h][b * rows_b : (b + 1) * rows_b], key_t, ((1,), (0,)))
                    expo = jnp.where(seen, jnp.exp(scores), 0.0).astype(bf16)
                    parts.append(dot(expo, values[h], ((1,), (0,))))
                totals = jnp.where(low_b, pltpu.roll(parts[0], 64, 1), pltpu.roll(parts[1], 64, 1))
                o_buf[i, b] = (jnp.where(low_b, parts[0], parts[1]) / totals).astype(bf16)
            o_ref[g, :, lanes((me * pairs + p) * 128, 128)] = o_buf[i, 0]
            for j in range(1, seq_n):
                ship(i, j).start()

            @pl.when(i == 0)
            def _():
                for count, _, ops in grads:
                    each(0, count, ops.step)

            half = turns // 2

            @pl.when(i == half - 1)
            def _():
                each(2 * quarter, 3 * quarter, exp_in.step)

            @pl.when(i == half)
            def _():
                each(0, out_count, out_in.step)
                each(3 * quarter, exp_count, exp_in.step)

        each(0, turns, turn)
        session.finish()
        h1_in.sent()
        for copy in copies:
            copy.wait()

        def last(i):
            for j in range(1, seq_n):
                ship(i, j).wait()

        each(0, turns, last)

    full = pl.BlockSpec(memory_space=VM)
    any_space = pl.BlockSpec(memory_space=pl.ANY)
    sems = pltpu.SemaphoreType.DMA((seq_n, turns))
    seq_sems = pltpu.SemaphoreType.DMA((seq_n, chunks))
    img_sems = pltpu.SemaphoreType.DMA((img_n, w_chunks))
    packed = (seq_n, images, rows_b, wide)
    return pl.pallas_call(
        kernel,
        out_shape=tuple(
            [
                jax.ShapeDtypeStruct((images, rows_b, width), bf16),
                jax.ShapeDtypeStruct(packed, f32),
                jax.ShapeDtypeStruct((seq_n,) + attn_input.shape, bf16),
                jax.ShapeDtypeStruct(weight, bf16),
            ]
            + session.outs
        ),
        in_specs=[full] * 2 + [any_space] + [full] * 4 + session.in_specs,
        out_specs=tuple([full] + [any_space] * 3 + session.out_specs),
        scratch_shapes=[
            VM((seq_n,) + attn_input.shape, bf16),
            VM(weight, bf16),
            VM(packed, f32),
            VM((turns, seq_n, rows_b, 128), bf16),
            sems,
            sems,
            seq_sems,
            seq_sems,
            pltpu.SemaphoreType.DMA((w_chunks,)),
            img_sems,
            img_sems,
            pltpu.SemaphoreType.DMA((3,)),
            pltpu.SemaphoreType.DMA((1,)),
        ]
        + session.scratch,
        compiler_params=params(cid),
        name="attend",
    )(attn_input, attn_own, attn_early, bias, scale, sid_k, sid_q, *session.ins)


def attend_back(
    cid, packed, h1, attn_w, d_out, bias, scale, sid_k, sid_q, expw_part, shrunk_part, outw_part, mid, d_mid, tokens, cotangent, lines
):
    seq_n, images, rows_b, wide = packed.shape
    img_n = lax.axis_size("img")
    outer = seq_n // 2
    pairs = wide // 384
    rows = seq_n * rows_b
    turns = images * pairs
    _, chunks, size, width = h1.shape
    local = chunks * size
    _, w_chunks, w_size, _ = attn_w.shape
    own = outw_part.shape[2]
    tile = 256
    blocks_per_tile = tile // (w_chunks * w_size)
    pieces = -(-width // wide)
    h_chunks, f_chunks = chunks // images, shrunk_part.shape[1] // images
    session = Session([], everyone_else("seq") + two_level("img", img_n))
    mids = [
        scatter_scratch(img_n, expw_part.shape[1:], bf16),
        scatter_scratch(seq_n, shrunk_part.shape[1:], bf16),
        scatter_scratch(seq_n, (img_n, own, width), bf16),
        scatter_scratch(img_n, (1, own, width), bf16),
        scatter_scratch(img_n, attn_w.shape[1:], bf16),
        scatter_scratch(seq_n, h1.shape[1:], bf16),
    ]

    def kernel(*refs):
        p_in, h_in, w_in, do_ref, b_ref, es_ref, sk_ref, sq_ref, expw_ref, f_ref, outw_ref = refs[:11]
        mid_in, dmid_in, tok_ref, dy_ref, line_ref = refs[11:16]
        st_ref, sum_ref, layer_ref, token_ref, attn_own, expw_own, outw_own = refs[16:23]
        f_own, dh1_own, late_sem = refs[23:26]
        scratch = refs[26:]
        p_ref, h_ref, w_ref, dp_ref, dh1, dattn, out_mid, load_sem = scratch[:8]
        k_buf, v_buf, e_buf, g_buf, dk_buf, dv_buf, do_buf, o_send, o_recv = scratch[8:17]
        expw_held, f_held, outw_held = scratch[17:20]
        more = scratch[20:]
        me = lax.axis_index("seq")
        session.greet()

        def ship(i, j):
            g, p = i // pairs, i % pairs
            return remote(
                do_ref.at[g, :, lanes(((me ^ j) * pairs + p) * 128, 128)],
                do_buf.at[i, j],
                o_send.at[j, i],
                o_recv.at[j, i],
                "seq",
                me ^ j,
            )

        def send(i):
            for j in range(1, seq_n):
                ship(i, j).start()

        each(0, turns, send)
        loads = [
            pltpu.make_async_copy(src, dst, load_sem.at[n])
            for n, (src, dst) in enumerate(
                (
                    (p_in, p_ref),
                    (outw_ref, outw_held),
                    (f_ref, f_held),
                    (expw_ref, expw_held),
                    (h_in, h_ref),
                    (w_in, w_ref),
                )
            )
        ]
        for load in loads:
            load.start()
        exp_out = scatter_ops("img", False, expw_ref, expw_own, *more[:7], held=expw_held)
        f_out = scatter_ops("seq", True, f_ref, f_own, *more[7:14], held=f_held)
        mid_out = scatter_ops(
            "seq", False, outw_ref, out_mid.at[:, 0], *more[14:21], inside=True, held=outw_held
        )
        outw_out = scatter_ops("img", False, out_mid, outw_own, *more[21:28])
        attn_out = scatter_ops("img", False, dattn, attn_own, *more[28:35])
        dh1_out = scatter_ops("seq", True, dh1, dh1_own, *more[35:42])
        exp_out.start()
        mid_out.start()
        f_out.start()
        exp_chunks = expw_ref.shape[1]
        loads[0].wait()

        def turn(i):
            g, p = i // pairs, i % pairs
            query, key, value, low_half, r_query, r_key = load_heads(p_ref, b_ref[p], g, p, rows)
            scale_row = es_ref[p]
            q_unit = query * r_query
            k_unit = key * r_key
            q_full = q_unit * scale_row
            k_buf[...] = k_unit.astype(bf16).reshape(seq_n, rows_b, 128)
            v_buf[...] = value.astype(bf16).reshape(seq_n, rows_b, 128)
            do_buf[i, 0] = do_ref[g, :, lanes((me * pairs + p) * 128, 128)]
            for j in range(1, seq_n):
                ship(i, j).wait_recv()
            d_out = do_buf[i].reshape(rows, 128).astype(f32)
            sid_q = sq_ref[g]
            masks = [low_half, jnp.logical_not(low_half)]
            q_f = [jnp.where(mine, q_full, 0.0) for mine in masks]
            do_f = [jnp.where(mine, d_out, 0.0) for mine in masks]
            q_h = [x.astype(bf16) for x in q_f]
            do_h = [x.astype(bf16) for x in do_f]
            q_t = [jnp.transpose(x).astype(bf16) for x in q_f]
            do_t = [jnp.transpose(x).astype(bf16) for x in do_f]
            total = [jnp.zeros((1, rows), f32)] * 2
            mixed = [jnp.zeros((1, rows), f32)] * 2
            for b in range(seq_n):
                seen = sk_ref[g, b] <= sid_q
                for h in range(2):
                    scores = dot(k_buf[b], q_t[h], ((1,), (0,)))
                    expo = jnp.where(seen, jnp.exp(scores), 0.0)
                    grad = dot(v_buf[b], do_t[h], ((1,), (0,)))
                    e_buf[h, b] = expo
                    g_buf[h, b] = grad
                    total[h] = total[h] + jnp.sum(expo, axis=0, keepdims=True)
                    mixed[h] = mixed[h] + jnp.sum(expo * grad, axis=0, keepdims=True)
            inverse = [1.0 / x for x in total]
            delta = [x * y for x, y in zip(mixed, inverse)]
            acc = [jnp.zeros((128, rows), f32)] * 2
            for b in range(seq_n):
                dv = dk = jnp.zeros((rows_b, 128), f32)
                for h in range(2):
                    probs = e_buf[h, b] * inverse[h]
                    scores_grad = (probs * (g_buf[h, b] - delta[h])).astype(bf16)
                    dv = dv + dot(probs.astype(bf16), do_h[h], ((1,), (0,)))
                    dk = dk + dot(scores_grad, q_h[h], ((1,), (0,)))
                    acc[h] = acc[h] + dot(k_buf[b], scores_grad, ((0,), (0,)))
                dv_buf[b] = dv
                dk_buf[b] = dk
            parts = [acc[0][:64], acc[1][64:]]
            dq = jnp.transpose(jnp.concatenate(parts, axis=0)).astype(bf16).astype(f32)
            dk = dk_buf[...].reshape(rows, 128).astype(bf16).astype(f32)
            dv = dv_buf[...].reshape(rows, 128).astype(bf16).astype(f32)
            dq_raw = scale_row * r_query * (dq - q_unit * half_sums(q_unit * dq, low_half))
            dk_raw = r_key * (dk - k_unit * half_sums(k_unit * dk, low_half))
            together = jnp.concatenate([dq_raw, dk_raw, dv], axis=1).astype(bf16)
            dp_ref[:, g, :, lanes(p * 384, 384)] = together.reshape(seq_n, rows_b, 384)
            sums = [
                jnp.sum(dq_raw, axis=0, keepdims=True),
                jnp.sum(dv, axis=0, keepdims=True),
                jnp.sum(dq * q_full, axis=0, keepdims=True),
                jnp.zeros((5, 128), f32),
            ]
            st_ref[i] = jnp.concatenate(sums, axis=0)

            @pl.when(i == 0)
            def _():
                for load in loads[1:4]:
                    load.wait()
                each(0, img_n, mid_out.step)
                each(0, shrunk_part.shape[1], f_out.step)

            each((i * exp_chunks) // turns, ((i + 1) * exp_chunks) // turns, exp_out.step)

        each(0, turns, turn)
        late = []
        for n, src in enumerate((mid_in, dmid_in)):
            for k in range(pieces):
                low, high = k * wide, min((k + 1) * wide, width)
                dst = p_ref.at[n * pieces + k, :, :, : high - low]
                late.append(pltpu.make_async_copy(src.at[:, :, low:high], dst, late_sem.at[len(late)]))
        for copy in late:
            copy.start()

        def held_rows(n, g):
            parts = [p_ref[n * pieces + k, g, :, : min(wide, width - k * wide)] for k in range(pieces)]
            return jnp.concatenate(parts, axis=1)

        def layer(g):
            total = f_own[pl.ds(g * f_chunks, f_chunks)].reshape(rows_b, width) + line_ref[g, 2:3]
            layer_ref[g] = (held_rows(0, g) + line_ref[g, 1:2] * total).astype(bf16)
            sum_ref[g, 2:3] = jnp.sum(dy_ref[g].astype(f32) * total, axis=0, keepdims=True)

        def token(g):
            grad = dh1_own[pl.ds(g * h_chunks, h_chunks)].reshape(rows_b, width)
            normed, factor = centre(tok_ref[g].astype(f32))
            back = centre_back(normed, factor, grad * line_ref[g, 0:1])
            token_ref[g] = (held_rows(1, g) + back).astype(bf16)
            sum_ref[g, 0:1] = jnp.sum(grad * normed, axis=0, keepdims=True)
            sum_ref[g, 1:2] = jnp.sum(grad, axis=0, keepdims=True)

        mid_out.finish()
        outw_out.start()
        for load in loads[4:]:
            load.wait()

        def columns(t):
            return lanes(t * tile, tile)

        def weight_grad(t):
            left = h_ref[:, :, :, columns(t)].reshape(seq_n * local, tile)
            part = dot(left, dp_ref[...].reshape(seq_n * local, wide), ((0,), (0,)))
            dattn[pl.ds(t * blocks_per_tile, blocks_per_tile)] = part.astype(bf16).reshape(
                blocks_per_tile, w_chunks, w_size, wide
            )

        def input_grad(j):
            def run(t):
                weight = w_ref[pl.ds(t * blocks_per_tile, blocks_per_tile)].reshape(tile, wide)
                part = dot(dp_ref[j].reshape(local, wide), weight, ((1,), (1,)))
                dh1[j, :, :, columns(t)] = part.astype(bf16).reshape(chunks, size, tile)

            each(0, width // tile, run)

        each(0, width // tile, weight_grad)
        attn_out.start()
        outw_out.step(0)
        exp_out.finish()
        for o in range(1, outer):
            for j in (2 * o + 1, 2 * o):
                input_grad(j)
        dh1_out.start_outer()
        each(0, chunks, dh1_out.step)
        each(0, w_chunks // 2, attn_out.step)
        input_grad(1)
        each(w_chunks // 2, (3 * w_chunks) // 4, attn_out.step)
        input_grad(0)
        dh1_out.start_inner()
        each((3 * w_chunks) // 4, w_chunks, attn_out.step)
        outw_out.finish()
        f_out.finish()
        sum_ref[...] = jnp.zeros_like(sum_ref)
        for copy in late:
            copy.wait()
        each(0, images, layer)
        dh1_out.finish()
        each(0, images, token)
        attn_out.finish()

        def last(i):
            for j in range(1, seq_n):
                ship(i, j).wait_send()

        each(0, turns, last)

    full = pl.BlockSpec(memory_space=VM)
    any_space = pl.BlockSpec(memory_space=pl.ANY)
    sems = pltpu.SemaphoreType.DMA((seq_n, turns))
    return pl.pallas_call(
        kernel,
        out_shape=(
            jax.ShapeDtypeStruct((turns, 8, 128), f32),
            jax.ShapeDtypeStruct((images, 8, width), f32),
            jax.ShapeDtypeStruct(tokens.shape, bf16),
            jax.ShapeDtypeStruct(tokens.shape, bf16),
            jax.ShapeDtypeStruct(attn_w.shape[1:], bf16),
            jax.ShapeDtypeStruct(expw_part.shape[1:], bf16),
            jax.ShapeDtypeStruct((1, own, width), f32),
        ),
        in_specs=[any_space] * 3 + [full] * 5 + [any_space] * 5 + [full] * 3,
        out_specs=(full,) * 7,
        scratch_shapes=[
            VM(shrunk_part.shape[1:], f32),
            VM(h1.shape[1:], f32),
            pltpu.SemaphoreType.DMA((2 * pieces,)),
            VM(packed.shape, f32),
            VM(h1.shape, bf16),
            VM(attn_w.shape, bf16),
            VM(packed.shape, bf16),
            VM(h1.shape, bf16),
            VM(attn_w.shape, bf16),
            VM((img_n, 1, own, width), bf16),
            pltpu.SemaphoreType.DMA((6,)),
            VM((seq_n, rows_b, 128), bf16),
            VM((seq_n, rows_b, 128), bf16),
            VM((2, seq_n, rows_b, rows), f32),
            VM((2, seq_n, rows_b, rows), f32),
            VM((seq_n, rows_b, 128), f32),
            VM((seq_n, rows_b, 128), f32),
            VM((turns, seq_n, rows_b, 128), bf16),
            sems,
            sems,
            VM(expw_part.shape, bf16),
            VM(shrunk_part.shape, bf16),
            VM(outw_part.shape, bf16),
        ]
        + [x for scratch in mids for x in scratch],
        compiler_params=params(cid),
        name="attend_back",
    )(
        packed, h1, attn_w, d_out, bias, scale, sid_k, sid_q, expw_part, shrunk_part, outw_part, mid, d_mid, tokens, cotangent, lines
    )


def gelu_both(x):
    root = 0.7978845608028654
    square = x * x
    bent = jnp.tanh(root * x * (1.0 + 0.044715 * square))
    half = 0.5 * (1.0 + bent)
    slope = half + 0.5 * x * (1.0 - bent * bent) * (root * (1.0 + 3 * 0.044715 * square))
    return x * half, slope


def feed_forward(cid, tokens, context, out_w, cotangent, lines, grad_parts, grad_own, shr_own, exp_w, e_bias):
    seq_n, img_n = lax.axis_size("seq"), lax.axis_size("img")
    outer = seq_n // 2
    rows, width = tokens.shape
    hid_l = exp_w.shape[1]
    ready, later = len(grad_parts), len(grad_own)
    images = ready + later
    g_chunks, g_size, _ = grad_own[0].shape
    chunks, size = images * g_chunks, g_size
    rows_p = rows // images
    w_chunks, w_size, _ = shr_own.shape
    hid_o = w_chunks * w_size
    tile = 256
    blocks_per_tile = tile // hid_o
    session = Session([], two_level("seq", seq_n) + two_level("img", img_n))

    def kernel(tok_ref, ctx_ref, ow_ref, dy_ref, line_ref, *refs):
        df_refs = refs[:images]
        shr_ref, exp_ref, eb_ref = refs[images : images + 3]
        mid_out, dmid_ref, do_ref, dout_ref, sum_ref, dshr_own, f_out, dexp_out, expb_ref = refs[images + 3 : images + 12]
        x_ref, dh2_ref, attn, da, mid_ref, f_ref, dexp_ref, out_sem = refs[images + 12 : images + 20]
        h2, df, shr, act, slope, dshr, dh2, df_sem, hs, hr, ss, sr, sk, shr_low, *more = refs[images + 20 :]
        stores = [
            pltpu.make_async_copy(src, dst, out_sem.at[n])
            for n, (src, dst) in enumerate(((mid_ref, mid_out), (f_ref, f_out), (dexp_ref, dexp_out)))
        ]
        shr_low[...] = shr_ref[...].astype(bf16)
        df_in = [
            gather_ops("seq", True, df_refs[ready + g], df.at[:, ready + g], *more[14 + 3 * g : 17 + 3 * g])
            for g in range(later)
        ]
        session.greet()
        h2_in = gather_ops("seq", True, x_ref, h2, None, hs, hr)
        shr_in = gather_ops("img", False, shr_low, shr, sk, ss, sr)
        dh2_out = scatter_ops("seq", True, dh2, dh2_ref, *more[:7])
        dshr_out = scatter_ops("img", False, dshr, dshr_own, *more[7:14])
        shr_in.start()

        def columns(t):
            return lanes(t * tile, tile)

        def project(t):
            part = dot(ctx_ref[...], ow_ref[:, columns(t)], ((1,), (0,)))
            attn[:, columns(t)] = part + line_ref[0, 3:4, columns(t)]

        each(0, width // tile, project)
        def middle(g):
            here = some_rows(g * rows_p, rows_p)
            mid = tok_ref[here].astype(f32) + line_ref[g, 0:1] * attn[here]
            mid_ref[here] = mid
            normed, _ = centre(mid)
            low = (normed * line_ref[g, 1:2] + line_ref[g, 2:3]).astype(bf16)
            x_ref[pl.ds(g * g_chunks, g_chunks)] = low.reshape(g_chunks, g_size, width)

        each(0, images, middle)
        stores[0].start()
        h2_in.start()
        for ops in df_in:
            ops.start()
        loads = [pltpu.make_async_copy(ref, df.at[:, g], df_sem.at[g]) for g, ref in enumerate(df_refs[:ready])]
        for load in loads:
            load.start()
        h2[0] = x_ref[...]
        expb_ref[...] = jnp.zeros_like(expb_ref)

        def expand(j):
            def run(t):
                u = dot(h2[j].reshape(rows, width), exp_ref[:, columns(t)], ((1,), (0,))) + eb_ref[:, columns(t)]
                value, grad = gelu_both(u)
                act[j, :, columns(t)] = value.astype(bf16)
                slope[j, :, columns(t)] = grad.astype(bf16)

            each(0, hid_l // tile, run)

        def back_act(j):
            def run(t):
                weight = shr[pl.ds(t * blocks_per_tile, blocks_per_tile)].reshape(tile, width)
                grad = dot(df[j].reshape(rows, width), weight, ((1,), (1,)))
                grad = (slope[j, :, columns(t)].astype(f32) * grad).astype(bf16)
                slope[j, :, columns(t)] = grad
                expb_ref[:, columns(t)] += jnp.sum(grad.astype(f32), axis=0, keepdims=True)

            each(0, hid_l // tile, run)

        def back_input(j):
            def run(t):
                weight = exp_ref[pl.ds(pl.multiple_of(t * tile, tile), tile), :]
                part = dot(slope[j], weight, ((1,), (1,)))
                dh2[j, :, :, columns(t)] = part.astype(bf16).reshape(chunks, size, tile)

            each(0, width // tile, run)

        def shrink(j):
            def run(t):
                weight = shr[:, :, :, columns(t)].reshape(hid_l, tile)
                part = dot(act[j], weight, ((1,), (0,)))
                f_ref[j, :, :, columns(t)] = part.astype(bf16).reshape(chunks, size, tile)

            each(0, width // tile, run)

        def shrink_grad(t):
            left = act[:, :, columns(t)].reshape(seq_n * rows, tile)
            part = dot(left, df[...].reshape(seq_n * rows, width), ((0,), (0,)))
            part = part.astype(bf16).reshape(blocks_per_tile, w_chunks, w_size, width)
            dshr[pl.ds(t * blocks_per_tile, blocks_per_tile)] = part

        def expand_grad(t):
            left = h2[:, :, :, columns(t)].reshape(seq_n * rows, tile)
            part = dot(left, slope[...].reshape(seq_n * rows, hid_l), ((0,), (0,)))
            dexp_ref[pl.ds(pl.multiple_of(t * tile, tile), tile), :] = part.astype(bf16)

        expand(0)
        h2_in.near()
        expand(1)
        half = chunks // 2
        each(0, half, h2_in.step)
        each(0, w_chunks // 2, shr_in.step)
        each(half, chunks, h2_in.step)
        for o in range(1, outer):
            expand(2 * o)
        each(w_chunks // 2, w_chunks, shr_in.step)
        for ops in df_in:
            each(0, g_chunks, ops.step)
        for o in range(1, outer):
            h2_in.handed(o)
            expand(2 * o + 1)
        for ops in df_in:
            ops.finish()
        for load in loads:
            load.wait()
        each(0, hid_l // tile, shrink_grad)
        shr_in.near()
        for o in range(1, img_n // 2):
            shr_in.handed(o)
        shr_in.sent()
        dshr_out.start()
        for o in range(1, outer):
            for j in (2 * o + 1, 2 * o):
                back_act(j)
                back_input(j)
        def dshr_steps(k):
            each((k * w_chunks) // 4, ((k + 1) * w_chunks) // 4, dshr_out.step)

        dh2_out.start_outer()
        dshr_steps(0)
        each(0, chunks, dh2_out.step)
        back_act(1)
        dshr_steps(1)
        back_input(1)
        back_act(0)
        dshr_steps(2)
        back_input(0)
        dh2_out.start_inner()
        shrink(0)
        dshr_steps(3)
        h2_in.sent()
        for j in range(1, seq_n):
            shrink(j)
        stores[1].start()
        each(0, width // tile, expand_grad)
        stores[2].start()
        dh2_out.finish()
        sum_ref[...] = jnp.zeros_like(sum_ref)
        def middle_back(g):
            here = some_rows(g * rows_p, rows_p)
            grad = dh2_ref[pl.ds(g * g_chunks, g_chunks)].reshape(rows_p, width)
            normed, factor = centre(mid_ref[here])
            back = centre_back(normed, factor, grad * line_ref[g, 1:2])
            back = dy_ref[here].astype(f32) + back
            dmid_ref[here] = back
            low = (back * line_ref[g, 0:1]).astype(bf16)
            da[here] = low
            sum_ref[g, 0:1] = jnp.sum(grad * normed, axis=0, keepdims=True)
            sum_ref[g, 1:2] = jnp.sum(grad, axis=0, keepdims=True)
            sum_ref[g, 2:3] = jnp.sum(back * attn[here], axis=0, keepdims=True)
            sum_ref[g, 3:4] = jnp.sum(low.astype(f32), axis=0, keepdims=True)

        each(0, images, middle_back)

        def context_grad(t):
            weight = ow_ref[pl.ds(pl.multiple_of(t * tile, tile), tile), :]
            do_ref[:, columns(t)] = dot(da[...], weight, ((1,), (1,))).astype(bf16)

        def out_grad(t):
            part = dot(ctx_ref[:, columns(t)], da[...], ((0,), (0,)))
            dout_ref[pl.ds(pl.multiple_of(t * tile, tile), tile), :] = part.astype(bf16)

        each(0, width // tile, context_grad)
        each(0, width // tile, out_grad)
        dshr_out.finish()
        for store in stores:
            store.wait()

    full = pl.BlockSpec(memory_space=VM)
    any_space = pl.BlockSpec(memory_space=pl.ANY)
    seq_sems = pltpu.SemaphoreType.DMA((seq_n, chunks))
    img_sems = pltpu.SemaphoreType.DMA((img_n, w_chunks))
    grad_sems = pltpu.SemaphoreType.DMA((seq_n, g_chunks))
    return pl.pallas_call(
        kernel,
        out_shape=(
            jax.ShapeDtypeStruct((rows, width), f32),
            jax.ShapeDtypeStruct((rows, width), f32),
            jax.ShapeDtypeStruct((rows, width), bf16),
            jax.ShapeDtypeStruct((width, width), bf16),
            jax.ShapeDtypeStruct((images, 8, width), f32),
            jax.ShapeDtypeStruct(shr_own.shape, f32),
            jax.ShapeDtypeStruct((seq_n, chunks, size, width), bf16),
            jax.ShapeDtypeStruct(exp_w.shape, bf16),
            jax.ShapeDtypeStruct((1, hid_l), f32),
        ),
        in_specs=[full] * 5 + [any_space] * ready + [full] * (later + 3),
        out_specs=(any_space,) + (full,) * 5 + (any_space,) * 2 + (full,),
        scratch_shapes=[
            VM((chunks, size, width), bf16),
            VM((chunks, size, width), f32),
            VM((rows, width), f32),
            VM((rows, width), bf16),
            VM((rows, width), f32),
            VM((seq_n, chunks, size, width), bf16),
            VM(exp_w.shape, bf16),
            pltpu.SemaphoreType.DMA((3,)),
            VM((seq_n, chunks, size, width), bf16),
            VM((seq_n, images, g_chunks, g_size, width), bf16),
            VM((img_n,) + shr_own.shape, bf16),
            VM((seq_n, rows, hid_l), bf16),
            VM((seq_n, rows, hid_l), bf16),
            VM((img_n,) + shr_own.shape, bf16),
            VM((seq_n, chunks, size, width), bf16),
            pltpu.SemaphoreType.DMA((max(ready, 1),)),
            seq_sems,
            seq_sems,
            img_sems,
            img_sems,
            pltpu.SemaphoreType.DMA((w_chunks,)),
            VM(shr_own.shape, bf16),
        ]
        + scatter_scratch(seq_n, (chunks, size, width), bf16)
        + scatter_scratch(img_n, shr_own.shape, bf16)
        + [pltpu.SemaphoreType.DMA((g_chunks,)), grad_sems, grad_sems] * later,
        compiler_params=params(cid),
        name="feed_forward",
    )(tokens, context, out_w, cotangent, lines, *grad_parts, *grad_own, shr_own, exp_w, e_bias)


def normalize(values):
    centered = values - jnp.mean(values, axis=-1, keepdims=True)
    return centered * lax.rsqrt(jnp.mean(centered * centered, axis=-1, keepdims=True) + 1e-06)


def pad_to(x, size, axis):
    widths = [(0, 0)] * x.ndim
    widths[axis] = (0, size - x.shape[axis])
    return jnp.pad(x, widths)


def mm(a, b):
    return jnp.dot(a, b, preferred_element_type=f32)


def mm_nt(a, b):
    return lax.dot_general(a, b, (((1,), (1,)), ((), ())), preferred_element_type=f32)


def mm_tn(a, b):
    return lax.dot_general(a, b, (((0,), (0,)), ((), ())), preferred_element_type=f32)


def body(
    tokens,
    cotangent,
    condition,
    scale_sizes,
    mod_weight,
    mod_bias,
    attn_weight,
    query_bias,
    value_bias,
    out_weight,
    out_bias,
    expand_weight,
    expand_bias,
    shrink_weight,
    shrink_bias,
    log_scale,
):
    images, rows, width = tokens.shape
    heads = log_scale.shape[0]
    headdim = width // heads
    seq_n = lax.axis_size("seq")
    img_n = lax.axis_size("img")
    seq_i = lax.axis_index("seq")
    img_i = lax.axis_index("img")
    rank = img_i * seq_n + seq_i
    ranks = img_n * seq_n
    own = width // ranks
    rows_p = -(-rows // 16) * 16
    dim_l = width // seq_n
    pairs = dim_l // 128
    hidden = expand_bias.shape[0] * ranks
    hid_l = hidden // seq_n
    hid_o = hidden // ranks
    mods = mod_weight.shape[1]
    mod_o = mods // ranks

    mod_l = mods // seq_n
    blk = own * seq_n

    weights = (mod_weight, attn_weight, expand_weight)
    if own % 16 or hid_o % 128:
        attn_cut = (
            attn_weight.astype(bf16)
            .reshape(own, 3, seq_n, pairs, 128)
            .transpose(2, 0, 3, 1, 4)
            .reshape(seq_n, own, 3 * dim_l)
        )
        exp_cut = (
            expand_weight.astype(bf16)
            .reshape(own, img_n, seq_n, hid_o)
            .transpose(2, 0, 1, 3)
            .reshape(seq_n, own, hid_l)
        )
        mod_cut = mod_weight.astype(bf16).reshape(own, seq_n, mod_l).transpose(1, 0, 2)
        weights = (mod_cut, attn_cut, exp_cut)
    silu_cond = jax.nn.silu(condition).astype(bf16).astype(f32)
    small_bias = jnp.concatenate([query_bias, value_bias, out_bias, shrink_bias, expand_bias, mod_bias])
    small_bias = lax.reduce_precision(small_bias, 8, 7)
    bias_n = small_bias.shape[0]
    bias_rows = -(-bias_n // 1024) * 8
    small_bias = pad_to(small_bias, bias_rows * 128, 0).reshape(1, bias_rows, 128)
    cond_cut = silu_cond.reshape(images, img_n, seq_n, own).transpose(1, 2, 0, 3).reshape(img_n, seq_n * images, own)
    small = jnp.concatenate(
        [pad_to(cond_cut, 128, 2), jnp.broadcast_to(small_bias, (img_n, bias_rows, 128))], axis=1
    )
    early = seq_n // 4 if own % 16 == 0 else 0
    mod_all, bias_all, cond_rows, modw_cut, attn_b, exp_b, attn_early, out_img = opening(
        1, *weights, out_weight, small, seq_n, images, pairs, early
    )
    out_img = out_img.reshape(img_n, own, width)
    if early:
        attn_b = attn_b[early:]
    exp_b = exp_b.reshape(blk, hid_l)

    def weight_chunks(x):
        step = blk // 8 if blk % 128 == 0 else blk // 4
        return x.reshape(x.shape[:-2] + (blk // step, step, x.shape[-1]))

    def hidden_chunks(x):
        step = 16
        return x.reshape(x.shape[:-2] + (hid_o // step, step, x.shape[-1]))

    tiles = mod_l // 128
    modulation = mod_all[:, : tiles * images].reshape(seq_n, tiles, images, 128).transpose(2, 0, 1, 3)
    bias_all = bias_all.reshape(seq_n, img_n, bias_rows * 128)[:, :, :bias_n].transpose(1, 0, 2)
    q_bias = bias_all[:, :, :own].reshape(width)
    v_bias = bias_all[:, :, own : 2 * own].reshape(width)
    o_bias = bias_all[:, :, 2 * own : 3 * own].reshape(width)
    s_bias = bias_all[:, :, 3 * own : 4 * own].reshape(width)
    e_bias = bias_all[:, :, 4 * own : 4 * own + hid_o]
    e_bias = lax.dynamic_slice_in_dim(e_bias, seq_i, 1, 1).reshape(hid_l)
    m_bias = bias_all[:, :, 4 * own + hid_o :].reshape(mods)
    modulation = modulation.reshape(images, mods) + m_bias[None]
    qb_l = lax.dynamic_slice_in_dim(q_bias, seq_i * dim_l, dim_l, 0).reshape(pairs, 1, 128)
    vb_l = lax.dynamic_slice_in_dim(v_bias, seq_i * dim_l, dim_l, 0).reshape(pairs, 1, 128)
    pair_bias = jnp.concatenate([qb_l, jnp.zeros_like(qb_l), vb_l], axis=2)
    head_scale = jnp.exp(jnp.repeat(log_scale, headdim))
    pair_scale = lax.dynamic_slice_in_dim(head_scale, seq_i * dim_l, dim_l, 0).reshape(pairs, 1, 128)
    gain_attn, gain_mlp, scale_attn, scale_mlp, shift_attn, shift_mlp = jnp.split(
        modulation[:, None, :], 6, axis=-1
    )

    scales = jnp.arange(scale_sizes.shape[1])
    ends = jnp.sum(jnp.where(scales[:, None] <= scales[None], scale_sizes[:, :, None], 0), axis=1)
    offset = jnp.arange(rows_p, dtype=jnp.int32)
    place = (seq_i ^ jnp.arange(seq_n, dtype=jnp.int32))[:, None] * rows + offset[None]
    sid = jnp.sum((place[None, :, :, None] >= ends[:, None, None, :]).astype(jnp.int32), axis=-1)
    sid = jnp.where(offset[None, None] < rows, sid, 1 << 20)
    sid_q = sid.reshape(images, 1, seq_n * rows_p)
    sid_k = sid[..., None]

    tokens_low = pad_to(tokens, rows_p, 1)
    grad_low = pad_to(cotangent, rows_p, 1)
    resid_in = tokens_low.astype(f32)
    grad_out = grad_low.astype(f32)
    local = images * rows_p

    def chunked(x):
        return x.reshape(x.shape[: x.ndim - 3] + (local // 16, 16, width))

    normed_in = normalize(resid_in)
    attn_input = (normed_in * (1.0 + scale_attn) + shift_attn).astype(bf16)
    grad_shrunk = (grad_out * gain_mlp).astype(bf16)
    grad_chunks = grad_shrunk.reshape(images, rows_p // 16, 16, width)
    ready = images // 2
    context_low, packed, h1, attn_w, *gathered = attend(
        5,
        chunked(attn_input),
        attn_b if early else weight_chunks(attn_b.reshape(blk, 3 * dim_l)),
        attn_early,
        early,
        pair_bias,
        pair_scale,
        sid_k,
        sid_q,
        out_img,
        weight_chunks(exp_b),
        [grad_chunks[g] for g in range(ready)],
    )
    df_ready, out_w, exp_w = gathered[:ready], gathered[ready], gathered[ready + 1]
    context_low = context_low.reshape(local, width)
    out_w = out_w.reshape(width, width)
    exp_w = exp_w.reshape(width, hid_l)
    shrb_part = jnp.sum(grad_shrunk.astype(f32), axis=(0, 1))
    lines = [gain_attn, 1.0 + scale_mlp, shift_mlp, jnp.broadcast_to(o_bias, (images, 1, width))]
    lines = jnp.concatenate(lines + [jnp.zeros((images, 4, width), f32)], axis=1)
    resid_mid, grad_mid, grad_context, outw_part, mid_sums, shrw_own, shrunk_part, expw_part, expb_part = feed_forward(
        7,
        tokens_low.reshape(local, width),
        context_low,
        out_w,
        grad_low.reshape(local, width),
        lines,
        df_ready,
        [grad_chunks[g] for g in range(ready, images)],
        hidden_chunks(shrink_weight),
        exp_w,
        e_bias.reshape(1, hid_l),
    )
    resid_mid = resid_mid.reshape(images, rows_p, width)
    grad_mid = grad_mid.reshape(images, rows_p, width)
    grad_context = grad_context.reshape(images, rows_p, width)
    outw_part = outw_part.reshape(img_n, seq_n, own, width)
    grad_scale_mlp, grad_shift_mlp, grad_gain_attn = mid_sums[:, 0], mid_sums[:, 1], mid_sums[:, 2]
    outb_part = jnp.sum(mid_sums[:, 3], axis=0)
    shrw_own = shrw_own.reshape(hid_o, width)
    expb_part = expb_part.reshape(hid_l)
    expw_part = expw_part.reshape(img_n, blk, hid_l)

    lines = [1.0 + scale_attn, gain_mlp, jnp.broadcast_to(s_bias, (images, 1, width))]
    lines = jnp.concatenate(lines + [jnp.zeros((images, 5, width), f32)], axis=1)
    sums, row_sums, layer_out, token_grad, attnw_blk, expw_blk, outw_own = attend_back(
        11,
        packed,
        h1,
        attn_w,
        grad_context,
        pair_bias,
        pair_scale,
        sid_k,
        sid_q,
        weight_chunks(expw_part),
        shrunk_part,
        outw_part,
        resid_mid,
        grad_mid,
        tokens_low,
        grad_low,
        lines,
    )
    grad_scale_attn, grad_shift_attn, grad_gain_mlp = row_sums[:, 0], row_sums[:, 1], row_sums[:, 2]
    sums = jnp.sum(sums.reshape(images, pairs, 8, 128), axis=0)
    qb_part = sums[:, 0].reshape(dim_l)
    vb_part = sums[:, 1].reshape(dim_l)
    logs_part = jnp.sum(sums[:, 2].reshape(dim_l // headdim, headdim), axis=1)
    outw_own = outw_own.reshape(own, width)

    grad_mod = jnp.concatenate(
        [grad_gain_attn, grad_gain_mlp, grad_scale_attn, grad_scale_mlp, grad_shift_attn, grad_shift_mlp],
        axis=-1,
    )
    grad_mod = grad_mod.reshape(images, seq_n, tiles, 128).transpose(1, 2, 0, 3).reshape(seq_n, tiles * images, 128)
    grad_mod = pad_to(grad_mod, -(-tiles * images // 8) * 8, 1)

    def lined(vector, count):
        return pad_to(vector.reshape(count, -1), 128, 1)

    heads_l = heads // seq_n
    logs_row = lax.dynamic_update_slice_in_dim(jnp.zeros((128,), f32), logs_part, seq_i * heads_l, 0)
    bias_mine = jnp.concatenate(
        [
            lined(shrb_part, img_n),
            lined(outb_part, img_n),
            pad_to(logs_row[None], 8, 0),
            lined(qb_part, img_n // seq_n),
            lined(vb_part, img_n // seq_n),
        ]
    )
    bias_mine = pad_to(bias_mine, -(-bias_mine.shape[0] // 8) * 8, 0)
    mine = jnp.concatenate([grad_mod, jnp.broadcast_to(bias_mine[None], (seq_n,) + bias_mine.shape)], axis=1)
    modw_own, attnw_own, expw_own, bias_own, modb_all, cond_sum = closing(
        13,
        mine,
        lined(expb_part, img_n),
        cond_rows,
        modw_cut,
        attnw_blk.reshape(seq_n, own, 3 * dim_l),
        expw_blk.reshape(seq_n, own, hid_l),
        images,
        pairs,
    )

    modw_own, attnw_own, expw_own, outw_own, shrw_own, shrb_own, outb_own, qb_own, vb_own, expb_own, logs_total = finishing(
        modw_own, attnw_own, expw_own, bias_own, outw_own, shrw_own, heads
    )
    modb_own = lax.dynamic_slice_in_dim(modb_all[:, :tiles].reshape(mods), rank * mod_o, mod_o, 0)
    grad_silu = cond_sum[:, :, :own].reshape(img_n, seq_n, images, own).transpose(2, 0, 1, 3).reshape(images, width)
    cond_grad = jax.vjp(jax.nn.silu, condition)[1](grad_silu)[0]
    return (
        layer_out[:, :rows],
        token_grad[:, :rows],
        cond_grad,
        modw_own,
        modb_own,
        attnw_own,
        qb_own,
        vb_own,
        outw_own,
        outb_own,
        expw_own,
        expb_own,
        shrw_own,
        shrb_own,
        logs_total,
    )


def solution(mesh):
    both = P(("img", "seq"))
    rows = P(("img", "seq"), None)
    return jax.shard_map(
        body,
        mesh=mesh,
        in_specs=(
            P("img", "seq", None),
            P("img", "seq", None),
            P("img", None),
            P("img", None),
            rows,
            both,
            rows,
            both,
            both,
            rows,
            both,
            rows,
            both,
            rows,
            both,
            P(),
        ),
        out_specs=(
            P("img", "seq", None),
            P("img", "seq", None),
            P("img", None),
            rows,
            both,
            rows,
            both,
            both,
            rows,
            both,
            rows,
            both,
            rows,
            both,
            P(),
        ),
        check_vma=False,
    )
```

```python
from types import SimpleNamespace

import jax
import jax.numpy as jnp
from jax import lax
from jax.experimental import pallas as pl
from jax.experimental.pallas import tpu as pltpu
from jax.sharding import PartitionSpec as P

HIGH = lax.Precision.HIGHEST
MESH = pl.DeviceIdType.MESH
bf16 = jnp.bfloat16
f32 = jnp.float32
VM = pltpu.VMEM
LIMIT = 62 << 20


class Plan:
    def __init__(self, ins, out, scratch, peers, count, bind, out_space=VM):
        self.ins, self.out, self.out_space = ins, out, out_space
        self.scratch, self.peers, self.count, self.bind = scratch, peers, count, bind
        self.window = None

    def during(self, low, high):
        self.window = (low, high)
        return self


def remote(src, dst, send, recv, axis, peer):
    return pltpu.make_async_remote_copy(
        src_ref=src, dst_ref=dst, send_sem=send, recv_sem=recv, device_id={axis: peer}, device_id_type=MESH
    )


def each(low, high, run):
    def once(i, carry):
        run(i)
        return carry

    lax.fori_loop(low, high, once, 0)


def direct_ops(axis, x_ref, out_ref, send, recv, everyone=False, src_rel=False, dst_rel=False):
    n = lax.axis_size(axis)
    me = lax.axis_index(axis)

    def copy(j):
        src = x_ref if everyone else x_ref.at[j if src_rel else me ^ j]
        return remote(src, out_ref.at[j if dst_rel else me], send.at[j], recv.at[j], axis, me ^ j)

    def start():
        for j in range(1, n):
            copy(j).start()
        out_ref[0 if dst_rel else me] = x_ref[...] if everyone else x_ref[0 if src_rel else me]

    def finish():
        for j in range(1, n):
            copy(j).wait()

    return start, finish


def two_level(axis, n):
    return [(axis, 1)] + [(axis, 2 * o) for o in range(1, n // 2)]


def gather_ops(axis, rel, x_ref, out_ref, own, send, recv, inside=False):
    n = lax.axis_size(axis)
    outer = n // 2
    chunks = x_ref.shape[0]
    me = lax.axis_index(axis)

    def place(sender, j, c):
        block = j if rel else sender
        return out_ref.at[c, block] if inside else out_ref.at[block, c]

    def keep(c):
        return pltpu.make_async_copy(x_ref.at[c], place(me, 0, c), own.at[c])

    def push(j, c):
        return remote(x_ref.at[c], place(me, j, c), send.at[j, c], recv.at[j, c], axis, me ^ j)

    def hand(j, c):
        far = me ^ j
        return remote(place(far, j, c), place(far, j + 1, c), send.at[j + 1, c], recv.at[j + 1, c], axis, me ^ 1)

    def start():
        def first(c):
            for o in range(1, outer):
                push(2 * o, c).start()

        def second(c):
            push(1, c).start()
            if own is not None:
                keep(c).start()

        each(0, chunks, first)
        each(0, chunks, second)

    def step(c):
        for o in range(1, outer):
            push(2 * o, c).wait_recv()
            hand(2 * o, c).start()

    def near():
        each(0, chunks, lambda c: push(1, c).wait_recv())

    def handed(o):
        each(0, chunks, lambda c: hand(2 * o, c).wait_recv())

    def sent():
        def last(c):
            for o in range(1, outer):
                push(2 * o, c).wait_send()
                hand(2 * o, c).wait_send()
            push(1, c).wait_send()
            if own is not None:
                keep(c).wait()

        each(0, chunks, last)

    def finish():
        near()
        for o in range(1, outer):
            handed(o)
        sent()

    return SimpleNamespace(start=start, step=step, near=near, handed=handed, sent=sent, finish=finish)


def gather(x, axis, rel, inside=False):
    n = lax.axis_size(axis)
    chunks = x.shape[0]

    def bind(x_ref, out_ref, own, send, recv):
        return gather_ops(axis, rel, x_ref, out_ref, own, send, recv, inside)

    sems = pltpu.SemaphoreType.DMA((n, chunks))
    shape = (chunks, n) + x.shape[1:] if inside else (n,) + x.shape
    out = jax.ShapeDtypeStruct(shape, x.dtype)
    scratch = [pltpu.SemaphoreType.DMA((chunks,)), sems, sems]
    return Plan([x], out, scratch, two_level(axis, n), chunks, bind, pl.ANY)


def scatter_ops(axis, rel, x_ref, out_ref, near_buf, send_buf, far_buf, s1, r1, s2, r2, inside=False, held=None):
    n = lax.axis_size(axis)
    outer = n // 2
    chunks = out_ref.shape[0]
    me = lax.axis_index(axis)

    def part(j, c, ref=x_ref):
        block = j if rel else me ^ j
        return ref.at[c, block] if inside else ref.at[block, c]

    def mine(j, c):
        return part(j, c, x_ref if held is None else held)[...].astype(f32)

    def near(o, c):
        return remote(part(2 * o + 1, c), near_buf.at[o, c], s1.at[o, c], r1.at[o, c], axis, me ^ 1)

    def far(o, c):
        return remote(send_buf.at[o, c], far_buf.at[o, c], s2.at[o, c], r2.at[o, c], axis, me ^ (2 * o))

    def start_outer():
        def first(c):
            for o in range(1, outer):
                near(o, c).start()

        each(0, chunks, first)

    def start_inner():
        each(0, chunks, lambda c: near(0, c).start())

    def start():
        start_outer()
        start_inner()

    def step_one(o, c):
        near(o, c).wait_recv()
        total = mine(2 * o, c) + near_buf[o, c].astype(f32)
        send_buf[o, c] = total.astype(send_buf.dtype)
        far(o, c).start()

    def step(c):
        for o in range(1, outer):
            step_one(o, c)

    def start_one(o):
        each(0, chunks, lambda c: near(o, c).start())

    def by_blocks(per_tile, make):
        order = []
        for k in reversed(range(n // per_tile)):
            outers = [o for o in range(1, outer) if (2 * o + 1) // per_tile == k]

            def one(k=k, outers=outers):
                make((me // per_tile) ^ k)
                for o in outers:
                    start_one(o)
                if k == 0:
                    start_inner()

            if k:
                one()
            order += outers
        halves = []
        for o in order:
            for low, high in ((0, (chunks + 1) // 2), ((chunks + 1) // 2, chunks)):
                halves.append(lambda o=o, low=low, high=high: each(low, high, lambda c: step_one(o, c)))
        return one, halves

    def finish():
        def last(c):
            near(0, c).wait_recv()
            total = mine(0, c) + near_buf[0, c].astype(f32)
            for o in range(1, outer):
                far(o, c).wait_recv()
                total = total + far_buf[o, c].astype(f32)
            out_ref[c] = total.astype(out_ref.dtype)
            for o in range(outer):
                near(o, c).wait_send()
            for o in range(1, outer):
                far(o, c).wait_send()

        each(0, chunks, last)

    return SimpleNamespace(
        start=start,
        start_outer=start_outer,
        start_inner=start_inner,
        step=step,
        finish=finish,
        by_blocks=by_blocks,
    )


def in_turns(halves, turns):
    taken = [0, 0]

    def take():
        taken[1] += 1
        upto = -(-len(halves) * taken[1] // turns)
        for half in halves[taken[0] : upto]:
            half()
        taken[0] = upto

    return take


def scatter_scratch(n, inner, dtype):
    half = VM((n // 2,) + inner, dtype)
    sems = pltpu.SemaphoreType.DMA((n // 2, inner[0]))
    return [half, half, half, sems, sems, sems, sems]


class Session:
    def __init__(self, plans, more_peers=()):
        self.plans = plans
        self.ins = [x for p in plans for x in p.ins]
        self.outs = [p.out for p in plans]
        self.in_specs = [pl.BlockSpec(memory_space=VM)] * len(self.ins)
        self.out_specs = [pl.BlockSpec(memory_space=p.out_space) for p in plans]
        self.scratch = [scr for p in plans for scr in p.scratch]
        self.peers = sorted({peer for p in plans for peer in p.peers} | set(more_peers))

    def greet(self):
        barrier = pltpu.get_barrier_semaphore()
        for axis, j in self.peers:
            pl.semaphore_signal(barrier, inc=1, device_id={axis: lax.axis_index(axis) ^ j}, device_id_type=MESH)
        pl.semaphore_wait(barrier, len(self.peers))

    def bind(self, ins, outs, scratch):
        at_in = at_scr = 0
        self.bound = []
        for p, out in zip(self.plans, outs):
            mine = ins[at_in : at_in + len(p.ins)]
            own = scratch[at_scr : at_scr + len(p.scratch)]
            self.bound.append((p.count, p.window, p.bind(*mine, out, *own)))
            at_in += len(p.ins)
            at_scr += len(p.scratch)

    def start(self):
        for _, _, ops in self.bound:
            ops.start()

    def steps(self, i, total):
        for count, window, ops in self.bound:
            low, high = window or (0, total)
            span = high - low

            def some(ops=ops, count=count, low=low, span=span):
                if count == span:
                    ops.step(i - low)
                else:
                    each(((i - low) * count) // span, ((i - low + 1) * count) // span, ops.step)

            if not count:
                continue
            if span == total:
                some()
            else:
                pl.when(jnp.logical_and(i >= low, i < high))(some)

    def finish(self):
        for _, _, ops in self.bound:
            ops.finish()


def everyone_else(*axes):
    return [(axis, j) for axis in axes for j in range(1, lax.axis_size(axis))]


def pairs_of_sems(*axes):
    return [pltpu.SemaphoreType.DMA((lax.axis_size(axis),)) for axis in axes for _ in range(2)]


def params(cid):
    return pltpu.CompilerParams(collective_id=cid, has_side_effects=True, vmem_limit_bytes=LIMIT)


def opening(cid, mod_w, attn_w, exp_w, out_w, small, seq_n, images, pairs, early):
    raw = mod_w.dtype == f32
    own, width = out_w.shape
    dim_l = pairs * 128
    img_n, rows, _ = small.shape
    cuts = [x.size // (seq_n * own) for x in (mod_w, attn_w, exp_w)]
    mod_l, _, hid_l = cuts
    hid_o = hid_l // img_n
    head = seq_n * images
    tiles = mod_l // 128
    slim = -(-tiles * images // 8) * 8
    count = max(early, 1)
    shapes = [(seq_n, own, c) for c in cuts]
    session = Session([], everyone_else("img", "seq"))

    def kernel(
        mod_in, attn_in, exp_in, out_in, small_ref,
        modo_ref, bias_ref, lhs_ref, modw_ref, attnw_ref, expw_ref, early_ref, outw_ref,
        small_all, part_buf, part_all, sum_buf, *more
    ):
        if raw:
            mod_ref, attn_ref, exp_ref, out_ref, *sems = more
            out_ref[0] = out_in[...].astype(bf16)
            for q in range(seq_n):
                mod_ref[q] = mod_in[:, q * mod_l : (q + 1) * mod_l].astype(bf16)
        else:
            mod_ref, attn_ref, exp_ref = mod_in, attn_in, exp_in
            out_ref, *sems = more
            out_ref[0] = out_in[...].astype(bf16)
        early_in = gather_ops("img", False, attnw_ref.at[:count], early_ref, *sems[14:17])
        out_go = gather_ops("img", False, out_ref, outw_ref, *sems[17:20])
        session.greet()
        small_go, small_end = direct_ops("img", small_ref, small_all, *sems[:2])
        mod_go, mod_end = direct_ops("seq", mod_ref, modw_ref, *sems[2:4])
        attn_go, attn_end = direct_ops("seq", attn_ref, attnw_ref, *sems[4:6])
        exp_go, exp_end = direct_ops("seq", exp_ref, expw_ref, *sems[12:14])
        small_go()
        mod_go()
        if raw:
            for q in range(seq_n):
                for p in range(pairs):
                    for k in range(3):
                        at = k * width + q * dim_l + p * 128
                        to = p * 384 + k * 128
                        attn_ref[q, :, to : to + 128] = attn_in[:, at : at + 128].astype(bf16)
        attn_go()
        if raw:
            for q in range(seq_n):
                for i in range(img_n):
                    at = (i * seq_n + q) * hid_o
                    exp_ref[q, :, i * hid_o : (i + 1) * hid_o] = exp_in[:, at : at + hid_o].astype(bf16)
        exp_go()
        out_go.start()
        part_buf[...] = jnp.zeros_like(part_buf)
        small_end()
        bias_go, bias_end = direct_ops("seq", small_all.at[:, head:], bias_ref, *sems[6:8], everyone=True)
        bias_go()
        for i in range(img_n):
            for q in range(seq_n):
                lhs_ref[q, i * images : (i + 1) * images] = small_all[i, q * images : (q + 1) * images]
        mod_end()
        part = jnp.zeros((img_n * images, mod_l), f32)
        for q in range(seq_n):
            part = part + dot(lhs_ref[q][:, :own].astype(bf16), modw_ref[q], ((1,), (0,)))
        for i in range(img_n):
            for t in range(tiles):
                part_buf[i, t * images : (t + 1) * images] = part[
                    i * images : (i + 1) * images, t * 128 : (t + 1) * 128
                ]
        part_go, part_end = direct_ops("img", part_buf, part_all, *sems[8:10])
        part_go()
        out_go.step(0)
        attn_end()
        if early:
            early_in.start()
        part_end()
        total = part_all[0]
        for i in range(1, img_n):
            total = total + part_all[i]
        sum_buf[...] = total
        sum_go, sum_end = direct_ops("seq", sum_buf, modo_ref, *sems[10:12], everyone=True)
        sum_go()
        if early:
            each(0, early, early_in.step)
        bias_end()
        sum_end()
        exp_end()
        out_go.finish()
        if early:
            early_in.finish()

    full = pl.BlockSpec(memory_space=VM)
    any_space = pl.BlockSpec(memory_space=pl.ANY)
    sending = [VM(x, bf16) for x in shapes] if raw else []
    return pl.pallas_call(
        kernel,
        out_shape=(
            jax.ShapeDtypeStruct((seq_n, slim, 128), f32),
            jax.ShapeDtypeStruct((seq_n, img_n, rows - head, 128), f32),
            jax.ShapeDtypeStruct((seq_n, img_n * images, 128), f32),
            *[jax.ShapeDtypeStruct(x, bf16) for x in shapes],
            jax.ShapeDtypeStruct((img_n, count) + shapes[1][1:], bf16),
            jax.ShapeDtypeStruct((img_n, 1, own, width), bf16),
        ),
        in_specs=[full] * 5,
        out_specs=(full,) * 6 + (any_space,) * 2,
        scratch_shapes=[
            VM(small.shape, f32),
            VM((img_n, slim, 128), f32),
            VM((img_n, slim, 128), f32),
            VM((slim, 128), f32),
        ]
        + sending
        + [VM((1, own, width), bf16)]
        + pairs_of_sems("img", "seq", "seq", "seq", "img", "seq", "seq")
        + [pltpu.SemaphoreType.DMA((count,))]
        + [pltpu.SemaphoreType.DMA((img_n, count))] * 2
        + [pltpu.SemaphoreType.DMA((1,))]
        + [pltpu.SemaphoreType.DMA((img_n, 1))] * 2,
        compiler_params=params(cid),
        name="opening",
    )(mod_w, attn_w, exp_w, out_w, small)


def finishing(modw, attnw, expw, bias, outw, shrw, heads):
    own, width = outw.shape
    hid_o = shrw.shape[0]

    def kernel(modw_ref, attnw_ref, expw_ref, bias_ref, outw_ref, shrw_ref, *outs):
        for src, out in zip((modw_ref, attnw_ref, expw_ref, outw_ref, shrw_ref), outs):
            out[...] = src[...].astype(f32)
        shift = (128 - lax.axis_index("seq") * own) % 128
        rolled = pltpu.roll(bias_ref[...], shift, 1)
        for row in range(4):
            outs[5 + row][...] = rolled[row : row + 1, :own]
        outs[9][...] = bias_ref[4:5, :hid_o]
        outs[10][...] = bias_ref[5:6, :heads]

    full = pl.BlockSpec(memory_space=VM)
    shapes = [modw.shape, attnw.shape, expw.shape, outw.shape, shrw.shape] + [(1, own)] * 4 + [(1, hid_o), (1, heads)]
    got = pl.pallas_call(
        kernel,
        out_shape=tuple(jax.ShapeDtypeStruct(x, f32) for x in shapes),
        in_specs=[full] * 6,
        out_specs=(full,) * len(shapes),
        compiler_params=pltpu.CompilerParams(vmem_limit_bytes=LIMIT),
        name="finishing",
    )(modw, attnw, expw, bias, outw, shrw)
    return list(got[:5]) + [x.reshape(-1) for x in got[5:]]


def closing(cid, mine, expb, lhs, modw, attn_back, exp_back, images, pairs):
    seq_n, own, mod_l = modw.shape
    img_n = expb.shape[0]
    rows = mine.shape[1]
    head = seq_n * images
    tiles = mod_l // 128
    slim = -(-tiles * images // 8) * 8
    share = img_n // seq_n
    dim_l = pairs * 128
    width = dim_l * seq_n
    hid_l = exp_back.shape[2]
    hid_o = hid_l // img_n
    aligned = hid_o % 128 == 0
    flat = -(-tiles // 8) * 8

    def kernel(
        mine_ref, expb_ref, lhs_ref, modw_ref, attn_ref, exp_ref,
        modw_own, attn_own, exp_own, bias_ref, modb_ref, cond_ref,
        seen, block, got, dd, mw_send, mw_recv, mb_send, gs_send, gs_all, gs_seen, attn_all, exp_all, *sems
    ):
        barrier = Session([], everyone_else("img", "seq"))
        barrier.greet()
        mine_go, mine_end = direct_ops("seq", mine_ref, seen, *sems[:2])
        attn_go, attn_end = direct_ops("seq", attn_ref, attn_all, *sems[2:4])
        exp_go, exp_end = direct_ops("seq", exp_ref, exp_all, *sems[14:16])
        mine_go()
        attn_go()
        exp_go()
        block[...] = jnp.zeros_like(block)
        gs_send[...] = jnp.zeros_like(gs_send)
        mb_send[...] = jnp.zeros_like(mb_send)
        mine_end()
        total = seen[0]
        for q in range(1, seq_n):
            total = total + seen[q]
        at = slim + 2 * img_n
        for i in range(img_n):
            block[i, :slim] = total[:slim]
            block[i, slim : slim + 1] = total[slim + i : slim + i + 1]
            block[i, slim + 1 : slim + 2] = total[slim + img_n + i : slim + img_n + i + 1]
            row = at + 8 + i % share
            block[i, slim + 2 : slim + 3] = seen[i // share, row : row + 1]
            block[i, slim + 3 : slim + 4] = seen[i // share, row + share : row + share + 1]
            block[i, slim + 4 : slim + 5] = expb_ref[i : i + 1]
            block[i, slim + 5 : slim + 6] = total[at : at + 1]
        img_go, img_end = direct_ops("img", block, got, *sems[4:6])
        img_go()
        attn_end()
        exp_end()
        for q in range(seq_n):
            for p in range(pairs):
                for k in range(3):
                    to = k * width + q * dim_l + p * 128
                    at_c = p * 384 + k * 128
                    attn_own[:, to : to + 128] = attn_all[q, :, at_c : at_c + 128]
            if aligned:
                for i in range(img_n):
                    to = (i * seq_n + q) * hid_o
                    exp_own[:, to : to + hid_o] = exp_all[q, :, i * hid_o : (i + 1) * hid_o]
            else:
                exp_own[:, q * hid_l : (q + 1) * hid_l] = exp_all[q]
        img_end()
        sums = got[0]
        for i in range(1, img_n):
            sums = sums + got[i]
        bias_ref[...] = sums[slim:]
        for t in range(tiles):
            mb_send[t : t + 1] = jnp.sum(sums[t * images : (t + 1) * images], axis=0, keepdims=True)
            for i in range(img_n):
                dd[i * images : (i + 1) * images, t * 128 : (t + 1) * 128] = got[i, t * images : (t + 1) * images]
        grad = dd[...]
        high = grad.astype(bf16)
        low = (grad - high.astype(f32)).astype(bf16)
        for q in range(seq_n):
            out = dot(high, modw_ref[q], ((1,), (1,))) + dot(low, modw_ref[q], ((1,), (1,)))
            for i in range(img_n):
                gs_send[i, q * images : (q + 1) * images, :own] = out[i * images : (i + 1) * images]
        gs_go, gs_end = direct_ops("img", gs_send, gs_all, *sems[6:8])
        gs_go()
        for q in range(seq_n):
            mw_send[q] = dot(lhs_ref[q][:, :own].astype(bf16), high, ((0,), (0,))).astype(bf16)
        mb_go, mb_end = direct_ops("seq", mb_send, modb_ref, *sems[10:12], everyone=True)
        mb_go()
        gs_end()
        all_go, all_end = direct_ops("seq", gs_all, gs_seen, *sems[12:14], everyone=True)
        all_go()
        mw_go, mw_end = direct_ops("seq", mw_send, mw_recv, *sems[8:10])
        mw_go()
        mb_end()
        all_end()
        out = gs_seen[0]
        for q in range(1, seq_n):
            out = out + gs_seen[q]
        cond_ref[...] = out
        mw_end()
        for q in range(seq_n):
            modw_own[:, q * mod_l : (q + 1) * mod_l] = mw_recv[q]

    full = pl.BlockSpec(memory_space=VM)
    got = pl.pallas_call(
        kernel,
        out_shape=(
            jax.ShapeDtypeStruct((own, mod_l * seq_n), bf16),
            jax.ShapeDtypeStruct((own, 3 * width), bf16),
            jax.ShapeDtypeStruct((own, hid_l * seq_n), bf16),
            jax.ShapeDtypeStruct((8, 128), f32),
            jax.ShapeDtypeStruct((seq_n, flat, 128), f32),
            jax.ShapeDtypeStruct((img_n, head, 128), f32),
        ),
        in_specs=[full] * 6,
        out_specs=(full,) * 6,
        scratch_shapes=[
            VM((seq_n, rows, 128), f32),
            VM((img_n, slim + 8, 128), f32),
            VM((img_n, slim + 8, 128), f32),
            VM((img_n * images, mod_l), f32),
            VM((seq_n, own, mod_l), bf16),
            VM((seq_n, own, mod_l), bf16),
            VM((flat, 128), f32),
            VM((img_n, head, 128), f32),
            VM((img_n, head, 128), f32),
            VM((seq_n, img_n, head, 128), f32),
            VM(attn_back.shape, bf16),
            VM(exp_back.shape, bf16),
        ]
        + pairs_of_sems("seq", "seq", "img", "img", "seq", "seq", "seq", "seq"),
        compiler_params=params(cid),
        name="closing",
    )(mine, expb, lhs, modw, attn_back, exp_back)
    got = list(got)
    if not aligned:
        got[2] = got[2].reshape(own, seq_n, img_n, hid_o).transpose(0, 2, 1, 3).reshape(own, hid_l * seq_n)
    return got


def half_sums(values, low_half):
    first = jnp.sum(jnp.where(low_half, values, 0.0), axis=-1, keepdims=True)
    second = jnp.sum(jnp.where(low_half, 0.0, values), axis=-1, keepdims=True)
    return jnp.where(low_half, first, second)


def dot(a, b, dims):
    return lax.dot_general(a, b, (dims, ((), ())), preferred_element_type=f32)


def lanes(start, size):
    return pl.ds(pl.multiple_of(start, 128), size)


def load_heads(p_ref, bias, g, p, rows):
    both = p_ref[:, g, :, lanes(p * 384, 384)].reshape(rows, 384)
    query = both[:, :128] + bias[:, :128]
    key = both[:, 128:256]
    value = both[:, 256:] + bias[:, 256:]
    low_half = lax.broadcasted_iota(jnp.int32, (rows, 128), 1) < 64
    r_query = lax.rsqrt(half_sums(query * query, low_half) + 1e-06)
    r_key = lax.rsqrt(half_sums(key * key, low_half) + 1e-06)
    return query, key, value, low_half, r_query, r_key


def some_rows(start, size):
    return pl.ds(pl.multiple_of(start, 16), size)


def centre(v):
    centered = v - jnp.mean(v, axis=-1, keepdims=True)
    factor = lax.rsqrt(jnp.mean(centered * centered, axis=-1, keepdims=True) + 1e-06)
    return centered * factor, factor


def centre_back(normed, factor, grad):
    return factor * (grad - jnp.mean(grad, axis=-1, keepdims=True) - normed * jnp.mean(grad * normed, axis=-1, keepdims=True))


def attend(cid, attn_input, attn_own, attn_early, early, bias, scale, sid_k, sid_q, out_img, exp_own, grad_own):
    seq_n, img_n = lax.axis_size("seq"), lax.axis_size("img")
    outer = seq_n // 2
    chunks, size, width = attn_input.shape
    local = chunks * size
    images = sid_q.shape[0]
    rows_b = local // images
    rows = seq_n * rows_b
    wide = attn_own.shape[2]
    pairs = wide // 384
    turns = images * pairs
    tile = 256 if wide % 256 == 0 else 128
    w_chunks = attn_own.shape[0] - early
    plans = [gather(x, "seq", True) for x in grad_own] + [gather(out_img, "seq", False, True), gather(exp_own, "img", False)]
    session = Session(plans, everyone_else("seq") + two_level("img", img_n))
    ins, outs = 7 + len(session.ins), 4 + len(plans)
    weight = (img_n,) + attn_own.shape

    def kernel(*refs):
        x_ref, w_ref, early_ref, b_ref, es_ref, sk_ref, sq_ref = refs[:7]
        o_ref, p_out, h_out, w_out = refs[ins : ins + 4]
        scratch = refs[ins + outs :]
        h1, attn_w, packed, o_buf, o_send, o_recv, hs, hr, wk, ws, wr, out_sem, early_sem = scratch[:13]
        me = lax.axis_index("seq")
        session.greet()
        session.bind(refs[7:ins], refs[ins + 4 : ins + outs], scratch[13:])
        h1_in = gather_ops("seq", True, x_ref, h1, None, hs, hr)
        w_in = gather_ops("img", False, w_ref.at[early:], attn_w.at[:, early:], wk, ws, wr)
        if early:
            load = pltpu.make_async_copy(early_ref, attn_w.at[:, :early], early_sem.at[0])
            load.start()
        h1_in.start()
        w_in.start()
        session.start()
        *grads, (out_count, _, out_in), (exp_count, _, exp_in) = session.bound
        h1[0] = x_ref[...]

        def ship(i, j):
            g, p = i // pairs, i % pairs
            return remote(
                o_buf.at[i, j],
                o_ref.at[g, :, lanes((me * pairs + p) * 128, 128)],
                o_send.at[j, i],
                o_recv.at[j, i],
                "seq",
                me ^ j,
            )

        each(0, chunks // 2, h1_in.step)
        each(0, w_chunks // 2, w_in.step)
        each(chunks // 2, chunks, h1_in.step)
        each(w_chunks // 2, w_chunks, w_in.step)
        h1_in.near()
        for o in range(1, outer):
            h1_in.handed(o)
        w_in.near()
        for o in range(1, img_n // 2):
            w_in.handed(o)
        w_in.sent()
        if early:
            load.wait()
        quarter = exp_count // 4
        each(0, quarter, exp_in.step)

        def project(k):
            j, t = k // (wide // tile), k % (wide // tile)
            columns = lanes(t * tile, tile)
            part = dot(h1[j].reshape(local, width), attn_w[:, :, :, columns].reshape(width, tile), ((1,), (0,)))
            packed[j, :, :, columns] = part.reshape(images, rows_b, tile)

        each(0, seq_n * (wide // tile), project)
        each(quarter, 2 * quarter, exp_in.step)
        copies = [
            pltpu.make_async_copy(src, dst, out_sem.at[n])
            for n, (src, dst) in enumerate(((packed, p_out), (h1, h_out), (attn_w, w_out)))
        ]
        for copy in copies:
            copy.start()

        def turn(i):
            g, p = i // pairs, i % pairs
            query, key, value, low_half, r_query, r_key = load_heads(packed, b_ref[p], g, p, rows)
            query_low = query * r_query * es_ref[p]
            key_t = jnp.transpose(key * r_key).astype(bf16)
            sid_k = sq_ref[g]
            masks = [low_half, jnp.logical_not(low_half)]
            queries = [jnp.where(mine, query_low, 0.0).astype(bf16) for mine in masks]
            values = [jnp.where(mine, value, 1.0).astype(bf16) for mine in masks]
            low_b = low_half[:rows_b]
            for b in range(seq_n):
                seen = sid_k <= sk_ref[g, b]
                parts = []
                for h in range(2):
                    scores = dot(queries[h][b * rows_b : (b + 1) * rows_b], key_t, ((1,), (0,)))
                    expo = jnp.where(seen, jnp.exp(scores), 0.0).astype(bf16)
                    parts.append(dot(expo, values[h], ((1,), (0,))))
                totals = jnp.where(low_b, pltpu.roll(parts[0], 64, 1), pltpu.roll(parts[1], 64, 1))
                o_buf[i, b] = (jnp.where(low_b, parts[0], parts[1]) / totals).astype(bf16)
            o_ref[g, :, lanes((me * pairs + p) * 128, 128)] = o_buf[i, 0]
            for j in range(1, seq_n):
                ship(i, j).start()

            @pl.when(i == 0)
            def _():
                for count, _, ops in grads:
                    each(0, count, ops.step)

            half = turns // 2

            @pl.when(i == half - 1)
            def _():
                each(2 * quarter, 3 * quarter, exp_in.step)

            @pl.when(i == half)
            def _():
                each(0, out_count, out_in.step)
                each(3 * quarter, exp_count, exp_in.step)

        each(0, turns, turn)
        session.finish()
        h1_in.sent()
        for copy in copies:
            copy.wait()

        def last(i):
            for j in range(1, seq_n):
                ship(i, j).wait()

        each(0, turns, last)

    full = pl.BlockSpec(memory_space=VM)
    any_space = pl.BlockSpec(memory_space=pl.ANY)
    sems = pltpu.SemaphoreType.DMA((seq_n, turns))
    seq_sems = pltpu.SemaphoreType.DMA((seq_n, chunks))
    img_sems = pltpu.SemaphoreType.DMA((img_n, w_chunks))
    packed = (seq_n, images, rows_b, wide)
    return pl.pallas_call(
        kernel,
        out_shape=tuple(
            [
                jax.ShapeDtypeStruct((images, rows_b, width), bf16),
                jax.ShapeDtypeStruct(packed, f32),
                jax.ShapeDtypeStruct((seq_n,) + attn_input.shape, bf16),
                jax.ShapeDtypeStruct(weight, bf16),
            ]
            + session.outs
        ),
        in_specs=[full] * 2 + [any_space] + [full] * 4 + session.in_specs,
        out_specs=tuple([full] + [any_space] * 3 + session.out_specs),
        scratch_shapes=[
            VM((seq_n,) + attn_input.shape, bf16),
            VM(weight, bf16),
            VM(packed, f32),
            VM((turns, seq_n, rows_b, 128), bf16),
            sems,
            sems,
            seq_sems,
            seq_sems,
            pltpu.SemaphoreType.DMA((w_chunks,)),
            img_sems,
            img_sems,
            pltpu.SemaphoreType.DMA((3,)),
            pltpu.SemaphoreType.DMA((1,)),
        ]
        + session.scratch,
        compiler_params=params(cid),
        name="attend",
    )(attn_input, attn_own, attn_early, bias, scale, sid_k, sid_q, *session.ins)


def attend_back(
    cid, packed, h1, attn_w, d_out, bias, scale, sid_k, sid_q, expw_part, shrunk_part, outw_part, mid, d_mid, tokens, cotangent, lines
):
    seq_n, images, rows_b, wide = packed.shape
    img_n = lax.axis_size("img")
    outer = seq_n // 2
    pairs = wide // 384
    rows = seq_n * rows_b
    turns = images * pairs
    _, chunks, size, width = h1.shape
    local = chunks * size
    _, w_chunks, w_size, _ = attn_w.shape
    own = outw_part.shape[2]
    tile = 256
    blocks_per_tile = tile // (w_chunks * w_size)
    pieces = -(-width // wide)
    h_chunks, f_chunks = chunks // images, shrunk_part.shape[1] // images
    session = Session([], everyone_else("seq") + two_level("img", img_n))
    mids = [
        scatter_scratch(img_n, expw_part.shape[1:], bf16),
        scatter_scratch(seq_n, shrunk_part.shape[1:], bf16),
        scatter_scratch(seq_n, (img_n, own, width), bf16),
        scatter_scratch(img_n, (1, own, width), bf16),
        scatter_scratch(img_n, attn_w.shape[1:], bf16),
        scatter_scratch(seq_n, h1.shape[1:], bf16),
    ]

    def kernel(*refs):
        p_in, h_in, w_in, do_ref, b_ref, es_ref, sk_ref, sq_ref, expw_ref, f_ref, outw_ref = refs[:11]
        mid_in, dmid_in, tok_ref, dy_ref, line_ref = refs[11:16]
        st_ref, sum_ref, layer_ref, token_ref, attn_own, expw_own, outw_own = refs[16:23]
        f_own, dh1_own, late_sem = refs[23:26]
        scratch = refs[26:]
        p_ref, h_ref, w_ref, dp_ref, dh1, dattn, out_mid, load_sem = scratch[:8]
        k_buf, v_buf, e_buf, g_buf, dk_buf, dv_buf, do_buf, o_send, o_recv = scratch[8:17]
        expw_held, f_held, outw_held = scratch[17:20]
        more = scratch[20:]
        me = lax.axis_index("seq")
        session.greet()

        def ship(i, j):
            g, p = i // pairs, i % pairs
            return remote(
                do_ref.at[g, :, lanes(((me ^ j) * pairs + p) * 128, 128)],
                do_buf.at[i, j],
                o_send.at[j, i],
                o_recv.at[j, i],
                "seq",
                me ^ j,
            )

        def send(i):
            for j in range(1, seq_n):
                ship(i, j).start()

        each(0, turns, send)
        loads = [
            pltpu.make_async_copy(src, dst, load_sem.at[n])
            for n, (src, dst) in enumerate(
                (
                    (p_in, p_ref),
                    (outw_ref, outw_held),
                    (f_ref, f_held),
                    (expw_ref, expw_held),
                    (h_in, h_ref),
                    (w_in, w_ref),
                )
            )
        ]
        for load in loads:
            load.start()
        exp_out = scatter_ops("img", False, expw_ref, expw_own, *more[:7], held=expw_held)
        f_out = scatter_ops("seq", True, f_ref, f_own, *more[7:14], held=f_held)
        mid_out = scatter_ops(
            "seq", False, outw_ref, out_mid.at[:, 0], *more[14:21], inside=True, held=outw_held
        )
        outw_out = scatter_ops("img", False, out_mid, outw_own, *more[21:28])
        attn_out = scatter_ops("img", False, dattn, attn_own, *more[28:35])
        dh1_out = scatter_ops("seq", True, dh1, dh1_own, *more[35:42])
        exp_out.start()
        mid_out.start()
        f_out.start()
        exp_chunks = expw_ref.shape[1]
        loads[0].wait()

        def turn(i):
            g, p = i // pairs, i % pairs
            query, key, value, low_half, r_query, r_key = load_heads(p_ref, b_ref[p], g, p, rows)
            scale_row = es_ref[p]
            q_unit = query * r_query
            k_unit = key * r_key
            q_full = q_unit * scale_row
            k_buf[...] = k_unit.astype(bf16).reshape(seq_n, rows_b, 128)
            v_buf[...] = value.astype(bf16).reshape(seq_n, rows_b, 128)
            do_buf[i, 0] = do_ref[g, :, lanes((me * pairs + p) * 128, 128)]
            for j in range(1, seq_n):
                ship(i, j).wait_recv()
            d_out = do_buf[i].reshape(rows, 128).astype(f32)
            sid_q = sq_ref[g]
            masks = [low_half, jnp.logical_not(low_half)]
            q_f = [jnp.where(mine, q_full, 0.0) for mine in masks]
            do_f = [jnp.where(mine, d_out, 0.0) for mine in masks]
            q_h = [x.astype(bf16) for x in q_f]
            do_h = [x.astype(bf16) for x in do_f]
            q_t = [jnp.transpose(x).astype(bf16) for x in q_f]
            do_t = [jnp.transpose(x).astype(bf16) for x in do_f]
            total = [jnp.zeros((1, rows), f32)] * 2
            mixed = [jnp.zeros((1, rows), f32)] * 2
            for b in range(seq_n):
                seen = sk_ref[g, b] <= sid_q
                for h in range(2):
                    scores = dot(k_buf[b], q_t[h], ((1,), (0,)))
                    expo = jnp.where(seen, jnp.exp(scores), 0.0)
                    grad = dot(v_buf[b], do_t[h], ((1,), (0,)))
                    e_buf[h, b] = expo
                    g_buf[h, b] = grad
                    total[h] = total[h] + jnp.sum(expo, axis=0, keepdims=True)
                    mixed[h] = mixed[h] + jnp.sum(expo * grad, axis=0, keepdims=True)
            inverse = [1.0 / x for x in total]
            delta = [x * y for x, y in zip(mixed, inverse)]
            acc = [jnp.zeros((128, rows), f32)] * 2
            for b in range(seq_n):
                dv = dk = jnp.zeros((rows_b, 128), f32)
                for h in range(2):
                    probs = e_buf[h, b] * inverse[h]
                    scores_grad = (probs * (g_buf[h, b] - delta[h])).astype(bf16)
                    dv = dv + dot(probs.astype(bf16), do_h[h], ((1,), (0,)))
                    dk = dk + dot(scores_grad, q_h[h], ((1,), (0,)))
                    acc[h] = acc[h] + dot(k_buf[b], scores_grad, ((0,), (0,)))
                dv_buf[b] = dv
                dk_buf[b] = dk
            parts = [acc[0][:64], acc[1][64:]]
            dq = jnp.transpose(jnp.concatenate(parts, axis=0)).astype(bf16).astype(f32)
            dk = dk_buf[...].reshape(rows, 128).astype(bf16).astype(f32)
            dv = dv_buf[...].reshape(rows, 128).astype(bf16).astype(f32)
            dq_raw = scale_row * r_query * (dq - q_unit * half_sums(q_unit * dq, low_half))
            dk_raw = r_key * (dk - k_unit * half_sums(k_unit * dk, low_half))
            together = jnp.concatenate([dq_raw, dk_raw, dv], axis=1).astype(bf16)
            dp_ref[:, g, :, lanes(p * 384, 384)] = together.reshape(seq_n, rows_b, 384)
            sums = [
                jnp.sum(dq_raw, axis=0, keepdims=True),
                jnp.sum(dv, axis=0, keepdims=True),
                jnp.sum(dq * q_full, axis=0, keepdims=True),
                jnp.zeros((5, 128), f32),
            ]
            st_ref[i] = jnp.concatenate(sums, axis=0)

            @pl.when(i == 0)
            def _():
                for load in loads[1:4]:
                    load.wait()
                each(0, img_n, mid_out.step)
                each(0, shrunk_part.shape[1], f_out.step)

            each((i * exp_chunks) // turns, ((i + 1) * exp_chunks) // turns, exp_out.step)

        each(0, turns, turn)
        late = []
        for n, src in enumerate((mid_in, dmid_in)):
            for k in range(pieces):
                low, high = k * wide, min((k + 1) * wide, width)
                dst = p_ref.at[n * pieces + k, :, :, : high - low]
                late.append(pltpu.make_async_copy(src.at[:, :, low:high], dst, late_sem.at[len(late)]))
        for copy in late:
            copy.start()

        def held_rows(n, g):
            parts = [p_ref[n * pieces + k, g, :, : min(wide, width - k * wide)] for k in range(pieces)]
            return jnp.concatenate(parts, axis=1)

        def layer(g):
            total = f_own[pl.ds(g * f_chunks, f_chunks)].reshape(rows_b, width) + line_ref[g, 2:3]
            layer_ref[g] = (held_rows(0, g) + line_ref[g, 1:2] * total).astype(bf16)
            sum_ref[g, 2:3] = jnp.sum(dy_ref[g].astype(f32) * total, axis=0, keepdims=True)

        def token(g):
            grad = dh1_own[pl.ds(g * h_chunks, h_chunks)].reshape(rows_b, width)
            normed, factor = centre(tok_ref[g].astype(f32))
            back = centre_back(normed, factor, grad * line_ref[g, 0:1])
            token_ref[g] = (held_rows(1, g) + back).astype(bf16)
            sum_ref[g, 0:1] = jnp.sum(grad * normed, axis=0, keepdims=True)
            sum_ref[g, 1:2] = jnp.sum(grad, axis=0, keepdims=True)

        mid_out.finish()
        outw_out.start()
        for load in loads[4:]:
            load.wait()

        def columns(t):
            return lanes(t * tile, tile)

        def weight_grad(t):
            left = h_ref[:, :, :, columns(t)].reshape(seq_n * local, tile)
            part = dot(left, dp_ref[...].reshape(seq_n * local, wide), ((0,), (0,)))
            dattn[pl.ds(t * blocks_per_tile, blocks_per_tile)] = part.astype(bf16).reshape(
                blocks_per_tile, w_chunks, w_size, wide
            )

        def input_grad(j):
            def run(t):
                weight = w_ref[pl.ds(t * blocks_per_tile, blocks_per_tile)].reshape(tile, wide)
                part = dot(dp_ref[j].reshape(local, wide), weight, ((1,), (1,)))
                dh1[j, :, :, columns(t)] = part.astype(bf16).reshape(chunks, size, tile)

            each(0, width // tile, run)

        own_tile, halves = attn_out.by_blocks(blocks_per_tile, weight_grad)
        take = in_turns(halves, 6)
        outw_out.step(0)
        for k in range(seq_n - 1, 1, -1):
            input_grad(k)
            if k in (3, 2):
                take()
        dh1_out.start_outer()
        own_tile()
        each(0, chunks, dh1_out.step)
        take()
        exp_out.finish()
        input_grad(1)
        take()
        input_grad(0)
        dh1_out.start_inner()
        take()
        take()
        outw_out.finish()
        f_out.finish()
        sum_ref[...] = jnp.zeros_like(sum_ref)
        for copy in late:
            copy.wait()
        each(0, images, layer)
        dh1_out.finish()
        each(0, images, token)
        attn_out.finish()

        def last(i):
            for j in range(1, seq_n):
                ship(i, j).wait_send()

        each(0, turns, last)

    full = pl.BlockSpec(memory_space=VM)
    any_space = pl.BlockSpec(memory_space=pl.ANY)
    sems = pltpu.SemaphoreType.DMA((seq_n, turns))
    return pl.pallas_call(
        kernel,
        out_shape=(
            jax.ShapeDtypeStruct((turns, 8, 128), f32),
            jax.ShapeDtypeStruct((images, 8, width), f32),
            jax.ShapeDtypeStruct(tokens.shape, bf16),
            jax.ShapeDtypeStruct(tokens.shape, bf16),
            jax.ShapeDtypeStruct(attn_w.shape[1:], bf16),
            jax.ShapeDtypeStruct(expw_part.shape[1:], bf16),
            jax.ShapeDtypeStruct((1, own, width), f32),
        ),
        in_specs=[any_space] * 3 + [full] * 5 + [any_space] * 5 + [full] * 3,
        out_specs=(full,) * 7,
        scratch_shapes=[
            VM(shrunk_part.shape[1:], f32),
            VM(h1.shape[1:], f32),
            pltpu.SemaphoreType.DMA((2 * pieces,)),
            VM(packed.shape, f32),
            VM(h1.shape, bf16),
            VM(attn_w.shape, bf16),
            VM(packed.shape, bf16),
            VM(h1.shape, bf16),
            VM(attn_w.shape, bf16),
            VM((img_n, 1, own, width), bf16),
            pltpu.SemaphoreType.DMA((6,)),
            VM((seq_n, rows_b, 128), bf16),
            VM((seq_n, rows_b, 128), bf16),
            VM((2, seq_n, rows_b, rows), f32),
            VM((2, seq_n, rows_b, rows), f32),
            VM((seq_n, rows_b, 128), f32),
            VM((seq_n, rows_b, 128), f32),
            VM((turns, seq_n, rows_b, 128), bf16),
            sems,
            sems,
            VM(expw_part.shape, bf16),
            VM(shrunk_part.shape, bf16),
            VM(outw_part.shape, bf16),
        ]
        + [x for scratch in mids for x in scratch],
        compiler_params=params(cid),
        name="attend_back",
    )(
        packed, h1, attn_w, d_out, bias, scale, sid_k, sid_q, expw_part, shrunk_part, outw_part, mid, d_mid, tokens, cotangent, lines
    )


def gelu_both(x):
    root = 0.7978845608028654
    square = x * x
    bent = jnp.tanh(root * x * (1.0 + 0.044715 * square))
    half = 0.5 * (1.0 + bent)
    slope = half + 0.5 * x * (1.0 - bent * bent) * (root * (1.0 + 3 * 0.044715 * square))
    return x * half, slope


def feed_forward(cid, tokens, context, out_w, cotangent, lines, grad_parts, grad_own, shr_own, exp_w, e_bias):
    seq_n, img_n = lax.axis_size("seq"), lax.axis_size("img")
    outer = seq_n // 2
    rows, width = tokens.shape
    hid_l = exp_w.shape[1]
    ready, later = len(grad_parts), len(grad_own)
    images = ready + later
    g_chunks, g_size, _ = grad_own[0].shape
    chunks, size = images * g_chunks, g_size
    rows_p = rows // images
    w_chunks, w_size, _ = shr_own.shape
    hid_o = w_chunks * w_size
    tile, broad = 256, min(512, hid_l)
    blocks_per_tile = tile // hid_o
    session = Session([], two_level("seq", seq_n) + two_level("img", img_n))

    def kernel(tok_ref, ctx_ref, ow_ref, dy_ref, line_ref, *refs):
        df_refs = refs[:images]
        shr_ref, exp_ref, eb_ref = refs[images : images + 3]
        mid_out, dmid_ref, do_ref, dout_ref, sum_ref, dshr_own, f_out, dexp_out, expb_ref = refs[images + 3 : images + 12]
        x_ref, dh2_ref, attn, da, mid_ref, f_ref, dexp_ref, out_sem = refs[images + 12 : images + 20]
        h2, df, shr, act, slope, dshr, dh2, df_sem, hs, hr, ss, sr, sk, shr_low, *more = refs[images + 20 :]
        stores = [
            pltpu.make_async_copy(src, dst, out_sem.at[n])
            for n, (src, dst) in enumerate(((mid_ref, mid_out), (f_ref, f_out), (dexp_ref, dexp_out)))
        ]
        shr_low[...] = shr_ref[...].astype(bf16)
        df_in = [
            gather_ops("seq", True, df_refs[ready + g], df.at[:, ready + g], *more[14 + 3 * g : 17 + 3 * g])
            for g in range(later)
        ]
        session.greet()
        h2_in = gather_ops("seq", True, x_ref, h2, None, hs, hr)
        shr_in = gather_ops("img", False, shr_low, shr, sk, ss, sr)
        dh2_out = scatter_ops("seq", True, dh2, dh2_ref, *more[:7])
        dshr_out = scatter_ops("img", False, dshr, dshr_own, *more[7:14])
        shr_in.start()

        def columns(t):
            return lanes(t * tile, tile)

        def project(t):
            part = dot(ctx_ref[...], ow_ref[:, columns(t)], ((1,), (0,)))
            attn[:, columns(t)] = part + line_ref[0, 3:4, columns(t)]

        each(0, width // tile, project)
        def middle(g):
            here = some_rows(g * rows_p, rows_p)
            mid = tok_ref[here].astype(f32) + line_ref[g, 0:1] * attn[here]
            mid_ref[here] = mid
            normed, _ = centre(mid)
            low = (normed * line_ref[g, 1:2] + line_ref[g, 2:3]).astype(bf16)
            x_ref[pl.ds(g * g_chunks, g_chunks)] = low.reshape(g_chunks, g_size, width)

        each(0, images, middle)
        stores[0].start()
        h2_in.start()
        for ops in df_in:
            ops.start()
        loads = [pltpu.make_async_copy(ref, df.at[:, g], df_sem.at[g]) for g, ref in enumerate(df_refs[:ready])]
        for load in loads:
            load.start()
        h2[0] = x_ref[...]
        expb_ref[...] = jnp.zeros_like(expb_ref)

        def expand(j):
            def run(t):
                here = lanes(t * broad, broad)
                u = dot(h2[j].reshape(rows, width), exp_ref[:, here], ((1,), (0,))) + eb_ref[:, here]
                value, grad = gelu_both(u)
                act[j, :, here] = value.astype(bf16)
                slope[j, :, here] = grad.astype(bf16)

            each(0, hid_l // broad, run)

        def back_act(j):
            def run(t):
                here = lanes(t * broad, broad)
                weight = shr[pl.ds(t * (broad // hid_o), broad // hid_o)].reshape(broad, width)
                grad = dot(df[j].reshape(rows, width), weight, ((1,), (1,)))
                grad = (slope[j, :, here].astype(f32) * grad).astype(bf16)
                slope[j, :, here] = grad
                expb_ref[:, here] += jnp.sum(grad.astype(f32), axis=0, keepdims=True)

            each(0, hid_l // broad, run)

        def back_input(j):
            def run(t):
                weight = exp_ref[pl.ds(pl.multiple_of(t * tile, tile), tile), :]
                part = dot(slope[j], weight, ((1,), (1,)))
                dh2[j, :, :, columns(t)] = part.astype(bf16).reshape(chunks, size, tile)

            each(0, width // tile, run)

        def shrink(j):
            def run(t):
                weight = shr[:, :, :, columns(t)].reshape(hid_l, tile)
                part = dot(act[j], weight, ((1,), (0,)))
                f_ref[j, :, :, columns(t)] = part.astype(bf16).reshape(chunks, size, tile)

            each(0, width // tile, run)

        def shrink_grad(t):
            left = act[:, :, columns(t)].reshape(seq_n * rows, tile)
            part = dot(left, df[...].reshape(seq_n * rows, width), ((0,), (0,)))
            part = part.astype(bf16).reshape(blocks_per_tile, w_chunks, w_size, width)
            dshr[pl.ds(t * blocks_per_tile, blocks_per_tile)] = part

        def expand_grad(t):
            left = h2[:, :, :, columns(t)].reshape(seq_n * rows, tile)
            part = dot(left, slope[...].reshape(seq_n * rows, hid_l), ((0,), (0,)))
            dexp_ref[pl.ds(pl.multiple_of(t * tile, tile), tile), :] = part.astype(bf16)

        h2_in.near()
        each(0, 2, expand)
        half = chunks // 2
        each(0, half, h2_in.step)
        each(0, w_chunks // 2, shr_in.step)
        each(half, chunks, h2_in.step)
        each(w_chunks // 2, w_chunks, shr_in.step)
        for o in range(1, outer):
            h2_in.handed(o)
        for ops in df_in:
            each(0, g_chunks // 2, ops.step)
        each(2, seq_n, expand)
        for ops in df_in:
            each(g_chunks // 2, g_chunks, ops.step)
            ops.finish()
        for load in loads:
            load.wait()
        own_tile, halves = dshr_out.by_blocks(blocks_per_tile, shrink_grad)
        take = in_turns(halves, 6)
        shr_in.near()
        for o in range(1, img_n // 2):
            shr_in.handed(o)
        shr_in.sent()
        for k in range(seq_n - 1, 1, -1):
            back_act(k)
            back_input(k)
            if k in (3, 2):
                take()
        dh2_out.start_outer()
        own_tile()
        each(0, chunks, dh2_out.step)
        take()
        back_act(1)
        take()
        back_input(1)
        back_act(0)
        take()
        back_input(0)
        dh2_out.start_inner()
        shrink(0)
        take()
        h2_in.sent()
        each(1, seq_n, shrink)
        stores[1].start()
        each(0, width // tile, expand_grad)
        stores[2].start()
        dh2_out.finish()
        sum_ref[...] = jnp.zeros_like(sum_ref)
        def middle_back(g):
            here = some_rows(g * rows_p, rows_p)
            grad = dh2_ref[pl.ds(g * g_chunks, g_chunks)].reshape(rows_p, width)
            normed, factor = centre(mid_ref[here])
            back = centre_back(normed, factor, grad * line_ref[g, 1:2])
            back = dy_ref[here].astype(f32) + back
            dmid_ref[here] = back
            low = (back * line_ref[g, 0:1]).astype(bf16)
            da[here] = low
            sum_ref[g, 0:1] = jnp.sum(grad * normed, axis=0, keepdims=True)
            sum_ref[g, 1:2] = jnp.sum(grad, axis=0, keepdims=True)
            sum_ref[g, 2:3] = jnp.sum(back * attn[here], axis=0, keepdims=True)
            sum_ref[g, 3:4] = jnp.sum(low.astype(f32), axis=0, keepdims=True)

        each(0, images, middle_back)

        def context_grad(t):
            weight = ow_ref[pl.ds(pl.multiple_of(t * tile, tile), tile), :]
            do_ref[:, columns(t)] = dot(da[...], weight, ((1,), (1,))).astype(bf16)

        def out_grad(t):
            part = dot(ctx_ref[:, columns(t)], da[...], ((0,), (0,)))
            dout_ref[pl.ds(pl.multiple_of(t * tile, tile), tile), :] = part.astype(bf16)

        each(0, width // tile, context_grad)
        each(0, width // tile, out_grad)
        dshr_out.finish()
        for store in stores:
            store.wait()

    full = pl.BlockSpec(memory_space=VM)
    any_space = pl.BlockSpec(memory_space=pl.ANY)
    seq_sems = pltpu.SemaphoreType.DMA((seq_n, chunks))
    img_sems = pltpu.SemaphoreType.DMA((img_n, w_chunks))
    grad_sems = pltpu.SemaphoreType.DMA((seq_n, g_chunks))
    return pl.pallas_call(
        kernel,
        out_shape=(
            jax.ShapeDtypeStruct((rows, width), f32),
            jax.ShapeDtypeStruct((rows, width), f32),
            jax.ShapeDtypeStruct((rows, width), bf16),
            jax.ShapeDtypeStruct((width, width), bf16),
            jax.ShapeDtypeStruct((images, 8, width), f32),
            jax.ShapeDtypeStruct(shr_own.shape, f32),
            jax.ShapeDtypeStruct((seq_n, chunks, size, width), bf16),
            jax.ShapeDtypeStruct(exp_w.shape, bf16),
            jax.ShapeDtypeStruct((1, hid_l), f32),
        ),
        in_specs=[full] * 5 + [any_space] * ready + [full] * (later + 3),
        out_specs=(any_space,) + (full,) * 5 + (any_space,) * 2 + (full,),
        scratch_shapes=[
            VM((chunks, size, width), bf16),
            VM((chunks, size, width), f32),
            VM((rows, width), f32),
            VM((rows, width), bf16),
            VM((rows, width), f32),
            VM((seq_n, chunks, size, width), bf16),
            VM(exp_w.shape, bf16),
            pltpu.SemaphoreType.DMA((3,)),
            VM((seq_n, chunks, size, width), bf16),
            VM((seq_n, images, g_chunks, g_size, width), bf16),
            VM((img_n,) + shr_own.shape, bf16),
            VM((seq_n, rows, hid_l), bf16),
            VM((seq_n, rows, hid_l), bf16),
            VM((img_n,) + shr_own.shape, bf16),
            VM((seq_n, chunks, size, width), bf16),
            pltpu.SemaphoreType.DMA((max(ready, 1),)),
            seq_sems,
            seq_sems,
            img_sems,
            img_sems,
            pltpu.SemaphoreType.DMA((w_chunks,)),
            VM(shr_own.shape, bf16),
        ]
        + scatter_scratch(seq_n, (chunks, size, width), bf16)
        + scatter_scratch(img_n, shr_own.shape, bf16)
        + [pltpu.SemaphoreType.DMA((g_chunks,)), grad_sems, grad_sems] * later,
        compiler_params=params(cid),
        name="feed_forward",
    )(tokens, context, out_w, cotangent, lines, *grad_parts, *grad_own, shr_own, exp_w, e_bias)


def normalize(values):
    centered = values - jnp.mean(values, axis=-1, keepdims=True)
    return centered * lax.rsqrt(jnp.mean(centered * centered, axis=-1, keepdims=True) + 1e-06)


def pad_to(x, size, axis):
    widths = [(0, 0)] * x.ndim
    widths[axis] = (0, size - x.shape[axis])
    return jnp.pad(x, widths)


def mm(a, b):
    return jnp.dot(a, b, preferred_element_type=f32)


def mm_nt(a, b):
    return lax.dot_general(a, b, (((1,), (1,)), ((), ())), preferred_element_type=f32)


def mm_tn(a, b):
    return lax.dot_general(a, b, (((0,), (0,)), ((), ())), preferred_element_type=f32)


def body(
    tokens,
    cotangent,
    condition,
    scale_sizes,
    mod_weight,
    mod_bias,
    attn_weight,
    query_bias,
    value_bias,
    out_weight,
    out_bias,
    expand_weight,
    expand_bias,
    shrink_weight,
    shrink_bias,
    log_scale,
):
    images, rows, width = tokens.shape
    heads = log_scale.shape[0]
    headdim = width // heads
    seq_n = lax.axis_size("seq")
    img_n = lax.axis_size("img")
    seq_i = lax.axis_index("seq")
    img_i = lax.axis_index("img")
    rank = img_i * seq_n + seq_i
    ranks = img_n * seq_n
    own = width // ranks
    rows_p = -(-rows // 16) * 16
    dim_l = width // seq_n
    pairs = dim_l // 128
    hidden = expand_bias.shape[0] * ranks
    hid_l = hidden // seq_n
    hid_o = hidden // ranks
    mods = mod_weight.shape[1]
    mod_o = mods // ranks

    mod_l = mods // seq_n
    blk = own * seq_n

    weights = (mod_weight, attn_weight, expand_weight)
    if own % 16 or hid_o % 128:
        attn_cut = (
            attn_weight.astype(bf16)
            .reshape(own, 3, seq_n, pairs, 128)
            .transpose(2, 0, 3, 1, 4)
            .reshape(seq_n, own, 3 * dim_l)
        )
        exp_cut = (
            expand_weight.astype(bf16)
            .reshape(own, img_n, seq_n, hid_o)
            .transpose(2, 0, 1, 3)
            .reshape(seq_n, own, hid_l)
        )
        mod_cut = mod_weight.astype(bf16).reshape(own, seq_n, mod_l).transpose(1, 0, 2)
        weights = (mod_cut, attn_cut, exp_cut)
    silu_cond = jax.nn.silu(condition).astype(bf16).astype(f32)
    small_bias = jnp.concatenate([query_bias, value_bias, out_bias, shrink_bias, expand_bias, mod_bias])
    small_bias = lax.reduce_precision(small_bias, 8, 7)
    bias_n = small_bias.shape[0]
    bias_rows = -(-bias_n // 1024) * 8
    small_bias = pad_to(small_bias, bias_rows * 128, 0).reshape(1, bias_rows, 128)
    cond_cut = silu_cond.reshape(images, img_n, seq_n, own).transpose(1, 2, 0, 3).reshape(img_n, seq_n * images, own)
    small = jnp.concatenate(
        [pad_to(cond_cut, 128, 2), jnp.broadcast_to(small_bias, (img_n, bias_rows, 128))], axis=1
    )
    early = seq_n // 4 if own % 16 == 0 else 0
    mod_all, bias_all, cond_rows, modw_cut, attn_b, exp_b, attn_early, out_img = opening(
        1, *weights, out_weight, small, seq_n, images, pairs, early
    )
    out_img = out_img.reshape(img_n, own, width)
    exp_b = exp_b.reshape(blk, hid_l)

    def weight_chunks(x):
        step = blk // 8 if blk % 128 == 0 else blk // 4
        return x.reshape(x.shape[:-2] + (blk // step, step, x.shape[-1]))

    def hidden_chunks(x):
        step = 16
        return x.reshape(x.shape[:-2] + (hid_o // step, step, x.shape[-1]))

    tiles = mod_l // 128
    modulation = mod_all[:, : tiles * images].reshape(seq_n, tiles, images, 128).transpose(2, 0, 1, 3)
    bias_all = bias_all.reshape(seq_n, img_n, bias_rows * 128)[:, :, :bias_n].transpose(1, 0, 2)
    q_bias = bias_all[:, :, :own].reshape(width)
    v_bias = bias_all[:, :, own : 2 * own].reshape(width)
    o_bias = bias_all[:, :, 2 * own : 3 * own].reshape(width)
    s_bias = bias_all[:, :, 3 * own : 4 * own].reshape(width)
    e_bias = bias_all[:, :, 4 * own : 4 * own + hid_o]
    e_bias = lax.dynamic_slice_in_dim(e_bias, seq_i, 1, 1).reshape(hid_l)
    m_bias = bias_all[:, :, 4 * own + hid_o :].reshape(mods)
    modulation = modulation.reshape(images, mods) + m_bias[None]
    qb_l = lax.dynamic_slice_in_dim(q_bias, seq_i * dim_l, dim_l, 0).reshape(pairs, 1, 128)
    vb_l = lax.dynamic_slice_in_dim(v_bias, seq_i * dim_l, dim_l, 0).reshape(pairs, 1, 128)
    pair_bias = jnp.concatenate([qb_l, jnp.zeros_like(qb_l), vb_l], axis=2)
    head_scale = jnp.exp(jnp.repeat(log_scale, headdim))
    pair_scale = lax.dynamic_slice_in_dim(head_scale, seq_i * dim_l, dim_l, 0).reshape(pairs, 1, 128)
    gain_attn, gain_mlp, scale_attn, scale_mlp, shift_attn, shift_mlp = jnp.split(
        modulation[:, None, :], 6, axis=-1
    )

    scales = jnp.arange(scale_sizes.shape[1])
    ends = jnp.sum(jnp.where(scales[:, None] <= scales[None], scale_sizes[:, :, None], 0), axis=1)
    offset = jnp.arange(rows_p, dtype=jnp.int32)
    place = (seq_i ^ jnp.arange(seq_n, dtype=jnp.int32))[:, None] * rows + offset[None]
    sid = jnp.sum((place[None, :, :, None] >= ends[:, None, None, :]).astype(jnp.int32), axis=-1)
    sid = jnp.where(offset[None, None] < rows, sid, 1 << 20)
    sid_q = sid.reshape(images, 1, seq_n * rows_p)
    sid_k = sid[..., None]

    tokens_low = pad_to(tokens, rows_p, 1)
    grad_low = pad_to(cotangent, rows_p, 1)
    resid_in = tokens_low.astype(f32)
    grad_out = grad_low.astype(f32)
    local = images * rows_p

    def chunked(x):
        return x.reshape(x.shape[: x.ndim - 3] + (local // 16, 16, width))

    normed_in = normalize(resid_in)
    attn_input = (normed_in * (1.0 + scale_attn) + shift_attn).astype(bf16)
    grad_shrunk = (grad_out * gain_mlp).astype(bf16)
    grad_chunks = grad_shrunk.reshape(images, rows_p // 16, 16, width)
    ready = images // 2
    context_low, packed, h1, attn_w, *gathered = attend(
        5,
        chunked(attn_input),
        attn_b if early else weight_chunks(attn_b.reshape(blk, 3 * dim_l)),
        attn_early,
        early,
        pair_bias,
        pair_scale,
        sid_k,
        sid_q,
        out_img,
        weight_chunks(exp_b),
        [grad_chunks[g] for g in range(ready)],
    )
    df_ready, out_w, exp_w = gathered[:ready], gathered[ready], gathered[ready + 1]
    context_low = context_low.reshape(local, width)
    out_w = out_w.reshape(width, width)
    exp_w = exp_w.reshape(width, hid_l)
    shrb_part = jnp.sum(grad_shrunk.astype(f32), axis=(0, 1))
    lines = [gain_attn, 1.0 + scale_mlp, shift_mlp, jnp.broadcast_to(o_bias, (images, 1, width))]
    lines = jnp.concatenate(lines + [jnp.zeros((images, 4, width), f32)], axis=1)
    resid_mid, grad_mid, grad_context, outw_part, mid_sums, shrw_own, shrunk_part, expw_part, expb_part = feed_forward(
        7,
        tokens_low.reshape(local, width),
        context_low,
        out_w,
        grad_low.reshape(local, width),
        lines,
        df_ready,
        [grad_chunks[g] for g in range(ready, images)],
        hidden_chunks(shrink_weight),
        exp_w,
        e_bias.reshape(1, hid_l),
    )
    resid_mid = resid_mid.reshape(images, rows_p, width)
    grad_mid = grad_mid.reshape(images, rows_p, width)
    grad_context = grad_context.reshape(images, rows_p, width)
    outw_part = outw_part.reshape(img_n, seq_n, own, width)
    grad_scale_mlp, grad_shift_mlp, grad_gain_attn = mid_sums[:, 0], mid_sums[:, 1], mid_sums[:, 2]
    outb_part = jnp.sum(mid_sums[:, 3], axis=0)
    shrw_own = shrw_own.reshape(hid_o, width)
    expb_part = expb_part.reshape(hid_l)
    expw_part = expw_part.reshape(img_n, blk, hid_l)

    lines = [1.0 + scale_attn, gain_mlp, jnp.broadcast_to(s_bias, (images, 1, width))]
    lines = jnp.concatenate(lines + [jnp.zeros((images, 5, width), f32)], axis=1)
    sums, row_sums, layer_out, token_grad, attnw_blk, expw_blk, outw_own = attend_back(
        11,
        packed,
        h1,
        attn_w,
        grad_context,
        pair_bias,
        pair_scale,
        sid_k,
        sid_q,
        weight_chunks(expw_part),
        shrunk_part,
        outw_part,
        resid_mid,
        grad_mid,
        tokens_low,
        grad_low,
        lines,
    )
    grad_scale_attn, grad_shift_attn, grad_gain_mlp = row_sums[:, 0], row_sums[:, 1], row_sums[:, 2]
    sums = jnp.sum(sums.reshape(images, pairs, 8, 128), axis=0)
    qb_part = sums[:, 0].reshape(dim_l)
    vb_part = sums[:, 1].reshape(dim_l)
    logs_part = jnp.sum(sums[:, 2].reshape(dim_l // headdim, headdim), axis=1)
    outw_own = outw_own.reshape(own, width)

    grad_mod = jnp.concatenate(
        [grad_gain_attn, grad_gain_mlp, grad_scale_attn, grad_scale_mlp, grad_shift_attn, grad_shift_mlp],
        axis=-1,
    )
    grad_mod = grad_mod.reshape(images, seq_n, tiles, 128).transpose(1, 2, 0, 3).reshape(seq_n, tiles * images, 128)
    grad_mod = pad_to(grad_mod, -(-tiles * images // 8) * 8, 1)

    def lined(vector, count):
        return pad_to(vector.reshape(count, -1), 128, 1)

    heads_l = heads // seq_n
    logs_row = lax.dynamic_update_slice_in_dim(jnp.zeros((128,), f32), logs_part, seq_i * heads_l, 0)
    bias_mine = jnp.concatenate(
        [
            lined(shrb_part, img_n),
            lined(outb_part, img_n),
            pad_to(logs_row[None], 8, 0),
            lined(qb_part, img_n // seq_n),
            lined(vb_part, img_n // seq_n),
        ]
    )
    bias_mine = pad_to(bias_mine, -(-bias_mine.shape[0] // 8) * 8, 0)
    mine = jnp.concatenate([grad_mod, jnp.broadcast_to(bias_mine[None], (seq_n,) + bias_mine.shape)], axis=1)
    modw_own, attnw_own, expw_own, bias_own, modb_all, cond_sum = closing(
        13,
        mine,
        lined(expb_part, img_n),
        cond_rows,
        modw_cut,
        attnw_blk.reshape(seq_n, own, 3 * dim_l),
        expw_blk.reshape(seq_n, own, hid_l),
        images,
        pairs,
    )

    modw_own, attnw_own, expw_own, outw_own, shrw_own, shrb_own, outb_own, qb_own, vb_own, expb_own, logs_total = finishing(
        modw_own, attnw_own, expw_own, bias_own, outw_own, shrw_own, heads
    )
    modb_own = lax.dynamic_slice_in_dim(modb_all[:, :tiles].reshape(mods), rank * mod_o, mod_o, 0)
    grad_silu = cond_sum[:, :, :own].reshape(img_n, seq_n, images, own).transpose(2, 0, 1, 3).reshape(images, width)
    cond_grad = jax.vjp(jax.nn.silu, condition)[1](grad_silu)[0]
    return (
        layer_out[:, :rows],
        token_grad[:, :rows],
        cond_grad,
        modw_own,
        modb_own,
        attnw_own,
        qb_own,
        vb_own,
        outw_own,
        outb_own,
        expw_own,
        expb_own,
        shrw_own,
        shrb_own,
        logs_total,
    )


def solution(mesh):
    both = P(("img", "seq"))
    rows = P(("img", "seq"), None)
    return jax.shard_map(
        body,
        mesh=mesh,
        in_specs=(
            P("img", "seq", None),
            P("img", "seq", None),
            P("img", None),
            P("img", None),
            rows,
            both,
            rows,
            both,
            both,
            rows,
            both,
            rows,
            both,
            rows,
            both,
            P(),
        ),
        out_specs=(
            P("img", "seq", None),
            P("img", "seq", None),
            P("img", None),
            rows,
            both,
            rows,
            both,
            both,
            rows,
            both,
            rows,
            both,
            rows,
            both,
            P(),
        ),
        check_vma=False,
    )
```
